32 devices in a mesh: dp: 4 (over x, core), blk: 8 (over z, y).
Axes of the slice: x: 2, y: 2, z: 4, core: 2. Of those that a mesh axis runs over, the one named last changes fastest.
Arguments:
- hidden_in: bfloat16 [2048, 8, 1024], P('blk', 'dp'), may hold values from -6 to 6
- first_values: bfloat16 [2048, 8, 1024], P('blk', 'dp'), may hold values from -13 to 13
- doc_lengths: int32 [8, 8], P('dp'), may hold values from 1 to 1024, 2048 in all within a row
- w_query: bfloat16 [1024, 1024], replicated, may hold values from -0.25 to 0.25
- w_key: bfloat16 [1024, 1024], replicated, may hold values from -0.25 to 0.25
- w_value: bfloat16 [1024, 1024], replicated, may hold values from -0.1875 to 0.1875
- w_out: bfloat16 [1024, 1024], replicated, may hold values from -0.75 to 0.75
- w_gate: bfloat16 [1024, 2816], replicated, may hold values from -0.1875 to 0.1875
- w_up: bfloat16 [1024, 2816], replicated, may hold values from -0.1875 to 0.1875
- w_down: bfloat16 [2816, 1024], replicated, may hold values from -0.109375 to 0.109375
- attn_gain: float32 [1024], replicated, may hold values from 0.5 to 1.5
- ffn_gain: float32 [1024], replicated, may hold values from 0.5 to 1.5
- out_cotangent: bfloat16 [2048, 8, 1024], P('blk', 'dp'), may hold values from -6 to 6
Outputs:
- block_out: bfloat16 [2048, 8, 1024], P('blk', 'dp')
- grad_input: float32 [2048, 8, 1024], P('blk', 'dp')
- grad_first: float32 [2048, 8, 1024], P('blk', 'dp')
- grad_query: float32 [1024, 1024], P('dp', 'blk')
- grad_key: float32 [1024, 1024], P('dp', 'blk')
- grad_value: float32 [1024, 1024], P('dp', 'blk')
- grad_project: float32 [1024, 1024], P('dp', 'blk')
- grad_gate: float32 [1024, 2816], P('dp', 'blk')
- grad_up: float32 [1024, 2816], P('dp', 'blk')
- grad_down: float32 [2816, 1024], P('dp', 'blk')
- grad_attn_gain: float32 [1024], replicated
- grad_ffn_gain: float32 [1024], replicated
- first_msq: float32 [], replicated
- mixed_msq: float32 [], replicated
The draws below stay inside these ranges and needn't reach their ends.
Inputs may be any that keep to these rules, and one draw needn't show every extreme that they name: `doc_lengths`: the 8 lengths of a row sum to 2048.
All inputs are finite; a program needn't handle non-finite values.
Results may differ from the reference program's by a relative error of at most 0.033.
Values may be sent and summed in bfloat16 or wider, within the bound.
A program may use at most 320 MiB of HBM per device.

```python
import math
import jax
import jax.numpy as jnp
import numpy as np
from jax import lax

D = 1024
HEADS = 16
HEAD_DIM = 64
FF = 2816
LENGTH = 2048
DOCS = 8
SEQS = 8


def draw_first_values(key, part):
    key_main = jax.random.fold_in(key, 0)
    along_row = jnp.arange(LENGTH, dtype=jnp.float32)[:, None, None] / LENGTH
    along_seqs = jnp.arange(SEQS, dtype=jnp.float32)[None, :, None] / SEQS
    scales = 0.5 * jnp.exp(jnp.log(3.0) * along_row + jnp.log(1.7) * along_seqs)
    entries = jnp.clip(jax.random.normal(key_main, (LENGTH, SEQS, D), jnp.float32), -5.0, 5.0)
    return (entries * scales).astype(jnp.bfloat16)


def level_of(stream_key, dims, pieces, low, largest):
    gain, own = 1.0, jax.random.fold_in(stream_key, 6)
    for position, shards_of in pieces:
        heights = jnp.exp(jax.random.uniform(jax.random.fold_in(own, position), (shards_of,), jnp.float32, low / len(pieces), largest / len(pieces)))
        gain = gain * jnp.repeat(heights, dims[position] // shards_of).reshape([-1 if axis == position else 1 for axis in range(len(dims))])
    return gain


def length_profile(number_of, total, limit, skew):
    weights = [(1 << 20) // math.isqrt(grade ** skew) + 1 for grade in range(2, number_of + 1)]
    rest, holding = total - limit - (number_of - 1), [1] * (number_of - 1)
    while rest > 0:
        candidates = [i for i in range(number_of - 1) if holding[i] < limit]
        pool, budget = sum([weights[i] for i in candidates]), rest
        for i in candidates:
            addition = min(limit - holding[i], max(1, budget * weights[i] // pool), rest)
            holding[i] = holding[i] + addition
            rest = rest - addition
    return np.array([limit] + holding)


def uneven_parts(key, number_of, total, reach, slope):
    if number_of == 2:
        one = jax.random.randint(key, (), max(1, total - reach), min(reach, total - 1) + 1)
        return jnp.stack([one, total - one])
    tallies = jnp.asarray(length_profile(number_of, total, reach, slope), jnp.int32)
    couples = (number_of - 1) // 2
    giver, taker = tallies[1:1 + 2 * couples:2], tallies[2:2 + 2 * couples:2]
    slack = jnp.minimum(giver - 1, reach - taker)
    moved = jax.random.randint(jax.random.fold_in(key, 1), (couples,), 0, 1 << 20) % (slack + 1)
    tallies = tallies.at[1:1 + 2 * couples:2].set(giver - moved).at[2:2 + 2 * couples:2].set(taker + moved)
    return tallies[jax.random.permutation(jax.random.fold_in(key, 2), number_of)]


def noise(key, shape, width, reach, pieces=(), kind=jnp.bfloat16):
    array = width * jax.random.normal(key, shape, jnp.float32)
    if pieces:
        array = array * level_of(key, shape, pieces, -0.22, 0.18)
    return jnp.clip(array, -reach, reach).astype(kind)


def setup_inputs(seed: int = 0) -> dict:
    key_of = jax.random.split(jax.random.key(seed), 14)
    return {
        "hidden_in": noise(key_of[0], (LENGTH, SEQS, D), 1.0, 6.0, ((0, 8), (1, 4))),
        "first_values": draw_first_values(jax.random.fold_in(key_of[13], 71), 0),
        "doc_lengths": jax.vmap(lambda own: uneven_parts(own, DOCS, LENGTH, LENGTH // 2, 2))(jax.random.split(key_of[2], SEQS)).reshape((SEQS, DOCS)).astype(jnp.int32),
        "w_query": noise(key_of[3], (D, D), (D // 2) ** -0.5, 0.25),
        "w_key": noise(key_of[4], (D, D), (D // 2) ** -0.5, 0.25),
        "w_value": noise(key_of[5], (D, D), D ** -0.5, 0.1875),
        "w_out": noise(key_of[6], (D, D), (D // 16) ** -0.5, 0.75),
        "w_gate": noise(key_of[7], (D, FF), D ** -0.5, 0.1875),
        "w_up": noise(key_of[8], (D, FF), D ** -0.5, 0.1875),
        "w_down": noise(key_of[9], (FF, D), FF ** -0.5, 0.109375),
        "attn_gain": jnp.clip(1.0 + 0.1 * jax.random.normal(key_of[10], (D,), jnp.float32), 0.5, 1.5),
        "ffn_gain": jnp.clip(1.0 + 0.1 * jax.random.normal(key_of[11], (D,), jnp.float32), 0.5, 1.5),
        "out_cotangent": noise(key_of[12], (LENGTH, SEQS, D), 1.0, 6.0, ((0, 8), (1, 4))),
    }


@jax.custom_vjp
def low(v):
    return lax.optimization_barrier(v.astype(jnp.bfloat16)).astype(jnp.float32)

@jax.custom_vjp
def low_back(v):
    return v

def low_keep(v):
    return (low(v), None)

def low_pass(kept, grad):
    return (grad,)

def back_keep(v):
    return (v, None)

def back_low(kept, grad):
    return (low(grad),)
low.defvjp(low_keep, low_pass)
low_back.defvjp(back_keep, back_low)
epsilon = 1e-06

def documents(doc_lengths, row_length):
    doc_ends = jnp.cumsum(doc_lengths, axis=1).astype(jnp.int32)
    places = jnp.arange(row_length, dtype=jnp.int32)
    passed = (doc_ends[:, None, :] <= places[None, :, None]).astype(jnp.int32)
    segment = lax.optimization_barrier(jnp.sum(passed, axis=2)).astype(jnp.int32)
    doc_start = lax.optimization_barrier(jnp.sum(passed * doc_lengths[:, None, :], axis=2)).astype(jnp.int32)
    return (segment, (places[None, :] - doc_start).astype(jnp.int32))

def matmul(left, right):
    return jnp.dot(left, right, precision=lax.Precision.HIGHEST)

def rms_scaled(values, gain_vec):
    return values * lax.rsqrt(lax.optimization_barrier(jnp.mean(values * values, axis=-1, keepdims=True)) + epsilon) * gain_vec

def rotate(values, positions):
    half_dim = HEAD_DIM // 2
    inverse_freq = jnp.power(10000.0, -jnp.arange(half_dim, dtype=jnp.float32) * 2.0 / HEAD_DIM)
    angles = positions.astype(jnp.float32)[:, None] * inverse_freq[None, :]
    cos_table = jnp.cos(angles)[:, None, :]
    sin_table = jnp.sin(angles)[:, None, :]
    shaped = values.reshape(values.shape[0], HEADS, HEAD_DIM)
    first_half = shaped[..., :half_dim]
    second_half = shaped[..., half_dim:]
    turned = jnp.concatenate([first_half * cos_table - second_half * sin_table, second_half * cos_table + first_half * sin_table], axis=-1)
    return turned.reshape(values.shape)

def attend(queries, keys_rot, mixed_low, segment):
    length = queries.shape[0]
    q_rows = min(512, length)
    n_blocks = length // q_rows
    key_four = keys_rot.reshape(length, HEADS, HEAD_DIM)
    value_four = mixed_low.reshape(length, HEADS, HEAD_DIM)
    key_index = jnp.arange(length, dtype=jnp.int32)
    score_scale = HEAD_DIM ** (-0.5)

    def one_block(block_item):
        query_block, start = block_item
        scores = low_back(jnp.einsum('qhd,khd->hqk', query_block, key_four, precision=lax.Precision.HIGHEST) * score_scale)
        query_index = start + jnp.arange(q_rows, dtype=jnp.int32)
        segment_query = lax.dynamic_slice_in_dim(segment, start, q_rows)
        allowed = (key_index[None, :] <= query_index[:, None]) & (segment[None, :] == segment_query[:, None])
        scores = jnp.where(allowed[None], scores, -1e+30)
        shifted = jnp.exp(scores - lax.optimization_barrier(jnp.max(scores, axis=-1, keepdims=True)))
        probs = shifted / lax.optimization_barrier(jnp.sum(shifted, axis=-1, keepdims=True))
        result = jnp.einsum('hqk,khd->qhd', low(probs), value_four, precision=lax.Precision.HIGHEST)
        return result.reshape(q_rows, HEADS * HEAD_DIM)
    starts = jnp.arange(n_blocks, dtype=jnp.int32) * q_rows
    blocks = lax.map(jax.checkpoint(one_block), (queries.reshape(n_blocks, q_rows, HEADS, HEAD_DIM), starts))
    return blocks.reshape(length, HEADS * HEAD_DIM)

def layer(resid_in, first_vals, w_query, w_key, w_value, w_out, w_gate, w_up, w_down, attn_gain, ffn_gain, segment, positions):
    normed_in = low(rms_scaled(resid_in, attn_gain))
    queries = low(rotate(low_back(matmul(normed_in, w_query)), positions))
    keys_rot = low(rotate(low_back(matmul(normed_in, w_key)), positions))
    mixed = 0.5 * low_back(matmul(normed_in, w_value)) + 0.5 * first_vals
    attended = low(low_back(attend(queries, keys_rot, low(mixed), segment)))
    resid_mid = resid_in + low_back(matmul(attended, w_out))
    normed_mid = low(rms_scaled(resid_mid, ffn_gain))
    gate_pre = low_back(matmul(normed_mid, w_gate))
    up_pre = low_back(matmul(normed_mid, w_up))
    inner_low = low(jax.nn.silu(gate_pre) * up_pre)
    return (resid_mid + low_back(matmul(inner_low, w_down)), mixed)

def reference(hidden_in, first_values, doc_lengths, w_query, w_key, w_value, w_out, w_gate, w_up, w_down, attn_gain, ffn_gain, out_cotangent):
    params = tuple((weight_arr.astype(jnp.float32) for weight_arr in (w_query, w_key, w_value, w_out, w_gate, w_up, w_down, attn_gain, ffn_gain)))
    segment_all, position_all = documents(doc_lengths, LENGTH)
    rows_in = jnp.transpose(hidden_in.astype(jnp.float32), (1, 0, 2))
    rows_first = jnp.transpose(first_values.astype(jnp.float32), (1, 0, 2))
    rows_cot = jnp.transpose(out_cotangent.astype(jnp.float32), (1, 0, 2))

    def one_row(totals, row_item):
        row_in, row_first, row_cot, segment, positions = row_item

        def layer_of(resid_in, first_vals, *weights_now):
            return layer(resid_in, first_vals, *weights_now, segment, positions)
        out_row, pullback, mixed = jax.vjp(layer_of, row_in, row_first, *params, has_aux=True)
        grads = pullback(row_cot)
        totals = tuple((acc_total + new_grad for acc_total, new_grad in zip(totals, grads[2:])))
        return (totals, (out_row, grads[0], grads[1], jnp.sum(mixed * mixed)))
    zero_grads = tuple((jnp.zeros_like(weight_arr) for weight_arr in params))
    totals, (outs_rows, grad_in_rows, grad_first_rows, mixed_sq) = lax.scan(one_row, zero_grads, (rows_in, rows_first, rows_cot, segment_all, position_all))
    n_entries = SEQS * LENGTH * D
    first_f = first_values.astype(jnp.float32)
    return (jnp.transpose(outs_rows, (1, 0, 2)).astype(jnp.bfloat16), jnp.transpose(grad_in_rows, (1, 0, 2)), jnp.transpose(grad_first_rows, (1, 0, 2)), totals[0], totals[1], totals[2], totals[3], totals[4], totals[5], totals[6], totals[7], totals[8], jnp.sum(first_f * first_f) / n_entries, jnp.sum(mixed_sq) / n_entries)
```

```python
import functools

import jax
import jax.numpy as jnp
from jax import lax
from jax.experimental import pallas as pl
from jax.experimental.pallas import tpu as pltpu
from jax.sharding import PartitionSpec as P

HEADS = 16
HEAD_DIM = 64
NEG = -1e30
EPS = 1e-06
F32 = jnp.float32
BF16 = jnp.bfloat16
VMEM_LIMIT = 56 * 2**20


def dot(a, b):
    return jnp.dot(a, b, preferred_element_type=F32)


def dot_nt(a, b):
    return lax.dot_general(a, b, (((1,), (1,)), ((), ())), preferred_element_type=F32)


def dot_tn(a, b):
    return lax.dot_general(a, b, (((0,), (0,)), ((), ())), preferred_element_type=F32)


def swap_halves(v):
    half = HEAD_DIM // 2
    width = v.shape[-1]
    lane = lax.broadcasted_iota(jnp.int32, v.shape, v.ndim - 1)
    left = pltpu.roll(v, width - half, v.ndim - 1)
    right = pltpu.roll(v, half, v.ndim - 1)
    return jnp.where(lane % HEAD_DIM < half, left, right)


def qkv_kernel(rows, length, width, normed_ref, first_ref, cos_ref, sin_ref, wq_ref, wk_ref, wv_ref, *outs):
    out_refs, sums_ref = outs[:rows], outs[rows]
    chunk = wq_ref.shape[1]
    first_sum = jnp.zeros((1, chunk), F32)
    mixed_sum = jnp.zeros((1, chunk), F32)
    for r in range(rows):
        at = pl.ds(r * length, length)
        normed = normed_ref[at, :]
        cos, sin = cos_ref[at, :], sin_ref[at, :]
        for which, w_ref in ((0, wq_ref), (1, wk_ref)):
            raw = dot(normed, w_ref[...])
            for c in range(chunk // 128):
                part = raw[:, c * 128 : (c + 1) * 128]
                turned = (part * cos + swap_halves(part) * sin).astype(BF16)
                for s in range(128 // width):
                    out_refs[r][c * (128 // width) + s, which] = turned[:, s * width : (s + 1) * width]
        first = first_ref[at, :].astype(F32)
        mixed = 0.5 * dot(normed, wv_ref[...]) + 0.5 * first
        first_sum = first_sum + jnp.sum(first * first, axis=0, keepdims=True)
        mixed_sum = mixed_sum + jnp.sum(mixed * mixed, axis=0, keepdims=True)
        low = mixed.astype(BF16)
        for s in range(chunk // width):
            out_refs[r][s, 2] = low[:, s * width : (s + 1) * width]
    sums_ref[0, 0:1] = first_sum
    sums_ref[0, 1:2] = mixed_sum


def project_qkv(normed, first, cos, sin, w_query, w_key, w_value, rows, n_blk):
    tokens, model = normed.shape
    length, width = tokens // rows, model // n_blk
    chunk = 256
    steps = model // chunk
    full = lambda cols: pl.BlockSpec((tokens, cols), lambda j: (0, 0))
    weight = pl.BlockSpec((model, chunk), lambda j: (0, j))
    return pl.pallas_call(
        functools.partial(qkv_kernel, rows, length, width),
        grid=(steps,),
        in_specs=[
            full(model),
            pl.BlockSpec((tokens, chunk), lambda j: (0, j)),
            full(128),
            full(128),
            weight,
            weight,
            weight,
        ],
        out_specs=[pl.BlockSpec((chunk // width, 3, length, width), lambda j: (j, 0, 0, 0))] * rows
        + [pl.BlockSpec((1, 2, chunk), lambda j: (j, 0, 0))],
        out_shape=[jax.ShapeDtypeStruct((n_blk, 3, length, width), BF16)] * rows
        + [jax.ShapeDtypeStruct((steps, 2, chunk), F32)],
        compiler_params=pltpu.CompilerParams(vmem_limit_bytes=VMEM_LIMIT),
        cost_estimate=pl.CostEstimate(
            flops=6 * tokens * model * model, bytes_accessed=6 * model * model + 10 * tokens * model, transcendentals=0
        ),
        name="qkv",
    )(normed, first, cos, sin, w_query, w_key, w_value)


def doc_ends(lens_ref, row, n_docs):
    ends, total = [], jnp.int32(0)
    for d in range(n_docs):
        total = total + lens_ref[row * n_docs + d]
        ends.append(total)
    return ends


def start_rows(ends, tile, length, heads):
    place = tile * length + lax.broadcasted_iota(jnp.int32, (1, length), 1)
    start = jnp.zeros((1, length), jnp.int32)
    for end in ends:
        start = jnp.where(end <= place, end, start)
    return jnp.concatenate([start] * heads, axis=1), jnp.concatenate([place] * heads, axis=1)


def head_masks(heads, width):
    lane = lax.broadcasted_iota(jnp.int32, (1, width), 1) // HEAD_DIM
    return [jnp.where(lane == h, 1.0, 0.0).astype(BF16) for h in range(heads)]


def by_head(values, masks):
    return jnp.concatenate([values * mask for mask in masks], axis=0)


def attn_fwd_kernel(row, n_docs, heads, lens_ref, qkv_ref, o_ref, low_ref, lse_ref, acc_ref):
    length, width = qkv_ref.shape[2:]
    i = pl.program_id(0)
    ends = doc_ends(lens_ref, row, n_docs)
    start, place = start_rows(ends, i, length, heads)
    lowest = jnp.int32(0)
    for end in ends:
        lowest = jnp.where(end <= i * length, end, lowest)
    lowest = lax.div(lowest, jnp.int32(length))
    masks = head_masks(heads, width)
    queries = by_head(qkv_ref[i, 0] * jnp.asarray(HEAD_DIM**-0.5, BF16), masks)

    def tile(step, carry):
        run_max, run_sum = carry
        j = i - step
        scores = dot_nt(qkv_ref[j, 1], queries)
        key = j * length + lax.broadcasted_iota(jnp.int32, scores.shape, 0)
        scores = jnp.where((key <= place) & (key >= start), scores, NEG)
        new_max = jnp.maximum(run_max, jnp.max(scores, axis=0, keepdims=True))
        weights = jnp.exp(scores - new_max)
        factor = jnp.exp(run_max - new_max)
        run_sum = run_sum * factor + jnp.sum(weights, axis=0, keepdims=True)
        acc_ref[...] = acc_ref[...] * factor + dot_tn(qkv_ref[j, 2], weights.astype(BF16))
        return new_max, run_sum

    acc_ref[...] = jnp.zeros_like(acc_ref)
    run_max, run_sum = lax.fori_loop(
        0,
        i - lowest + 1,
        tile,
        (jnp.full((1, heads * length), NEG, F32), jnp.zeros((1, heads * length), F32)),
    )
    result = acc_ref[...] / run_sum
    joined = jnp.concatenate(
        [
            result[h * HEAD_DIM : (h + 1) * HEAD_DIM, h * length : (h + 1) * length]
            for h in range(heads)
        ],
        axis=0,
    )
    attended = joined.T
    o_ref[0] = attended
    low_ref[0] = attended.astype(BF16)
    total = run_max + jnp.log(run_sum)
    for h in range(heads):
        lse_ref[0, h : h + 1, :] = total[:, h * length : (h + 1) * length]


def attn_fwd(lens, qkv, row, n_docs):
    n_blk, _, length, width = qkv.shape
    heads = width // HEAD_DIM
    tile = pl.BlockSpec((1, length, width), lambda i, lens: (i, 0, 0))
    return pl.pallas_call(
        functools.partial(attn_fwd_kernel, row, n_docs, heads),
        grid_spec=pltpu.PrefetchScalarGridSpec(
            num_scalar_prefetch=1,
            grid=(n_blk,),
            in_specs=[pl.BlockSpec(qkv.shape, lambda i, lens: (0, 0, 0, 0))],
            out_specs=[tile, tile, pl.BlockSpec((1, heads, length), lambda i, lens: (i, 0, 0))],
            scratch_shapes=[pltpu.VMEM((width, heads * length), F32)],
        ),
        out_shape=[
            jax.ShapeDtypeStruct((n_blk, length, width), F32),
            jax.ShapeDtypeStruct((n_blk, length, width), BF16),
            jax.ShapeDtypeStruct((n_blk, heads, length), F32),
        ],
        compiler_params=pltpu.CompilerParams(vmem_limit_bytes=VMEM_LIMIT),
        cost_estimate=pl.CostEstimate(flops=10**10, bytes_accessed=3 * 10**6, transcendentals=10**7),
        name="attn_fwd",
    )(lens, qkv)


def attn_bwd_kernel(row, n_docs, heads, lens_ref, qkv_ref, do_ref, o_ref, lse_ref, out_ref, dq_ref, delta_ref):
    n_blk, _, length, width = qkv_ref.shape
    j = pl.program_id(0)
    ends = doc_ends(lens_ref, row, n_docs)
    masks = head_masks(heads, width)
    scale = HEAD_DIM**-0.5

    @pl.when(j == 0)
    def _():
        def one(i, _):
            prod = (do_ref[i].astype(F32) * o_ref[i]).T
            for h in range(heads):
                delta_ref[i, h : h + 1, :] = jnp.sum(
                    prod[h * HEAD_DIM : (h + 1) * HEAD_DIM], axis=0, keepdims=True
                )
            dq_ref[i] = jnp.zeros((length, width), F32)
            return 0

        lax.fori_loop(0, n_blk, one, 0)

    last = jnp.int32(n_blk * length)
    final = (j + 1) * length - 1
    for end in reversed(ends):
        last = jnp.where(end > final, end, last)
    highest = lax.div(last - 1, jnp.int32(length))
    keys, values = qkv_ref[j, 1], qkv_ref[j, 2]
    key_heads = [keys * mask for mask in masks]

    def tile(i, carry):
        d_key, d_value = carry
        start, place = start_rows(ends, i, length, heads)
        queries = by_head(qkv_ref[i, 0] * jnp.asarray(scale, BF16), masks)
        d_out = by_head(do_ref[i], masks)
        lse = jnp.concatenate([lse_ref[i, h : h + 1, :] for h in range(heads)], axis=1)
        delta = jnp.concatenate([delta_ref[i, h : h + 1, :] for h in range(heads)], axis=1)
        scores = dot_nt(keys, queries)
        key = j * length + lax.broadcasted_iota(jnp.int32, scores.shape, 0)
        probs = jnp.exp(jnp.where((key <= place) & (key >= start), scores - lse, NEG))
        d_probs = dot_nt(values, d_out)
        d_scores = (probs * (d_probs - delta)).astype(BF16)
        d_value = d_value + dot(probs.astype(BF16), d_out)
        d_key = d_key + dot(d_scores, queries)
        d_query = dq_ref[i]
        for h in range(heads):
            d_query = d_query + dot_tn(d_scores[:, h * length : (h + 1) * length], key_heads[h])
        dq_ref[i] = d_query
        return d_key, d_value

    zero = jnp.zeros((length, width), F32)
    d_key, d_value = lax.fori_loop(j, highest + 1, tile, (zero, zero))
    out_ref[0, 0] = (dq_ref[j] * scale).astype(BF16)
    out_ref[0, 1] = d_key.astype(BF16)
    out_ref[0, 2] = d_value.astype(BF16)


def attn_bwd(lens, qkv, d_out, attended, lse, row, n_docs):
    n_blk, _, length, width = qkv.shape
    heads = width // HEAD_DIM
    whole = lambda a: pl.BlockSpec(a.shape, lambda j, lens: (0,) * a.ndim)
    return pl.pallas_call(
        functools.partial(attn_bwd_kernel, row, n_docs, heads),
        grid_spec=pltpu.PrefetchScalarGridSpec(
            num_scalar_prefetch=1,
            grid=(n_blk,),
            in_specs=[whole(qkv), whole(d_out), whole(attended), whole(lse)],
            out_specs=pl.BlockSpec((1, 3, length, width), lambda j, lens: (j, 0, 0, 0)),
            scratch_shapes=[
                pltpu.VMEM((n_blk, length, width), F32),
                pltpu.VMEM((n_blk, heads, length), F32),
            ],
        ),
        out_shape=jax.ShapeDtypeStruct((n_blk, 3, length, width), BF16),
        compiler_params=pltpu.CompilerParams(vmem_limit_bytes=VMEM_LIMIT),
        cost_estimate=pl.CostEstimate(flops=2 * 10**10, bytes_accessed=6 * 10**6, transcendentals=10**7),
        name="attn_bwd",
    )(lens, qkv, d_out, attended, lse)


def exchange(values):
    return lax.all_to_all(values, "blk", 0, 0, tiled=True)


def bits_of(axis):
    return lax.axis_size(axis).bit_length() - 1


def halve(current, axis, name, bit):
    size = lax.axis_size(name)
    mine = (lax.axis_index(name) >> bit) & 1
    half = current.shape[axis] // 2
    keep = lax.dynamic_slice_in_dim(current, mine * half, half, axis)
    send = lax.dynamic_slice_in_dim(current, (1 - mine) * half, half, axis)
    got = lax.ppermute(send, name, [(k, k ^ (1 << bit)) for k in range(size)])
    return (keep.astype(F32) + got.astype(F32)).astype(BF16)


def core_first(values):
    n_dp = lax.axis_size("dp")
    tokens, cols = values.shape
    return values.reshape(tokens, n_dp // 2, 2, cols // n_dp).transpose(0, 2, 1, 3).reshape(tokens, cols)


def y_first(values):
    n_blk = lax.axis_size("blk")
    tokens, cols = values.shape
    return values.reshape(tokens, n_blk // 2, 2, cols // n_blk).transpose(0, 2, 1, 3).reshape(tokens, cols)


def scatter_steps(y_early):
    dp_bits, blk_bits = bits_of("dp"), bits_of("blk")
    rest = [("dp", b) for b in reversed(range(1, dp_bits))]
    blk = [("blk", 0)] + [("blk", b) for b in reversed(range(1, blk_bits))]
    if y_early:
        return [("dp", 0)] + blk[:1] + rest + blk[1:]
    return [("dp", 0)] + rest + blk


def scatter(grad, rows_name, y_early):
    n_rows = lax.axis_size(rows_name)
    rows, cols = grad.shape
    current = grad.reshape((n_rows // 2, 2, rows // n_rows, cols))
    for name, bit in scatter_steps(y_early):
        if name != rows_name:
            current = halve(current, 3, name, bit)
        elif bit == 0:
            current = halve(current, 1, name, bit)
        else:
            current = halve(current, 0, name, bit)
    return current.reshape(rows // n_rows, current.shape[3])


def total(values):
    for name in ("dp", "blk"):
        size = lax.axis_size(name)
        for bit in range(bits_of(name)):
            values = values + lax.ppermute(values, name, [(k, k ^ (1 << bit)) for k in range(size)])
    return values


def rms_parts(values):
    inverse_rms = lax.rsqrt(jnp.mean(values * values, axis=-1, keepdims=True) + EPS)
    return values * inverse_rms, inverse_rms


def norm_back(d_normed, normed, inverse_rms):
    return inverse_rms * (d_normed - normed * jnp.mean(d_normed * normed, axis=-1, keepdims=True))


def rope_tables(doc_lengths, offset, length):
    half = HEAD_DIM // 2
    places = offset + jnp.arange(length, dtype=jnp.int32)
    ends = jnp.cumsum(doc_lengths, axis=1)
    start = jnp.max(jnp.where(ends[:, None, :] <= places[None, :, None], ends[:, None, :], 0), axis=2)
    position = (places[None, :] - start).astype(F32).reshape(-1, 1)
    lane = jnp.arange(128, dtype=jnp.int32)
    freq = jnp.power(10000.0, -(lane % half).astype(F32) * 2.0 / HEAD_DIM)
    angles = position * freq[None, :]
    sign = jnp.where(lane % HEAD_DIM < half, -1.0, 1.0)
    return jnp.cos(angles), jnp.sin(angles) * sign[None, :]


def rotate_back(values, cos, sin):
    half = HEAD_DIM // 2
    shaped = values.reshape(values.shape[:2] + (values.shape[2] // HEAD_DIM, 2, half))
    swapped = shaped[:, :, :, ::-1, :].reshape(values.shape)
    return values * cos - swapped * sin


def body(
    hidden_in,
    first_values,
    doc_lengths,
    w_query,
    w_key,
    w_value,
    w_out,
    w_gate,
    w_up,
    w_down,
    attn_gain,
    ffn_gain,
    out_cotangent,
):
    length, rows, model = hidden_in.shape
    n_docs = doc_lengths.shape[1]
    n_blk, n_dp = lax.axis_size("blk"), lax.axis_size("dp")
    width = model // n_blk
    tokens = rows * length
    flat = lambda a: jnp.transpose(a, (1, 0, 2)).reshape(tokens, model)
    unflat = lambda a: jnp.transpose(a.reshape(rows, length, model), (1, 0, 2))
    lens = doc_lengths.reshape(-1)

    resid_in = flat(hidden_in).astype(F32)
    normed_one, inv_one = rms_parts(resid_in)
    normed_in = (normed_one * attn_gain).astype(BF16)
    cos, sin = rope_tables(doc_lengths, lax.axis_index("blk") * length, length)
    *qkv_own, sums = project_qkv(normed_in, flat(first_values), cos, sin, w_query, w_key, w_value, rows, n_blk)
    cot = flat(out_cotangent)

    qkv, attended, lse, gathered = [], [], [], []
    for r in range(rows):
        qkv.append(exchange(qkv_own[r]))
    for r in range(rows):
        o_f, o_low, lse_r = attn_fwd(lens, qkv[r], r, n_docs)
        attended.append(o_f)
        lse.append(lse_r)
        gathered.append(exchange(o_low))
    attn_low = jnp.concatenate([jnp.transpose(g, (1, 0, 2)).reshape(length, model) for g in gathered], axis=0)

    resid_mid = resid_in + dot(attn_low, w_out)
    normed_two, inv_two = rms_parts(resid_mid)
    normed_mid = (normed_two * ffn_gain).astype(BF16)
    gate_pre = dot(normed_mid, w_gate)
    up_pre = dot(normed_mid, w_up)
    gate_act = jax.nn.silu(gate_pre)
    inner_low = (gate_act * up_pre).astype(BF16)
    block_out = (resid_mid + dot(inner_low, w_down)).astype(BF16)
    d_inner = dot_nt(cot, w_down)
    sigmoid_gate = jax.nn.sigmoid(gate_pre)
    d_gate = (d_inner * up_pre * sigmoid_gate * (1.0 + gate_pre * (1.0 - sigmoid_gate))).astype(BF16)
    d_up = (d_inner * gate_act).astype(BF16)
    d_normed_mid = dot_nt(d_gate, w_gate) + dot_nt(d_up, w_up)
    gain_two_grad = jnp.sum(d_normed_mid * normed_two, axis=0)
    d_resid_mid = cot.astype(F32) + norm_back(d_normed_mid * ffn_gain, normed_two, inv_two)
    d_branch = d_resid_mid.astype(BF16)
    d_attn = dot_nt(d_branch, w_out).astype(BF16)

    grads = []
    d_own = []
    for r in range(rows):
        piece = jnp.transpose(d_attn[r * length : (r + 1) * length].reshape(length, n_blk, width), (1, 0, 2))
        d_own.append(exchange(piece))
    mid_cf = core_first(normed_mid)
    grad_down = scatter(dot_tn(inner_low, y_first(cot)).astype(BF16), "dp", False)
    grad_gate = scatter(dot_tn(d_gate, mid_cf).astype(BF16), "blk", False)
    grad_up = scatter(dot_tn(d_up, mid_cf).astype(BF16), "blk", True)
    grad_project = scatter(dot_tn(d_branch, core_first(attn_low)).astype(BF16), "blk", True)

    back = []
    for r in range(rows):
        back.append(exchange(attn_bwd(lens, qkv[r], d_own[r], attended[r], lse[r], r, n_docs)))

    def owned(which, rotated):
        parts = []
        for r in range(rows):
            values = back[r][:, which].astype(F32)
            if rotated:
                at = slice(r * length, (r + 1) * length)
                values = rotate_back(values, cos[at, :width], sin[at, :width])
            parts.append(jnp.transpose(values, (1, 0, 2)).reshape(length, model))
        return jnp.concatenate(parts, axis=0)

    d_query = owned(0, True).astype(BF16)
    d_key = owned(1, True).astype(BF16)
    grad_first = 0.5 * owned(2, False)
    d_value = grad_first.astype(BF16)
    in_cf = core_first(normed_in)
    grad_query = scatter(dot_tn(d_query, in_cf).astype(BF16), "blk", True)
    grad_key = scatter(dot_tn(d_key, in_cf).astype(BF16), "blk", False)
    grad_value = scatter(dot_tn(d_value, in_cf).astype(BF16), "blk", True)
    d_normed_in = dot_nt(d_query, w_query) + dot_nt(d_key, w_key) + dot_nt(d_value, w_value)
    gain_one_grad = jnp.sum(d_normed_in * normed_one, axis=0)
    grad_input = d_resid_mid + norm_back(d_normed_in * attn_gain, normed_one, inv_one)

    squares = jnp.sum(sums, axis=(0, 2))
    squares = jnp.concatenate([squares, jnp.zeros((126,), F32)])
    early = total(jnp.concatenate([gain_two_grad, squares]))
    gain_one = total(gain_one_grad)
    n_entries = n_blk * length * rows * n_dp * model
    return (
        block_out_shape(unflat(block_out)),
        unflat(grad_input),
        unflat(grad_first),
        grad_query.T.astype(F32),
        grad_key.T.astype(F32),
        grad_value.T.astype(F32),
        grad_project.T.astype(F32),
        grad_gate.T.astype(F32),
        grad_up.T.astype(F32),
        grad_down.astype(F32),
        gain_one,
        early[:model],
        early[model] / n_entries,
        early[model + 1] / n_entries,
    )


def block_out_shape(values):
    return values


def solution(mesh):
    tokens = P("blk", "dp", None)
    return jax.shard_map(
        body,
        mesh=mesh,
        in_specs=(tokens, tokens, P("dp", None)) + (P(),) * 9 + (tokens,),
        out_specs=(tokens,) * 3 + (P("dp", "blk"),) * 7 + (P(),) * 4,
        check_vma=False,
    )
```

```python
import functools

import jax
import jax.numpy as jnp
from jax import lax
from jax.experimental import pallas as pl
from jax.experimental.pallas import tpu as pltpu
from jax.sharding import PartitionSpec as P

HEADS = 16
HEAD_DIM = 64
NEG = -1e30
EPS = 1e-06
F32 = jnp.float32
BF16 = jnp.bfloat16
VMEM_LIMIT = 56 * 2**20
MESH = pl.DeviceIdType.MESH


def dot(a, b):
    return jnp.dot(a, b, preferred_element_type=F32)


def dot_nt(a, b):
    return lax.dot_general(a, b, (((1,), (1,)), ((), ())), preferred_element_type=F32)


def dot_tn(a, b):
    return lax.dot_general(a, b, (((0,), (0,)), ((), ())), preferred_element_type=F32)


def swap_halves(v):
    half = HEAD_DIM // 2
    width = v.shape[-1]
    lane = lax.broadcasted_iota(jnp.int32, v.shape, v.ndim - 1)
    left = pltpu.roll(v, width - half, v.ndim - 1)
    right = pltpu.roll(v, half, v.ndim - 1)
    return jnp.where(lane % HEAD_DIM < half, left, right)


def qkv_kernel(rows, length, width, hidden_ref, first_ref, cos_ref, sin_ref, gain_ref, wq_ref, wk_ref, wv_ref, *outs):
    out_refs, (normed_ref, sums_ref) = outs[:rows], outs[rows:]
    chunk = wq_ref.shape[1]

    @pl.when(pl.program_id(0) == 0)
    def _():
        for r in range(rows):
            at = pl.ds(r * length, length)
            normed, _ = rms_parts(hidden_ref[at, :].astype(F32))
            normed_ref[at, :] = (normed * gain_ref[...]).astype(BF16)

    first_sum = jnp.zeros((1, chunk), F32)
    mixed_sum = jnp.zeros((1, chunk), F32)
    for r in range(rows):
        at = pl.ds(r * length, length)
        normed = normed_ref[at, :]
        cos, sin = cos_ref[at, :], sin_ref[at, :]
        for which, w_ref in ((0, wq_ref), (1, wk_ref)):
            raw = dot(normed, w_ref[...])
            for c in range(chunk // 128):
                part = raw[:, c * 128 : (c + 1) * 128]
                turned = (part * cos + swap_halves(part) * sin).astype(BF16)
                for s in range(128 // width):
                    out_refs[r][c * (128 // width) + s, which] = turned[:, s * width : (s + 1) * width]
        first = first_ref[at, :].astype(F32)
        mixed = 0.5 * dot(normed, wv_ref[...]) + 0.5 * first
        first_sum = first_sum + jnp.sum(first * first, axis=0, keepdims=True)
        mixed_sum = mixed_sum + jnp.sum(mixed * mixed, axis=0, keepdims=True)
        low = mixed.astype(BF16)
        for s in range(chunk // width):
            out_refs[r][s, 2] = low[:, s * width : (s + 1) * width]
    sums_ref[0, 0:1] = first_sum
    sums_ref[0, 1:2] = mixed_sum


def project_qkv(hidden, first, cos, sin, gain, w_query, w_key, w_value, rows, n_blk):
    tokens, model = hidden.shape
    length, width = tokens // rows, model // n_blk
    chunk = 256
    steps = model // chunk
    full = lambda rows, cols: pl.BlockSpec((rows, cols), lambda j: (0, 0))
    weight = pl.BlockSpec((model, chunk), lambda j: (0, j))
    return pl.pallas_call(
        functools.partial(qkv_kernel, rows, length, width),
        grid=(steps,),
        in_specs=[
            full(tokens, model),
            pl.BlockSpec((tokens, chunk), lambda j: (0, j)),
            full(tokens, 128),
            full(tokens, 128),
            full(1, model),
            weight,
            weight,
            weight,
        ],
        out_specs=[pl.BlockSpec((chunk // width, 3, length, width), lambda j: (j, 0, 0, 0))] * rows
        + [full(tokens, model), pl.BlockSpec((1, 2, chunk), lambda j: (j, 0, 0))],
        out_shape=[jax.ShapeDtypeStruct((n_blk, 3, length, width), BF16)] * rows
        + [jax.ShapeDtypeStruct((tokens, model), BF16), jax.ShapeDtypeStruct((steps, 2, chunk), F32)],
        compiler_params=pltpu.CompilerParams(vmem_limit_bytes=VMEM_LIMIT),
        cost_estimate=pl.CostEstimate(
            flops=6 * tokens * model * model, bytes_accessed=6 * model * model + 10 * tokens * model, transcendentals=0
        ),
        name="qkv",
    )(hidden, first, cos, sin, gain, w_query, w_key, w_value)


def doc_ends(lens_ref, row, n_docs):
    ends, total = [], jnp.int32(0)
    for d in range(n_docs):
        total = total + lens_ref[row * n_docs + d]
        ends.append(total)
    return ends


def start_rows(ends, tile, length, heads):
    place = tile * length + lax.broadcasted_iota(jnp.int32, (1, length), 1)
    start = jnp.zeros((1, length), jnp.int32)
    for end in ends:
        start = jnp.where(end <= place, end, start)
    return jnp.concatenate([start] * heads, axis=1), jnp.concatenate([place] * heads, axis=1)


def head_masks(heads, width):
    lane = lax.broadcasted_iota(jnp.int32, (1, width), 1) // HEAD_DIM
    return [jnp.where(lane == h, 1.0, 0.0).astype(BF16) for h in range(heads)]


def by_head(values, masks):
    return jnp.concatenate([values * mask for mask in masks], axis=0)


def attn_fwd_kernel(row, n_docs, heads, lens_ref, qkv_ref, o_ref, low_ref, lse_ref, acc_ref):
    length, width = qkv_ref.shape[2:]
    i = pl.program_id(0)
    ends = doc_ends(lens_ref, row, n_docs)
    start, place = start_rows(ends, i, length, heads)
    lowest = jnp.int32(0)
    for end in ends:
        lowest = jnp.where(end <= i * length, end, lowest)
    lowest = lax.div(lowest, jnp.int32(length))
    masks = head_masks(heads, width)
    queries = by_head(qkv_ref[i, 0] * jnp.asarray(HEAD_DIM**-0.5, BF16), masks)

    def tile(step, carry):
        run_max, run_sum = carry
        j = i - step
        scores = dot_nt(qkv_ref[j, 1], queries)
        key = j * length + lax.broadcasted_iota(jnp.int32, scores.shape, 0)
        scores = jnp.where((key <= place) & (key >= start), scores, NEG)
        new_max = jnp.maximum(run_max, jnp.max(scores, axis=0, keepdims=True))
        weights = jnp.exp(scores - new_max)
        factor = jnp.exp(run_max - new_max)
        run_sum = run_sum * factor + jnp.sum(weights, axis=0, keepdims=True)
        acc_ref[...] = acc_ref[...] * factor + dot_tn(qkv_ref[j, 2], weights.astype(BF16))
        return new_max, run_sum

    acc_ref[...] = jnp.zeros_like(acc_ref)
    run_max, run_sum = lax.fori_loop(
        0,
        i - lowest + 1,
        tile,
        (jnp.full((1, heads * length), NEG, F32), jnp.zeros((1, heads * length), F32)),
    )
    result = acc_ref[...] / run_sum
    joined = jnp.concatenate(
        [
            result[h * HEAD_DIM : (h + 1) * HEAD_DIM, h * length : (h + 1) * length]
            for h in range(heads)
        ],
        axis=0,
    )
    attended = joined.T
    o_ref[0] = attended
    low_ref[0] = attended.astype(BF16)
    total = run_max + jnp.log(run_sum)
    for h in range(heads):
        lse_ref[0, h : h + 1, :] = total[:, h * length : (h + 1) * length]


def attn_fwd(lens, qkv, row, n_docs):
    n_blk, _, length, width = qkv.shape
    heads = width // HEAD_DIM
    tile = pl.BlockSpec((1, length, width), lambda i, lens: (i, 0, 0))
    return pl.pallas_call(
        functools.partial(attn_fwd_kernel, row, n_docs, heads),
        grid_spec=pltpu.PrefetchScalarGridSpec(
            num_scalar_prefetch=1,
            grid=(n_blk,),
            in_specs=[pl.BlockSpec(qkv.shape, lambda i, lens: (0, 0, 0, 0))],
            out_specs=[tile, tile, pl.BlockSpec((1, heads, length), lambda i, lens: (i, 0, 0))],
            scratch_shapes=[pltpu.VMEM((width, heads * length), F32)],
        ),
        out_shape=[
            jax.ShapeDtypeStruct((n_blk, length, width), F32),
            jax.ShapeDtypeStruct((n_blk, length, width), BF16),
            jax.ShapeDtypeStruct((n_blk, heads, length), F32),
        ],
        compiler_params=pltpu.CompilerParams(vmem_limit_bytes=VMEM_LIMIT),
        cost_estimate=pl.CostEstimate(flops=10**10, bytes_accessed=3 * 10**6, transcendentals=10**7),
        name="attn_fwd",
    )(lens, qkv)


def attn_bwd_kernel(row, n_docs, heads, lens_ref, qkv_ref, do_ref, o_ref, lse_ref, out_ref, dq_ref, delta_ref):
    n_blk, _, length, width = qkv_ref.shape
    j = pl.program_id(0)
    ends = doc_ends(lens_ref, row, n_docs)
    masks = head_masks(heads, width)
    scale = HEAD_DIM**-0.5

    @pl.when(j == 0)
    def _():
        def one(i, _):
            prod = (do_ref[i].astype(F32) * o_ref[i]).T
            for h in range(heads):
                delta_ref[i, h : h + 1, :] = jnp.sum(
                    prod[h * HEAD_DIM : (h + 1) * HEAD_DIM], axis=0, keepdims=True
                )
            dq_ref[i] = jnp.zeros((length, width), F32)
            return 0

        lax.fori_loop(0, n_blk, one, 0)

    last = jnp.int32(n_blk * length)
    final = (j + 1) * length - 1
    for end in reversed(ends):
        last = jnp.where(end > final, end, last)
    highest = lax.div(last - 1, jnp.int32(length))
    keys, values = qkv_ref[j, 1], qkv_ref[j, 2]
    key_heads = [keys * mask for mask in masks]

    def tile(i, carry):
        d_key, d_value = carry
        start, place = start_rows(ends, i, length, heads)
        queries = by_head(qkv_ref[i, 0] * jnp.asarray(scale, BF16), masks)
        d_out = by_head(do_ref[i], masks)
        lse = jnp.concatenate([lse_ref[i, h : h + 1, :] for h in range(heads)], axis=1)
        delta = jnp.concatenate([delta_ref[i, h : h + 1, :] for h in range(heads)], axis=1)
        scores = dot_nt(keys, queries)
        key = j * length + lax.broadcasted_iota(jnp.int32, scores.shape, 0)
        probs = jnp.exp(jnp.where((key <= place) & (key >= start), scores - lse, NEG))
        d_probs = dot_nt(values, d_out)
        d_scores = (probs * (d_probs - delta)).astype(BF16)
        d_value = d_value + dot(probs.astype(BF16), d_out)
        d_key = d_key + dot(d_scores, queries)
        d_query = dq_ref[i]
        for h in range(heads):
            d_query = d_query + dot_tn(d_scores[:, h * length : (h + 1) * length], key_heads[h])
        dq_ref[i] = d_query
        return d_key, d_value

    zero = jnp.zeros((length, width), F32)
    d_key, d_value = lax.fori_loop(j, highest + 1, tile, (zero, zero))
    out_ref[0, 0] = (dq_ref[j] * scale).astype(BF16)
    out_ref[0, 1] = d_key.astype(BF16)
    out_ref[0, 2] = d_value.astype(BF16)


def attn_bwd(lens, qkv, d_out, attended, lse, row, n_docs):
    n_blk, _, length, width = qkv.shape
    heads = width // HEAD_DIM
    whole = lambda a: pl.BlockSpec(a.shape, lambda j, lens: (0,) * a.ndim)
    return pl.pallas_call(
        functools.partial(attn_bwd_kernel, row, n_docs, heads),
        grid_spec=pltpu.PrefetchScalarGridSpec(
            num_scalar_prefetch=1,
            grid=(n_blk,),
            in_specs=[whole(qkv), whole(d_out), whole(attended), whole(lse)],
            out_specs=pl.BlockSpec((1, 3, length, width), lambda j, lens: (j, 0, 0, 0)),
            scratch_shapes=[
                pltpu.VMEM((n_blk, length, width), F32),
                pltpu.VMEM((n_blk, heads, length), F32),
            ],
        ),
        out_shape=jax.ShapeDtypeStruct((n_blk, 3, length, width), BF16),
        compiler_params=pltpu.CompilerParams(vmem_limit_bytes=VMEM_LIMIT),
        cost_estimate=pl.CostEstimate(flops=2 * 10**10, bytes_accessed=6 * 10**6, transcendentals=10**7),
        name="attn_bwd",
    )(lens, qkv, d_out, attended, lse)


def exchange(values):
    return lax.all_to_all(values, "blk", 0, 0, tiled=True)


def bits_of(axis):
    return lax.axis_size(axis).bit_length() - 1


def halve(current, axis, name, bit):
    size = lax.axis_size(name)
    mine = (lax.axis_index(name) >> bit) & 1
    half = current.shape[axis] // 2
    keep = lax.dynamic_slice_in_dim(current, mine * half, half, axis)
    send = lax.dynamic_slice_in_dim(current, (1 - mine) * half, half, axis)
    got = lax.ppermute(send, name, [(k, k ^ (1 << bit)) for k in range(size)])
    return (keep.astype(F32) + got.astype(F32)).astype(BF16)


def core_first(values):
    n_dp = lax.axis_size("dp")
    tokens, cols = values.shape
    return values.reshape(tokens, n_dp // 2, 2, cols // n_dp).transpose(0, 2, 1, 3).reshape(tokens, cols)


def y_first(values):
    n_blk = lax.axis_size("blk")
    tokens, cols = values.shape
    return values.reshape(tokens, n_blk // 2, 2, cols // n_blk).transpose(0, 2, 1, 3).reshape(tokens, cols)


def scatter_steps(y_early):
    dp_bits, blk_bits = bits_of("dp"), bits_of("blk")
    rest = [("dp", b) for b in reversed(range(1, dp_bits))]
    blk = [("blk", 0)] + [("blk", b) for b in reversed(range(1, blk_bits))]
    if y_early:
        return [("dp", 0)] + blk[:1] + rest + blk[1:]
    return [("dp", 0)] + rest + blk


def scatter(grad, rows_name, y_early):
    n_rows = lax.axis_size(rows_name)
    rows, cols = grad.shape
    current = grad.reshape((n_rows // 2, 2, rows // n_rows, cols))
    for name, bit in scatter_steps(y_early):
        if name != rows_name:
            current = halve(current, 3, name, bit)
        elif bit == 0:
            current = halve(current, 1, name, bit)
        else:
            current = halve(current, 0, name, bit)
    return current.reshape(rows // n_rows, current.shape[3])


def total(values):
    for name in ("dp", "blk"):
        size = lax.axis_size(name)
        for bit in range(bits_of(name)):
            values = values + lax.ppermute(values, name, [(k, k ^ (1 << bit)) for k in range(size)])
    return values


def place_of(order, dp, blk):
    place = 0
    for name, bit in order:
        place = 2 * place + (((dp if name == "dp" else blk) >> bit) & 1)
    return place


def chunks_of(block_rows, block_cols):
    cols = block_cols // 128
    return 4 // cols, cols, block_rows // (4 // cols)


def wgrad_kernel(orders, n_left, n_right, left_is_dp, n_out, left_ref, *refs):
    right_refs, out_refs, turned_ref = refs[:n_out], refs[n_out : 2 * n_out], refs[2 * n_out]
    left_rows, right_cols = left_ref.shape[1] // n_left, right_refs[0].shape[1] // n_right
    row_parts, col_parts, size = chunks_of(left_rows, right_cols)
    q = pl.program_id(0)

    @pl.when(q == 0)
    def _():
        turned_ref[...] = left_ref[...].T

    row_part, col_part = q // col_parts, q % col_parts
    left = jnp.concatenate(
        [
            turned_ref[pl.ds(pl.multiple_of(k * left_rows + row_part * size, 16), size), :]
            for k in range(n_left)
        ],
        axis=0,
    )
    for order, right_ref, out_ref in zip(orders, right_refs, out_refs):
        if col_parts == 1:
            right = right_ref[...]
        else:
            right = jnp.concatenate(
                [
                    right_ref[:, pl.ds(pl.multiple_of(k * right_cols + col_part * 128, 128), 128)]
                    for k in range(n_right)
                ],
                axis=1,
            )
        result = dot(left, right).astype(BF16)
        for k in range(n_left):
            for m in range(n_right):
                dp, blk = (k, m) if left_is_dp else (m, k)
                out_ref[0, place_of(order, dp, blk)] = result[k * size : (k + 1) * size, m * 128 : (m + 1) * 128]


def wgrad(orders, left, rights, left_is_dp):
    n_dp, n_blk = lax.axis_size("dp"), lax.axis_size("blk")
    n_left, n_right = (n_dp, n_blk) if left_is_dp else (n_blk, n_dp)
    tokens, left_cols = left.shape
    right_cols = rights[0].shape[1]
    row_parts, col_parts, size = chunks_of(left_cols // n_left, right_cols // n_right)
    full = lambda a: pl.BlockSpec(a.shape, lambda q: (0, 0))
    n_out = len(rights)
    return pl.pallas_call(
        functools.partial(wgrad_kernel, orders, n_left, n_right, left_is_dp, n_out),
        grid=(4,),
        in_specs=[full(left)] + [full(a) for a in rights],
        out_specs=[pl.BlockSpec((1, n_dp * n_blk, size, 128), lambda q: (q, 0, 0, 0))] * n_out,
        out_shape=[jax.ShapeDtypeStruct((4, n_dp * n_blk, size, 128), BF16)] * n_out,
        scratch_shapes=[pltpu.VMEM((left_cols, tokens), BF16)],
        compiler_params=pltpu.CompilerParams(vmem_limit_bytes=VMEM_LIMIT),
        cost_estimate=pl.CostEstimate(
            flops=2 * n_out * tokens * left_cols * right_cols,
            bytes_accessed=2 * tokens * (left_cols + n_out * right_cols) + 2 * n_out * left_cols * right_cols,
            transcendentals=0,
        ),
        name="wgrad",
    )(left, *rights)


def partner(name, bit):
    here = {"dp": lax.axis_index("dp"), "blk": lax.axis_index("blk")}
    mine = (here[name] // (1 << bit)) % 2
    other = dict(here)
    other[name] = here[name] + (1 - 2 * mine) * (1 << bit)
    return mine, (other["dp"], other["blk"])


def scatter_kernel(orders, *refs):
    n_streams, n_stages = len(orders), len(orders[0])
    take = lambda n: [next(source) for _ in range(n)]
    source = iter(refs)
    grads, outs, works = take(n_streams), take(n_streams), take(n_streams)
    landed = [take(n_stages) for _ in range(n_streams)]
    local_sem, send_sem, recv_sem = take(3)
    n_chunks = grads[0].shape[0]
    blocks = grads[0].shape[1]

    barrier = pltpu.get_barrier_semaphore()
    for name, bit in orders[0]:
        pl.semaphore_signal(barrier, inc=1, device_id=partner(name, bit)[1], device_id_type=MESH)
    pl.semaphore_wait(barrier, n_stages)

    def base_of(k, stage):
        base = 0
        for earlier in range(1, stage):
            base = base + partner(*orders[k][earlier])[0] * (blocks >> (earlier + 1))
        return base

    def local(k, c):
        mine = partner(*orders[k][0])[0]
        half = blocks // 2
        return pltpu.make_async_copy(grads[k].at[c, pl.ds(mine * half, half)], works[k].at[c], local_sem.at[k, c])

    def remote(k, stage, c):
        mine, device = partner(*orders[k][stage])
        half = blocks >> (stage + 1)
        if stage == 0:
            sent = grads[k].at[c, pl.ds((1 - mine) * half, half)]
        else:
            sent = works[k].at[c, pl.ds(base_of(k, stage) + (1 - mine) * half, half)]
        return pltpu.make_async_remote_copy(
            src_ref=sent,
            dst_ref=landed[k][stage].at[c],
            send_sem=send_sem.at[k, stage, c],
            recv_sem=recv_sem.at[k, stage, c],
            device_id=device,
            device_id_type=MESH,
        )

    def add(k, stage, c):
        count = blocks >> (stage + 1)
        base = base_of(k, stage + 1)
        if stage == n_stages - 1:
            outs[k][c] = works[k][c, base].astype(F32) + landed[k][stage][c, 0].astype(F32)
            return

        def one(d, _):
            kept = works[k][c, base + d].astype(F32) + landed[k][stage][c, d].astype(F32)
            works[k][c, base + d] = kept.astype(BF16)
            return 0

        lax.fori_loop(0, count, one, 0)

    def step(t, _):
        for stage in range(n_stages + 1):
            c = t - stage

            @pl.when((c >= 0) & (c < n_chunks))
            def _():
                for k in range(n_streams):
                    if stage == 0:
                        local(k, c).start()
                    else:
                        if stage == 1:
                            local(k, c).wait()
                        remote(k, stage - 1, c).wait_recv()
                        add(k, stage - 1, c)
                    if stage < n_stages:
                        remote(k, stage, c).start()

        return 0

    lax.fori_loop(0, n_chunks + n_stages, step, 0)

    def finish(c, _):
        for k in range(n_streams):
            for stage in range(n_stages):
                remote(k, stage, c).wait_send()
        return 0

    lax.fori_loop(0, n_chunks, finish, 0)


def scatter_sum(grads, orders, collective_id):
    n_streams, n_stages = len(grads), len(orders[0])
    n_chunks, blocks = grads[0].shape[:2]
    size = sum(a.size for a in grads)
    return pl.pallas_call(
        functools.partial(scatter_kernel, orders),
        in_specs=[pl.BlockSpec(memory_space=pl.ANY)] * n_streams,
        out_specs=[pl.BlockSpec(memory_space=pltpu.VMEM)] * n_streams,
        out_shape=[jax.ShapeDtypeStruct((n_chunks,) + a.shape[2:], F32) for a in grads],
        scratch_shapes=[pltpu.VMEM((n_chunks, blocks // 2) + a.shape[2:], BF16) for a in grads]
        + [
            pltpu.VMEM((n_chunks, blocks >> (stage + 1)) + a.shape[2:], BF16)
            for a in grads
            for stage in range(n_stages)
        ]
        + [
            pltpu.SemaphoreType.DMA((n_streams, n_chunks)),
            pltpu.SemaphoreType.DMA((n_streams, n_stages, n_chunks)),
            pltpu.SemaphoreType.DMA((n_streams, n_stages, n_chunks)),
        ],
        compiler_params=pltpu.CompilerParams(
            collective_id=collective_id, has_side_effects=True, vmem_limit_bytes=VMEM_LIMIT
        ),
        cost_estimate=pl.CostEstimate(flops=size, bytes_accessed=8 * size, transcendentals=0),
        name="scatter_sum",
    )(*grads)


def whole_block(pieces, block_rows, block_cols):
    row_parts, col_parts, size = chunks_of(block_rows, block_cols)
    shaped = pieces.reshape(row_parts, col_parts, size, 128)
    return jnp.transpose(shaped, (0, 2, 1, 3)).reshape(block_rows, block_cols)


def ffn_kernel(rows, n_blk, *refs):
    source = iter(refs)
    take = lambda n: [next(source) for _ in range(n)]
    gathered = take(rows)
    hidden_ref, cot_ref, gain_ref, wo_ref, wg_ref, wu_ref, wd_ref = take(7)
    low_ref, mid_ref, inner_ref, dgate_ref, dup_ref, out_ref, dres_ref, dbranch_ref, dgain_ref = take(9)
    d_attn = take(rows)
    resid_ref, acc_ref, dmid_ref = take(3)
    length, width = gathered[0].shape[1:]
    step = pl.program_id(0)

    @pl.when(step == 0)
    def _():
        for r in range(rows):
            at = pl.ds(r * length, length)
            for s in range(n_blk):
                low_ref[at, s * width : (s + 1) * width] = gathered[r][s]
            resid = hidden_ref[at, :].astype(F32) + dot(low_ref[at, :], wo_ref[...])
            resid_ref[at, :] = resid
            normed, _ = rms_parts(resid)
            mid_ref[at, :] = (normed * gain_ref[...]).astype(BF16)
        acc_ref[...] = jnp.zeros_like(acc_ref)
        dmid_ref[...] = jnp.zeros_like(dmid_ref)

    for r in range(rows):
        at = pl.ds(r * length, length)
        gate = dot(mid_ref[at, :], wg_ref[...])
        up = dot(mid_ref[at, :], wu_ref[...])
        d_inner = dot_nt(cot_ref[at, :], wd_ref[...])
        sigma = 1.0 / (1.0 + jnp.exp(-gate))
        act = gate * sigma
        inner = (act * up).astype(BF16)
        d_gate = (d_inner * up * (sigma * (1.0 + gate * (1.0 - sigma)))).astype(BF16)
        d_up = (d_inner * act).astype(BF16)
        inner_ref[at, :] = inner
        dgate_ref[at, :] = d_gate
        dup_ref[at, :] = d_up
        acc_ref[at, :] += dot(inner, wd_ref[...])
        dmid_ref[at, :] += dot_nt(d_gate, wg_ref[...]) + dot_nt(d_up, wu_ref[...])

    @pl.when(step == pl.num_programs(0) - 1)
    def _():
        d_gain = jnp.zeros(dgain_ref.shape, F32)
        for r in range(rows):
            at = pl.ds(r * length, length)
            resid = resid_ref[at, :]
            out_ref[at, :] = (resid + acc_ref[at, :]).astype(BF16)
            normed, inverse = rms_parts(resid)
            d_mid = dmid_ref[at, :]
            d_gain = d_gain + jnp.sum(d_mid * normed, axis=0, keepdims=True)
            d_resid = cot_ref[at, :].astype(F32) + norm_back(d_mid * gain_ref[...], normed, inverse)
            dres_ref[at, :] = d_resid
            d_branch = d_resid.astype(BF16)
            dbranch_ref[at, :] = d_branch
            back = dot_nt(d_branch, wo_ref[...]).astype(BF16)
            for s in range(n_blk):
                d_attn[r][s] = back[:, s * width : (s + 1) * width]
        dgain_ref[...] = d_gain


def feed_forward(gathered, hidden, cot, gain, w_out, w_gate, w_up, w_down):
    rows = len(gathered)
    n_blk, length, width = gathered[0].shape
    tokens, model = hidden.shape
    inner = w_gate.shape[1]
    chunk = 256
    full = lambda a: pl.BlockSpec(a.shape, lambda j: (0,) * len(a.shape))
    once = lambda a: pl.BlockSpec(a.shape, lambda j: (0,) * len(a.shape), pipeline_mode=pl.Buffered(1))
    cols = pl.BlockSpec((model, chunk), lambda j: (0, j))
    shape = jax.ShapeDtypeStruct
    token_cols = pl.BlockSpec((tokens, chunk), lambda j: (0, j))
    outs = (
        [shape((tokens, model), BF16)] * 2
        + [shape((tokens, inner), BF16)] * 3
        + [shape((tokens, model), BF16), shape((tokens, model), F32), shape((tokens, model), BF16)]
        + [shape((1, model), F32)]
        + [shape((n_blk, length, width), BF16)] * rows
    )
    return pl.pallas_call(
        functools.partial(ffn_kernel, rows, n_blk),
        grid=(inner // chunk,),
        in_specs=[once(a) for a in gathered]
        + [once(hidden), once(cot), once(gain), once(w_out), cols, cols, pl.BlockSpec((chunk, model), lambda j: (j, 0))],
        out_specs=[full(outs[0])] * 2 + [token_cols] * 3 + [full(a) for a in outs[5:]],
        out_shape=outs,
        scratch_shapes=[pltpu.VMEM((tokens, model), F32)] * 3,
        compiler_params=pltpu.CompilerParams(vmem_limit_bytes=VMEM_LIMIT),
        cost_estimate=pl.CostEstimate(
            flops=12 * tokens * model * inner + 4 * tokens * model * model,
            bytes_accessed=6 * model * inner + 6 * tokens * inner + 20 * tokens * model,
            transcendentals=tokens * inner,
        ),
        name="ffn",
    )(*gathered, hidden, cot, gain, w_out, w_gate, w_up, w_down)


def turn_back_kernel(rows, cos_ref, sin_ref, *refs):
    backs, (low_ref, first_ref) = refs[:rows], refs[rows:]
    n_blk, _, length, width = backs[0].shape
    which = pl.program_id(0)
    for r in range(rows):
        at = pl.ds(r * length, length)
        for s in range(n_blk):
            cols = slice(s * width, (s + 1) * width)
            values = backs[r][s, 0].astype(F32)

            @pl.when(which < 2)
            def _():
                cos, sin = cos_ref[at, :width], sin_ref[at, :width]
                wide = values if width == 128 else jnp.concatenate([values, values], axis=1)
                swapped = swap_halves(wide)[:, :width]
                low_ref[0, at, cols] = (values * cos - swapped * sin).astype(BF16)

            @pl.when(which == 2)
            def _():
                first_ref[at, cols] = 0.5 * values
                low_ref[0, at, cols] = (0.5 * values).astype(BF16)


def turn_back(backs, cos, sin):
    rows = len(backs)
    n_blk, _, length, width = backs[0].shape
    tokens, model = rows * length, n_blk * width
    full = lambda a: pl.BlockSpec(a.shape, lambda w: (0, 0))
    return pl.pallas_call(
        functools.partial(turn_back_kernel, rows),
        grid=(3,),
        in_specs=[full(cos), full(sin)] + [pl.BlockSpec((n_blk, 1, length, width), lambda w: (0, w, 0, 0))] * rows,
        out_specs=[
            pl.BlockSpec((1, tokens, model), lambda w: (w, 0, 0)),
            pl.BlockSpec((tokens, model), lambda w: (0, 0)),
        ],
        out_shape=[jax.ShapeDtypeStruct((3, tokens, model), BF16), jax.ShapeDtypeStruct((tokens, model), F32)],
        compiler_params=pltpu.CompilerParams(vmem_limit_bytes=VMEM_LIMIT),
        name="turn_back",
    )(cos, sin, *backs)


def input_grad_kernel(hidden_ref, dres_ref, gain_ref, low_ref, wq_ref, wk_ref, wv_ref, out_ref, dgain_ref):
    tokens = hidden_ref.shape[0]
    half = tokens // 2
    d_gain = jnp.zeros(dgain_ref.shape, F32)
    for r in range(2):
        at = pl.ds(r * half, half)
        d_normed = (
            dot_nt(low_ref[0, at, :], wq_ref[...])
            + dot_nt(low_ref[1, at, :], wk_ref[...])
            + dot_nt(low_ref[2, at, :], wv_ref[...])
        )
        normed, inverse = rms_parts(hidden_ref[at, :].astype(F32))
        d_gain = d_gain + jnp.sum(d_normed * normed, axis=0, keepdims=True)
        out_ref[at, :] = dres_ref[at, :] + norm_back(d_normed * gain_ref[...], normed, inverse)
    dgain_ref[...] = d_gain


def input_grad(hidden, d_resid, gain, low, w_query, w_key, w_value):
    tokens, model = hidden.shape
    return pl.pallas_call(
        input_grad_kernel,
        out_shape=[jax.ShapeDtypeStruct((tokens, model), F32), jax.ShapeDtypeStruct((1, model), F32)],
        compiler_params=pltpu.CompilerParams(vmem_limit_bytes=VMEM_LIMIT),
        cost_estimate=pl.CostEstimate(
            flops=6 * tokens * model * model, bytes_accessed=6 * model * model + 16 * tokens * model, transcendentals=0
        ),
        name="input_grad",
    )(hidden, d_resid, gain, low, w_query, w_key, w_value)


def rms_parts(values):
    inverse_rms = lax.rsqrt(jnp.mean(values * values, axis=-1, keepdims=True) + EPS)
    return values * inverse_rms, inverse_rms


def norm_back(d_normed, normed, inverse_rms):
    return inverse_rms * (d_normed - normed * jnp.mean(d_normed * normed, axis=-1, keepdims=True))


def rope_tables(doc_lengths, offset, length):
    half = HEAD_DIM // 2
    places = offset + jnp.arange(length, dtype=jnp.int32)
    ends = jnp.cumsum(doc_lengths, axis=1)
    start = jnp.max(jnp.where(ends[:, None, :] <= places[None, :, None], ends[:, None, :], 0), axis=2)
    position = (places[None, :] - start).astype(F32).reshape(-1, 1)
    lane = jnp.arange(128, dtype=jnp.int32)
    freq = jnp.power(10000.0, -(lane % half).astype(F32) * 2.0 / HEAD_DIM)
    angles = position * freq[None, :]
    sign = jnp.where(lane % HEAD_DIM < half, -1.0, 1.0)
    return jnp.cos(angles), jnp.sin(angles) * sign[None, :]


def body(
    hidden_in,
    first_values,
    doc_lengths,
    w_query,
    w_key,
    w_value,
    w_out,
    w_gate,
    w_up,
    w_down,
    attn_gain,
    ffn_gain,
    out_cotangent,
):
    length, rows, model = hidden_in.shape
    n_docs = doc_lengths.shape[1]
    n_blk, n_dp = lax.axis_size("blk"), lax.axis_size("dp")
    width = model // n_blk
    tokens = rows * length
    flat = lambda a: jnp.transpose(a, (1, 0, 2)).reshape(tokens, model)
    unflat = lambda a: jnp.transpose(a.reshape(rows, length, model), (1, 0, 2))
    lens = doc_lengths.reshape(-1)

    hidden, cot, first = flat(hidden_in), flat(out_cotangent), flat(first_values)
    row_gain = lambda gain: gain.reshape(1, model)

    cos, sin = rope_tables(doc_lengths, lax.axis_index("blk") * length, length)
    *qkv_own, normed_in, sums = project_qkv(
        hidden, first, cos, sin, row_gain(attn_gain), w_query, w_key, w_value, rows, n_blk
    )
    qkv, attended, lse, gathered = [], [], [], []
    for r in range(rows):
        qkv.append(exchange(qkv_own[r]))
    for r in range(rows):
        o_f, o_low, lse_r = attn_fwd(lens, qkv[r], r, n_docs)
        attended.append(o_f)
        lse.append(lse_r)
        gathered.append(exchange(o_low))
    attn_low, normed_mid, inner_low, d_gate, d_up, block_out, d_resid_mid, d_branch, d_gain_two, *d_attn = feed_forward(
        gathered, hidden, cot, row_gain(ffn_gain), w_out, w_gate, w_up, w_down
    )
    d_own = [exchange(d_attn[r]) for r in range(rows)]

    inner = w_gate.shape[1]
    by_blocks = (model // n_dp) % 128 == 0 and width == 128 and (inner // n_blk) % 32 == 0
    early, late = scatter_steps(False), scatter_steps(True)
    if by_blocks:
        (gate_blocks,) = wgrad([early], d_gate, [normed_mid], False)
        (up_blocks,) = wgrad([early], d_up, [normed_mid], False)
        (down_blocks,) = wgrad([late], inner_low, [cot], True)
        (project_blocks,) = wgrad([early], attn_low, [d_branch], True)
        ffn_blocks = (gate_blocks, up_blocks, down_blocks, project_blocks)

    back_own = [attn_bwd(lens, qkv[r], d_own[r], attended[r], lse[r], r, n_docs) for r in range(rows)]
    if by_blocks:
        back_own[-1], ffn_blocks = lax.optimization_barrier((back_own[-1], ffn_blocks))
    back = [exchange(b) for b in back_own]
    if by_blocks:
        sums_ffn = scatter_sum(ffn_blocks, (early, early, late, early), 0)
        back, sums_ffn = lax.optimization_barrier((back, sums_ffn))
    low, grad_first = turn_back(back, cos, sin)

    if by_blocks:
        qkv_blocks = wgrad([early, late, early], normed_in, [low[0], low[1], low[2]], True)
        sums_qkv = scatter_sum(qkv_blocks, (early, late, early), 1)
        block = lambda pieces, r, c: whole_block(pieces, r, c)
        grad_gate = block(sums_ffn[0], inner // n_blk, model // n_dp).T
        grad_up = block(sums_ffn[1], inner // n_blk, model // n_dp).T
        grad_down = block(sums_ffn[2], inner // n_dp, model // n_blk)
        grad_project = block(sums_ffn[3], model // n_dp, model // n_blk)
        grad_query, grad_key, grad_value = [block(a, model // n_dp, model // n_blk) for a in sums_qkv]
    else:
        mid_cf, in_cf = core_first(normed_mid), core_first(normed_in)
        sent = lambda a, b, name, y: scatter(dot_tn(a, b).astype(BF16), name, y).astype(F32)
        grad_down = sent(inner_low, y_first(cot), "dp", False)
        grad_gate = sent(d_gate, mid_cf, "blk", False).T
        grad_up = sent(d_up, mid_cf, "blk", True).T
        grad_project = sent(d_branch, core_first(attn_low), "blk", True).T
        grad_query, grad_key, grad_value = [sent(low[k], in_cf, "blk", True).T for k in range(3)]
    grad_input, d_gain_one = input_grad(hidden, d_resid_mid, row_gain(attn_gain), low, w_query, w_key, w_value)

    squares = jnp.sum(sums, axis=(0, 2))
    squares = jnp.concatenate([squares, jnp.zeros((126,), F32)])
    early_sums = total(jnp.concatenate([d_gain_two.reshape(model), squares]))
    gain_one = total(d_gain_one.reshape(model))
    n_entries = n_blk * length * rows * n_dp * model
    return (
        unflat(block_out),
        unflat(grad_input),
        unflat(grad_first),
        grad_query,
        grad_key,
        grad_value,
        grad_project,
        grad_gate,
        grad_up,
        grad_down,
        gain_one,
        early_sums[:model],
        early_sums[model] / n_entries,
        early_sums[model + 1] / n_entries,
    )


def solution(mesh):
    tokens = P("blk", "dp", None)
    return jax.shard_map(
        body,
        mesh=mesh,
        in_specs=(tokens, tokens, P("dp", None)) + (P(),) * 9 + (tokens,),
        out_specs=(tokens,) * 3 + (P("dp", "blk"),) * 7 + (P(),) * 4,
        check_vma=False,
    )
```

```python
import functools

import jax
import jax.numpy as jnp
from jax import lax
from jax.experimental import pallas as pl
from jax.experimental.pallas import tpu as pltpu
from jax.sharding import PartitionSpec as P

HEADS = 16
HEAD_DIM = 64
NEG = -1e30
EPS = 1e-06
F32 = jnp.float32
BF16 = jnp.bfloat16
VMEM_LIMIT = 56 * 2**20
MESH = pl.DeviceIdType.MESH


def dot(a, b):
    return jnp.dot(a, b, preferred_element_type=F32)


def dot_nt(a, b):
    return lax.dot_general(a, b, (((1,), (1,)), ((), ())), preferred_element_type=F32)


def dot_tn(a, b):
    return lax.dot_general(a, b, (((0,), (0,)), ((), ())), preferred_element_type=F32)


def swap_halves(v):
    half = HEAD_DIM // 2
    width = v.shape[-1]
    lane = lax.broadcasted_iota(jnp.int32, v.shape, v.ndim - 1)
    left = pltpu.roll(v, width - half, v.ndim - 1)
    right = pltpu.roll(v, half, v.ndim - 1)
    return jnp.where(lane % HEAD_DIM < half, left, right)


def qkv_kernel(rows, length, width, hidden_ref, first_ref, cos_ref, sin_ref, gain_ref, wq_ref, wk_ref, wv_ref, *outs):
    out_refs, (normed_ref, sums_ref) = outs[:rows], outs[rows:]
    chunk = wq_ref.shape[1]

    @pl.when(pl.program_id(0) == 0)
    def _():
        for r in range(rows):
            at = pl.ds(r * length, length)
            normed, _ = rms_parts(hidden_ref[at, :].astype(F32))
            normed_ref[at, :] = (normed * gain_ref[...]).astype(BF16)

    first_sum = jnp.zeros((1, chunk), F32)
    mixed_sum = jnp.zeros((1, chunk), F32)
    for r in range(rows):
        at = pl.ds(r * length, length)
        normed = normed_ref[at, :]
        cos, sin = cos_ref[at, :], sin_ref[at, :]
        for which, w_ref in ((0, wq_ref), (1, wk_ref)):
            raw = dot(normed, w_ref[...])
            for c in range(chunk // 128):
                part = raw[:, c * 128 : (c + 1) * 128]
                turned = (part * cos + swap_halves(part) * sin).astype(BF16)
                for s in range(128 // width):
                    out_refs[r][c * (128 // width) + s, which] = turned[:, s * width : (s + 1) * width]
        first = first_ref[at, :].astype(F32)
        mixed = 0.5 * dot(normed, wv_ref[...]) + 0.5 * first
        first_sum = first_sum + jnp.sum(first * first, axis=0, keepdims=True)
        mixed_sum = mixed_sum + jnp.sum(mixed * mixed, axis=0, keepdims=True)
        low = mixed.astype(BF16)
        for s in range(chunk // width):
            out_refs[r][s, 2] = low[:, s * width : (s + 1) * width]
    sums_ref[0, 0:1] = first_sum
    sums_ref[0, 1:2] = mixed_sum


def project_qkv(hidden, first, cos, sin, gain, w_query, w_key, w_value, rows, n_blk):
    tokens, model = hidden.shape
    length, width = tokens // rows, model // n_blk
    chunk = 256
    steps = model // chunk
    full = lambda rows, cols: pl.BlockSpec((rows, cols), lambda j: (0, 0))
    weight = pl.BlockSpec((model, chunk), lambda j: (0, j))
    return pl.pallas_call(
        functools.partial(qkv_kernel, rows, length, width),
        grid=(steps,),
        in_specs=[
            full(tokens, model),
            pl.BlockSpec((tokens, chunk), lambda j: (0, j)),
            full(tokens, 128),
            full(tokens, 128),
            full(1, model),
            weight,
            weight,
            weight,
        ],
        out_specs=[pl.BlockSpec((chunk // width, 3, length, width), lambda j: (j, 0, 0, 0))] * rows
        + [full(tokens, model), pl.BlockSpec((1, 2, chunk), lambda j: (j, 0, 0))],
        out_shape=[jax.ShapeDtypeStruct((n_blk, 3, length, width), BF16)] * rows
        + [jax.ShapeDtypeStruct((tokens, model), BF16), jax.ShapeDtypeStruct((steps, 2, chunk), F32)],
        compiler_params=pltpu.CompilerParams(vmem_limit_bytes=VMEM_LIMIT),
        cost_estimate=pl.CostEstimate(
            flops=6 * tokens * model * model, bytes_accessed=6 * model * model + 10 * tokens * model, transcendentals=0
        ),
        name="qkv",
    )(hidden, first, cos, sin, gain, w_query, w_key, w_value)


def doc_ends(lens_ref, row, n_docs):
    ends, total = [], jnp.int32(0)
    for d in range(n_docs):
        total = total + lens_ref[row * n_docs + d]
        ends.append(total)
    return ends


def start_rows(ends, tile, length, heads):
    place = tile * length + lax.broadcasted_iota(jnp.int32, (1, length), 1)
    start = jnp.zeros((1, length), jnp.int32)
    for end in ends:
        start = jnp.where(end <= place, end, start)
    return jnp.concatenate([start] * heads, axis=1), jnp.concatenate([place] * heads, axis=1)


def head_masks(heads, width):
    lane = lax.broadcasted_iota(jnp.int32, (1, width), 1) // HEAD_DIM
    return [jnp.where(lane == h, 1.0, 0.0).astype(BF16) for h in range(heads)]


def by_head(values, masks):
    return jnp.concatenate([values * mask for mask in masks], axis=0)


def attn_fwd_kernel(row, n_docs, heads, lens_ref, qkv_ref, o_ref, low_ref, lse_ref, acc_ref):
    length, width = qkv_ref.shape[2:]
    i = pl.program_id(0)
    ends = doc_ends(lens_ref, row, n_docs)
    start, place = start_rows(ends, i, length, heads)
    lowest = jnp.int32(0)
    for end in ends:
        lowest = jnp.where(end <= i * length, end, lowest)
    lowest = lax.div(lowest, jnp.int32(length))
    masks = head_masks(heads, width)
    queries = by_head(qkv_ref[i, 0] * jnp.asarray(HEAD_DIM**-0.5, BF16), masks)

    def tile(step, carry):
        run_max, run_sum = carry
        j = i - step
        scores = dot_nt(qkv_ref[j, 1], queries)
        key = j * length + lax.broadcasted_iota(jnp.int32, scores.shape, 0)
        scores = jnp.where((key <= place) & (key >= start), scores, NEG)
        new_max = jnp.maximum(run_max, jnp.max(scores, axis=0, keepdims=True))
        weights = jnp.exp(scores - new_max)
        factor = jnp.exp(run_max - new_max)
        run_sum = run_sum * factor + jnp.sum(weights, axis=0, keepdims=True)
        acc_ref[...] = acc_ref[...] * factor + dot_tn(qkv_ref[j, 2], weights.astype(BF16))
        return new_max, run_sum

    acc_ref[...] = jnp.zeros_like(acc_ref)
    run_max, run_sum = lax.fori_loop(
        0,
        i - lowest + 1,
        tile,
        (jnp.full((1, heads * length), NEG, F32), jnp.zeros((1, heads * length), F32)),
    )
    result = acc_ref[...] / run_sum
    joined = jnp.concatenate(
        [
            result[h * HEAD_DIM : (h + 1) * HEAD_DIM, h * length : (h + 1) * length]
            for h in range(heads)
        ],
        axis=0,
    )
    attended = joined.T
    o_ref[0] = attended
    low_ref[0] = attended.astype(BF16)
    total = run_max + jnp.log(run_sum)
    for h in range(heads):
        lse_ref[0, h : h + 1, :] = total[:, h * length : (h + 1) * length]


def attn_fwd(lens, qkv, row, n_docs):
    n_blk, _, length, width = qkv.shape
    heads = width // HEAD_DIM
    tile = pl.BlockSpec((1, length, width), lambda i, lens: (i, 0, 0))
    return pl.pallas_call(
        functools.partial(attn_fwd_kernel, row, n_docs, heads),
        grid_spec=pltpu.PrefetchScalarGridSpec(
            num_scalar_prefetch=1,
            grid=(n_blk,),
            in_specs=[pl.BlockSpec(qkv.shape, lambda i, lens: (0, 0, 0, 0))],
            out_specs=[tile, tile, pl.BlockSpec((1, heads, length), lambda i, lens: (i, 0, 0))],
            scratch_shapes=[pltpu.VMEM((width, heads * length), F32)],
        ),
        out_shape=[
            jax.ShapeDtypeStruct((n_blk, length, width), F32),
            jax.ShapeDtypeStruct((n_blk, length, width), BF16),
            jax.ShapeDtypeStruct((n_blk, heads, length), F32),
        ],
        compiler_params=pltpu.CompilerParams(vmem_limit_bytes=VMEM_LIMIT),
        cost_estimate=pl.CostEstimate(flops=10**10, bytes_accessed=3 * 10**6, transcendentals=10**7),
        name="attn_fwd",
    )(lens, qkv)


def attn_bwd_kernel(rows, n_docs, heads, lens_ref, *refs):
    scratch = refs[4 * rows :]
    for row in range(rows):

        @pl.when(pl.program_id(0) == row)
        def _():
            attn_bwd_row(row, n_docs, heads, lens_ref, *refs[4 * row : 4 * row + 4], *scratch)


def attn_bwd_row(row, n_docs, heads, lens_ref, qkv_ref, do_ref, o_ref, lse_ref, out_ref, dq_ref, delta_ref):
    n_blk, _, length, width = qkv_ref.shape
    j = pl.program_id(1)
    ends = doc_ends(lens_ref, row, n_docs)
    masks = head_masks(heads, width)
    scale = HEAD_DIM**-0.5

    @pl.when(j == 0)
    def _():
        def one(i, _):
            prod = (do_ref[i].astype(F32) * o_ref[i]).T
            for h in range(heads):
                delta_ref[i, h : h + 1, :] = jnp.sum(
                    prod[h * HEAD_DIM : (h + 1) * HEAD_DIM], axis=0, keepdims=True
                )
            dq_ref[i] = jnp.zeros((length, width), F32)
            return 0

        lax.fori_loop(0, n_blk, one, 0)

    last = jnp.int32(n_blk * length)
    final = (j + 1) * length - 1
    for end in reversed(ends):
        last = jnp.where(end > final, end, last)
    highest = lax.div(last - 1, jnp.int32(length))
    keys, values = qkv_ref[j, 1], qkv_ref[j, 2]
    key_heads = [keys * mask for mask in masks]

    def tile(i, carry):
        d_key, d_value = carry
        start, place = start_rows(ends, i, length, heads)
        queries = by_head(qkv_ref[i, 0] * jnp.asarray(scale, BF16), masks)
        d_out = by_head(do_ref[i], masks)
        lse = jnp.concatenate([lse_ref[i, h : h + 1, :] for h in range(heads)], axis=1)
        delta = jnp.concatenate([delta_ref[i, h : h + 1, :] for h in range(heads)], axis=1)
        scores = dot_nt(keys, queries)
        key = j * length + lax.broadcasted_iota(jnp.int32, scores.shape, 0)
        probs = jnp.exp(jnp.where((key <= place) & (key >= start), scores - lse, NEG))
        d_probs = dot_nt(values, d_out)
        d_scores = (probs * (d_probs - delta)).astype(BF16)
        d_value = d_value + dot(probs.astype(BF16), d_out)
        d_key = d_key + dot(d_scores, queries)
        d_query = dq_ref[i]
        for h in range(heads):
            d_query = d_query + dot_tn(d_scores[:, h * length : (h + 1) * length], key_heads[h])
        dq_ref[i] = d_query
        return d_key, d_value

    zero = jnp.zeros((length, width), F32)
    d_key, d_value = lax.fori_loop(j, highest + 1, tile, (zero, zero))
    out_ref[0, 0, 0] = (dq_ref[j] * scale).astype(BF16)
    out_ref[0, 0, 1] = d_key.astype(BF16)
    out_ref[0, 0, 2] = d_value.astype(BF16)


def attn_bwd(lens, qkv, d_out, attended, lse, n_docs):
    rows = len(qkv)
    n_blk, _, length, width = qkv[0].shape
    heads = width // HEAD_DIM
    whole = lambda a: pl.BlockSpec(a.shape, lambda r, j, lens: (0,) * a.ndim)
    arrays = [a for per_row in zip(qkv, d_out, attended, lse) for a in per_row]
    return pl.pallas_call(
        functools.partial(attn_bwd_kernel, rows, n_docs, heads),
        grid_spec=pltpu.PrefetchScalarGridSpec(
            num_scalar_prefetch=1,
            grid=(rows, n_blk),
            in_specs=[whole(a) for a in arrays],
            out_specs=pl.BlockSpec((1, 1, 3, length, width), lambda r, j, lens: (j, r, 0, 0, 0)),
            scratch_shapes=[
                pltpu.VMEM((n_blk, length, width), F32),
                pltpu.VMEM((n_blk, heads, length), F32),
            ],
        ),
        out_shape=jax.ShapeDtypeStruct((n_blk, rows, 3, length, width), BF16),
        compiler_params=pltpu.CompilerParams(vmem_limit_bytes=VMEM_LIMIT),
        cost_estimate=pl.CostEstimate(flops=4 * 10**9, bytes_accessed=12 * 10**6, transcendentals=10**7),
        name="attn_bwd",
    )(lens, *arrays)


def exchange(values):
    return lax.all_to_all(values, "blk", 0, 0, tiled=True)


def bits_of(axis):
    return lax.axis_size(axis).bit_length() - 1


def halve(current, axis, name, bit):
    size = lax.axis_size(name)
    mine = (lax.axis_index(name) >> bit) & 1
    half = current.shape[axis] // 2
    keep = lax.dynamic_slice_in_dim(current, mine * half, half, axis)
    send = lax.dynamic_slice_in_dim(current, (1 - mine) * half, half, axis)
    got = lax.ppermute(send, name, [(k, k ^ (1 << bit)) for k in range(size)])
    return (keep.astype(F32) + got.astype(F32)).astype(BF16)


def core_first(values):
    n_dp = lax.axis_size("dp")
    tokens, cols = values.shape
    return values.reshape(tokens, n_dp // 2, 2, cols // n_dp).transpose(0, 2, 1, 3).reshape(tokens, cols)


def y_first(values):
    n_blk = lax.axis_size("blk")
    tokens, cols = values.shape
    return values.reshape(tokens, n_blk // 2, 2, cols // n_blk).transpose(0, 2, 1, 3).reshape(tokens, cols)


def scatter_steps(y_early):
    dp_bits, blk_bits = bits_of("dp"), bits_of("blk")
    rest = [("dp", b) for b in reversed(range(1, dp_bits))]
    blk = [("blk", 0)] + [("blk", b) for b in reversed(range(1, blk_bits))]
    if y_early:
        return [("dp", 0)] + blk[:1] + rest + blk[1:]
    return [("dp", 0)] + rest + blk


def scatter(grad, rows_name, y_early):
    n_rows = lax.axis_size(rows_name)
    rows, cols = grad.shape
    current = grad.reshape((n_rows // 2, 2, rows // n_rows, cols))
    for name, bit in scatter_steps(y_early):
        if name != rows_name:
            current = halve(current, 3, name, bit)
        elif bit == 0:
            current = halve(current, 1, name, bit)
        else:
            current = halve(current, 0, name, bit)
    return current.reshape(rows // n_rows, current.shape[3])


def total(values):
    for name in ("dp", "blk"):
        size = lax.axis_size(name)
        for bit in range(bits_of(name)):
            values = values + lax.ppermute(values, name, [(k, k ^ (1 << bit)) for k in range(size)])
    return values


def chunks_of(block_rows, block_cols):
    cols = block_cols // 128
    return 4 // cols, cols, block_rows // (4 // cols)


def place_of(order, dp, blk):
    place = 0
    for name, bit in order[1:]:
        place = 2 * place + (((dp if name == "dp" else blk) >> bit) & 1)
    return place


def wgrad_kernel(orders, n_left, n_right, left_is_dp, n_out, left_ref, *refs):
    right_refs, out_refs, turned_ref = refs[:n_out], refs[n_out : 3 * n_out], refs[3 * n_out]
    left_rows, right_cols = left_ref.shape[1] // n_left, right_refs[0].shape[1] // n_right
    row_parts, col_parts, size = chunks_of(left_rows, right_cols)
    q = pl.program_id(0)
    core = lax.axis_index("dp") % 2

    @pl.when(q == 0)
    def _():
        turned_ref[...] = left_ref[...].T

    row_part, col_part = q // col_parts, q % col_parts
    for half in range(2):
        side = core if half == 0 else 1 - core
        left_places = [2 * k + side for k in range(n_left // 2)] if left_is_dp else list(range(n_left))
        right_places = list(range(n_right)) if left_is_dp else [2 * k + side for k in range(n_right // 2)]
        left = jnp.concatenate(
            [
                turned_ref[pl.ds(pl.multiple_of(k * left_rows + row_part * size, 16), size), :]
                for k in left_places
            ],
            axis=0,
        )
        for n, right_ref in enumerate(right_refs):
            if left_is_dp:
                right = right_ref[...]
            else:
                right = jnp.concatenate(
                    [
                        right_ref[:, pl.ds(pl.multiple_of(k * right_cols + col_part * 128, 128), 128)]
                        for k in right_places
                    ],
                    axis=1,
                )
            result = dot(left, right).astype(BF16)
            out_ref = out_refs[2 * n + half]
            for k in range(len(left_places)):
                for m in range(len(right_places)):
                    dp, blk = (2 * k, m) if left_is_dp else (2 * m, k)
                    out_ref[0, place_of(orders[n], dp, blk)] = result[
                        k * size : (k + 1) * size, m * 128 : (m + 1) * 128
                    ]


def wgrad(orders, left, rights, left_is_dp):
    n_dp, n_blk = lax.axis_size("dp"), lax.axis_size("blk")
    n_left, n_right = (n_dp, n_blk) if left_is_dp else (n_blk, n_dp)
    tokens, left_cols = left.shape
    right_cols = rights[0].shape[1]
    row_parts, col_parts, size = chunks_of(left_cols // n_left, right_cols // n_right)
    full = lambda a: pl.BlockSpec(a.shape, lambda q: (0, 0))
    n_out = len(rights)
    blocks = n_dp * n_blk // 2
    flat = pl.pallas_call(
        functools.partial(wgrad_kernel, orders, n_left, n_right, left_is_dp, n_out),
        grid=(4,),
        in_specs=[full(left)] + [full(a) for a in rights],
        out_specs=[pl.BlockSpec((1, blocks, size, 128), lambda q: (q, 0, 0, 0))] * (2 * n_out),
        out_shape=[jax.ShapeDtypeStruct((4, blocks, size, 128), BF16)] * (2 * n_out),
        scratch_shapes=[pltpu.VMEM((left_cols, tokens), BF16)],
        compiler_params=pltpu.CompilerParams(vmem_limit_bytes=VMEM_LIMIT),
        cost_estimate=pl.CostEstimate(
            flops=2 * n_out * tokens * left_cols * right_cols,
            bytes_accessed=2 * tokens * (left_cols + n_out * right_cols) + 2 * n_out * left_cols * right_cols,
            transcendentals=0,
        ),
        name="wgrad",
    )(left, *rights)
    return [tuple(flat[2 * n : 2 * n + 2]) for n in range(n_out)]


def blocks_dot(left_ref, right_ref, left_is_dp, side, col, order, n_dp, n_blk, out_ref, *at):
    size = left_ref.shape[2]
    tokens = left_ref.shape[3]
    if left_is_dp:
        left = jnp.concatenate([left_ref[2 * k + side, 0] for k in range(n_dp // 2)], axis=0)
        right = right_ref[...]
    else:
        cols = right_ref.shape[1] // n_dp
        left = left_ref[:, 0].reshape(n_blk * size, tokens)
        right = jnp.concatenate(
            [
                right_ref[:, pl.ds(pl.multiple_of((2 * k + side) * cols + col * 128, 128), 128)]
                for k in range(n_dp // 2)
            ],
            axis=1,
        )
    result = dot(left, right).astype(BF16)
    for d in range(n_dp // 2):
        for e in range(n_blk):
            k, m = (d, e) if left_is_dp else (e, d)
            out_ref[(*at, place_of(order, 2 * d, e))] = result[k * size : (k + 1) * size, m * 128 : (m + 1) * 128]


def ffn_wgrad_kernel(plans, n_dp, n_blk, rows, *refs):
    source = iter(refs)
    take = lambda n: [next(source) for _ in range(n)]
    n = len(plans)
    lefts, rights, moved, outs, arrived = take(n), take(n), take(rows), take(2 * n), take(rows)
    sents, landed, keeps = take(n), take(n), take(n)
    send_sem, recv_sem, own_sem, out_sem, in_sem = take(5)
    step = pl.program_id(0)
    core, device = partner("dp", 0)
    here = lax.axis_index("blk")

    def own(r):
        return pltpu.make_async_copy(moved[r].at[here], arrived[r].at[here], own_sem.at[r])

    def across(r, m):
        there = (here + m) % n_blk
        return pltpu.make_async_remote_copy(
            src_ref=moved[r].at[there],
            dst_ref=arrived[r].at[here],
            send_sem=out_sem.at[r, m],
            recv_sem=in_sem.at[r, m],
            device_id=(lax.axis_index("dp"), there),
            device_id_type=MESH,
        )

    @pl.when(step == 0)
    def _():
        barrier = pltpu.get_barrier_semaphore()
        pl.semaphore_signal(barrier, inc=1, device_id=device, device_id_type=MESH)
        for m in range(1, n_blk):
            there = (lax.axis_index("dp"), (here + m) % n_blk)
            pl.semaphore_signal(barrier, inc=1, device_id=there, device_id_type=MESH)
        pl.semaphore_wait(barrier, n_blk)
        for r in range(rows):
            own(r).start()
            for m in range(1, n_blk):
                across(r, m).start()

    def remote(n, c):
        return pltpu.make_async_remote_copy(
            src_ref=sents[n].at[c],
            dst_ref=landed[n].at[c],
            send_sem=send_sem.at[n, c],
            recv_sem=recv_sem.at[n, c],
            device_id=device,
            device_id_type=MESH,
        )

    for k, (order, left_is_dp, col_parts) in enumerate(plans):
        c = step - 4 * k

        @pl.when((c >= 0) & (c < 4))
        def _():
            make = lambda side, *out: blocks_dot(
                lefts[k], rights[k], left_is_dp, side, c % col_parts, order, n_dp, n_blk, *out
            )
            make(1 - core, sents[k], c)
            remote(k, c).start()
            make(core, keeps[k], c % 2)

        @pl.when((c >= 1) & (c < 5))
        def _():
            remote(k, c - 1).wait_recv()
            mine, _ = partner(*order[1])
            half = keeps[k].shape[1] // 2
            for out_ref, side in ((outs[2 * k], mine), (outs[2 * k + 1], 1 - mine)):

                def one(d, _):
                    at = side * half + d
                    out_ref[0, d] = keeps[k][(c - 1) % 2, at] + landed[k][c - 1, at]
                    return 0

                lax.fori_loop(0, half, one, 0)

    @pl.when(step == 4 * n)
    def _():
        for k in range(n):
            for c in range(4):
                remote(k, c).wait_send()
        for r in range(rows):
            own(r).wait()
            for m in range(1, n_blk):
                across(r, m).wait()


def ffn_wgrad(items, moved, collective_id):
    n_dp, n_blk = lax.axis_size("dp"), lax.axis_size("blk")
    lefts, rights, plans, left_specs, right_specs, out_specs, outs, scratch = [], [], [], [], [], [], [], []
    held = n_dp * n_blk // 2
    flops = 0
    for k, (order, left_is_dp, left, right) in enumerate(items):
        n_left, n_right = (n_dp, n_blk) if left_is_dp else (n_blk, n_dp)
        cols, tokens = left.shape
        row_parts, col_parts, size = chunks_of(cols // n_left, right.shape[1] // n_right)
        lefts.append(left.reshape(n_left, row_parts, size, tokens))
        rights.append(right)
        plans.append((order, left_is_dp, col_parts))
        flops += 2 * left.size * right.shape[1]
        left_specs.append(
            pl.BlockSpec(
                (n_left, 1, size, tokens),
                lambda p, k=k, col_parts=col_parts: (0, jnp.clip(p - 4 * k, 0, 3) // col_parts, 0, 0),
            )
        )
        right_specs.append(pl.BlockSpec(right.shape, lambda p: (0, 0), pipeline_mode=pl.Buffered(1)))
        out_specs += [
            pl.BlockSpec((1, held // 2, size, 128), lambda p, k=k: (jnp.clip(p - 1 - 4 * k, 0, 3), 0, 0, 0))
        ] * 2
        outs += [jax.ShapeDtypeStruct((4, held // 2, size, 128), BF16)] * 2
        scratch.append((held, size, 128))
    n = len(items)
    flat = pl.pallas_call(
        functools.partial(ffn_wgrad_kernel, plans, n_dp, n_blk, len(moved)),
        grid=(4 * n + 1,),
        in_specs=left_specs + right_specs + [pl.BlockSpec(memory_space=pl.ANY)] * len(moved),
        out_specs=out_specs + [pl.BlockSpec(memory_space=pl.ANY)] * len(moved),
        out_shape=outs + [jax.ShapeDtypeStruct(a.shape, a.dtype) for a in moved],
        scratch_shapes=[pltpu.VMEM((4,) + a, BF16) for a in scratch] * 2
        + [pltpu.VMEM((2,) + a, BF16) for a in scratch]
        + [pltpu.SemaphoreType.DMA((n, 4))] * 2
        + [pltpu.SemaphoreType.DMA((len(moved),))]
        + [pltpu.SemaphoreType.DMA((len(moved), n_blk))] * 2,
        compiler_params=pltpu.CompilerParams(
            collective_id=collective_id, has_side_effects=True, vmem_limit_bytes=VMEM_LIMIT
        ),
        cost_estimate=pl.CostEstimate(flops=flops, bytes_accessed=flops // 400, transcendentals=0),
        name="ffn_wgrad",
    )(*lefts, *rights, *moved)
    return [tuple(flat[2 * k : 2 * k + 2]) for k in range(n)], list(flat[2 * n :])


def swap(values, name, bit):
    size = lax.axis_size(name)
    return lax.ppermute(values, name, [(k, k ^ (1 << bit)) for k in range(size)])


def partner(name, bit):
    here = {"dp": lax.axis_index("dp"), "blk": lax.axis_index("blk")}
    mine = (here[name] // (1 << bit)) % 2
    other = dict(here)
    other[name] = here[name] + (1 - 2 * mine) * (1 << bit)
    return mine, (other["dp"], other["blk"])


def scatter_kernel(orders, fresh, *refs):
    n_streams, n_stages = len(orders), len(orders[0])
    source = iter(refs)
    take = lambda n: [next(source) for _ in range(n)]
    keeps, others, outs, works = take(n_streams), take(n_streams), take(n_streams), take(n_streams)
    landed = [take(n_stages) for _ in range(n_streams)]
    local_sem, other_sem, send_sem, recv_sem = take(4)
    n_chunks, held = keeps[0].shape[:2]
    greeted = sorted({stage for order in orders for stage in order[0 if fresh else 1 :]})

    barrier = pltpu.get_barrier_semaphore()
    for name, bit in greeted:
        pl.semaphore_signal(barrier, inc=1, device_id=partner(name, bit)[1], device_id_type=MESH)
    pl.semaphore_wait(barrier, len(greeted))

    def base_of(k, stage):
        base = 0
        for earlier in range(1, stage):
            base = base + partner(*orders[k][earlier])[0] * (held >> earlier)
        return base

    def local(k, c):
        return pltpu.make_async_copy(keeps[k].at[c], works[k].at[c], local_sem.at[k, c])

    def other(k, c):
        return pltpu.make_async_copy(others[k].at[c], landed[k][0].at[c], other_sem.at[k, c])

    def remote(k, stage, c):
        mine, device = partner(*orders[k][stage])
        half = held >> stage
        if stage == 0:
            sent = others[k].at[c]
        else:
            sent = works[k].at[c, pl.ds(base_of(k, stage) + (1 - mine) * half, half)]
        return pltpu.make_async_remote_copy(
            src_ref=sent,
            dst_ref=landed[k][stage].at[c],
            send_sem=send_sem.at[k, stage, c],
            recv_sem=recv_sem.at[k, stage, c],
            device_id=device,
            device_id_type=MESH,
        )

    def add(k, stage, c):
        base = base_of(k, stage + 1)
        if stage == n_stages - 1:
            outs[k][c] = works[k][c, base].astype(F32) + landed[k][stage][c, 0].astype(F32)
            return

        def one(d, _):
            works[k][c, base + d] = works[k][c, base + d] + landed[k][stage][c, d]
            return 0

        lax.fori_loop(0, held >> stage, one, 0)

    def step(t, _):
        for stage in range(n_stages + 1):
            c = t - stage

            @pl.when((c >= 0) & (c < n_chunks))
            def _():
                for k in range(n_streams):
                    if stage == 0:
                        local(k, c).start()
                        if not fresh:
                            other(k, c).start()
                    else:
                        if stage == 1:
                            local(k, c).wait()
                        if stage == 1 and not fresh:
                            other(k, c).wait()
                        else:
                            remote(k, stage - 1, c).wait_recv()
                        add(k, stage - 1, c)
                    if stage < n_stages and (fresh or stage > 0):
                        remote(k, stage, c).start()

        return 0

    lax.fori_loop(0, n_chunks + n_stages, step, 0)

    def finish(c, _):
        for k in range(n_streams):
            for stage in range(0 if fresh else 1, n_stages):
                remote(k, stage, c).wait_send()
        return 0

    lax.fori_loop(0, n_chunks, finish, 0)


def scatter_sum(pairs, orders, fresh, collective_id):
    n_streams, n_stages = len(pairs), len(orders[0])
    keeps, others = [pair[0] for pair in pairs], [pair[1] for pair in pairs]
    n_chunks, held = keeps[0].shape[:2]
    size = sum(a.size for a in keeps)
    return pl.pallas_call(
        functools.partial(scatter_kernel, orders, fresh),
        in_specs=[pl.BlockSpec(memory_space=pl.ANY)] * (2 * n_streams),
        out_specs=[pl.BlockSpec(memory_space=pltpu.VMEM)] * n_streams,
        out_shape=[jax.ShapeDtypeStruct((n_chunks,) + a.shape[2:], F32) for a in keeps],
        scratch_shapes=[pltpu.VMEM(a.shape, BF16) for a in keeps]
        + [
            pltpu.VMEM((n_chunks, held >> stage) + a.shape[2:], BF16)
            for a in keeps
            for stage in range(n_stages)
        ]
        + [pltpu.SemaphoreType.DMA((n_streams, n_chunks))] * 2
        + [pltpu.SemaphoreType.DMA((n_streams, n_stages, n_chunks))] * 2,
        compiler_params=pltpu.CompilerParams(
            collective_id=collective_id, has_side_effects=True, vmem_limit_bytes=VMEM_LIMIT
        ),
        cost_estimate=pl.CostEstimate(flops=10**11, bytes_accessed=16 * size, transcendentals=0),
        name="scatter_sum",
    )(*keeps, *others)


def whole_block(pieces, block_rows, block_cols):
    row_parts, col_parts, size = chunks_of(block_rows, block_cols)
    shaped = pieces.reshape(row_parts, col_parts, size, 128)
    return jnp.transpose(shaped, (0, 2, 1, 3)).reshape(block_rows, block_cols)


def ffn_kernel(rows, n_blk, *refs):
    source = iter(refs)
    take = lambda n: [next(source) for _ in range(n)]
    gathered = take(rows)
    hidden_ref, cot_ref, gain_ref, wo_ref, wg_ref, wu_ref, wd_ref = take(7)
    lowt_ref, mid_ref, inner_ref, dgate_ref, dup_ref, out_ref, dres_ref, dbranch_ref, dgain_ref = take(9)
    d_attn = take(rows)
    low_ref, resid_ref, acc_ref, dmid_ref = take(4)
    length, width = gathered[0].shape[1:]
    step = pl.program_id(0)

    @pl.when(step == 0)
    def _():
        for r in range(rows):
            at = pl.ds(r * length, length)
            for s in range(n_blk):
                low_ref[at, s * width : (s + 1) * width] = gathered[r][s]
            resid = hidden_ref[at, :].astype(F32) + dot(low_ref[at, :], wo_ref[...])
            resid_ref[at, :] = resid
            normed, _ = rms_parts(resid)
            mid_ref[at, :] = (normed * gain_ref[...]).astype(BF16)
        acc_ref[...] = jnp.zeros_like(acc_ref)
        dmid_ref[...] = jnp.zeros_like(dmid_ref)
        lowt_ref[...] = low_ref[...].T

    for r in range(rows):
        at = pl.ds(r * length, length)
        gate = dot(mid_ref[at, :], wg_ref[...])
        up = dot(mid_ref[at, :], wu_ref[...])
        d_inner = dot_nt(cot_ref[at, :], wd_ref[...])
        sigma = 1.0 / (1.0 + jnp.exp(-gate))
        act = gate * sigma
        inner = (act * up).astype(BF16)
        d_gate = (d_inner * up * (sigma * (1.0 + gate * (1.0 - sigma)))).astype(BF16)
        d_up = (d_inner * act).astype(BF16)
        inner_ref[:, at] = inner.T
        dgate_ref[:, at] = d_gate.T
        dup_ref[:, at] = d_up.T
        acc_ref[at, :] += dot(inner, wd_ref[...])
        dmid_ref[at, :] += dot_nt(d_gate, wg_ref[...]) + dot_nt(d_up, wu_ref[...])

    @pl.when(step == pl.num_programs(0) - 1)
    def _():
        d_gain = jnp.zeros(dgain_ref.shape, F32)
        for r in range(rows):
            at = pl.ds(r * length, length)
            resid = resid_ref[at, :]
            out_ref[at, :] = (resid + acc_ref[at, :]).astype(BF16)
            normed, inverse = rms_parts(resid)
            d_mid = dmid_ref[at, :]
            d_gain = d_gain + jnp.sum(d_mid * normed, axis=0, keepdims=True)
            d_resid = cot_ref[at, :].astype(F32) + norm_back(d_mid * gain_ref[...], normed, inverse)
            dres_ref[at, :] = d_resid
            d_branch = d_resid.astype(BF16)
            dbranch_ref[at, :] = d_branch
            back = dot_nt(d_branch, wo_ref[...]).astype(BF16)
            for s in range(n_blk):
                d_attn[r][s] = back[:, s * width : (s + 1) * width]
        dgain_ref[...] = d_gain


def feed_forward(gathered, hidden, cot, gain, w_out, w_gate, w_up, w_down):
    rows = len(gathered)
    n_blk, length, width = gathered[0].shape
    tokens, model = hidden.shape
    inner = w_gate.shape[1]
    chunk = 256
    full = lambda a: pl.BlockSpec(a.shape, lambda j: (0,) * len(a.shape))
    once = lambda a: pl.BlockSpec(a.shape, lambda j: (0,) * len(a.shape), pipeline_mode=pl.Buffered(1))
    cols = pl.BlockSpec((model, chunk), lambda j: (0, j))
    shape = jax.ShapeDtypeStruct
    inner_rows = pl.BlockSpec((chunk, tokens), lambda j: (j, 0))
    outs = (
        [shape((model, tokens), BF16), shape((tokens, model), BF16)]
        + [shape((inner, tokens), BF16)] * 3
        + [shape((tokens, model), BF16), shape((tokens, model), F32), shape((tokens, model), BF16)]
        + [shape((1, model), F32)]
        + [shape((n_blk, length, width), BF16)] * rows
    )
    return pl.pallas_call(
        functools.partial(ffn_kernel, rows, n_blk),
        grid=(inner // chunk,),
        in_specs=[once(a) for a in gathered]
        + [once(hidden), once(cot), once(gain), once(w_out), cols, cols, pl.BlockSpec((chunk, model), lambda j: (j, 0))],
        out_specs=[full(a) for a in outs[:2]] + [inner_rows] * 3 + [full(a) for a in outs[5:]],
        out_shape=outs,
        scratch_shapes=[pltpu.VMEM((tokens, model), BF16)] + [pltpu.VMEM((tokens, model), F32)] * 3,
        compiler_params=pltpu.CompilerParams(vmem_limit_bytes=VMEM_LIMIT),
        cost_estimate=pl.CostEstimate(
            flops=12 * tokens * model * inner + 4 * tokens * model * model,
            bytes_accessed=6 * model * inner + 6 * tokens * inner + 20 * tokens * model,
            transcendentals=tokens * inner,
        ),
        name="ffn",
    )(*gathered, hidden, cot, gain, w_out, w_gate, w_up, w_down)


def turn_back_kernel(cos_ref, sin_ref, back_ref, low_ref, first_ref):
    n_blk, rows, _, length, width = back_ref.shape
    which = pl.program_id(0)
    for r in range(rows):
        at = pl.ds(r * length, length)
        for s in range(n_blk):
            cols = slice(s * width, (s + 1) * width)
            values = back_ref[s, r, 0].astype(F32)

            @pl.when(which < 2)
            def _():
                cos, sin = cos_ref[at, :width], sin_ref[at, :width]
                wide = values if width == 128 else jnp.concatenate([values, values], axis=1)
                swapped = swap_halves(wide)[:, :width]
                low_ref[0, at, cols] = (values * cos - swapped * sin).astype(BF16)

            @pl.when(which == 2)
            def _():
                first_ref[at, cols] = 0.5 * values
                low_ref[0, at, cols] = (0.5 * values).astype(BF16)


def turn_back(back, cos, sin):
    n_blk, rows, _, length, width = back.shape
    tokens, model = rows * length, n_blk * width
    full = lambda a: pl.BlockSpec(a.shape, lambda w: (0, 0))
    return pl.pallas_call(
        turn_back_kernel,
        grid=(3,),
        in_specs=[full(cos), full(sin), pl.BlockSpec((n_blk, rows, 1, length, width), lambda w: (0, 0, w, 0, 0))],
        out_specs=[
            pl.BlockSpec((1, tokens, model), lambda w: (w, 0, 0)),
            pl.BlockSpec((tokens, model), lambda w: (0, 0)),
        ],
        out_shape=[jax.ShapeDtypeStruct((3, tokens, model), BF16), jax.ShapeDtypeStruct((tokens, model), F32)],
        compiler_params=pltpu.CompilerParams(vmem_limit_bytes=VMEM_LIMIT),
        name="turn_back",
    )(cos, sin, back)


def input_grad_kernel(hidden_ref, dres_ref, gain_ref, low_ref, wq_ref, wk_ref, wv_ref, out_ref, dgain_ref):
    tokens = hidden_ref.shape[0]
    half = tokens // 2
    d_gain = jnp.zeros(dgain_ref.shape, F32)
    for r in range(2):
        at = pl.ds(r * half, half)
        d_normed = (
            dot_nt(low_ref[0, at, :], wq_ref[...])
            + dot_nt(low_ref[1, at, :], wk_ref[...])
            + dot_nt(low_ref[2, at, :], wv_ref[...])
        )
        normed, inverse = rms_parts(hidden_ref[at, :].astype(F32))
        d_gain = d_gain + jnp.sum(d_normed * normed, axis=0, keepdims=True)
        out_ref[at, :] = dres_ref[at, :] + norm_back(d_normed * gain_ref[...], normed, inverse)
    dgain_ref[...] = d_gain


def input_grad(hidden, d_resid, gain, low, w_query, w_key, w_value):
    tokens, model = hidden.shape
    return pl.pallas_call(
        input_grad_kernel,
        out_shape=[jax.ShapeDtypeStruct((tokens, model), F32), jax.ShapeDtypeStruct((1, model), F32)],
        compiler_params=pltpu.CompilerParams(vmem_limit_bytes=VMEM_LIMIT),
        cost_estimate=pl.CostEstimate(
            flops=6 * tokens * model * model, bytes_accessed=6 * model * model + 16 * tokens * model, transcendentals=0
        ),
        name="input_grad",
    )(hidden, d_resid, gain, low, w_query, w_key, w_value)


def rms_parts(values):
    inverse_rms = lax.rsqrt(jnp.mean(values * values, axis=-1, keepdims=True) + EPS)
    return values * inverse_rms, inverse_rms


def norm_back(d_normed, normed, inverse_rms):
    return inverse_rms * (d_normed - normed * jnp.mean(d_normed * normed, axis=-1, keepdims=True))


def rope_tables(doc_lengths, offset, length):
    half = HEAD_DIM // 2
    places = offset + jnp.arange(length, dtype=jnp.int32)
    ends = jnp.cumsum(doc_lengths, axis=1)
    start = jnp.max(jnp.where(ends[:, None, :] <= places[None, :, None], ends[:, None, :], 0), axis=2)
    position = (places[None, :] - start).astype(F32).reshape(-1, 1)
    lane = jnp.arange(128, dtype=jnp.int32)
    freq = jnp.power(10000.0, -(lane % half).astype(F32) * 2.0 / HEAD_DIM)
    angles = position * freq[None, :]
    sign = jnp.where(lane % HEAD_DIM < half, -1.0, 1.0)
    return jnp.cos(angles), jnp.sin(angles) * sign[None, :]


def body(
    hidden_in,
    first_values,
    doc_lengths,
    w_query,
    w_key,
    w_value,
    w_out,
    w_gate,
    w_up,
    w_down,
    attn_gain,
    ffn_gain,
    out_cotangent,
):
    length, rows, model = hidden_in.shape
    n_docs = doc_lengths.shape[1]
    n_blk, n_dp = lax.axis_size("blk"), lax.axis_size("dp")
    width = model // n_blk
    tokens = rows * length
    flat = lambda a: jnp.transpose(a, (1, 0, 2)).reshape(tokens, model)
    unflat = lambda a: jnp.transpose(a.reshape(rows, length, model), (1, 0, 2))
    lens = doc_lengths.reshape(-1)

    hidden, cot, first = flat(hidden_in), flat(out_cotangent), flat(first_values)
    row_gain = lambda gain: gain.reshape(1, model)

    cos, sin = rope_tables(doc_lengths, lax.axis_index("blk") * length, length)
    *qkv_own, normed_in, sums = project_qkv(
        hidden, first, cos, sin, row_gain(attn_gain), w_query, w_key, w_value, rows, n_blk
    )
    qkv, attended, lse, gathered = [], [], [], []
    for r in range(rows):
        qkv.append(exchange(qkv_own[r]))
    for r in range(rows):
        o_f, o_low, lse_r = attn_fwd(lens, qkv[r], r, n_docs)
        attended.append(o_f)
        lse.append(lse_r)
        gathered.append(exchange(o_low))
    attn_low_t, normed_mid, inner_t, d_gate_t, d_up_t, block_out, d_resid_mid, d_branch, d_gain_two, *d_attn = feed_forward(
        gathered, hidden, cot, row_gain(ffn_gain), w_out, w_gate, w_up, w_down
    )

    inner = w_gate.shape[1]
    by_blocks = (model // n_dp) % 128 == 0 and width == 128 and (inner // n_blk) % 32 == 0
    early, late = scatter_steps(False), scatter_steps(True)
    if by_blocks:
        folded, d_own = ffn_wgrad(
            (
                (early, False, d_gate_t, normed_mid),
                (early, False, d_up_t, normed_mid),
                (late, True, inner_t, cot),
                (late, True, attn_low_t, d_branch),
            ),
            d_attn,
            2,
        )
        kept = [keep for keep, sent in folded]
        ffn_got = [swap(sent, *(early[1] if k < 2 else late[1])) for k, (_, sent) in enumerate(folded)]
        back_own = attn_bwd(lens, qkv, d_own, attended, lse, n_docs)
        back = exchange(back_own)
        token, kept = lax.optimization_barrier((back_own, kept))
        sums_ffn = scatter_sum(list(zip(kept, ffn_got)), (early[1:],) * 2 + (late[1:],) * 2, False, 0)
        back, sums_ffn = lax.optimization_barrier((back, sums_ffn))
    else:
        d_own = [exchange(d_attn[r]) for r in range(rows)]
        back = exchange(attn_bwd(lens, qkv, d_own, attended, lse, n_docs))
    low, grad_first = turn_back(back, cos, sin)

    if by_blocks:
        qkv_pairs = wgrad([early, late, early], normed_in, [low[0], low[1], low[2]], True)
        sums_qkv = scatter_sum(qkv_pairs, (early, late, early), True, 1)
        block = lambda pieces, r, c: whole_block(pieces, r, c)
        grad_gate = block(sums_ffn[0], inner // n_blk, model // n_dp).T
        grad_up = block(sums_ffn[1], inner // n_blk, model // n_dp).T
        grad_down = block(sums_ffn[2], inner // n_dp, model // n_blk)
        grad_project = block(sums_ffn[3], model // n_dp, model // n_blk)
        grad_query, grad_key, grad_value = [block(a, model // n_dp, model // n_blk) for a in sums_qkv]
    else:
        mid_cf, in_cf = core_first(normed_mid), core_first(normed_in)
        sent = lambda a, b, name, y: scatter(dot_tn(a, b).astype(BF16), name, y).astype(F32)
        grad_down = sent(inner_t.T, y_first(cot), "dp", False)
        grad_gate = sent(d_gate_t.T, mid_cf, "blk", False).T
        grad_up = sent(d_up_t.T, mid_cf, "blk", True).T
        grad_project = sent(d_branch, core_first(attn_low_t.T), "blk", True).T
        grad_query, grad_key, grad_value = [sent(low[k], in_cf, "blk", True).T for k in range(3)]
    grad_input, d_gain_one = input_grad(hidden, d_resid_mid, row_gain(attn_gain), low, w_query, w_key, w_value)

    squares = jnp.sum(sums, axis=(0, 2))
    small = jnp.concatenate([d_gain_one.reshape(model), d_gain_two.reshape(model), squares, jnp.zeros((126,), F32)])
    small = total(small)
    n_entries = n_blk * length * rows * n_dp * model
    return (
        unflat(block_out),
        unflat(grad_input),
        unflat(grad_first),
        grad_query,
        grad_key,
        grad_value,
        grad_project,
        grad_gate,
        grad_up,
        grad_down,
        small[:model],
        small[model : 2 * model],
        small[2 * model] / n_entries,
        small[2 * model + 1] / n_entries,
    )


def solution(mesh):
    tokens = P("blk", "dp", None)
    return jax.shard_map(
        body,
        mesh=mesh,
        in_specs=(tokens, tokens, P("dp", None)) + (P(),) * 9 + (tokens,),
        out_specs=(tokens,) * 3 + (P("dp", "blk"),) * 7 + (P(),) * 4,
        check_vma=False,
    )
```

```python
import functools

import jax
import jax.numpy as jnp
from jax import lax
from jax.experimental import pallas as pl
from jax.experimental.pallas import tpu as pltpu
from jax.sharding import PartitionSpec as P

HEADS = 16
HEAD_DIM = 64
NEG = -1e30
EPS = 1e-06
F32 = jnp.float32
BF16 = jnp.bfloat16
VMEM_LIMIT = 56 * 2**20
MESH = pl.DeviceIdType.MESH


def dot(a, b):
    return jnp.dot(a, b, preferred_element_type=F32)


def dot_nt(a, b):
    return lax.dot_general(a, b, (((1,), (1,)), ((), ())), preferred_element_type=F32)


def dot_tn(a, b):
    return lax.dot_general(a, b, (((0,), (0,)), ((), ())), preferred_element_type=F32)


def swap_halves(v):
    half = HEAD_DIM // 2
    width = v.shape[-1]
    lane = lax.broadcasted_iota(jnp.int32, v.shape, v.ndim - 1)
    left = pltpu.roll(v, width - half, v.ndim - 1)
    right = pltpu.roll(v, half, v.ndim - 1)
    return jnp.where(lane % HEAD_DIM < half, left, right)


def qkv_kernel(rows, length, width, hidden_ref, first_ref, cos_ref, sin_ref, gain_ref, wq_ref, wk_ref, wv_ref, *outs):
    out_refs, (normed_ref, sums_ref) = outs[:rows], outs[rows:]
    chunk = wq_ref.shape[1]

    @pl.when(pl.program_id(0) == 0)
    def _():
        for r in range(rows):
            at = pl.ds(r * length, length)
            normed, _ = rms_parts(hidden_ref[at, :].astype(F32))
            normed_ref[at, :] = (normed * gain_ref[...]).astype(BF16)

    first_sum = jnp.zeros((1, chunk), F32)
    mixed_sum = jnp.zeros((1, chunk), F32)
    for r in range(rows):
        at = pl.ds(r * length, length)
        normed = normed_ref[at, :]
        cos, sin = cos_ref[at, :], sin_ref[at, :]
        for which, w_ref in ((0, wq_ref), (1, wk_ref)):
            raw = dot(normed, w_ref[...])
            for c in range(chunk // 128):
                part = raw[:, c * 128 : (c + 1) * 128]
                turned = (part * cos + swap_halves(part) * sin).astype(BF16)
                for s in range(128 // width):
                    out_refs[r][c * (128 // width) + s, which] = turned[:, s * width : (s + 1) * width]
        first = first_ref[at, :].astype(F32)
        mixed = 0.5 * dot(normed, wv_ref[...]) + 0.5 * first
        first_sum = first_sum + jnp.sum(first * first, axis=0, keepdims=True)
        mixed_sum = mixed_sum + jnp.sum(mixed * mixed, axis=0, keepdims=True)
        low = mixed.astype(BF16)
        for s in range(chunk // width):
            out_refs[r][s, 2] = low[:, s * width : (s + 1) * width]
    sums_ref[0, 0:1] = first_sum
    sums_ref[0, 1:2] = mixed_sum


def project_qkv(hidden, first, cos, sin, gain, w_query, w_key, w_value, rows, n_blk):
    tokens, model = hidden.shape
    length, width = tokens // rows, model // n_blk
    chunk = 256
    steps = model // chunk
    full = lambda rows, cols: pl.BlockSpec((rows, cols), lambda j: (0, 0))
    weight = pl.BlockSpec((model, chunk), lambda j: (0, j))
    return pl.pallas_call(
        functools.partial(qkv_kernel, rows, length, width),
        grid=(steps,),
        in_specs=[
            full(tokens, model),
            pl.BlockSpec((tokens, chunk), lambda j: (0, j)),
            full(tokens, 128),
            full(tokens, 128),
            full(1, model),
            weight,
            weight,
            weight,
        ],
        out_specs=[pl.BlockSpec((chunk // width, 3, length, width), lambda j: (j, 0, 0, 0))] * rows
        + [full(tokens, model), pl.BlockSpec((1, 2, chunk), lambda j: (j, 0, 0))],
        out_shape=[jax.ShapeDtypeStruct((n_blk, 3, length, width), BF16)] * rows
        + [jax.ShapeDtypeStruct((tokens, model), BF16), jax.ShapeDtypeStruct((steps, 2, chunk), F32)],
        compiler_params=pltpu.CompilerParams(vmem_limit_bytes=VMEM_LIMIT),
        cost_estimate=pl.CostEstimate(
            flops=6 * tokens * model * model, bytes_accessed=6 * model * model + 10 * tokens * model, transcendentals=0
        ),
        name="qkv",
    )(hidden, first, cos, sin, gain, w_query, w_key, w_value)


def doc_ends(lens_ref, row, n_docs):
    ends, total = [], jnp.int32(0)
    for d in range(n_docs):
        total = total + lens_ref[row * n_docs + d]
        ends.append(total)
    return ends


def start_rows(ends, tile, length, heads):
    place = tile * length + lax.broadcasted_iota(jnp.int32, (1, length), 1)
    start = jnp.zeros((1, length), jnp.int32)
    for end in ends:
        start = jnp.where(end <= place, end, start)
    return jnp.concatenate([start] * heads, axis=1), jnp.concatenate([place] * heads, axis=1)


def head_masks(heads, width):
    lane = lax.broadcasted_iota(jnp.int32, (1, width), 1) // HEAD_DIM
    return [jnp.where(lane == h, 1.0, 0.0).astype(BF16) for h in range(heads)]


def by_head(values, masks):
    return jnp.concatenate([values * mask for mask in masks], axis=0)


def attn_fwd_kernel(row, n_docs, heads, lens_ref, qkv_ref, o_ref, low_ref, lse_ref, acc_ref):
    length, width = qkv_ref.shape[2:]
    i = pl.program_id(0)
    ends = doc_ends(lens_ref, row, n_docs)
    start, place = start_rows(ends, i, length, heads)
    lowest = jnp.int32(0)
    for end in ends:
        lowest = jnp.where(end <= i * length, end, lowest)
    lowest = lax.div(lowest, jnp.int32(length))
    masks = head_masks(heads, width)
    queries = by_head(qkv_ref[i, 0] * jnp.asarray(HEAD_DIM**-0.5, BF16), masks)

    def tile(step, carry):
        run_max, run_sum = carry
        j = i - step
        scores = dot_nt(qkv_ref[j, 1], queries)
        key = j * length + lax.broadcasted_iota(jnp.int32, scores.shape, 0)
        scores = jnp.where((key <= place) & (key >= start), scores, NEG)
        new_max = jnp.maximum(run_max, jnp.max(scores, axis=0, keepdims=True))
        weights = jnp.exp(scores - new_max)
        factor = jnp.exp(run_max - new_max)
        run_sum = run_sum * factor + jnp.sum(weights, axis=0, keepdims=True)
        acc_ref[...] = acc_ref[...] * factor + dot_tn(qkv_ref[j, 2], weights.astype(BF16))
        return new_max, run_sum

    acc_ref[...] = jnp.zeros_like(acc_ref)
    run_max, run_sum = lax.fori_loop(
        0,
        i - lowest + 1,
        tile,
        (jnp.full((1, heads * length), NEG, F32), jnp.zeros((1, heads * length), F32)),
    )
    result = acc_ref[...] / run_sum
    joined = jnp.concatenate(
        [
            result[h * HEAD_DIM : (h + 1) * HEAD_DIM, h * length : (h + 1) * length]
            for h in range(heads)
        ],
        axis=0,
    )
    attended = joined.T
    o_ref[0] = attended
    low_ref[0] = attended.astype(BF16)
    total = run_max + jnp.log(run_sum)
    for h in range(heads):
        lse_ref[0, h : h + 1, :] = total[:, h * length : (h + 1) * length]


def attn_fwd(lens, qkv, row, n_docs):
    n_blk, _, length, width = qkv.shape
    heads = width // HEAD_DIM
    tile = pl.BlockSpec((1, length, width), lambda i, lens: (i, 0, 0))
    return pl.pallas_call(
        functools.partial(attn_fwd_kernel, row, n_docs, heads),
        grid_spec=pltpu.PrefetchScalarGridSpec(
            num_scalar_prefetch=1,
            grid=(n_blk,),
            in_specs=[pl.BlockSpec(qkv.shape, lambda i, lens: (0, 0, 0, 0))],
            out_specs=[tile, tile, pl.BlockSpec((1, heads, length), lambda i, lens: (i, 0, 0))],
            scratch_shapes=[pltpu.VMEM((width, heads * length), F32)],
        ),
        out_shape=[
            jax.ShapeDtypeStruct((n_blk, length, width), F32),
            jax.ShapeDtypeStruct((n_blk, length, width), BF16),
            jax.ShapeDtypeStruct((n_blk, heads, length), F32),
        ],
        compiler_params=pltpu.CompilerParams(vmem_limit_bytes=VMEM_LIMIT),
        cost_estimate=pl.CostEstimate(flops=10**10, bytes_accessed=3 * 10**6, transcendentals=10**7),
        name="attn_fwd",
    )(lens, qkv)


def attn_bwd_kernel(rows, n_docs, heads, lens_ref, *refs):
    scratch = refs[4 * rows :]
    for row in range(rows):

        @pl.when(pl.program_id(0) == row)
        def _():
            attn_bwd_row(row, n_docs, heads, lens_ref, *refs[4 * row : 4 * row + 4], *scratch)


def attn_bwd_row(row, n_docs, heads, lens_ref, qkv_ref, do_ref, o_ref, lse_ref, out_ref, dq_ref, delta_ref):
    n_blk, _, length, width = qkv_ref.shape
    j = pl.program_id(1)
    ends = doc_ends(lens_ref, row, n_docs)
    masks = head_masks(heads, width)
    scale = HEAD_DIM**-0.5

    @pl.when(j == 0)
    def _():
        def one(i, _):
            prod = (do_ref[i].astype(F32) * o_ref[i]).T
            for h in range(heads):
                delta_ref[i, h : h + 1, :] = jnp.sum(
                    prod[h * HEAD_DIM : (h + 1) * HEAD_DIM], axis=0, keepdims=True
                )
            dq_ref[i] = jnp.zeros((length, width), F32)
            return 0

        lax.fori_loop(0, n_blk, one, 0)

    last = jnp.int32(n_blk * length)
    final = (j + 1) * length - 1
    for end in reversed(ends):
        last = jnp.where(end > final, end, last)
    highest = lax.div(last - 1, jnp.int32(length))
    keys, values = qkv_ref[j, 1], qkv_ref[j, 2]
    key_heads = [keys * mask for mask in masks]

    def tile(i, carry):
        d_key, d_value = carry
        start, place = start_rows(ends, i, length, heads)
        queries = by_head(qkv_ref[i, 0] * jnp.asarray(scale, BF16), masks)
        d_out = by_head(do_ref[i], masks)
        lse = jnp.concatenate([lse_ref[i, h : h + 1, :] for h in range(heads)], axis=1)
        delta = jnp.concatenate([delta_ref[i, h : h + 1, :] for h in range(heads)], axis=1)
        scores = dot_nt(keys, queries)
        key = j * length + lax.broadcasted_iota(jnp.int32, scores.shape, 0)
        probs = jnp.exp(jnp.where((key <= place) & (key >= start), scores - lse, NEG))
        d_probs = dot_nt(values, d_out)
        d_scores = (probs * (d_probs - delta)).astype(BF16)
        d_value = d_value + dot(probs.astype(BF16), d_out)
        d_key = d_key + dot(d_scores, queries)
        d_query = dq_ref[i]
        for h in range(heads):
            d_query = d_query + dot_tn(d_scores[:, h * length : (h + 1) * length], key_heads[h])
        dq_ref[i] = d_query
        return d_key, d_value

    zero = jnp.zeros((length, width), F32)
    d_key, d_value = lax.fori_loop(j, highest + 1, tile, (zero, zero))
    out_ref[0, 0, 0] = (dq_ref[j] * scale).astype(BF16)
    out_ref[0, 0, 1] = d_key.astype(BF16)
    out_ref[0, 0, 2] = d_value.astype(BF16)


def attn_bwd(lens, qkv, d_out, attended, lse, n_docs):
    rows = len(qkv)
    n_blk, _, length, width = qkv[0].shape
    heads = width // HEAD_DIM
    whole = lambda a: pl.BlockSpec(a.shape, lambda r, j, lens: (0,) * a.ndim)
    arrays = [a for per_row in zip(qkv, d_out, attended, lse) for a in per_row]
    return pl.pallas_call(
        functools.partial(attn_bwd_kernel, rows, n_docs, heads),
        grid_spec=pltpu.PrefetchScalarGridSpec(
            num_scalar_prefetch=1,
            grid=(rows, n_blk),
            in_specs=[whole(a) for a in arrays],
            out_specs=pl.BlockSpec((1, 1, 3, length, width), lambda r, j, lens: (j, r, 0, 0, 0)),
            scratch_shapes=[
                pltpu.VMEM((n_blk, length, width), F32),
                pltpu.VMEM((n_blk, heads, length), F32),
            ],
        ),
        out_shape=jax.ShapeDtypeStruct((n_blk, rows, 3, length, width), BF16),
        compiler_params=pltpu.CompilerParams(vmem_limit_bytes=VMEM_LIMIT),
        cost_estimate=pl.CostEstimate(flops=4 * 10**9, bytes_accessed=12 * 10**6, transcendentals=10**7),
        name="attn_bwd",
    )(lens, *arrays)


def exchange(values):
    return lax.all_to_all(values, "blk", 0, 0, tiled=True)


def bits_of(axis):
    return lax.axis_size(axis).bit_length() - 1


def halve(current, axis, name, bit):
    size = lax.axis_size(name)
    mine = (lax.axis_index(name) >> bit) & 1
    half = current.shape[axis] // 2
    keep = lax.dynamic_slice_in_dim(current, mine * half, half, axis)
    send = lax.dynamic_slice_in_dim(current, (1 - mine) * half, half, axis)
    got = lax.ppermute(send, name, [(k, k ^ (1 << bit)) for k in range(size)])
    return (keep.astype(F32) + got.astype(F32)).astype(BF16)


def core_first(values):
    n_dp = lax.axis_size("dp")
    tokens, cols = values.shape
    return values.reshape(tokens, n_dp // 2, 2, cols // n_dp).transpose(0, 2, 1, 3).reshape(tokens, cols)


def y_first(values):
    n_blk = lax.axis_size("blk")
    tokens, cols = values.shape
    return values.reshape(tokens, n_blk // 2, 2, cols // n_blk).transpose(0, 2, 1, 3).reshape(tokens, cols)


def scatter_steps(y_early):
    dp_bits, blk_bits = bits_of("dp"), bits_of("blk")
    rest = [("dp", b) for b in reversed(range(1, dp_bits))]
    blk = [("blk", 0)] + [("blk", b) for b in reversed(range(1, blk_bits))]
    if y_early:
        return [("dp", 0)] + blk[:1] + rest + blk[1:]
    return [("dp", 0)] + rest + blk


def block_order(y_early):
    rest = [("dp", b) for b in range(1, bits_of("dp"))]
    blk = [("blk", b) for b in range(bits_of("blk"))]
    if y_early:
        return [("dp", 0)] + blk[:1] + rest + blk[1:]
    return [("dp", 0)] + rest + blk


def scatter(grad, rows_name, y_early):
    n_rows = lax.axis_size(rows_name)
    rows, cols = grad.shape
    current = grad.reshape((n_rows // 2, 2, rows // n_rows, cols))
    for name, bit in scatter_steps(y_early):
        if name != rows_name:
            current = halve(current, 3, name, bit)
        elif bit == 0:
            current = halve(current, 1, name, bit)
        else:
            current = halve(current, 0, name, bit)
    return current.reshape(rows // n_rows, current.shape[3])


def total(values):
    for name in ("dp", "blk"):
        size = lax.axis_size(name)
        for bit in range(bits_of(name)):
            values = values + lax.ppermute(values, name, [(k, k ^ (1 << bit)) for k in range(size)])
    return values


def chunks_of(block_rows, block_cols):
    cols = block_cols // 128
    return 4 // cols, cols, block_rows // (4 // cols)


def place_of(order, dp, blk):
    place = 0
    for name, bit in order[1:]:
        place = 2 * place + (((dp if name == "dp" else blk) >> bit) & 1)
    return place


def blocks_dot(left_ref, right_ref, left_is_dp, side, col, order, n_dp, n_blk, out_ref, *at):
    size = left_ref.shape[2]
    tokens = left_ref.shape[3]
    if left_is_dp:
        left = jnp.concatenate([left_ref[2 * k + side, 0] for k in range(n_dp // 2)], axis=0)
        right = right_ref[...]
    else:
        cols = right_ref.shape[1] // n_dp
        left = left_ref[:, 0].reshape(n_blk * size, tokens)
        right = jnp.concatenate(
            [
                right_ref[:, pl.ds(pl.multiple_of((2 * k + side) * cols + col * 128, 128), 128)]
                for k in range(n_dp // 2)
            ],
            axis=1,
        )
    result = dot(left, right).astype(BF16)
    for d in range(n_dp // 2):
        for e in range(n_blk):
            k, m = (d, e) if left_is_dp else (e, d)
            out_ref[(*at, place_of(order, 2 * d, e))] = result[k * size : (k + 1) * size, m * 128 : (m + 1) * 128]


def ffn_wgrad_kernel(plans, n_dp, n_blk, rows, *refs):
    source = iter(refs)
    take = lambda n: [next(source) for _ in range(n)]
    n = len(plans)
    lefts, rights, moved, outs, arrived = take(n), take(n), take(rows), take(2 * n), take(rows)
    sents, landed, keeps = take(n), take(n), take(n)
    send_sem, recv_sem, own_sem, out_sem, in_sem = take(5)
    step = pl.program_id(0)
    core, device = partner("dp", 0)
    here = lax.axis_index("blk")

    def own(r):
        return pltpu.make_async_copy(moved[r].at[here], arrived[r].at[here], own_sem.at[r])

    def across(r, m):
        there = (here + m) % n_blk
        return pltpu.make_async_remote_copy(
            src_ref=moved[r].at[there],
            dst_ref=arrived[r].at[here],
            send_sem=out_sem.at[r, m],
            recv_sem=in_sem.at[r, m],
            device_id=(lax.axis_index("dp"), there),
            device_id_type=MESH,
        )

    @pl.when(step == 0)
    def _():
        barrier = pltpu.get_barrier_semaphore()
        pl.semaphore_signal(barrier, inc=1, device_id=device, device_id_type=MESH)
        for m in range(1, n_blk):
            there = (lax.axis_index("dp"), (here + m) % n_blk)
            pl.semaphore_signal(barrier, inc=1, device_id=there, device_id_type=MESH)
        pl.semaphore_wait(barrier, n_blk)
        for r in range(rows):
            own(r).start()
            for m in range(1, n_blk):
                across(r, m).start()

    def remote(n, c):
        return pltpu.make_async_remote_copy(
            src_ref=sents[n].at[c],
            dst_ref=landed[n].at[c],
            send_sem=send_sem.at[n, c],
            recv_sem=recv_sem.at[n, c],
            device_id=device,
            device_id_type=MESH,
        )

    for k, (order, left_is_dp, col_parts) in enumerate(plans):
        c = step - 4 * k

        @pl.when((c >= 0) & (c < 4))
        def _():
            make = lambda side, *out: blocks_dot(
                lefts[k], rights[k], left_is_dp, side, c % col_parts, order, n_dp, n_blk, *out
            )
            make(1 - core, sents[k], c)
            remote(k, c).start()
            make(core, keeps[k], c % 2)

        @pl.when((c >= 1) & (c < 5))
        def _():
            remote(k, c - 1).wait_recv()
            mine, _ = partner(*order[1])
            half = keeps[k].shape[1] // 2
            for out_ref, side in ((outs[2 * k], mine), (outs[2 * k + 1], 1 - mine)):

                def one(d, _):
                    at = side * half + d
                    out_ref[0, d] = keeps[k][(c - 1) % 2, at] + landed[k][c - 1, at]
                    return 0

                lax.fori_loop(0, half, one, 0)

    @pl.when(step == 4 * n)
    def _():
        for k in range(n):
            for c in range(4):
                remote(k, c).wait_send()
        for r in range(rows):
            own(r).wait()
            for m in range(1, n_blk):
                across(r, m).wait()


def ffn_wgrad(items, moved, collective_id):
    n_dp, n_blk = lax.axis_size("dp"), lax.axis_size("blk")
    lefts, rights, plans, left_specs, right_specs, out_specs, outs, scratch = [], [], [], [], [], [], [], []
    held = n_dp * n_blk // 2
    flops = 0
    for k, (order, left_is_dp, left, right) in enumerate(items):
        n_left, n_right = (n_dp, n_blk) if left_is_dp else (n_blk, n_dp)
        cols, tokens = left.shape
        row_parts, col_parts, size = chunks_of(cols // n_left, right.shape[1] // n_right)
        lefts.append(left.reshape(n_left, row_parts, size, tokens))
        rights.append(right)
        plans.append((order, left_is_dp, col_parts))
        flops += 2 * left.size * right.shape[1]
        left_specs.append(
            pl.BlockSpec(
                (n_left, 1, size, tokens),
                lambda p, k=k, col_parts=col_parts: (0, jnp.clip(p - 4 * k, 0, 3) // col_parts, 0, 0),
            )
        )
        right_specs.append(pl.BlockSpec(right.shape, lambda p: (0, 0), pipeline_mode=pl.Buffered(1)))
        out_specs += [
            pl.BlockSpec((1, held // 2, size, 128), lambda p, k=k: (jnp.clip(p - 1 - 4 * k, 0, 3), 0, 0, 0))
        ] * 2
        outs += [jax.ShapeDtypeStruct((4, held // 2, size, 128), BF16)] * 2
        scratch.append((held, size, 128))
    n = len(items)
    flat = pl.pallas_call(
        functools.partial(ffn_wgrad_kernel, plans, n_dp, n_blk, len(moved)),
        grid=(4 * n + 1,),
        in_specs=left_specs + right_specs + [pl.BlockSpec(memory_space=pl.ANY)] * len(moved),
        out_specs=out_specs + [pl.BlockSpec(memory_space=pl.ANY)] * len(moved),
        out_shape=outs + [jax.ShapeDtypeStruct(a.shape, a.dtype) for a in moved],
        scratch_shapes=[pltpu.VMEM((4,) + a, BF16) for a in scratch] * 2
        + [pltpu.VMEM((2,) + a, BF16) for a in scratch]
        + [pltpu.SemaphoreType.DMA((n, 4))] * 2
        + [pltpu.SemaphoreType.DMA((len(moved),))]
        + [pltpu.SemaphoreType.DMA((len(moved), n_blk))] * 2,
        compiler_params=pltpu.CompilerParams(
            collective_id=collective_id, has_side_effects=True, vmem_limit_bytes=VMEM_LIMIT
        ),
        cost_estimate=pl.CostEstimate(flops=flops, bytes_accessed=flops // 400, transcendentals=0),
        name="ffn_wgrad",
    )(*lefts, *rights, *moved)
    return [tuple(flat[2 * k : 2 * k + 2]) for k in range(n)], list(flat[2 * n :])


def fold_kernel(stages, *refs):
    n = len(stages)
    for k, (name, bit) in enumerate(stages):
        mine, _ = partner(name, bit)
        keep_ref, got_ref = refs[2 * k], refs[2 * k + 1]
        half = keep_ref.shape[1] // 2
        for out_ref, side in ((refs[2 * n + 2 * k], mine), (refs[2 * n + 2 * k + 1], 1 - mine)):

            def one(d, _):
                at = side * half + d
                out_ref[0, d] = keep_ref[0, at] + got_ref[0, at]
                return 0

            lax.fori_loop(0, half, one, 0)


def fold(pairs, stages):
    n = len(pairs)
    arrays = [a for pair in pairs for a in pair]
    block = lambda a, parts: pl.BlockSpec((1, a.shape[1] // parts) + a.shape[2:], lambda c: (c, 0, 0, 0))
    half = lambda a: jax.ShapeDtypeStruct((a.shape[0], a.shape[1] // 2) + a.shape[2:], BF16)
    flat = pl.pallas_call(
        functools.partial(fold_kernel, stages),
        grid=(arrays[0].shape[0],),
        in_specs=[block(a, 1) for a in arrays],
        out_specs=[block(a, 2) for a in arrays],
        out_shape=[half(a) for a in arrays],
        compiler_params=pltpu.CompilerParams(vmem_limit_bytes=VMEM_LIMIT),
        cost_estimate=pl.CostEstimate(flops=10**11, bytes_accessed=10**8, transcendentals=0),
        name="fold",
    )(*arrays)
    return [tuple(flat[2 * k : 2 * k + 2]) for k in range(n)]


def swap(values, name, bit):
    size = lax.axis_size(name)
    return lax.ppermute(values, name, [(k, k ^ (1 << bit)) for k in range(size)])


def partner(name, bit):
    here = {"dp": lax.axis_index("dp"), "blk": lax.axis_index("blk")}
    mine = (here[name] // (1 << bit)) % 2
    other = dict(here)
    other[name] = here[name] + (1 - 2 * mine) * (1 << bit)
    return mine, (other["dp"], other["blk"])


def whole_block(pieces, block_rows, block_cols):
    row_parts, col_parts, size = chunks_of(block_rows, block_cols)
    shaped = pieces.reshape(row_parts, col_parts, size, 128)
    return jnp.transpose(shaped, (0, 2, 1, 3)).reshape(block_rows, block_cols)


def ffn_kernel(rows, n_blk, *refs):
    source = iter(refs)
    take = lambda n: [next(source) for _ in range(n)]
    gathered = take(rows)
    hidden_ref, cot_ref, gain_ref, wo_ref, wg_ref, wu_ref, wd_ref = take(7)
    lowt_ref, mid_ref, inner_ref, dgate_ref, dup_ref, out_ref, dres_ref, dbranch_ref, dgain_ref = take(9)
    d_attn = take(rows)
    low_ref, resid_ref, acc_ref, dmid_ref = take(4)
    length, width = gathered[0].shape[1:]
    step = pl.program_id(0)

    @pl.when(step == 0)
    def _():
        for r in range(rows):
            at = pl.ds(r * length, length)
            for s in range(n_blk):
                low_ref[at, s * width : (s + 1) * width] = gathered[r][s]
            resid = hidden_ref[at, :].astype(F32) + dot(low_ref[at, :], wo_ref[...])
            resid_ref[at, :] = resid
            normed, _ = rms_parts(resid)
            mid_ref[at, :] = (normed * gain_ref[...]).astype(BF16)
        acc_ref[...] = jnp.zeros_like(acc_ref)
        dmid_ref[...] = jnp.zeros_like(dmid_ref)
        lowt_ref[...] = low_ref[...].T

    for r in range(rows):
        at = pl.ds(r * length, length)
        gate = dot(mid_ref[at, :], wg_ref[...])
        up = dot(mid_ref[at, :], wu_ref[...])
        d_inner = dot_nt(cot_ref[at, :], wd_ref[...])
        sigma = 1.0 / (1.0 + jnp.exp(-gate))
        act = gate * sigma
        inner = (act * up).astype(BF16)
        d_gate = (d_inner * up * (sigma * (1.0 + gate * (1.0 - sigma)))).astype(BF16)
        d_up = (d_inner * act).astype(BF16)
        inner_ref[:, at] = inner.T
        dgate_ref[:, at] = d_gate.T
        dup_ref[:, at] = d_up.T
        acc_ref[at, :] += dot(inner, wd_ref[...])
        dmid_ref[at, :] += dot_nt(d_gate, wg_ref[...]) + dot_nt(d_up, wu_ref[...])

    @pl.when(step == pl.num_programs(0) - 1)
    def _():
        d_gain = jnp.zeros(dgain_ref.shape, F32)
        for r in range(rows):
            at = pl.ds(r * length, length)
            resid = resid_ref[at, :]
            out_ref[at, :] = (resid + acc_ref[at, :]).astype(BF16)
            normed, inverse = rms_parts(resid)
            d_mid = dmid_ref[at, :]
            d_gain = d_gain + jnp.sum(d_mid * normed, axis=0, keepdims=True)
            d_resid = cot_ref[at, :].astype(F32) + norm_back(d_mid * gain_ref[...], normed, inverse)
            dres_ref[at, :] = d_resid
            d_branch = d_resid.astype(BF16)
            dbranch_ref[at, :] = d_branch
            back = dot_nt(d_branch, wo_ref[...]).astype(BF16)
            for s in range(n_blk):
                d_attn[r][s] = back[:, s * width : (s + 1) * width]
        dgain_ref[...] = d_gain


def feed_forward(gathered, hidden, cot, gain, w_out, w_gate, w_up, w_down):
    rows = len(gathered)
    n_blk, length, width = gathered[0].shape
    tokens, model = hidden.shape
    inner = w_gate.shape[1]
    chunk = 256
    full = lambda a: pl.BlockSpec(a.shape, lambda j: (0,) * len(a.shape))
    once = lambda a: pl.BlockSpec(a.shape, lambda j: (0,) * len(a.shape), pipeline_mode=pl.Buffered(1))
    cols = pl.BlockSpec((model, chunk), lambda j: (0, j))
    shape = jax.ShapeDtypeStruct
    inner_rows = pl.BlockSpec((chunk, tokens), lambda j: (j, 0))
    outs = (
        [shape((model, tokens), BF16), shape((tokens, model), BF16)]
        + [shape((inner, tokens), BF16)] * 3
        + [shape((tokens, model), BF16), shape((tokens, model), F32), shape((tokens, model), BF16)]
        + [shape((1, model), F32)]
        + [shape((n_blk, length, width), BF16)] * rows
    )
    return pl.pallas_call(
        functools.partial(ffn_kernel, rows, n_blk),
        grid=(inner // chunk,),
        in_specs=[once(a) for a in gathered]
        + [once(hidden), once(cot), once(gain), once(w_out), cols, cols, pl.BlockSpec((chunk, model), lambda j: (j, 0))],
        out_specs=[full(a) for a in outs[:2]] + [inner_rows] * 3 + [full(a) for a in outs[5:]],
        out_shape=outs,
        scratch_shapes=[pltpu.VMEM((tokens, model), BF16)] + [pltpu.VMEM((tokens, model), F32)] * 3,
        compiler_params=pltpu.CompilerParams(vmem_limit_bytes=VMEM_LIMIT),
        cost_estimate=pl.CostEstimate(
            flops=12 * tokens * model * inner + 4 * tokens * model * model,
            bytes_accessed=6 * model * inner + 6 * tokens * inner + 20 * tokens * model,
            transcendentals=tokens * inner,
        ),
        name="ffn",
    )(*gathered, hidden, cot, gain, w_out, w_gate, w_up, w_down)


class Halving:
    def __init__(self, order, work, sent, landed, send_sem, recv_sem):
        self.order, self.work, self.sent, self.landed = order, work, sent, landed
        self.send_sem, self.recv_sem = send_sem, recv_sem
        self.held = work.shape[1]

    def base(self, stage):
        base = 0
        for earlier in range(1, stage):
            base = base + partner(*self.order[earlier])[0] * (self.held >> earlier)
        return base

    def remote(self, stage, c):
        mine, device = partner(*self.order[stage])
        half = self.held >> stage
        if stage == 0:
            sent = self.sent.at[c]
        else:
            sent = self.work.at[c, pl.ds(self.base(stage) + (1 - mine) * half, half)]
        return pltpu.make_async_remote_copy(
            src_ref=sent,
            dst_ref=self.landed[stage].at[c],
            send_sem=self.send_sem.at[stage, c],
            recv_sem=self.recv_sem.at[stage, c],
            device_id=device,
            device_id_type=MESH,
        )

    def add(self, stage, c):
        base = self.base(stage + 1)

        def one(d, _):
            self.work[c, base + d] = self.work[c, base + d] + self.landed[stage][c, d]
            return 0

        lax.fori_loop(0, self.held >> stage, one, 0)

    def result(self, c):
        stage = len(self.order) - 1
        return self.work[c, self.base(stage + 1)].astype(F32) + self.landed[stage][c, 0].astype(F32)


def tail_kernel(ffn_orders, qkv_orders, n_dp, n_blk, *refs):
    source = iter(refs)
    take = lambda n: [next(source) for _ in range(n)]
    n_ffn, n_qkv = len(ffn_orders), 3
    ffn_stages, qkv_stages = len(ffn_orders[0]), len(qkv_orders[0])
    cos_ref, sin_ref, gain_ref, small_ref = take(4)
    loads = take(7)
    keeps, gots = take(n_ffn), take(n_ffn)
    ffn_outs, qkv_outs = take(n_ffn), take(n_qkv)
    first_ref, input_ref, total_ref = take(3)
    back_ref, turned_ref, hidden_ref, dres_ref, *weights = here = take(7)
    low_ref, acc_ref, vecs, vec_landed = take(4)
    load_sem, keep_sem, got_sem, vec_send, vec_recv = take(5)
    streams = []
    for k, order in enumerate(ffn_orders):
        work, *landed = take(1 + ffn_stages)
        streams.append(Halving(order, work, None, landed, *take(2)))
    late = []
    for u in range(n_qkv):
        late.append([])
        for order in qkv_orders:
            work, sent, *landed = take(2 + qkv_stages)
            late[u].append(Halving(order, work, sent, landed, *take(2)))
    _, rows, _, length, width = back_ref.shape
    core, _ = partner("dp", 0)
    n_chunks = keeps[0].shape[0]

    load = [pltpu.make_async_copy(a, b, load_sem.at[k]) for k, (a, b) in enumerate(zip(loads, here))]
    keep_copy = lambda k, c: pltpu.make_async_copy(keeps[k].at[c], streams[k].work.at[c], keep_sem.at[k, c])
    got_copy = lambda k, c: pltpu.make_async_copy(gots[k].at[c], streams[k].landed[0].at[c], got_sem.at[k, c])
    load[0].start()
    load[1].start()
    for c in range(n_chunks):
        for k in range(n_ffn):
            keep_copy(k, c).start()
            got_copy(k, c).start()
    for copy in load[2:]:
        copy.start()

    everyone = qkv_orders[0]
    barrier = pltpu.get_barrier_semaphore()
    for name, bit in everyone:
        pl.semaphore_signal(barrier, inc=1, device_id=partner(name, bit)[1], device_id_type=MESH)
    pl.semaphore_wait(barrier, len(everyone))

    def ffn(c, stage):
        for k, stream in enumerate(streams):
            if stage == 1:
                keep_copy(k, c).wait()
                got_copy(k, c).wait()
            else:
                stream.remote(stage - 1, c).wait_recv()
            if stage < ffn_stages:
                stream.add(stage - 1, c)
                stream.remote(stage, c).start()
            else:
                ffn_outs[k][c] = stream.result(c)

    def projections(which):
        for r in range(rows):
            at = pl.ds(r * length, length)
            for s in range(n_blk):
                cols = slice(s * width, (s + 1) * width)
                values = back_ref[s, r, which].astype(F32)
                if which < 2:
                    turned = values * cos_ref[at, :] - swap_halves(values) * sin_ref[at, :]
                else:
                    turned = 0.5 * values
                    first_ref[at, cols] = turned
                low_ref[which, at, cols] = turned.astype(BF16)
        for fresh in range(2):
            side = 1 - core if fresh == 0 else core
            left = jnp.concatenate([turned_ref[2 * k + side] for k in range(n_dp // 2)], axis=0)
            size, half = turned_ref.shape[1], turned_ref.shape[1] // 2
            result = dot(left, low_ref[which]).astype(BF16)
            for h, stream in enumerate(late[which]):
                out_ref = stream.sent if fresh == 0 else stream.work
                for d in range(n_dp // 2):
                    for e in range(n_blk):
                        out_ref[0, place_of(stream.order, 2 * d, e)] = result[
                            d * size + h * half : d * size + (h + 1) * half, e * width : (e + 1) * width
                        ]
                if fresh == 0:
                    stream.remote(0, 0).start()

    def late_step(which, stage):
        for h, stream in enumerate(late[which]):
            stream.remote(stage - 1, 0).wait_recv()
            if stage < qkv_stages:
                stream.add(stage - 1, 0)
                stream.remote(stage, 0).start()
            else:
                half = stream.work.shape[2]
                qkv_outs[which][h * half : (h + 1) * half, :] = stream.result(0)

    def vec_copy(e):
        return pltpu.make_async_remote_copy(
            src_ref=vecs.at[e],
            dst_ref=vec_landed.at[e],
            send_sem=vec_send.at[e],
            recv_sem=vec_recv.at[e],
            device_id=partner(*everyone[e])[1],
            device_id_type=MESH,
        )

    model = hidden_ref.shape[1]
    n_vec = len(everyone)

    def matmul():
        for k in range(2, 7):
            load[k].wait()
        for r in range(rows):
            at = pl.ds(r * length, length)
            acc_ref[at, :] = (
                dot_nt(low_ref[0, at, :], weights[0][...])
                + dot_nt(low_ref[1, at, :], weights[1][...])
                + dot_nt(low_ref[2, at, :], weights[2][...])
            )

    def norm():
        d_gain = jnp.zeros((1, model), F32)
        for r in range(rows):
            at = pl.ds(r * length, length)
            normed, inverse = rms_parts(hidden_ref[at, :].astype(F32))
            d_normed = acc_ref[at, :]
            d_gain = d_gain + jnp.sum(d_normed * normed, axis=0, keepdims=True)
            input_ref[at, :] = dres_ref[at, :] + norm_back(d_normed * gain_ref[...], normed, inverse)
        vecs[0, :, :model] = d_gain
        vecs[0, :, model:] = small_ref[...]
        vec_copy(0).start()

    def vec(e):
        vec_copy(e).wait_recv()
        summed = vecs[e] + vec_landed[e]
        if e == n_vec - 1:
            total_ref[...] = summed
        else:
            vecs[e + 1] = summed
            vec_copy(e + 1).start()

    chunks = range(n_chunks)
    for c in chunks:
        ffn(c, 1)
    load[0].wait()
    load[1].wait()
    projections(2)
    projections(1)
    late_step(2, 1)
    projections(0)
    late_step(1, 1)
    ffn(0, 2)
    late_step(0, 1)
    matmul()
    late_step(2, 2)
    ffn(1, 2)
    norm()
    late_step(1, 2)
    ffn(2, 2)
    vecs_left = list(range(n_vec))
    vec(vecs_left.pop(0))
    late_step(2, 3)
    late_step(0, 2)
    ffn(3, 2)
    vec(vecs_left.pop(0))
    late_step(1, 3)
    late_step(0, 3)
    for stage in range(4, qkv_stages + 1):
        vec(vecs_left.pop(0))
        for which in (2, 1, 0):
            late_step(which, stage)
    for c in chunks:
        for stage in range(3, ffn_stages + 1):
            ffn(c, stage)
    for e in vecs_left:
        vec(e)

    def finish(c, _):
        for stream in streams:
            for stage in range(1, ffn_stages):
                stream.remote(stage, c).wait_send()
        return 0

    lax.fori_loop(0, n_chunks, finish, 0)
    for stream in late[0] + late[1] + late[2]:
        for stage in range(qkv_stages):
            stream.remote(stage, 0).wait_send()
    for e in range(n_vec):
        vec_copy(e).wait_send()


def tail(ffn_pairs, ffn_orders, qkv_orders, back, normed_t, hidden, d_resid, weights, cos, sin, gain, small, collective_id):
    n_dp, n_blk = lax.axis_size("dp"), lax.axis_size("blk")
    tokens, model = hidden.shape
    keeps, gots = [pair[0] for pair in ffn_pairs], [pair[1] for pair in ffn_pairs]
    loads = [back, normed_t.reshape(n_dp, model // n_dp, tokens), hidden, d_resid, *weights]
    ffn_stages, qkv_stages, n_qkv = len(ffn_orders[0]), len(qkv_orders[0]), 3
    n_chunks = keeps[0].shape[0]
    block = (model // n_dp, model // n_blk)
    held = n_dp * n_blk // 2
    shape = jax.ShapeDtypeStruct
    vec = (1, model + small.shape[1])
    outs = (
        [shape((n_chunks,) + a.shape[2:], F32) for a in keeps]
        + [shape(block, F32)] * n_qkv
        + [shape((tokens, model), F32)] * 2
        + [shape(vec, F32)]
    )
    scratch = [pltpu.VMEM(a.shape, a.dtype) for a in loads]
    scratch += [
        pltpu.VMEM((n_qkv, tokens, model), BF16),
        pltpu.VMEM((tokens, model), F32),
        pltpu.VMEM((qkv_stages,) + vec, F32),
        pltpu.VMEM((qkv_stages,) + vec, F32),
        pltpu.SemaphoreType.DMA((len(loads),)),
        pltpu.SemaphoreType.DMA((len(keeps), n_chunks)),
        pltpu.SemaphoreType.DMA((len(keeps), n_chunks)),
        pltpu.SemaphoreType.DMA((qkv_stages,)),
        pltpu.SemaphoreType.DMA((qkv_stages,)),
    ]
    for a in keeps:
        scratch.append(pltpu.VMEM(a.shape, BF16))
        scratch += [pltpu.VMEM((n_chunks, a.shape[1] >> stage) + a.shape[2:], BF16) for stage in range(ffn_stages)]
        scratch += [pltpu.SemaphoreType.DMA((ffn_stages, n_chunks))] * 2
    part = (block[0] // len(qkv_orders), block[1])
    for _ in range(n_qkv * len(qkv_orders)):
        scratch += [pltpu.VMEM((1, held) + part, BF16)] * 2
        scratch += [pltpu.VMEM((1, held >> stage) + part, BF16) for stage in range(qkv_stages)]
        scratch += [pltpu.SemaphoreType.DMA((qkv_stages, 1))] * 2
    vmem, anywhere = pl.BlockSpec(memory_space=pltpu.VMEM), pl.BlockSpec(memory_space=pl.ANY)
    return pl.pallas_call(
        functools.partial(tail_kernel, ffn_orders, qkv_orders, n_dp, n_blk),
        in_specs=[vmem] * 4 + [anywhere] * (len(loads) + 2 * len(keeps)),
        out_specs=[vmem] * len(outs),
        out_shape=outs,
        scratch_shapes=scratch,
        compiler_params=pltpu.CompilerParams(
            collective_id=collective_id, has_side_effects=True, vmem_limit_bytes=60 * 2**20
        ),
        cost_estimate=pl.CostEstimate(flops=10**11, bytes_accessed=10**8, transcendentals=0),
        name="tail",
    )(cos, sin, gain, small, *loads, *keeps, *gots)


def turn_back_kernel(cos_ref, sin_ref, back_ref, low_ref, first_ref):
    n_blk, rows, _, length, width = back_ref.shape
    which = pl.program_id(0)
    for r in range(rows):
        at = pl.ds(r * length, length)
        for s in range(n_blk):
            cols = slice(s * width, (s + 1) * width)
            values = back_ref[s, r, 0].astype(F32)

            @pl.when(which < 2)
            def _():
                cos, sin = cos_ref[at, :width], sin_ref[at, :width]
                wide = values if width == 128 else jnp.concatenate([values, values], axis=1)
                swapped = swap_halves(wide)[:, :width]
                low_ref[0, at, cols] = (values * cos - swapped * sin).astype(BF16)

            @pl.when(which == 2)
            def _():
                first_ref[at, cols] = 0.5 * values
                low_ref[0, at, cols] = (0.5 * values).astype(BF16)


def turn_back(back, cos, sin):
    n_blk, rows, _, length, width = back.shape
    tokens, model = rows * length, n_blk * width
    full = lambda a: pl.BlockSpec(a.shape, lambda w: (0, 0))
    return pl.pallas_call(
        turn_back_kernel,
        grid=(3,),
        in_specs=[full(cos), full(sin), pl.BlockSpec((n_blk, rows, 1, length, width), lambda w: (0, 0, w, 0, 0))],
        out_specs=[
            pl.BlockSpec((1, tokens, model), lambda w: (w, 0, 0)),
            pl.BlockSpec((tokens, model), lambda w: (0, 0)),
        ],
        out_shape=[jax.ShapeDtypeStruct((3, tokens, model), BF16), jax.ShapeDtypeStruct((tokens, model), F32)],
        compiler_params=pltpu.CompilerParams(vmem_limit_bytes=VMEM_LIMIT),
        name="turn_back",
    )(cos, sin, back)


def input_grad_kernel(hidden_ref, dres_ref, gain_ref, low_ref, wq_ref, wk_ref, wv_ref, out_ref, dgain_ref):
    tokens = hidden_ref.shape[0]
    half = tokens // 2
    d_gain = jnp.zeros(dgain_ref.shape, F32)
    for r in range(2):
        at = pl.ds(r * half, half)
        d_normed = (
            dot_nt(low_ref[0, at, :], wq_ref[...])
            + dot_nt(low_ref[1, at, :], wk_ref[...])
            + dot_nt(low_ref[2, at, :], wv_ref[...])
        )
        normed, inverse = rms_parts(hidden_ref[at, :].astype(F32))
        d_gain = d_gain + jnp.sum(d_normed * normed, axis=0, keepdims=True)
        out_ref[at, :] = dres_ref[at, :] + norm_back(d_normed * gain_ref[...], normed, inverse)
    dgain_ref[...] = d_gain


def input_grad(hidden, d_resid, gain, low, w_query, w_key, w_value):
    tokens, model = hidden.shape
    return pl.pallas_call(
        input_grad_kernel,
        out_shape=[jax.ShapeDtypeStruct((tokens, model), F32), jax.ShapeDtypeStruct((1, model), F32)],
        compiler_params=pltpu.CompilerParams(vmem_limit_bytes=VMEM_LIMIT),
        cost_estimate=pl.CostEstimate(
            flops=6 * tokens * model * model, bytes_accessed=6 * model * model + 16 * tokens * model, transcendentals=0
        ),
        name="input_grad",
    )(hidden, d_resid, gain, low, w_query, w_key, w_value)


def rms_parts(values):
    inverse_rms = lax.rsqrt(jnp.mean(values * values, axis=-1, keepdims=True) + EPS)
    return values * inverse_rms, inverse_rms


def norm_back(d_normed, normed, inverse_rms):
    return inverse_rms * (d_normed - normed * jnp.mean(d_normed * normed, axis=-1, keepdims=True))


def rope_tables(doc_lengths, offset, length):
    half = HEAD_DIM // 2
    places = offset + jnp.arange(length, dtype=jnp.int32)
    ends = jnp.cumsum(doc_lengths, axis=1)
    start = jnp.max(jnp.where(ends[:, None, :] <= places[None, :, None], ends[:, None, :], 0), axis=2)
    position = (places[None, :] - start).astype(F32).reshape(-1, 1)
    lane = jnp.arange(128, dtype=jnp.int32)
    freq = jnp.power(10000.0, -(lane % half).astype(F32) * 2.0 / HEAD_DIM)
    angles = position * freq[None, :]
    sign = jnp.where(lane % HEAD_DIM < half, -1.0, 1.0)
    return jnp.cos(angles), jnp.sin(angles) * sign[None, :]


def body(
    hidden_in,
    first_values,
    doc_lengths,
    w_query,
    w_key,
    w_value,
    w_out,
    w_gate,
    w_up,
    w_down,
    attn_gain,
    ffn_gain,
    out_cotangent,
):
    length, rows, model = hidden_in.shape
    n_docs = doc_lengths.shape[1]
    n_blk, n_dp = lax.axis_size("blk"), lax.axis_size("dp")
    width = model // n_blk
    tokens = rows * length
    flat = lambda a: jnp.transpose(a, (1, 0, 2)).reshape(tokens, model)
    unflat = lambda a: jnp.transpose(a.reshape(rows, length, model), (1, 0, 2))
    lens = doc_lengths.reshape(-1)

    hidden, cot, first = flat(hidden_in), flat(out_cotangent), flat(first_values)
    row_gain = lambda gain: gain.reshape(1, model)

    cos, sin = rope_tables(doc_lengths, lax.axis_index("blk") * length, length)
    *qkv_own, normed_in, sums = project_qkv(
        hidden, first, cos, sin, row_gain(attn_gain), w_query, w_key, w_value, rows, n_blk
    )
    qkv, attended, lse, gathered = [], [], [], []
    for r in range(rows):
        qkv.append(exchange(qkv_own[r]))
    for r in range(rows):
        o_f, o_low, lse_r = attn_fwd(lens, qkv[r], r, n_docs)
        attended.append(o_f)
        lse.append(lse_r)
        gathered.append(exchange(o_low))
    attn_low_t, normed_mid, inner_t, d_gate_t, d_up_t, block_out, d_resid_mid, d_branch, d_gain_two, *d_attn = feed_forward(
        gathered, hidden, cot, row_gain(ffn_gain), w_out, w_gate, w_up, w_down
    )

    inner = w_gate.shape[1]
    by_blocks = (model // n_dp) % 128 == 0 and width == 128 and (inner // n_blk) % 32 == 0
    early, late = block_order(False), block_order(True)
    if by_blocks:
        folded, d_own = ffn_wgrad(
            (
                (early, False, d_gate_t, normed_mid),
                (early, False, d_up_t, normed_mid),
                (late, True, inner_t, cot),
                (late, True, attn_low_t, d_branch),
            ),
            d_attn,
            2,
        )
        kept = [keep for keep, sent in folded]
        orders = (early, early, late, late)
        ffn_got = [swap(sent, *order[1]) for order, (_, sent) in zip(orders, folded)]
        back_own = attn_bwd(lens, qkv, d_own, attended, lse, n_docs)
        back = exchange(back_own)
        second = [order[2] for order in orders]
        token, kept = lax.optimization_barrier((back_own, kept))
        folded = fold(list(zip(kept, ffn_got)), second)
        ffn_pairs = [(keep, swap(sent, *stage)) for (keep, sent), stage in zip(folded, second)]
    else:
        d_own = [exchange(d_attn[r]) for r in range(rows)]
        back = exchange(attn_bwd(lens, qkv, d_own, attended, lse, n_docs))

    squares = jnp.sum(sums, axis=(0, 2)).reshape(1, 2)
    small = jnp.concatenate([d_gain_two, squares, jnp.zeros((1, 126), F32)], axis=1)
    if by_blocks:
        *blocks, grad_first, grad_input, small = tail(
            ffn_pairs,
            tuple(order[2:] for order in orders),
            (early, late),
            back,
            normed_in.T,
            hidden,
            d_resid_mid,
            (w_query, w_key, w_value),
            cos,
            sin,
            row_gain(attn_gain),
            small,
            0,
        )
        small = small.reshape(-1)
        grad_gate = whole_block(blocks[0], inner // n_blk, model // n_dp).T
        grad_up = whole_block(blocks[1], inner // n_blk, model // n_dp).T
        grad_down = whole_block(blocks[2], inner // n_dp, model // n_blk)
        grad_project = whole_block(blocks[3], model // n_dp, model // n_blk)
        grad_query, grad_key, grad_value = blocks[4:]
    else:
        low, grad_first = turn_back(back, cos, sin)
        mid_cf, in_cf = core_first(normed_mid), core_first(normed_in)
        sent = lambda a, b, name, y: scatter(dot_tn(a, b).astype(BF16), name, y).astype(F32)
        grad_down = sent(inner_t.T, y_first(cot), "dp", False)
        grad_gate = sent(d_gate_t.T, mid_cf, "blk", False).T
        grad_up = sent(d_up_t.T, mid_cf, "blk", True).T
        grad_project = sent(d_branch, core_first(attn_low_t.T), "blk", True).T
        grad_query, grad_key, grad_value = [sent(low[k], in_cf, "blk", True).T for k in range(3)]
        grad_input, d_gain_one = input_grad(hidden, d_resid_mid, row_gain(attn_gain), low, w_query, w_key, w_value)
        small = total(jnp.concatenate([d_gain_one.reshape(model), small.reshape(-1)]))
    n_entries = n_blk * length * rows * n_dp * model
    return (
        unflat(block_out),
        unflat(grad_input),
        unflat(grad_first),
        grad_query,
        grad_key,
        grad_value,
        grad_project,
        grad_gate,
        grad_up,
        grad_down,
        small[:model],
        small[model : 2 * model],
        small[2 * model] / n_entries,
        small[2 * model + 1] / n_entries,
    )


def solution(mesh):
    tokens = P("blk", "dp", None)
    return jax.shard_map(
        body,
        mesh=mesh,
        in_specs=(tokens, tokens, P("dp", None)) + (P(),) * 9 + (tokens,),
        out_specs=(tokens,) * 3 + (P("dp", "blk"),) * 7 + (P(),) * 4,
        check_vma=False,
    )
```

```python
import functools

import jax
import jax.numpy as jnp
from jax import lax
from jax.experimental import pallas as pl
from jax.experimental.pallas import tpu as pltpu
from jax.sharding import PartitionSpec as P

HEADS = 16
HEAD_DIM = 64
NEG = -1e30
EPS = 1e-06
F32 = jnp.float32
BF16 = jnp.bfloat16
VMEM_LIMIT = 56 * 2**20
MESH = pl.DeviceIdType.MESH


def dot(a, b):
    return jnp.dot(a, b, preferred_element_type=F32)


def dot_nt(a, b):
    return lax.dot_general(a, b, (((1,), (1,)), ((), ())), preferred_element_type=F32)


def dot_tn(a, b):
    return lax.dot_general(a, b, (((0,), (0,)), ((), ())), preferred_element_type=F32)


def swap_halves(v):
    half = HEAD_DIM // 2
    width = v.shape[-1]
    lane = lax.broadcasted_iota(jnp.int32, v.shape, v.ndim - 1)
    left = pltpu.roll(v, width - half, v.ndim - 1)
    right = pltpu.roll(v, half, v.ndim - 1)
    return jnp.where(lane % HEAD_DIM < half, left, right)


def qkv_kernel(rows, length, width, hidden_ref, first_ref, cos_ref, sin_ref, gain_ref, wq_ref, wk_ref, wv_ref, *outs):
    out_refs, (normed_ref, sums_ref) = outs[:rows], outs[rows:]
    chunk = wq_ref.shape[1]

    @pl.when(pl.program_id(0) == 0)
    def _():
        for r in range(rows):
            at = pl.ds(r * length, length)
            normed, _ = rms_parts(hidden_ref[at, :].astype(F32))
            normed_ref[at, :] = (normed * gain_ref[...]).astype(BF16)

    first_sum = jnp.zeros((1, chunk), F32)
    mixed_sum = jnp.zeros((1, chunk), F32)
    for r in range(rows):
        at = pl.ds(r * length, length)
        normed = normed_ref[at, :]
        cos, sin = cos_ref[at, :], sin_ref[at, :]
        for which, w_ref in ((0, wq_ref), (1, wk_ref)):
            raw = dot(normed, w_ref[...])
            for c in range(chunk // 128):
                part = raw[:, c * 128 : (c + 1) * 128]
                turned = (part * cos + swap_halves(part) * sin).astype(BF16)
                for s in range(128 // width):
                    out_refs[r][c * (128 // width) + s, which] = turned[:, s * width : (s + 1) * width]
        first = first_ref[at, :].astype(F32)
        mixed = 0.5 * dot(normed, wv_ref[...]) + 0.5 * first
        first_sum = first_sum + jnp.sum(first * first, axis=0, keepdims=True)
        mixed_sum = mixed_sum + jnp.sum(mixed * mixed, axis=0, keepdims=True)
        low = mixed.astype(BF16)
        for s in range(chunk // width):
            out_refs[r][s, 2] = low[:, s * width : (s + 1) * width]
    sums_ref[0, 0:1] = first_sum
    sums_ref[0, 1:2] = mixed_sum


def project_qkv(hidden, first, cos, sin, gain, w_query, w_key, w_value, rows, n_blk):
    tokens, model = hidden.shape
    length, width = tokens // rows, model // n_blk
    chunk = 256
    steps = model // chunk
    full = lambda rows, cols: pl.BlockSpec((rows, cols), lambda j: (0, 0))
    weight = pl.BlockSpec((model, chunk), lambda j: (0, j))
    return pl.pallas_call(
        functools.partial(qkv_kernel, rows, length, width),
        grid=(steps,),
        in_specs=[
            full(tokens, model),
            pl.BlockSpec((tokens, chunk), lambda j: (0, j)),
            full(tokens, 128),
            full(tokens, 128),
            full(1, model),
            weight,
            weight,
            weight,
        ],
        out_specs=[pl.BlockSpec((chunk // width, 3, length, width), lambda j: (j, 0, 0, 0))] * rows
        + [full(tokens, model), pl.BlockSpec((1, 2, chunk), lambda j: (j, 0, 0))],
        out_shape=[jax.ShapeDtypeStruct((n_blk, 3, length, width), BF16)] * rows
        + [jax.ShapeDtypeStruct((tokens, model), BF16), jax.ShapeDtypeStruct((steps, 2, chunk), F32)],
        compiler_params=pltpu.CompilerParams(vmem_limit_bytes=VMEM_LIMIT),
        cost_estimate=pl.CostEstimate(
            flops=6 * tokens * model * model, bytes_accessed=6 * model * model + 10 * tokens * model, transcendentals=0
        ),
        name="qkv",
    )(hidden, first, cos, sin, gain, w_query, w_key, w_value)


def doc_ends(lens_ref, row, n_docs):
    ends, total = [], jnp.int32(0)
    for d in range(n_docs):
        total = total + lens_ref[row * n_docs + d]
        ends.append(total)
    return ends


def start_rows(ends, tile, length, heads):
    place = tile * length + lax.broadcasted_iota(jnp.int32, (1, length), 1)
    start = jnp.zeros((1, length), jnp.int32)
    for end in ends:
        start = jnp.where(end <= place, end, start)
    return jnp.concatenate([start] * heads, axis=1), jnp.concatenate([place] * heads, axis=1)


def head_masks(heads, width):
    lane = lax.broadcasted_iota(jnp.int32, (1, width), 1) // HEAD_DIM
    return [jnp.where(lane == h, 1.0, 0.0).astype(BF16) for h in range(heads)]


def by_head(values, masks):
    return jnp.concatenate([values * mask for mask in masks], axis=0)


def attn_fwd_kernel(row, n_docs, heads, lens_ref, qkv_ref, o_ref, low_ref, lse_ref, acc_ref):
    length, width = qkv_ref.shape[2:]
    i = pl.program_id(0)
    ends = doc_ends(lens_ref, row, n_docs)
    start, place = start_rows(ends, i, length, heads)
    lowest = jnp.int32(0)
    for end in ends:
        lowest = jnp.where(end <= i * length, end, lowest)
    lowest = lax.div(lowest, jnp.int32(length))
    masks = head_masks(heads, width)
    queries = by_head(qkv_ref[i, 0] * jnp.asarray(HEAD_DIM**-0.5, BF16), masks)

    def tile(step, carry):
        run_max, run_sum = carry
        j = i - step
        scores = dot_nt(qkv_ref[j, 1], queries)
        key = j * length + lax.broadcasted_iota(jnp.int32, scores.shape, 0)
        scores = jnp.where((key <= place) & (key >= start), scores, NEG)
        new_max = jnp.maximum(run_max, jnp.max(scores, axis=0, keepdims=True))
        weights = jnp.exp(scores - new_max)
        factor = jnp.exp(run_max - new_max)
        run_sum = run_sum * factor + jnp.sum(weights, axis=0, keepdims=True)
        acc_ref[...] = acc_ref[...] * factor + dot_tn(qkv_ref[j, 2], weights.astype(BF16))
        return new_max, run_sum

    acc_ref[...] = jnp.zeros_like(acc_ref)
    run_max, run_sum = lax.fori_loop(
        0,
        i - lowest + 1,
        tile,
        (jnp.full((1, heads * length), NEG, F32), jnp.zeros((1, heads * length), F32)),
    )
    result = acc_ref[...] / run_sum
    joined = jnp.concatenate(
        [
            result[h * HEAD_DIM : (h + 1) * HEAD_DIM, h * length : (h + 1) * length]
            for h in range(heads)
        ],
        axis=0,
    )
    attended = joined.T
    o_ref[0] = attended
    low_ref[0] = attended.astype(BF16)
    total = run_max + jnp.log(run_sum)
    for h in range(heads):
        lse_ref[0, h : h + 1, :] = total[:, h * length : (h + 1) * length]


def attn_fwd(lens, qkv, row, n_docs):
    n_blk, _, length, width = qkv.shape
    heads = width // HEAD_DIM
    tile = pl.BlockSpec((1, length, width), lambda i, lens: (i, 0, 0))
    return pl.pallas_call(
        functools.partial(attn_fwd_kernel, row, n_docs, heads),
        grid_spec=pltpu.PrefetchScalarGridSpec(
            num_scalar_prefetch=1,
            grid=(n_blk,),
            in_specs=[pl.BlockSpec(qkv.shape, lambda i, lens: (0, 0, 0, 0))],
            out_specs=[tile, tile, pl.BlockSpec((1, heads, length), lambda i, lens: (i, 0, 0))],
            scratch_shapes=[pltpu.VMEM((width, heads * length), F32)],
        ),
        out_shape=[
            jax.ShapeDtypeStruct((n_blk, length, width), F32),
            jax.ShapeDtypeStruct((n_blk, length, width), BF16),
            jax.ShapeDtypeStruct((n_blk, heads, length), F32),
        ],
        compiler_params=pltpu.CompilerParams(vmem_limit_bytes=VMEM_LIMIT),
        cost_estimate=pl.CostEstimate(flops=10**10, bytes_accessed=3 * 10**6, transcendentals=10**7),
        name="attn_fwd",
    )(lens, qkv)


def attn_bwd_kernel(rows, n_docs, heads, lens_ref, *refs):
    scratch = refs[4 * rows :]
    for row in range(rows):

        @pl.when(pl.program_id(0) == row)
        def _():
            attn_bwd_row(row, n_docs, heads, lens_ref, *refs[4 * row : 4 * row + 4], *scratch)


def attn_bwd_row(row, n_docs, heads, lens_ref, qkv_ref, do_ref, o_ref, lse_ref, out_ref, dq_ref, delta_ref):
    n_blk, _, length, width = qkv_ref.shape
    j = pl.program_id(1)
    ends = doc_ends(lens_ref, row, n_docs)
    masks = head_masks(heads, width)
    scale = HEAD_DIM**-0.5

    @pl.when(j == 0)
    def _():
        def one(i, _):
            prod = (do_ref[i].astype(F32) * o_ref[i]).T
            for h in range(heads):
                delta_ref[i, h : h + 1, :] = jnp.sum(
                    prod[h * HEAD_DIM : (h + 1) * HEAD_DIM], axis=0, keepdims=True
                )
            dq_ref[i] = jnp.zeros((length, width), F32)
            return 0

        lax.fori_loop(0, n_blk, one, 0)

    last = jnp.int32(n_blk * length)
    final = (j + 1) * length - 1
    for end in reversed(ends):
        last = jnp.where(end > final, end, last)
    highest = lax.div(last - 1, jnp.int32(length))
    keys, values = qkv_ref[j, 1], qkv_ref[j, 2]
    key_heads = [keys * mask for mask in masks]

    def tile(i, carry):
        d_key, d_value = carry
        start, place = start_rows(ends, i, length, heads)
        queries = by_head(qkv_ref[i, 0] * jnp.asarray(scale, BF16), masks)
        d_out = by_head(do_ref[i], masks)
        lse = jnp.concatenate([lse_ref[i, h : h + 1, :] for h in range(heads)], axis=1)
        delta = jnp.concatenate([delta_ref[i, h : h + 1, :] for h in range(heads)], axis=1)
        scores = dot_nt(keys, queries)
        key = j * length + lax.broadcasted_iota(jnp.int32, scores.shape, 0)
        probs = jnp.exp(jnp.where((key <= place) & (key >= start), scores - lse, NEG))
        d_probs = dot_nt(values, d_out)
        d_scores = (probs * (d_probs - delta)).astype(BF16)
        d_value = d_value + dot(probs.astype(BF16), d_out)
        d_key = d_key + dot(d_scores, queries)
        d_query = dq_ref[i]
        for h in range(heads):
            d_query = d_query + dot_tn(d_scores[:, h * length : (h + 1) * length], key_heads[h])
        dq_ref[i] = d_query
        return d_key, d_value

    zero = jnp.zeros((length, width), F32)
    d_key, d_value = lax.fori_loop(j, highest + 1, tile, (zero, zero))
    out_ref[0, 0, 0] = (dq_ref[j] * scale).astype(BF16)
    out_ref[0, 0, 1] = d_key.astype(BF16)
    out_ref[0, 0, 2] = d_value.astype(BF16)


def attn_bwd(lens, qkv, d_out, attended, lse, n_docs):
    rows = len(qkv)
    n_blk, _, length, width = qkv[0].shape
    heads = width // HEAD_DIM
    whole = lambda a: pl.BlockSpec(a.shape, lambda r, j, lens: (0,) * a.ndim)
    arrays = [a for per_row in zip(qkv, d_out, attended, lse) for a in per_row]
    return pl.pallas_call(
        functools.partial(attn_bwd_kernel, rows, n_docs, heads),
        grid_spec=pltpu.PrefetchScalarGridSpec(
            num_scalar_prefetch=1,
            grid=(rows, n_blk),
            in_specs=[whole(a) for a in arrays],
            out_specs=pl.BlockSpec((1, 1, 3, length, width), lambda r, j, lens: (j, r, 0, 0, 0)),
            scratch_shapes=[
                pltpu.VMEM((n_blk, length, width), F32),
                pltpu.VMEM((n_blk, heads, length), F32),
            ],
        ),
        out_shape=jax.ShapeDtypeStruct((n_blk, rows, 3, length, width), BF16),
        compiler_params=pltpu.CompilerParams(vmem_limit_bytes=VMEM_LIMIT),
        cost_estimate=pl.CostEstimate(flops=4 * 10**9, bytes_accessed=12 * 10**6, transcendentals=10**7),
        name="attn_bwd",
    )(lens, *arrays)


def exchange(values):
    return lax.all_to_all(values, "blk", 0, 0, tiled=True)


def bits_of(axis):
    return lax.axis_size(axis).bit_length() - 1


def halve(current, axis, name, bit):
    size = lax.axis_size(name)
    mine = (lax.axis_index(name) >> bit) & 1
    half = current.shape[axis] // 2
    keep = lax.dynamic_slice_in_dim(current, mine * half, half, axis)
    send = lax.dynamic_slice_in_dim(current, (1 - mine) * half, half, axis)
    got = lax.ppermute(send, name, [(k, k ^ (1 << bit)) for k in range(size)])
    return (keep.astype(F32) + got.astype(F32)).astype(BF16)


def core_first(values):
    n_dp = lax.axis_size("dp")
    tokens, cols = values.shape
    return values.reshape(tokens, n_dp // 2, 2, cols // n_dp).transpose(0, 2, 1, 3).reshape(tokens, cols)


def y_first(values):
    n_blk = lax.axis_size("blk")
    tokens, cols = values.shape
    return values.reshape(tokens, n_blk // 2, 2, cols // n_blk).transpose(0, 2, 1, 3).reshape(tokens, cols)


def scatter_steps(y_early):
    dp_bits, blk_bits = bits_of("dp"), bits_of("blk")
    rest = [("dp", b) for b in reversed(range(1, dp_bits))]
    blk = [("blk", 0)] + [("blk", b) for b in reversed(range(1, blk_bits))]
    if y_early:
        return [("dp", 0)] + blk[:1] + rest + blk[1:]
    return [("dp", 0)] + rest + blk


def block_order(y_early):
    rest = [("dp", b) for b in range(1, bits_of("dp"))]
    blk = [("blk", b) for b in range(bits_of("blk"))]
    if y_early:
        return [("dp", 0)] + blk[:1] + rest + blk[1:]
    return [("dp", 0)] + rest + blk


def z_order():
    rest = [("dp", b) for b in range(1, bits_of("dp"))]
    blk = [("blk", b) for b in range(bits_of("blk"))]
    return [("dp", 0)] + blk[1:2] + rest + blk[:1] + blk[2:]


def scatter(grad, rows_name, y_early):
    n_rows = lax.axis_size(rows_name)
    rows, cols = grad.shape
    current = grad.reshape((n_rows // 2, 2, rows // n_rows, cols))
    for name, bit in scatter_steps(y_early):
        if name != rows_name:
            current = halve(current, 3, name, bit)
        elif bit == 0:
            current = halve(current, 1, name, bit)
        else:
            current = halve(current, 0, name, bit)
    return current.reshape(rows // n_rows, current.shape[3])


def total(values):
    for name in ("dp", "blk"):
        size = lax.axis_size(name)
        for bit in range(bits_of(name)):
            values = values + lax.ppermute(values, name, [(k, k ^ (1 << bit)) for k in range(size)])
    return values


def chunks_of(block_rows, block_cols):
    cols = block_cols // 128
    return 4 // cols, cols, block_rows // (4 // cols)


def place_of(order, dp, blk):
    place = 0
    for name, bit in order[1:]:
        place = 2 * place + (((dp if name == "dp" else blk) >> bit) & 1)
    return place


def blocks_dot(left_ref, right_ref, left_is_dp, side, col, order, n_dp, n_blk, row, out_ref, *at):
    size = left_ref.shape[2]
    tokens = left_ref.shape[3]
    if left_is_dp:
        left = jnp.concatenate([left_ref[2 * k + side, 0] for k in range(n_dp // 2)], axis=0)
        right = right_ref[...]
    else:
        cols = right_ref.shape[1] // n_dp
        left = left_ref[:, 0].reshape(n_blk * size, tokens)
        right = jnp.concatenate(
            [
                right_ref[:, pl.ds(pl.multiple_of((2 * k + side) * cols + col * 128, 128), 128)]
                for k in range(n_dp // 2)
            ],
            axis=1,
        )
    result = dot(left, right).astype(BF16)
    for d in range(n_dp // 2):
        for e in range(n_blk):
            k, m = (d, e) if left_is_dp else (e, d)
            out_ref[(*at, place_of(order, 2 * d, e), slice(row, row + size))] = result[
                k * size : (k + 1) * size, m * 128 : (m + 1) * 128
            ]


def ffn_wgrad_kernel(plans, n_dp, n_blk, rows, *refs):
    source = iter(refs)
    take = lambda n: [next(source) for _ in range(n)]
    n, n_terms = len(plans), sum(len(terms) for _, terms, _ in plans)
    lefts, rights, moved, outs, arrived = take(n_terms), take(n_terms), take(rows), take(2 * n), take(rows)
    sents, landed, keeps = take(n), take(n), take(n)
    send_sem, recv_sem = take(2)
    own_sem, out_sem, in_sem = take(3) if rows else (None, None, None)
    step = pl.program_id(0)
    core, device = partner("dp", 0)
    here = lax.axis_index("blk")

    def own(r):
        return pltpu.make_async_copy(moved[r].at[here], arrived[r].at[here], own_sem.at[r])

    def across(r, m):
        there = (here + m) % n_blk
        return pltpu.make_async_remote_copy(
            src_ref=moved[r].at[there],
            dst_ref=arrived[r].at[here],
            send_sem=out_sem.at[r, m],
            recv_sem=in_sem.at[r, m],
            device_id=(lax.axis_index("dp"), there),
            device_id_type=MESH,
        )

    @pl.when(step == 0)
    def _():
        barrier = pltpu.get_barrier_semaphore()
        pl.semaphore_signal(barrier, inc=1, device_id=device, device_id_type=MESH)
        for m in range(1, n_blk if rows else 1):
            there = (lax.axis_index("dp"), (here + m) % n_blk)
            pl.semaphore_signal(barrier, inc=1, device_id=there, device_id_type=MESH)
        pl.semaphore_wait(barrier, n_blk if rows else 1)
        for r in range(rows):
            own(r).start()
            for m in range(1, n_blk):
                across(r, m).start()

    def remote(n, c):
        return pltpu.make_async_remote_copy(
            src_ref=sents[n].at[c],
            dst_ref=landed[n].at[c],
            send_sem=send_sem.at[n, c],
            recv_sem=recv_sem.at[n, c],
            device_id=device,
            device_id_type=MESH,
        )

    first = 0
    for k, (order, terms, pieces) in enumerate(plans):
        c = step - first
        first += pieces

        @pl.when((c >= 0) & (c < pieces))
        def _():
            def make(side, *out):
                for at, left_is_dp, col_parts, row in terms:
                    blocks_dot(lefts[at], rights[at], left_is_dp, side, c % col_parts, order, n_dp, n_blk, row, *out)

            make(1 - core, sents[k], c)
            remote(k, c).start()
            make(core, keeps[k], c % 2)

        @pl.when((c >= 1) & (c < pieces + 1))
        def _():
            remote(k, c - 1).wait_recv()
            mine, _ = partner(*order[1])
            half = keeps[k].shape[1] // 2
            for out_ref, side in ((outs[2 * k], mine), (outs[2 * k + 1], 1 - mine)):

                def one(d, _):
                    at = side * half + d
                    out_ref[0, d] = keeps[k][(c - 1) % 2, at] + landed[k][c - 1, at]
                    return 0

                lax.fori_loop(0, half, one, 0)

    @pl.when(step == first)
    def _():
        for k in range(n):
            for c in range(plans[k][2]):
                remote(k, c).wait_send()
        for r in range(rows):
            own(r).wait()
            for m in range(1, n_blk):
                across(r, m).wait()


def ffn_wgrad(items, moved, flops, collective_id):
    n_dp, n_blk = lax.axis_size("dp"), lax.axis_size("blk")
    lefts, rights, plans, left_specs, right_specs, out_specs, outs, scratch = [], [], [], [], [], [], [], []
    held = n_dp * n_blk // 2
    steps = 0
    for order, wanted, terms in items:
        count, row, plan = len(wanted), 0, []
        for left_is_dp, left, right in terms:
            n_left, n_right = (n_dp, n_blk) if left_is_dp else (n_blk, n_dp)
            cols, tokens = left.shape
            row_parts, col_parts, size = chunks_of(cols // n_left, right.shape[1] // n_right)
            plan.append((len(lefts), left_is_dp, col_parts, row))
            row += size
            lefts.append(left.reshape(n_left, row_parts, size, tokens))
            rights.append(right)
            left_specs.append(
                pl.BlockSpec(
                    (n_left, 1, size, tokens),
                    lambda p, at=steps, low=wanted[0], count=count, col_parts=col_parts: (
                        0,
                        (low + jnp.clip(p - at, 0, count - 1)) // col_parts,
                        0,
                        0,
                    ),
                )
            )
            right_specs.append(pl.BlockSpec(right.shape, lambda p: (0, 0), pipeline_mode=pl.Buffered(1)))
        plans.append((order, plan, count))
        out_specs += [
            pl.BlockSpec(
                (1, held // 2, row, 128), lambda p, at=steps, count=count: (jnp.clip(p - 1 - at, 0, count - 1), 0, 0, 0)
            )
        ] * 2
        outs += [jax.ShapeDtypeStruct((count, held // 2, row, 128), BF16)] * 2
        scratch.append((count, held, row, 128))
        steps += count
    n = len(items)
    flat = pl.pallas_call(
        functools.partial(ffn_wgrad_kernel, plans, n_dp, n_blk, len(moved)),
        grid=(steps + 1,),
        in_specs=left_specs + right_specs + [pl.BlockSpec(memory_space=pl.ANY)] * len(moved),
        out_specs=out_specs + [pl.BlockSpec(memory_space=pl.ANY)] * len(moved),
        out_shape=outs + [jax.ShapeDtypeStruct(a.shape, a.dtype) for a in moved],
        scratch_shapes=[pltpu.VMEM(a, BF16) for a in scratch] * 2
        + [pltpu.VMEM((2,) + a[1:], BF16) for a in scratch]
        + [pltpu.SemaphoreType.DMA((n, 4))] * 2
        + ([pltpu.SemaphoreType.DMA((len(moved),))] + [pltpu.SemaphoreType.DMA((len(moved), n_blk))] * 2 if moved else []),
        compiler_params=pltpu.CompilerParams(
            collective_id=collective_id, has_side_effects=True, vmem_limit_bytes=VMEM_LIMIT
        ),
        cost_estimate=pl.CostEstimate(flops=flops, bytes_accessed=10**7, transcendentals=0),
        name="ffn_wgrad",
    )(*lefts, *rights, *moved)
    return [tuple(flat[2 * k : 2 * k + 2]) for k in range(n)], list(flat[2 * n :])


def fold_kernel(stages, *refs):
    n = len(stages)
    for k, (name, bit) in enumerate(stages):
        mine, _ = partner(name, bit)
        keep_ref, got_ref = refs[2 * k], refs[2 * k + 1]
        half = keep_ref.shape[1] // 2
        for out_ref, side in ((refs[2 * n + 2 * k], mine), (refs[2 * n + 2 * k + 1], 1 - mine)):

            def one(d, _):
                at = side * half + d
                out_ref[0, d] = keep_ref[0, at] + got_ref[0, at]
                return 0

            lax.fori_loop(0, half, one, 0)


def fold(pairs, stages, flops):
    n = len(pairs)
    arrays = [a for pair in pairs for a in pair]
    block = lambda a, parts: pl.BlockSpec((1, a.shape[1] // parts) + a.shape[2:], lambda c: (c, 0, 0, 0))
    half = lambda a: jax.ShapeDtypeStruct((a.shape[0], a.shape[1] // 2) + a.shape[2:], BF16)
    flat = pl.pallas_call(
        functools.partial(fold_kernel, stages),
        grid=(arrays[0].shape[0],),
        in_specs=[block(a, 1) for a in arrays],
        out_specs=[block(a, 2) for a in arrays],
        out_shape=[half(a) for a in arrays],
        compiler_params=pltpu.CompilerParams(vmem_limit_bytes=VMEM_LIMIT),
        cost_estimate=pl.CostEstimate(flops=flops, bytes_accessed=10**7, transcendentals=0),
        name="fold",
    )(*arrays)
    return [tuple(flat[2 * k : 2 * k + 2]) for k in range(n)]


def swap(values, name, bit):
    size = lax.axis_size(name)
    return lax.ppermute(values, name, [(k, k ^ (1 << bit)) for k in range(size)])


def partner(name, bit):
    here = {"dp": lax.axis_index("dp"), "blk": lax.axis_index("blk")}
    mine = (here[name] // (1 << bit)) % 2
    other = dict(here)
    other[name] = here[name] + (1 - 2 * mine) * (1 << bit)
    return mine, (other["dp"], other["blk"])


def whole_block(pieces, block_rows, block_cols):
    row_parts, col_parts, size = chunks_of(block_rows, block_cols)
    shaped = pieces.reshape(row_parts, col_parts, size, 128)
    return jnp.transpose(shaped, (0, 2, 1, 3)).reshape(block_rows, block_cols)


def ffn_kernel(rows, n_blk, *refs):
    source = iter(refs)
    take = lambda n: [next(source) for _ in range(n)]
    gathered = take(rows)
    hidden_ref, cot_ref, gain_ref, wo_ref, wg_ref, wu_ref, wd_ref = take(7)
    lowt_ref, mid_ref, inner_ref, dgate_ref, dup_ref, out_ref, dres_ref, dbranch_ref, dgain_ref = take(9)
    d_attn = take(rows)
    low_ref, resid_ref, acc_ref, dmid_ref = take(4)
    length, width = gathered[0].shape[1:]
    step = pl.program_id(0)

    @pl.when(step == 0)
    def _():
        for r in range(rows):
            at = pl.ds(r * length, length)
            for s in range(n_blk):
                low_ref[at, s * width : (s + 1) * width] = gathered[r][s]
            resid = hidden_ref[at, :].astype(F32) + dot(low_ref[at, :], wo_ref[...])
            resid_ref[at, :] = resid
            normed, _ = rms_parts(resid)
            mid_ref[at, :] = (normed * gain_ref[...]).astype(BF16)
        acc_ref[...] = jnp.zeros_like(acc_ref)
        dmid_ref[...] = jnp.zeros_like(dmid_ref)
        lowt_ref[...] = low_ref[...].T

    for r in range(rows):
        at = pl.ds(r * length, length)
        gate = dot(mid_ref[at, :], wg_ref[...])
        up = dot(mid_ref[at, :], wu_ref[...])
        d_inner = dot_nt(cot_ref[at, :], wd_ref[...])
        sigma = 1.0 / (1.0 + jnp.exp(-gate))
        act = gate * sigma
        inner = (act * up).astype(BF16)
        d_gate = (d_inner * up * (sigma * (1.0 + gate * (1.0 - sigma)))).astype(BF16)
        d_up = (d_inner * act).astype(BF16)
        inner_ref[:, at] = inner.T
        dgate_ref[:, at] = d_gate.T
        dup_ref[:, at] = d_up.T
        acc_ref[at, :] += dot(inner, wd_ref[...])
        dmid_ref[at, :] += dot_nt(d_gate, wg_ref[...]) + dot_nt(d_up, wu_ref[...])

    @pl.when(step == pl.num_programs(0) - 1)
    def _():
        d_gain = jnp.zeros(dgain_ref.shape, F32)
        for r in range(rows):
            at = pl.ds(r * length, length)
            resid = resid_ref[at, :]
            out_ref[at, :] = (resid + acc_ref[at, :]).astype(BF16)
            normed, inverse = rms_parts(resid)
            d_mid = dmid_ref[at, :]
            d_gain = d_gain + jnp.sum(d_mid * normed, axis=0, keepdims=True)
            d_resid = cot_ref[at, :].astype(F32) + norm_back(d_mid * gain_ref[...], normed, inverse)
            dres_ref[at, :] = d_resid
            d_branch = d_resid.astype(BF16)
            dbranch_ref[at, :] = d_branch
            back = dot_nt(d_branch, wo_ref[...]).astype(BF16)
            for s in range(n_blk):
                d_attn[r][s] = back[:, s * width : (s + 1) * width]
        dgain_ref[...] = d_gain


def feed_forward(gathered, hidden, cot, gain, w_out, w_gate, w_up, w_down):
    rows = len(gathered)
    n_blk, length, width = gathered[0].shape
    tokens, model = hidden.shape
    inner = w_gate.shape[1]
    chunk = 256
    full = lambda a: pl.BlockSpec(a.shape, lambda j: (0,) * len(a.shape))
    once = lambda a: pl.BlockSpec(a.shape, lambda j: (0,) * len(a.shape), pipeline_mode=pl.Buffered(1))
    cols = pl.BlockSpec((model, chunk), lambda j: (0, j))
    shape = jax.ShapeDtypeStruct
    inner_rows = pl.BlockSpec((chunk, tokens), lambda j: (j, 0))
    outs = (
        [shape((model, tokens), BF16), shape((tokens, model), BF16)]
        + [shape((inner, tokens), BF16)] * 3
        + [shape((tokens, model), BF16), shape((tokens, model), F32), shape((tokens, model), BF16)]
        + [shape((1, model), F32)]
        + [shape((n_blk, length, width), BF16)] * rows
    )
    return pl.pallas_call(
        functools.partial(ffn_kernel, rows, n_blk),
        grid=(inner // chunk,),
        in_specs=[once(a) for a in gathered]
        + [once(hidden), once(cot), once(gain), once(w_out), cols, cols, pl.BlockSpec((chunk, model), lambda j: (j, 0))],
        out_specs=[full(a) for a in outs[:2]] + [inner_rows] * 3 + [full(a) for a in outs[5:]],
        out_shape=outs,
        scratch_shapes=[pltpu.VMEM((tokens, model), BF16)] + [pltpu.VMEM((tokens, model), F32)] * 3,
        compiler_params=pltpu.CompilerParams(vmem_limit_bytes=VMEM_LIMIT),
        cost_estimate=pl.CostEstimate(
            flops=12 * tokens * model * inner + 4 * tokens * model * model,
            bytes_accessed=6 * model * inner + 6 * tokens * inner + 20 * tokens * model,
            transcendentals=tokens * inner,
        ),
        name="ffn",
    )(*gathered, hidden, cot, gain, w_out, w_gate, w_up, w_down)


class Halving:
    def __init__(self, order, work, sent, landed, send_sem, recv_sem):
        self.order, self.work, self.sent, self.landed = order, work, sent, landed
        self.send_sem, self.recv_sem = send_sem, recv_sem
        self.held = work.shape[1]

    def base(self, stage):
        base = 0
        for earlier in range(1, stage):
            base = base + partner(*self.order[earlier])[0] * (self.held >> earlier)
        return base

    def remote(self, stage, c):
        mine, device = partner(*self.order[stage])
        half = self.held >> stage
        if stage == 0:
            sent = self.sent.at[c]
        else:
            sent = self.work.at[c, pl.ds(self.base(stage) + (1 - mine) * half, half)]
        return pltpu.make_async_remote_copy(
            src_ref=sent,
            dst_ref=self.landed[stage].at[c],
            send_sem=self.send_sem.at[stage, c],
            recv_sem=self.recv_sem.at[stage, c],
            device_id=device,
            device_id_type=MESH,
        )

    def add(self, stage, c):
        base = self.base(stage + 1)

        def one(d, _):
            self.work[c, base + d] = self.work[c, base + d] + self.landed[stage][c, d]
            return 0

        lax.fori_loop(0, self.held >> stage, one, 0)

    def result(self, c):
        stage = len(self.order) - 1
        return self.work[c, self.base(stage + 1)].astype(F32) + self.landed[stage][c, 0].astype(F32)


def tail_kernel(ffn_orders, qkv_orders, n_dp, n_blk, *refs):
    source = iter(refs)
    take = lambda n: [next(source) for _ in range(n)]
    n_ffn, n_qkv = len(ffn_orders), 3
    ffn_stages, qkv_stages = len(ffn_orders[0]), len(qkv_orders[0])
    cos_ref, sin_ref, gain_ref, small_ref = take(4)
    loads = take(7)
    keeps, gots = take(n_ffn), take(n_ffn)
    ffn_outs, qkv_outs = take(n_ffn), take(n_qkv)
    first_ref, input_ref, total_ref = take(3)
    back_ref, turned_ref, hidden_ref, dres_ref, *weights = here = take(7)
    low_ref, acc_ref, vecs, vec_landed = take(4)
    load_sem, keep_sem, got_sem, vec_send, vec_recv = take(5)
    streams = []
    for k, order in enumerate(ffn_orders):
        work, *landed = take(1 + ffn_stages)
        streams.append(Halving(order, work, None, landed, *take(2)))
    late = []
    for u in range(n_qkv):
        late.append([])
        for order in qkv_orders:
            work, sent, *landed = take(2 + qkv_stages)
            late[u].append(Halving(order, work, sent, landed, *take(2)))
    _, rows, _, length, width = back_ref.shape
    core, _ = partner("dp", 0)
    counts = [a.shape[0] for a in keeps]

    load = [pltpu.make_async_copy(a, b, load_sem.at[k]) for k, (a, b) in enumerate(zip(loads, here))]
    keep_copy = lambda k, c: pltpu.make_async_copy(keeps[k].at[c], streams[k].work.at[c], keep_sem.at[k, c])
    got_copy = lambda k, c: pltpu.make_async_copy(gots[k].at[c], streams[k].landed[0].at[c], got_sem.at[k, c])
    load[0].start()
    load[1].start()
    for c in range(max(counts)):
        for k in range(n_ffn):
            if c < counts[k]:
                keep_copy(k, c).start()
                got_copy(k, c).start()
    for copy in load[2:]:
        copy.start()

    everyone = qkv_orders[0]
    barrier = pltpu.get_barrier_semaphore()
    for name, bit in everyone:
        pl.semaphore_signal(barrier, inc=1, device_id=partner(name, bit)[1], device_id_type=MESH)
    pl.semaphore_wait(barrier, len(everyone))

    def ffn(c, stage):
        for k, stream in enumerate(streams):
            if c >= counts[k]:
                continue
            if stage == 1:
                keep_copy(k, c).wait()
                got_copy(k, c).wait()
            else:
                stream.remote(stage - 1, c).wait_recv()
            if stage < ffn_stages:
                stream.add(stage - 1, c)
                stream.remote(stage, c).start()
            else:
                ffn_outs[k][c] = stream.result(c)

    def projections(which):
        for r in range(rows):
            at = pl.ds(r * length, length)
            for s in range(n_blk):
                cols = slice(s * width, (s + 1) * width)
                values = back_ref[s, r, which].astype(F32)
                if which < 2:
                    turned = values * cos_ref[at, :] - swap_halves(values) * sin_ref[at, :]
                else:
                    turned = 0.5 * values
                    first_ref[at, cols] = turned
                low_ref[which, at, cols] = turned.astype(BF16)
        for fresh in range(2):
            side = 1 - core if fresh == 0 else core
            left = jnp.concatenate([turned_ref[2 * k + side] for k in range(n_dp // 2)], axis=0)
            size, half = turned_ref.shape[1], turned_ref.shape[1] // 2
            result = dot(left, low_ref[which]).astype(BF16)
            for h, stream in enumerate(late[which]):
                out_ref = stream.sent if fresh == 0 else stream.work
                for d in range(n_dp // 2):
                    for e in range(n_blk):
                        out_ref[0, place_of(stream.order, 2 * d, e)] = result[
                            d * size + h * half : d * size + (h + 1) * half, e * width : (e + 1) * width
                        ]
                if fresh == 0:
                    stream.remote(0, 0).start()

    def late_step(which, stage):
        for h, stream in enumerate(late[which]):
            stream.remote(stage - 1, 0).wait_recv()
            if stage < qkv_stages:
                stream.add(stage - 1, 0)
                stream.remote(stage, 0).start()
            else:
                half = stream.work.shape[2]
                qkv_outs[which][h * half : (h + 1) * half, :] = stream.result(0)

    def vec_copy(e):
        return pltpu.make_async_remote_copy(
            src_ref=vecs.at[e],
            dst_ref=vec_landed.at[e],
            send_sem=vec_send.at[e],
            recv_sem=vec_recv.at[e],
            device_id=partner(*everyone[e])[1],
            device_id_type=MESH,
        )

    model = hidden_ref.shape[1]
    n_vec = len(everyone)

    def matmul():
        for k in range(2, 7):
            load[k].wait()
        for r in range(rows):
            at = pl.ds(r * length, length)
            acc_ref[at, :] = (
                dot_nt(low_ref[0, at, :], weights[0][...])
                + dot_nt(low_ref[1, at, :], weights[1][...])
                + dot_nt(low_ref[2, at, :], weights[2][...])
            )

    def norm():
        d_gain = jnp.zeros((1, model), F32)
        for r in range(rows):
            at = pl.ds(r * length, length)
            normed, inverse = rms_parts(hidden_ref[at, :].astype(F32))
            d_normed = acc_ref[at, :]
            d_gain = d_gain + jnp.sum(d_normed * normed, axis=0, keepdims=True)
            input_ref[at, :] = dres_ref[at, :] + norm_back(d_normed * gain_ref[...], normed, inverse)
        vecs[0, :, :model] = d_gain
        vecs[0, :, model:] = small_ref[...]
        vec_copy(0).start()

    def vec(e):
        vec_copy(e).wait_recv()
        summed = vecs[e] + vec_landed[e]
        if e == n_vec - 1:
            total_ref[...] = summed
        else:
            vecs[e + 1] = summed
            vec_copy(e + 1).start()

    chunks = range(max(counts))
    for c in chunks:
        ffn(c, 1)
    load[0].wait()
    load[1].wait()
    projections(2)
    projections(1)
    late_step(2, 1)
    projections(0)
    late_step(1, 1)
    ffn(0, 2)
    late_step(0, 1)
    matmul()
    late_step(2, 2)
    ffn(1, 2)
    norm()
    late_step(1, 2)
    ffn(2, 2)
    vecs_left = list(range(n_vec))
    vec(vecs_left.pop(0))
    late_step(2, 3)
    late_step(0, 2)
    ffn(3, 2)
    vec(vecs_left.pop(0))
    late_step(1, 3)
    late_step(0, 3)
    for stage in range(4, qkv_stages + 1):
        vec(vecs_left.pop(0))
        for which in (2, 1, 0):
            late_step(which, stage)
    for c in chunks:
        for stage in range(3, ffn_stages + 1):
            ffn(c, stage)
    for e in vecs_left:
        vec(e)

    for stream, count in zip(streams, counts):
        for c in range(count):
            for stage in range(1, ffn_stages):
                stream.remote(stage, c).wait_send()
    for stream in late[0] + late[1] + late[2]:
        for stage in range(qkv_stages):
            stream.remote(stage, 0).wait_send()
    for e in range(n_vec):
        vec_copy(e).wait_send()


def tail(ffn_pairs, ffn_orders, qkv_orders, back, normed_t, hidden, d_resid, weights, cos, sin, gain, small, collective_id):
    n_dp, n_blk = lax.axis_size("dp"), lax.axis_size("blk")
    tokens, model = hidden.shape
    keeps, gots = [pair[0] for pair in ffn_pairs], [pair[1] for pair in ffn_pairs]
    loads = [back, normed_t.reshape(n_dp, model // n_dp, tokens), hidden, d_resid, *weights]
    ffn_stages, qkv_stages, n_qkv = len(ffn_orders[0]), len(qkv_orders[0]), 3
    n_chunks = max(a.shape[0] for a in keeps)
    block = (model // n_dp, model // n_blk)
    held = n_dp * n_blk // 2
    shape = jax.ShapeDtypeStruct
    vec = (1, model + small.shape[1])
    outs = (
        [shape(a.shape[:1] + a.shape[2:], F32) for a in keeps]
        + [shape(block, F32)] * n_qkv
        + [shape((tokens, model), F32)] * 2
        + [shape(vec, F32)]
    )
    scratch = [pltpu.VMEM(a.shape, a.dtype) for a in loads]
    scratch += [
        pltpu.VMEM((n_qkv, tokens, model), BF16),
        pltpu.VMEM((tokens, model), F32),
        pltpu.VMEM((qkv_stages,) + vec, F32),
        pltpu.VMEM((qkv_stages,) + vec, F32),
        pltpu.SemaphoreType.DMA((len(loads),)),
        pltpu.SemaphoreType.DMA((len(keeps), n_chunks)),
        pltpu.SemaphoreType.DMA((len(keeps), n_chunks)),
        pltpu.SemaphoreType.DMA((qkv_stages,)),
        pltpu.SemaphoreType.DMA((qkv_stages,)),
    ]
    for a in keeps:
        scratch.append(pltpu.VMEM(a.shape, BF16))
        scratch += [pltpu.VMEM((a.shape[0], a.shape[1] >> stage) + a.shape[2:], BF16) for stage in range(ffn_stages)]
        scratch += [pltpu.SemaphoreType.DMA((ffn_stages, a.shape[0]))] * 2
    part = (block[0] // len(qkv_orders), block[1])
    for _ in range(n_qkv * len(qkv_orders)):
        scratch += [pltpu.VMEM((1, held) + part, BF16)] * 2
        scratch += [pltpu.VMEM((1, held >> stage) + part, BF16) for stage in range(qkv_stages)]
        scratch += [pltpu.SemaphoreType.DMA((qkv_stages, 1))] * 2
    vmem, anywhere = pl.BlockSpec(memory_space=pltpu.VMEM), pl.BlockSpec(memory_space=pl.ANY)
    return pl.pallas_call(
        functools.partial(tail_kernel, ffn_orders, qkv_orders, n_dp, n_blk),
        in_specs=[vmem] * 4 + [anywhere] * (len(loads) + 2 * len(keeps)),
        out_specs=[vmem] * len(outs),
        out_shape=outs,
        scratch_shapes=scratch,
        compiler_params=pltpu.CompilerParams(
            collective_id=collective_id, has_side_effects=True, vmem_limit_bytes=60 * 2**20
        ),
        cost_estimate=pl.CostEstimate(flops=10**11, bytes_accessed=10**8, transcendentals=0),
        name="tail",
    )(cos, sin, gain, small, *loads, *keeps, *gots)


def turn_back_kernel(cos_ref, sin_ref, back_ref, low_ref, first_ref):
    n_blk, rows, _, length, width = back_ref.shape
    which = pl.program_id(0)
    for r in range(rows):
        at = pl.ds(r * length, length)
        for s in range(n_blk):
            cols = slice(s * width, (s + 1) * width)
            values = back_ref[s, r, 0].astype(F32)

            @pl.when(which < 2)
            def _():
                cos, sin = cos_ref[at, :width], sin_ref[at, :width]
                wide = values if width == 128 else jnp.concatenate([values, values], axis=1)
                swapped = swap_halves(wide)[:, :width]
                low_ref[0, at, cols] = (values * cos - swapped * sin).astype(BF16)

            @pl.when(which == 2)
            def _():
                first_ref[at, cols] = 0.5 * values
                low_ref[0, at, cols] = (0.5 * values).astype(BF16)


def turn_back(back, cos, sin):
    n_blk, rows, _, length, width = back.shape
    tokens, model = rows * length, n_blk * width
    full = lambda a: pl.BlockSpec(a.shape, lambda w: (0, 0))
    return pl.pallas_call(
        turn_back_kernel,
        grid=(3,),
        in_specs=[full(cos), full(sin), pl.BlockSpec((n_blk, rows, 1, length, width), lambda w: (0, 0, w, 0, 0))],
        out_specs=[
            pl.BlockSpec((1, tokens, model), lambda w: (w, 0, 0)),
            pl.BlockSpec((tokens, model), lambda w: (0, 0)),
        ],
        out_shape=[jax.ShapeDtypeStruct((3, tokens, model), BF16), jax.ShapeDtypeStruct((tokens, model), F32)],
        compiler_params=pltpu.CompilerParams(vmem_limit_bytes=VMEM_LIMIT),
        name="turn_back",
    )(cos, sin, back)


def input_grad_kernel(hidden_ref, dres_ref, gain_ref, low_ref, wq_ref, wk_ref, wv_ref, out_ref, dgain_ref):
    tokens = hidden_ref.shape[0]
    half = tokens // 2
    d_gain = jnp.zeros(dgain_ref.shape, F32)
    for r in range(2):
        at = pl.ds(r * half, half)
        d_normed = (
            dot_nt(low_ref[0, at, :], wq_ref[...])
            + dot_nt(low_ref[1, at, :], wk_ref[...])
            + dot_nt(low_ref[2, at, :], wv_ref[...])
        )
        normed, inverse = rms_parts(hidden_ref[at, :].astype(F32))
        d_gain = d_gain + jnp.sum(d_normed * normed, axis=0, keepdims=True)
        out_ref[at, :] = dres_ref[at, :] + norm_back(d_normed * gain_ref[...], normed, inverse)
    dgain_ref[...] = d_gain


def input_grad(hidden, d_resid, gain, low, w_query, w_key, w_value):
    tokens, model = hidden.shape
    return pl.pallas_call(
        input_grad_kernel,
        out_shape=[jax.ShapeDtypeStruct((tokens, model), F32), jax.ShapeDtypeStruct((1, model), F32)],
        compiler_params=pltpu.CompilerParams(vmem_limit_bytes=VMEM_LIMIT),
        cost_estimate=pl.CostEstimate(
            flops=6 * tokens * model * model, bytes_accessed=6 * model * model + 16 * tokens * model, transcendentals=0
        ),
        name="input_grad",
    )(hidden, d_resid, gain, low, w_query, w_key, w_value)


def rms_parts(values):
    inverse_rms = lax.rsqrt(jnp.mean(values * values, axis=-1, keepdims=True) + EPS)
    return values * inverse_rms, inverse_rms


def norm_back(d_normed, normed, inverse_rms):
    return inverse_rms * (d_normed - normed * jnp.mean(d_normed * normed, axis=-1, keepdims=True))


def rope_tables(doc_lengths, offset, length):
    half = HEAD_DIM // 2
    places = offset + jnp.arange(length, dtype=jnp.int32)
    ends = jnp.cumsum(doc_lengths, axis=1)
    start = jnp.max(jnp.where(ends[:, None, :] <= places[None, :, None], ends[:, None, :], 0), axis=2)
    position = (places[None, :] - start).astype(F32).reshape(-1, 1)
    lane = jnp.arange(128, dtype=jnp.int32)
    freq = jnp.power(10000.0, -(lane % half).astype(F32) * 2.0 / HEAD_DIM)
    angles = position * freq[None, :]
    sign = jnp.where(lane % HEAD_DIM < half, -1.0, 1.0)
    return jnp.cos(angles), jnp.sin(angles) * sign[None, :]


def body(
    hidden_in,
    first_values,
    doc_lengths,
    w_query,
    w_key,
    w_value,
    w_out,
    w_gate,
    w_up,
    w_down,
    attn_gain,
    ffn_gain,
    out_cotangent,
):
    length, rows, model = hidden_in.shape
    n_docs = doc_lengths.shape[1]
    n_blk, n_dp = lax.axis_size("blk"), lax.axis_size("dp")
    width = model // n_blk
    tokens = rows * length
    flat = lambda a: jnp.transpose(a, (1, 0, 2)).reshape(tokens, model)
    unflat = lambda a: jnp.transpose(a.reshape(rows, length, model), (1, 0, 2))
    lens = doc_lengths.reshape(-1)

    hidden, cot, first = flat(hidden_in), flat(out_cotangent), flat(first_values)
    row_gain = lambda gain: gain.reshape(1, model)

    cos, sin = rope_tables(doc_lengths, lax.axis_index("blk") * length, length)
    *qkv_own, normed_in, sums = project_qkv(
        hidden, first, cos, sin, row_gain(attn_gain), w_query, w_key, w_value, rows, n_blk
    )
    qkv, attended, lse, gathered = [], [], [], []
    for r in range(rows):
        qkv.append(exchange(qkv_own[r]))
    for r in range(rows):
        o_f, o_low, lse_r = attn_fwd(lens, qkv[r], r, n_docs)
        attended.append(o_f)
        lse.append(lse_r)
        gathered.append(exchange(o_low))
    attn_low_t, normed_mid, inner_t, d_gate_t, d_up_t, block_out, d_resid_mid, d_branch, d_gain_two, *d_attn = feed_forward(
        gathered, hidden, cot, row_gain(ffn_gain), w_out, w_gate, w_up, w_down
    )

    inner = w_gate.shape[1]
    by_blocks = (model // n_dp) % 128 == 0 and width == 128 and (inner // n_blk) % 32 == 0
    early, late, middle = block_order(False), block_order(True), z_order()
    if by_blocks:
        orders = (early, late, middle)
        pieces = (0, 1, 2, 3)
        exchanged = lambda pairs, stages: [(keep, swap(sent, *stage)) for (keep, sent), stage in zip(pairs, stages)]
        folded, d_own = ffn_wgrad(
            (
                (early, pieces, [(False, d_gate_t, normed_mid)]),
                (late, pieces, [(False, d_up_t, normed_mid)]),
                (middle, pieces, [(True, inner_t, cot)]),
            ),
            d_attn,
            10**9,
            1,
        )
        ffn_pairs = exchanged(folded, [order[1] for order in orders])
        back_own = attn_bwd(lens, qkv, d_own, attended, lse, n_docs)
        back = exchange(back_own)
        kept = [keep for keep, got in ffn_pairs]
        token, kept = lax.optimization_barrier((back_own, kept))
        second = [order[2] for order in orders]
        folded = fold([(keep, got) for keep, (_, got) in zip(kept, ffn_pairs)], second, 10**9)
        ffn_pairs = exchanged(folded, second)
        folded, attn_low_t = lax.optimization_barrier((folded, attn_low_t))
        ffn_pairs = [(keep, got) for (keep, _), (_, got) in zip(folded, ffn_pairs)]
        project, _ = ffn_wgrad(((early, pieces, [(True, attn_low_t, d_branch)]),), [], 10**11, 2)
        project = exchanged(project, [early[1]])
        ffn_pairs += exchanged(fold(project, [early[2]], 10**9), [early[2]])
        orders += (early,)
    else:
        d_own = [exchange(d_attn[r]) for r in range(rows)]
        back = exchange(attn_bwd(lens, qkv, d_own, attended, lse, n_docs))

    squares = jnp.sum(sums, axis=(0, 2)).reshape(1, 2)
    small = jnp.concatenate([d_gain_two, squares, jnp.zeros((1, 126), F32)], axis=1)
    if by_blocks:
        *blocks, grad_first, grad_input, small = tail(
            ffn_pairs,
            tuple(order[2:] for order in orders),
            (early, late),
            back,
            normed_in.T,
            hidden,
            d_resid_mid,
            (w_query, w_key, w_value),
            cos,
            sin,
            row_gain(attn_gain),
            small,
            0,
        )
        small = small.reshape(-1)
        grad_gate = whole_block(blocks[0], inner // n_blk, model // n_dp).T
        grad_up = whole_block(blocks[1], inner // n_blk, model // n_dp).T
        grad_down = blocks[2].reshape(inner // n_dp, model // n_blk)
        grad_project = blocks[3].reshape(model // n_dp, model // n_blk)
        grad_query, grad_key, grad_value = blocks[4:]
    else:
        low, grad_first = turn_back(back, cos, sin)
        mid_cf, in_cf = core_first(normed_mid), core_first(normed_in)
        sent = lambda a, b, name, y: scatter(dot_tn(a, b).astype(BF16), name, y).astype(F32)
        grad_down = sent(inner_t.T, y_first(cot), "dp", False)
        grad_gate = sent(d_gate_t.T, mid_cf, "blk", False).T
        grad_up = sent(d_up_t.T, mid_cf, "blk", True).T
        grad_project = sent(d_branch, core_first(attn_low_t.T), "blk", True).T
        grad_query, grad_key, grad_value = [sent(low[k], in_cf, "blk", True).T for k in range(3)]
        grad_input, d_gain_one = input_grad(hidden, d_resid_mid, row_gain(attn_gain), low, w_query, w_key, w_value)
        small = total(jnp.concatenate([d_gain_one.reshape(model), small.reshape(-1)]))
    n_entries = n_blk * length * rows * n_dp * model
    return (
        unflat(block_out),
        unflat(grad_input),
        unflat(grad_first),
        grad_query,
        grad_key,
        grad_value,
        grad_project,
        grad_gate,
        grad_up,
        grad_down,
        small[:model],
        small[model : 2 * model],
        small[2 * model] / n_entries,
        small[2 * model + 1] / n_entries,
    )


def solution(mesh):
    tokens = P("blk", "dp", None)
    return jax.shard_map(
        body,
        mesh=mesh,
        in_specs=(tokens, tokens, P("dp", None)) + (P(),) * 9 + (tokens,),
        out_specs=(tokens,) * 3 + (P("dp", "blk"),) * 7 + (P(),) * 4,
        check_vma=False,
    )
```

```python
import functools

import jax
import jax.numpy as jnp
from jax import lax
from jax.experimental import pallas as pl
from jax.experimental.pallas import tpu as pltpu
from jax.sharding import PartitionSpec as P

HEADS = 16
HEAD_DIM = 64
NEG = -1e30
EPS = 1e-06
F32 = jnp.float32
BF16 = jnp.bfloat16
VMEM_LIMIT = 56 * 2**20
MESH = pl.DeviceIdType.MESH


def dot(a, b):
    return jnp.dot(a, b, preferred_element_type=F32)


def dot_nt(a, b):
    return lax.dot_general(a, b, (((1,), (1,)), ((), ())), preferred_element_type=F32)


def dot_tn(a, b):
    return lax.dot_general(a, b, (((0,), (0,)), ((), ())), preferred_element_type=F32)


def swap_halves(v):
    half = HEAD_DIM // 2
    width = v.shape[-1]
    lane = lax.broadcasted_iota(jnp.int32, v.shape, v.ndim - 1)
    left = pltpu.roll(v, width - half, v.ndim - 1)
    right = pltpu.roll(v, half, v.ndim - 1)
    return jnp.where(lane % HEAD_DIM < half, left, right)


def qkv_kernel(rows, length, width, hidden_ref, first_ref, cos_ref, sin_ref, gain_ref, wq_ref, wk_ref, wv_ref, *outs):
    out_refs, (normed_ref, sums_ref) = outs[:rows], outs[rows:]
    chunk = wq_ref.shape[1]

    @pl.when(pl.program_id(0) == 0)
    def _():
        for r in range(rows):
            at = pl.ds(r * length, length)
            normed, _ = rms_parts(hidden_ref[at, :].astype(F32))
            normed_ref[at, :] = (normed * gain_ref[...]).astype(BF16)

    first_sum = jnp.zeros((1, chunk), F32)
    mixed_sum = jnp.zeros((1, chunk), F32)
    for r in range(rows):
        at = pl.ds(r * length, length)
        normed = normed_ref[at, :]
        cos, sin = cos_ref[at, :], sin_ref[at, :]
        for which, w_ref in ((0, wq_ref), (1, wk_ref)):
            raw = dot(normed, w_ref[...])
            for c in range(chunk // 128):
                part = raw[:, c * 128 : (c + 1) * 128]
                turned = (part * cos + swap_halves(part) * sin).astype(BF16)
                for s in range(128 // width):
                    out_refs[r][c * (128 // width) + s, which] = turned[:, s * width : (s + 1) * width]
        first = first_ref[at, :].astype(F32)
        mixed = 0.5 * dot(normed, wv_ref[...]) + 0.5 * first
        first_sum = first_sum + jnp.sum(first * first, axis=0, keepdims=True)
        mixed_sum = mixed_sum + jnp.sum(mixed * mixed, axis=0, keepdims=True)
        low = mixed.astype(BF16)
        for s in range(chunk // width):
            out_refs[r][s, 2] = low[:, s * width : (s + 1) * width]
    sums_ref[0, 0:1] = first_sum
    sums_ref[0, 1:2] = mixed_sum


def project_qkv(hidden, first, cos, sin, gain, w_query, w_key, w_value, rows, n_blk):
    tokens, model = hidden.shape
    length, width = tokens // rows, model // n_blk
    chunk = 256
    steps = model // chunk
    full = lambda rows, cols: pl.BlockSpec((rows, cols), lambda j: (0, 0))
    weight = pl.BlockSpec((model, chunk), lambda j: (0, j))
    return pl.pallas_call(
        functools.partial(qkv_kernel, rows, length, width),
        grid=(steps,),
        in_specs=[
            full(tokens, model),
            pl.BlockSpec((tokens, chunk), lambda j: (0, j)),
            full(tokens, 128),
            full(tokens, 128),
            full(1, model),
            weight,
            weight,
            weight,
        ],
        out_specs=[pl.BlockSpec((chunk // width, 3, length, width), lambda j: (j, 0, 0, 0))] * rows
        + [full(tokens, model), pl.BlockSpec((1, 2, chunk), lambda j: (j, 0, 0))],
        out_shape=[jax.ShapeDtypeStruct((n_blk, 3, length, width), BF16)] * rows
        + [jax.ShapeDtypeStruct((tokens, model), BF16), jax.ShapeDtypeStruct((steps, 2, chunk), F32)],
        compiler_params=pltpu.CompilerParams(vmem_limit_bytes=VMEM_LIMIT),
        cost_estimate=pl.CostEstimate(
            flops=6 * tokens * model * model, bytes_accessed=6 * model * model + 10 * tokens * model, transcendentals=0
        ),
        name="qkv",
    )(hidden, first, cos, sin, gain, w_query, w_key, w_value)


def doc_ends(lens_ref, row, n_docs):
    ends, total = [], jnp.int32(0)
    for d in range(n_docs):
        total = total + lens_ref[row * n_docs + d]
        ends.append(total)
    return ends


def start_rows(ends, tile, length, heads):
    place = tile * length + lax.broadcasted_iota(jnp.int32, (1, length), 1)
    start = jnp.zeros((1, length), jnp.int32)
    for end in ends:
        start = jnp.where(end <= place, end, start)
    return jnp.concatenate([start] * heads, axis=1), jnp.concatenate([place] * heads, axis=1)


def head_masks(heads, width):
    lane = lax.broadcasted_iota(jnp.int32, (1, width), 1) // HEAD_DIM
    return [jnp.where(lane == h, 1.0, 0.0).astype(BF16) for h in range(heads)]


def by_head(values, masks):
    return jnp.concatenate([values * mask for mask in masks], axis=0)


def attn_fwd_kernel(row, n_docs, heads, lens_ref, qkv_ref, o_ref, low_ref, lse_ref, acc_ref):
    length, width = qkv_ref.shape[2:]
    i = pl.program_id(0)
    ends = doc_ends(lens_ref, row, n_docs)
    start, place = start_rows(ends, i, length, heads)
    lowest = jnp.int32(0)
    for end in ends:
        lowest = jnp.where(end <= i * length, end, lowest)
    lowest = lax.div(lowest, jnp.int32(length))
    masks = head_masks(heads, width)
    queries = by_head(qkv_ref[i, 0] * jnp.asarray(HEAD_DIM**-0.5, BF16), masks)

    def tile(step, carry):
        run_max, run_sum = carry
        j = i - step
        scores = dot_nt(qkv_ref[j, 1], queries)
        key = j * length + lax.broadcasted_iota(jnp.int32, scores.shape, 0)
        scores = jnp.where((key <= place) & (key >= start), scores, NEG)
        new_max = jnp.maximum(run_max, jnp.max(scores, axis=0, keepdims=True))
        weights = jnp.exp(scores - new_max)
        factor = jnp.exp(run_max - new_max)
        run_sum = run_sum * factor + jnp.sum(weights, axis=0, keepdims=True)
        acc_ref[...] = acc_ref[...] * factor + dot_tn(qkv_ref[j, 2], weights.astype(BF16))
        return new_max, run_sum

    acc_ref[...] = jnp.zeros_like(acc_ref)
    run_max, run_sum = lax.fori_loop(
        0,
        i - lowest + 1,
        tile,
        (jnp.full((1, heads * length), NEG, F32), jnp.zeros((1, heads * length), F32)),
    )
    result = acc_ref[...] / run_sum
    joined = jnp.concatenate(
        [
            result[h * HEAD_DIM : (h + 1) * HEAD_DIM, h * length : (h + 1) * length]
            for h in range(heads)
        ],
        axis=0,
    )
    attended = joined.T
    o_ref[0] = attended
    low_ref[0] = attended.astype(BF16)
    total = run_max + jnp.log(run_sum)
    for h in range(heads):
        lse_ref[0, h : h + 1, :] = total[:, h * length : (h + 1) * length]


def attn_fwd(lens, qkv, row, n_docs):
    n_blk, _, length, width = qkv.shape
    heads = width // HEAD_DIM
    tile = pl.BlockSpec((1, length, width), lambda i, lens: (i, 0, 0))
    return pl.pallas_call(
        functools.partial(attn_fwd_kernel, row, n_docs, heads),
        grid_spec=pltpu.PrefetchScalarGridSpec(
            num_scalar_prefetch=1,
            grid=(n_blk,),
            in_specs=[pl.BlockSpec(qkv.shape, lambda i, lens: (0, 0, 0, 0))],
            out_specs=[tile, tile, pl.BlockSpec((1, heads, length), lambda i, lens: (i, 0, 0))],
            scratch_shapes=[pltpu.VMEM((width, heads * length), F32)],
        ),
        out_shape=[
            jax.ShapeDtypeStruct((n_blk, length, width), F32),
            jax.ShapeDtypeStruct((n_blk, length, width), BF16),
            jax.ShapeDtypeStruct((n_blk, heads, length), F32),
        ],
        compiler_params=pltpu.CompilerParams(vmem_limit_bytes=VMEM_LIMIT),
        cost_estimate=pl.CostEstimate(flops=10**10, bytes_accessed=3 * 10**6, transcendentals=10**7),
        name="attn_fwd",
    )(lens, qkv)


def attn_bwd_kernel(rows, n_docs, heads, lens_ref, *refs):
    scratch = refs[4 * rows :]
    for row in range(rows):

        @pl.when(pl.program_id(0) == row)
        def _():
            attn_bwd_row(row, n_docs, heads, lens_ref, *refs[4 * row : 4 * row + 4], *scratch)


def attn_bwd_row(row, n_docs, heads, lens_ref, qkv_ref, do_ref, o_ref, lse_ref, out_ref, dq_ref, delta_ref):
    n_blk, _, length, width = qkv_ref.shape
    j = pl.program_id(1)
    ends = doc_ends(lens_ref, row, n_docs)
    masks = head_masks(heads, width)
    scale = HEAD_DIM**-0.5

    @pl.when(j == 0)
    def _():
        def one(i, _):
            prod = (do_ref[i].astype(F32) * o_ref[i]).T
            for h in range(heads):
                delta_ref[i, h : h + 1, :] = jnp.sum(
                    prod[h * HEAD_DIM : (h + 1) * HEAD_DIM], axis=0, keepdims=True
                )
            dq_ref[i] = jnp.zeros((length, width), F32)
            return 0

        lax.fori_loop(0, n_blk, one, 0)

    last = jnp.int32(n_blk * length)
    final = (j + 1) * length - 1
    for end in reversed(ends):
        last = jnp.where(end > final, end, last)
    highest = lax.div(last - 1, jnp.int32(length))
    keys, values = qkv_ref[j, 1], qkv_ref[j, 2]
    key_heads = [keys * mask for mask in masks]

    def tile(i, carry):
        d_key, d_value = carry
        start, place = start_rows(ends, i, length, heads)
        queries = by_head(qkv_ref[i, 0] * jnp.asarray(scale, BF16), masks)
        d_out = by_head(do_ref[i], masks)
        lse = jnp.concatenate([lse_ref[i, h : h + 1, :] for h in range(heads)], axis=1)
        delta = jnp.concatenate([delta_ref[i, h : h + 1, :] for h in range(heads)], axis=1)
        scores = dot_nt(keys, queries)
        key = j * length + lax.broadcasted_iota(jnp.int32, scores.shape, 0)
        probs = jnp.exp(jnp.where((key <= place) & (key >= start), scores - lse, NEG))
        d_probs = dot_nt(values, d_out)
        d_scores = (probs * (d_probs - delta)).astype(BF16)
        d_value = d_value + dot(probs.astype(BF16), d_out)
        d_key = d_key + dot(d_scores, queries)
        d_query = dq_ref[i]
        for h in range(heads):
            d_query = d_query + dot_tn(d_scores[:, h * length : (h + 1) * length], key_heads[h])
        dq_ref[i] = d_query
        return d_key, d_value

    zero = jnp.zeros((length, width), F32)
    d_key, d_value = lax.fori_loop(j, highest + 1, tile, (zero, zero))
    out_ref[0, 0, 0] = (dq_ref[j] * scale).astype(BF16)
    out_ref[0, 0, 1] = d_key.astype(BF16)
    out_ref[0, 0, 2] = d_value.astype(BF16)


def attn_bwd(lens, qkv, d_out, attended, lse, n_docs):
    rows = len(qkv)
    n_blk, _, length, width = qkv[0].shape
    heads = width // HEAD_DIM
    whole = lambda a: pl.BlockSpec(a.shape, lambda r, j, lens: (0,) * a.ndim)
    arrays = [a for per_row in zip(qkv, d_out, attended, lse) for a in per_row]
    return pl.pallas_call(
        functools.partial(attn_bwd_kernel, rows, n_docs, heads),
        grid_spec=pltpu.PrefetchScalarGridSpec(
            num_scalar_prefetch=1,
            grid=(rows, n_blk),
            in_specs=[whole(a) for a in arrays],
            out_specs=pl.BlockSpec((1, 1, 3, length, width), lambda r, j, lens: (j, r, 0, 0, 0)),
            scratch_shapes=[
                pltpu.VMEM((n_blk, length, width), F32),
                pltpu.VMEM((n_blk, heads, length), F32),
            ],
        ),
        out_shape=jax.ShapeDtypeStruct((n_blk, rows, 3, length, width), BF16),
        compiler_params=pltpu.CompilerParams(vmem_limit_bytes=VMEM_LIMIT),
        cost_estimate=pl.CostEstimate(flops=4 * 10**9, bytes_accessed=12 * 10**6, transcendentals=10**7),
        name="attn_bwd",
    )(lens, *arrays)


def exchange(values):
    return lax.all_to_all(values, "blk", 0, 0, tiled=True)


def bits_of(axis):
    return lax.axis_size(axis).bit_length() - 1


def halve(current, axis, name, bit):
    size = lax.axis_size(name)
    mine = (lax.axis_index(name) >> bit) & 1
    half = current.shape[axis] // 2
    keep = lax.dynamic_slice_in_dim(current, mine * half, half, axis)
    send = lax.dynamic_slice_in_dim(current, (1 - mine) * half, half, axis)
    got = lax.ppermute(send, name, [(k, k ^ (1 << bit)) for k in range(size)])
    return (keep.astype(F32) + got.astype(F32)).astype(BF16)


def core_first(values):
    n_dp = lax.axis_size("dp")
    tokens, cols = values.shape
    return values.reshape(tokens, n_dp // 2, 2, cols // n_dp).transpose(0, 2, 1, 3).reshape(tokens, cols)


def y_first(values):
    n_blk = lax.axis_size("blk")
    tokens, cols = values.shape
    return values.reshape(tokens, n_blk // 2, 2, cols // n_blk).transpose(0, 2, 1, 3).reshape(tokens, cols)


def scatter_steps(y_early):
    dp_bits, blk_bits = bits_of("dp"), bits_of("blk")
    rest = [("dp", b) for b in reversed(range(1, dp_bits))]
    blk = [("blk", 0)] + [("blk", b) for b in reversed(range(1, blk_bits))]
    if y_early:
        return [("dp", 0)] + blk[:1] + rest + blk[1:]
    return [("dp", 0)] + rest + blk


def block_order(y_early):
    rest = [("dp", b) for b in range(1, bits_of("dp"))]
    blk = [("blk", b) for b in range(bits_of("blk"))]
    if y_early:
        return [("dp", 0)] + blk[:1] + rest + blk[1:]
    return [("dp", 0)] + rest + blk


def z_order():
    rest = [("dp", b) for b in range(1, bits_of("dp"))]
    blk = [("blk", b) for b in range(bits_of("blk"))]
    return [("dp", 0)] + blk[1:2] + rest + blk[:1] + blk[2:]


def scatter(grad, rows_name, y_early):
    n_rows = lax.axis_size(rows_name)
    rows, cols = grad.shape
    current = grad.reshape((n_rows // 2, 2, rows // n_rows, cols))
    for name, bit in scatter_steps(y_early):
        if name != rows_name:
            current = halve(current, 3, name, bit)
        elif bit == 0:
            current = halve(current, 1, name, bit)
        else:
            current = halve(current, 0, name, bit)
    return current.reshape(rows // n_rows, current.shape[3])


def total(values):
    for name in ("dp", "blk"):
        size = lax.axis_size(name)
        for bit in range(bits_of(name)):
            values = values + lax.ppermute(values, name, [(k, k ^ (1 << bit)) for k in range(size)])
    return values


def chunks_of(block_rows, block_cols):
    cols = block_cols // 128
    return 4 // cols, cols, block_rows // (4 // cols)


def place_of(order, dp, blk):
    place = 0
    for name, bit in order[1:]:
        place = 2 * place + (((dp if name == "dp" else blk) >> bit) & 1)
    return place


def blocks_dot(left_ref, right_ref, left_is_dp, side, col, order, n_dp, n_blk, row, out_ref, *at):
    size = left_ref.shape[2]
    tokens = left_ref.shape[3]
    if left_is_dp:
        left = jnp.concatenate([left_ref[2 * k + side, 0] for k in range(n_dp // 2)], axis=0)
        right = right_ref[...]
    else:
        cols = right_ref.shape[1] // n_dp
        left = left_ref[:, 0].reshape(n_blk * size, tokens)
        right = jnp.concatenate(
            [
                right_ref[:, pl.ds(pl.multiple_of((2 * k + side) * cols + col * 128, 128), 128)]
                for k in range(n_dp // 2)
            ],
            axis=1,
        )
    result = dot(left, right).astype(BF16)
    for d in range(n_dp // 2):
        for e in range(n_blk):
            k, m = (d, e) if left_is_dp else (e, d)
            out_ref[(*at, place_of(order, 2 * d, e), slice(row, row + size))] = result[
                k * size : (k + 1) * size, m * 128 : (m + 1) * 128
            ]


def ffn_wgrad_kernel(plans, n_dp, n_blk, rows, *refs):
    source = iter(refs)
    take = lambda n: [next(source) for _ in range(n)]
    n, n_terms = len(plans), sum(len(terms) for _, terms, _ in plans)
    lefts, rights, moved, outs, arrived = take(n_terms), take(n_terms), take(rows), take(2 * n), take(rows)
    sents, landed, keeps = take(n), take(n), take(n)
    send_sem, recv_sem = take(2)
    own_sem, out_sem, in_sem = take(3) if rows else (None, None, None)
    step = pl.program_id(0)
    core, device = partner("dp", 0)
    here = lax.axis_index("blk")

    def own(r):
        return pltpu.make_async_copy(moved[r].at[here], arrived[r].at[here], own_sem.at[r])

    def across(r, m):
        there = (here + m) % n_blk
        return pltpu.make_async_remote_copy(
            src_ref=moved[r].at[there],
            dst_ref=arrived[r].at[here],
            send_sem=out_sem.at[r, m],
            recv_sem=in_sem.at[r, m],
            device_id=(lax.axis_index("dp"), there),
            device_id_type=MESH,
        )

    @pl.when(step == 0)
    def _():
        barrier = pltpu.get_barrier_semaphore()
        pl.semaphore_signal(barrier, inc=1, device_id=device, device_id_type=MESH)
        for m in range(1, n_blk if rows else 1):
            there = (lax.axis_index("dp"), (here + m) % n_blk)
            pl.semaphore_signal(barrier, inc=1, device_id=there, device_id_type=MESH)
        pl.semaphore_wait(barrier, n_blk if rows else 1)
        for r in range(rows):
            own(r).start()
            for m in range(1, n_blk):
                across(r, m).start()

    def remote(n, c):
        return pltpu.make_async_remote_copy(
            src_ref=sents[n].at[c],
            dst_ref=landed[n].at[c],
            send_sem=send_sem.at[n, c],
            recv_sem=recv_sem.at[n, c],
            device_id=device,
            device_id_type=MESH,
        )

    first = 0
    for k, (order, terms, pieces) in enumerate(plans):
        c = step - first
        first += pieces

        @pl.when((c >= 0) & (c < pieces))
        def _():
            def make(side, *out):
                for at, left_is_dp, col_parts, row in terms:
                    blocks_dot(lefts[at], rights[at], left_is_dp, side, c % col_parts, order, n_dp, n_blk, row, *out)

            make(1 - core, sents[k], c)
            remote(k, c).start()
            make(core, keeps[k], c % 2)

        @pl.when((c >= 1) & (c < pieces + 1))
        def _():
            remote(k, c - 1).wait_recv()
            mine, _ = partner(*order[1])
            half = keeps[k].shape[1] // 2
            for out_ref, side in ((outs[2 * k], mine), (outs[2 * k + 1], 1 - mine)):

                def one(d, _):
                    at = side * half + d
                    out_ref[0, d] = keeps[k][(c - 1) % 2, at] + landed[k][c - 1, at]
                    return 0

                lax.fori_loop(0, half, one, 0)

    @pl.when(step == first)
    def _():
        for k in range(n):
            for c in range(plans[k][2]):
                remote(k, c).wait_send()
        for r in range(rows):
            own(r).wait()
            for m in range(1, n_blk):
                across(r, m).wait()


def ffn_wgrad(items, moved, flops, collective_id):
    n_dp, n_blk = lax.axis_size("dp"), lax.axis_size("blk")
    lefts, rights, plans, left_specs, right_specs, out_specs, outs, scratch = [], [], [], [], [], [], [], []
    held = n_dp * n_blk // 2
    steps = 0
    for order, wanted, terms in items:
        count, row, plan = len(wanted), 0, []
        for left_is_dp, left, right in terms:
            n_left, n_right = (n_dp, n_blk) if left_is_dp else (n_blk, n_dp)
            cols, tokens = left.shape
            row_parts, col_parts, size = chunks_of(cols // n_left, right.shape[1] // n_right)
            plan.append((len(lefts), left_is_dp, col_parts, row))
            row += size
            lefts.append(left.reshape(n_left, row_parts, size, tokens))
            rights.append(right)
            left_specs.append(
                pl.BlockSpec(
                    (n_left, 1, size, tokens),
                    lambda p, at=steps, low=wanted[0], count=count, col_parts=col_parts: (
                        0,
                        (low + jnp.clip(p - at, 0, count - 1)) // col_parts,
                        0,
                        0,
                    ),
                )
            )
            right_specs.append(pl.BlockSpec(right.shape, lambda p: (0, 0), pipeline_mode=pl.Buffered(1)))
        plans.append((order, plan, count))
        out_specs += [
            pl.BlockSpec(
                (1, held // 2, row, 128), lambda p, at=steps, count=count: (jnp.clip(p - 1 - at, 0, count - 1), 0, 0, 0)
            )
        ] * 2
        outs += [jax.ShapeDtypeStruct((count, held // 2, row, 128), BF16)] * 2
        scratch.append((count, held, row, 128))
        steps += count
    n = len(items)
    flat = pl.pallas_call(
        functools.partial(ffn_wgrad_kernel, plans, n_dp, n_blk, len(moved)),
        grid=(steps + 1,),
        in_specs=left_specs + right_specs + [pl.BlockSpec(memory_space=pl.ANY)] * len(moved),
        out_specs=out_specs + [pl.BlockSpec(memory_space=pl.ANY)] * len(moved),
        out_shape=outs + [jax.ShapeDtypeStruct(a.shape, a.dtype) for a in moved],
        scratch_shapes=[pltpu.VMEM(a, BF16) for a in scratch] * 2
        + [pltpu.VMEM((2,) + a[1:], BF16) for a in scratch]
        + [pltpu.SemaphoreType.DMA((n, 4))] * 2
        + ([pltpu.SemaphoreType.DMA((len(moved),))] + [pltpu.SemaphoreType.DMA((len(moved), n_blk))] * 2 if moved else []),
        compiler_params=pltpu.CompilerParams(
            collective_id=collective_id, has_side_effects=True, vmem_limit_bytes=VMEM_LIMIT
        ),
        cost_estimate=pl.CostEstimate(flops=flops, bytes_accessed=10**7, transcendentals=0),
        name="ffn_wgrad",
    )(*lefts, *rights, *moved)
    return [tuple(flat[2 * k : 2 * k + 2]) for k in range(n)], list(flat[2 * n :])


def fold_kernel(stages, *refs):
    n = len(stages)
    for k, (name, bit) in enumerate(stages):
        mine, _ = partner(name, bit)
        keep_ref, got_ref = refs[2 * k], refs[2 * k + 1]
        half = keep_ref.shape[1] // 2
        for out_ref, side in ((refs[2 * n + 2 * k], mine), (refs[2 * n + 2 * k + 1], 1 - mine)):

            def one(d, _):
                at = side * half + d
                out_ref[0, d] = keep_ref[0, at] + got_ref[0, at]
                return 0

            lax.fori_loop(0, half, one, 0)


def fold(pairs, stages, flops):
    n = len(pairs)
    arrays = [a for pair in pairs for a in pair]
    block = lambda a, parts: pl.BlockSpec((1, a.shape[1] // parts) + a.shape[2:], lambda c: (c, 0, 0, 0))
    half = lambda a: jax.ShapeDtypeStruct((a.shape[0], a.shape[1] // 2) + a.shape[2:], BF16)
    flat = pl.pallas_call(
        functools.partial(fold_kernel, stages),
        grid=(arrays[0].shape[0],),
        in_specs=[block(a, 1) for a in arrays],
        out_specs=[block(a, 2) for a in arrays],
        out_shape=[half(a) for a in arrays],
        compiler_params=pltpu.CompilerParams(vmem_limit_bytes=VMEM_LIMIT),
        cost_estimate=pl.CostEstimate(flops=flops, bytes_accessed=10**7, transcendentals=0),
        name="fold",
    )(*arrays)
    return [tuple(flat[2 * k : 2 * k + 2]) for k in range(n)]


def swap(values, name, bit):
    size = lax.axis_size(name)
    return lax.ppermute(values, name, [(k, k ^ (1 << bit)) for k in range(size)])


def partner(name, bit):
    here = {"dp": lax.axis_index("dp"), "blk": lax.axis_index("blk")}
    mine = (here[name] // (1 << bit)) % 2
    other = dict(here)
    other[name] = here[name] + (1 - 2 * mine) * (1 << bit)
    return mine, (other["dp"], other["blk"])


def ffn_kernel(gathered_ref, hidden_ref, cot_ref, gain_ref, wo_ref, wg_ref, wu_ref, wd_ref, *refs):
    out_refs, (low_ref, resid_ref, acc_ref, dmid_ref) = refs[-14:-4], refs[-4:]
    lowt_ref, mid_ref, inner_ref, dgate_ref, dup_ref, out_ref, dres_ref, dbranch_ref, dgain_ref, dattn_ref = out_refs
    n_blk, length, width = gathered_ref.shape
    step = pl.program_id(0)

    @pl.when(step == 0)
    def _():
        for s in range(n_blk):
            low_ref[:, s * width : (s + 1) * width] = gathered_ref[s]
        resid = hidden_ref[...].astype(F32) + dot(low_ref[...], wo_ref[...])
        resid_ref[...] = resid
        normed, _ = rms_parts(resid)
        mid_ref[...] = (normed * gain_ref[...]).astype(BF16)
        acc_ref[...] = jnp.zeros_like(acc_ref)
        dmid_ref[...] = jnp.zeros_like(dmid_ref)
        lowt_ref[...] = low_ref[...].T

    gate = dot(mid_ref[...], wg_ref[...])
    up = dot(mid_ref[...], wu_ref[...])
    d_inner = dot_nt(cot_ref[...], wd_ref[...])
    sigma = 1.0 / (1.0 + jnp.exp(-gate))
    act = gate * sigma
    inner = (act * up).astype(BF16)
    d_gate = (d_inner * up * (sigma * (1.0 + gate * (1.0 - sigma)))).astype(BF16)
    d_up = (d_inner * act).astype(BF16)
    inner_ref[...] = inner.T
    dgate_ref[...] = d_gate.T
    dup_ref[...] = d_up.T
    acc_ref[...] += dot(inner, wd_ref[...])
    dmid_ref[...] += dot_nt(d_gate, wg_ref[...]) + dot_nt(d_up, wu_ref[...])

    @pl.when(step == pl.num_programs(0) - 1)
    def _():
        resid = resid_ref[...]
        out_ref[...] = (resid + acc_ref[...]).astype(BF16)
        normed, inverse = rms_parts(resid)
        d_mid = dmid_ref[...]
        dgain_ref[...] = jnp.sum(d_mid * normed, axis=0, keepdims=True)
        d_resid = cot_ref[...].astype(F32) + norm_back(d_mid * gain_ref[...], normed, inverse)
        dres_ref[...] = d_resid
        d_branch = d_resid.astype(BF16)
        dbranch_ref[...] = d_branch
        back = dot_nt(d_branch, wo_ref[...]).astype(BF16)
        for s in range(n_blk):
            dattn_ref[s] = back[:, s * width : (s + 1) * width]


def feed_forward(row, before, gathered, hidden, cot, gain, w_out, w_gate, w_up, w_down):
    n_blk, length, width = gathered.shape
    tokens, model = hidden.shape
    inner = w_gate.shape[1]
    chunk = 256
    once = lambda a: pl.BlockSpec(a.shape, lambda j: (0,) * len(a.shape), pipeline_mode=pl.Buffered(1))
    whole = lambda a: pl.BlockSpec(a.shape, lambda j: (0,) * len(a.shape))
    cols = pl.BlockSpec((model, chunk), lambda j: (0, j))
    own = pl.BlockSpec((length, model), lambda j: (row, 0), pipeline_mode=pl.Buffered(1))
    mine = pl.BlockSpec((length, model), lambda j: (row, 0))
    turned = pl.BlockSpec((chunk, length), lambda j: (j, row))
    shape = jax.ShapeDtypeStruct
    shared = (
        [shape((model, tokens), BF16), shape((tokens, model), BF16)]
        + [shape((inner, tokens), BF16)] * 3
        + [shape((tokens, model), BF16), shape((tokens, model), F32), shape((tokens, model), BF16)]
    )
    outs = shared + [shape((1, model), F32), shape((n_blk, length, width), BF16)]
    before = list(before or [])
    return pl.pallas_call(
        ffn_kernel,
        grid=(inner // chunk,),
        in_specs=[once(gathered), own, own, once(gain), once(w_out)]
        + [cols, cols, pl.BlockSpec((chunk, model), lambda j: (j, 0))]
        + [pl.BlockSpec(memory_space=pl.ANY)] * len(before),
        out_specs=[pl.BlockSpec((model, length), lambda j: (0, row)), mine]
        + [turned] * 3
        + [mine] * 3
        + [whole(a) for a in outs[8:]],
        out_shape=outs,
        scratch_shapes=[pltpu.VMEM((length, model), BF16)] + [pltpu.VMEM((length, model), F32)] * 3,
        input_output_aliases={8 + k: k for k in range(len(before))},
        compiler_params=pltpu.CompilerParams(vmem_limit_bytes=VMEM_LIMIT),
        cost_estimate=pl.CostEstimate(
            flops=12 * length * model * inner + 4 * length * model * model,
            bytes_accessed=6 * model * inner + 6 * length * inner + 20 * length * model,
            transcendentals=length * inner,
        ),
        name="ffn",
    )(gathered, hidden, cot, gain, w_out, w_gate, w_up, w_down, *before)


class Halving:
    def __init__(self, order, work, sent, landed, send_sem, recv_sem):
        self.order, self.work, self.sent, self.landed = order, work, sent, landed
        self.send_sem, self.recv_sem = send_sem, recv_sem
        self.held = work.shape[1]

    def base(self, stage):
        base = 0
        for earlier in range(1, stage):
            base = base + partner(*self.order[earlier])[0] * (self.held >> earlier)
        return base

    def remote(self, stage, c):
        mine, device = partner(*self.order[stage])
        half = self.held >> stage
        if stage == 0:
            sent = self.sent.at[c]
        else:
            sent = self.work.at[c, pl.ds(self.base(stage) + (1 - mine) * half, half)]
        return pltpu.make_async_remote_copy(
            src_ref=sent,
            dst_ref=self.landed[stage].at[c],
            send_sem=self.send_sem.at[stage, c],
            recv_sem=self.recv_sem.at[stage, c],
            device_id=device,
            device_id_type=MESH,
        )

    def add(self, stage, c):
        base = self.base(stage + 1)

        def one(d, _):
            self.work[c, base + d] = self.work[c, base + d] + self.landed[stage][c, d]
            return 0

        lax.fori_loop(0, self.held >> stage, one, 0)

    def result(self, c):
        stage = len(self.order) - 1
        return self.work[c, self.base(stage + 1)].astype(F32) + self.landed[stage][c, 0].astype(F32)


def store_piece(out_ref, c, piece):
    size = piece.shape[0]
    if out_ref.shape[1] == 128:
        out_ref[c * size : (c + 1) * size, :] = piece
    else:
        cols = out_ref.shape[0] // 128
        row, col = c // cols, c % cols
        out_ref[col * 128 : (col + 1) * 128, row * size : (row + 1) * size] = piece.T


def tail_kernel(ffn_orders, qkv_orders, n_dp, n_blk, *refs):
    source = iter(refs)
    take = lambda n: [next(source) for _ in range(n)]
    n_ffn, n_qkv = len(ffn_orders), 3
    ffn_stages, qkv_stages = len(ffn_orders[0]), len(qkv_orders[0])
    cos_ref, sin_ref, gain_ref, small_ref = take(4)
    loads = take(7)
    keeps, gots = take(n_ffn), take(n_ffn)
    ffn_outs, qkv_outs = take(n_ffn), take(n_qkv)
    first_ref, input_ref, total_ref = take(3)
    back_ref, turned_ref, hidden_ref, dres_ref, *weights = here = take(7)
    low_ref, acc_ref, vecs, vec_landed = take(4)
    load_sem, keep_sem, got_sem, vec_send, vec_recv = take(5)
    streams = []
    for k, order in enumerate(ffn_orders):
        work, *landed = take(1 + ffn_stages)
        streams.append(Halving(order, work, None, landed, *take(2)))
    late = []
    for u in range(n_qkv):
        late.append([])
        for order in qkv_orders:
            work, sent, *landed = take(2 + qkv_stages)
            late[u].append(Halving(order, work, sent, landed, *take(2)))
    _, rows, _, length, width = back_ref.shape
    core, _ = partner("dp", 0)
    counts = [a.shape[0] for a in keeps]

    load = [pltpu.make_async_copy(a, b, load_sem.at[k]) for k, (a, b) in enumerate(zip(loads, here))]
    keep_copy = lambda k, c: pltpu.make_async_copy(keeps[k].at[c], streams[k].work.at[c], keep_sem.at[k, c])
    got_copy = lambda k, c: pltpu.make_async_copy(gots[k].at[c], streams[k].landed[0].at[c], got_sem.at[k, c])
    load[0].start()
    load[1].start()
    for c in range(max(counts)):
        for k in range(n_ffn):
            if c < counts[k]:
                keep_copy(k, c).start()
                got_copy(k, c).start()
    for copy in load[2:]:
        copy.start()

    everyone = qkv_orders[0]
    barrier = pltpu.get_barrier_semaphore()
    for name, bit in everyone:
        pl.semaphore_signal(barrier, inc=1, device_id=partner(name, bit)[1], device_id_type=MESH)
    pl.semaphore_wait(barrier, len(everyone))

    def ffn(c, stage):
        for k, stream in enumerate(streams):
            if c >= counts[k]:
                continue
            if stage == 1:
                keep_copy(k, c).wait()
                got_copy(k, c).wait()
            else:
                stream.remote(stage - 1, c).wait_recv()
            if stage < ffn_stages:
                stream.add(stage - 1, c)
                stream.remote(stage, c).start()
            else:
                store_piece(ffn_outs[k], c, stream.result(c))

    def projections(which):
        for r in range(rows):
            at = pl.ds(r * length, length)
            for s in range(n_blk):
                cols = slice(s * width, (s + 1) * width)
                values = back_ref[s, r, which].astype(F32)
                if which < 2:
                    turned = values * cos_ref[at, :] - swap_halves(values) * sin_ref[at, :]
                else:
                    turned = 0.5 * values
                    first_ref[:, r, cols] = turned
                low_ref[which, at, cols] = turned.astype(BF16)
        for fresh in range(2):
            side = 1 - core if fresh == 0 else core
            left = jnp.concatenate([turned_ref[2 * k + side] for k in range(n_dp // 2)], axis=0)
            size, half = turned_ref.shape[1], turned_ref.shape[1] // 2
            result = dot(left, low_ref[which]).astype(BF16)
            for h, stream in enumerate(late[which]):
                out_ref = stream.sent if fresh == 0 else stream.work
                for d in range(n_dp // 2):
                    for e in range(n_blk):
                        out_ref[0, place_of(stream.order, 2 * d, e)] = result[
                            d * size + h * half : d * size + (h + 1) * half, e * width : (e + 1) * width
                        ]
                if fresh == 0:
                    stream.remote(0, 0).start()

    def late_step(which, stage):
        for h, stream in enumerate(late[which]):
            stream.remote(stage - 1, 0).wait_recv()
            if stage < qkv_stages:
                stream.add(stage - 1, 0)
                stream.remote(stage, 0).start()
            else:
                half = stream.work.shape[2]
                qkv_outs[which][h * half : (h + 1) * half, :] = stream.result(0)

    def vec_copy(e):
        return pltpu.make_async_remote_copy(
            src_ref=vecs.at[e],
            dst_ref=vec_landed.at[e],
            send_sem=vec_send.at[e],
            recv_sem=vec_recv.at[e],
            device_id=partner(*everyone[e])[1],
            device_id_type=MESH,
        )

    model = hidden_ref.shape[1]
    n_vec = len(everyone)

    def matmul():
        for k in range(2, 7):
            load[k].wait()
        for r in range(rows):
            at = pl.ds(r * length, length)
            acc_ref[at, :] = (
                dot_nt(low_ref[0, at, :], weights[0][...])
                + dot_nt(low_ref[1, at, :], weights[1][...])
                + dot_nt(low_ref[2, at, :], weights[2][...])
            )

    def norm():
        d_gain = jnp.zeros((1, model), F32)
        for r in range(rows):
            at = pl.ds(r * length, length)
            normed, inverse = rms_parts(hidden_ref[at, :].astype(F32))
            d_normed = acc_ref[at, :]
            d_gain = d_gain + jnp.sum(d_normed * normed, axis=0, keepdims=True)
            input_ref[:, r, :] = dres_ref[at, :] + norm_back(d_normed * gain_ref[...], normed, inverse)
        vecs[0, :, :model] = d_gain
        vecs[0, :, model:] = small_ref[...]
        vec_copy(0).start()

    def vec(e):
        vec_copy(e).wait_recv()
        summed = vecs[e] + vec_landed[e]
        if e == n_vec - 1:
            total_ref[...] = summed
        else:
            vecs[e + 1] = summed
            vec_copy(e + 1).start()

    chunks = range(max(counts))
    for c in chunks:
        ffn(c, 1)
    load[0].wait()
    load[1].wait()
    projections(2)
    projections(1)
    late_step(2, 1)
    projections(0)
    late_step(1, 1)
    ffn(0, 2)
    late_step(0, 1)
    matmul()
    late_step(2, 2)
    ffn(1, 2)
    norm()
    late_step(1, 2)
    ffn(2, 2)
    vecs_left = list(range(n_vec))
    vec(vecs_left.pop(0))
    late_step(2, 3)
    late_step(0, 2)
    ffn(3, 2)
    vec(vecs_left.pop(0))
    late_step(1, 3)
    late_step(0, 3)
    for stage in range(4, qkv_stages + 1):
        vec(vecs_left.pop(0))
        for which in (2, 1, 0):
            late_step(which, stage)
    for c in chunks:
        for stage in range(3, ffn_stages + 1):
            ffn(c, stage)
    for e in vecs_left:
        vec(e)

    for stream, count in zip(streams, counts):
        for c in range(count):
            for stage in range(1, ffn_stages):
                stream.remote(stage, c).wait_send()
    for stream in late[0] + late[1] + late[2]:
        for stage in range(qkv_stages):
            stream.remote(stage, 0).wait_send()
    for e in range(n_vec):
        vec_copy(e).wait_send()


def tail(ffn_pairs, ffn_blocks, ffn_orders, qkv_orders, back, normed_t, hidden, d_resid, weights, cos, sin, gain, small, collective_id):
    n_dp, n_blk = lax.axis_size("dp"), lax.axis_size("blk")
    tokens, model = hidden.shape
    rows, length = back.shape[1], back.shape[3]
    keeps, gots = [pair[0] for pair in ffn_pairs], [pair[1] for pair in ffn_pairs]
    loads = [back, normed_t.reshape(n_dp, model // n_dp, tokens), hidden, d_resid, *weights]
    ffn_stages, qkv_stages, n_qkv = len(ffn_orders[0]), len(qkv_orders[0]), 3
    n_chunks = max(a.shape[0] for a in keeps)
    block = (model // n_dp, model // n_blk)
    held = n_dp * n_blk // 2
    shape = jax.ShapeDtypeStruct
    vec = (1, model + small.shape[1])
    outs = (
        [shape(a, F32) for a in ffn_blocks]
        + [shape(block, F32)] * n_qkv
        + [shape((length, rows, model), F32)] * 2
        + [shape(vec, F32)]
    )
    scratch = [pltpu.VMEM(a.shape, a.dtype) for a in loads]
    scratch += [
        pltpu.VMEM((n_qkv, tokens, model), BF16),
        pltpu.VMEM((tokens, model), F32),
        pltpu.VMEM((qkv_stages,) + vec, F32),
        pltpu.VMEM((qkv_stages,) + vec, F32),
        pltpu.SemaphoreType.DMA((len(loads),)),
        pltpu.SemaphoreType.DMA((len(keeps), n_chunks)),
        pltpu.SemaphoreType.DMA((len(keeps), n_chunks)),
        pltpu.SemaphoreType.DMA((qkv_stages,)),
        pltpu.SemaphoreType.DMA((qkv_stages,)),
    ]
    for a in keeps:
        scratch.append(pltpu.VMEM(a.shape, BF16))
        scratch += [pltpu.VMEM((a.shape[0], a.shape[1] >> stage) + a.shape[2:], BF16) for stage in range(ffn_stages)]
        scratch += [pltpu.SemaphoreType.DMA((ffn_stages, a.shape[0]))] * 2
    part = (block[0] // len(qkv_orders), block[1])
    for _ in range(n_qkv * len(qkv_orders)):
        scratch += [pltpu.VMEM((1, held) + part, BF16)] * 2
        scratch += [pltpu.VMEM((1, held >> stage) + part, BF16) for stage in range(qkv_stages)]
        scratch += [pltpu.SemaphoreType.DMA((qkv_stages, 1))] * 2
    vmem, anywhere = pl.BlockSpec(memory_space=pltpu.VMEM), pl.BlockSpec(memory_space=pl.ANY)
    return pl.pallas_call(
        functools.partial(tail_kernel, ffn_orders, qkv_orders, n_dp, n_blk),
        in_specs=[vmem] * 4 + [anywhere] * (len(loads) + 2 * len(keeps)),
        out_specs=[vmem] * len(outs),
        out_shape=outs,
        scratch_shapes=scratch,
        compiler_params=pltpu.CompilerParams(
            collective_id=collective_id, has_side_effects=True, vmem_limit_bytes=60 * 2**20
        ),
        cost_estimate=pl.CostEstimate(flops=10**11, bytes_accessed=10**8, transcendentals=0),
        name="tail",
    )(cos, sin, gain, small, *loads, *keeps, *gots)


def turn_back_kernel(cos_ref, sin_ref, back_ref, low_ref, first_ref):
    n_blk, rows, _, length, width = back_ref.shape
    which = pl.program_id(0)
    for r in range(rows):
        at = pl.ds(r * length, length)
        for s in range(n_blk):
            cols = slice(s * width, (s + 1) * width)
            values = back_ref[s, r, 0].astype(F32)

            @pl.when(which < 2)
            def _():
                cos, sin = cos_ref[at, :width], sin_ref[at, :width]
                wide = values if width == 128 else jnp.concatenate([values, values], axis=1)
                swapped = swap_halves(wide)[:, :width]
                low_ref[0, at, cols] = (values * cos - swapped * sin).astype(BF16)

            @pl.when(which == 2)
            def _():
                first_ref[at, cols] = 0.5 * values
                low_ref[0, at, cols] = (0.5 * values).astype(BF16)


def turn_back(back, cos, sin):
    n_blk, rows, _, length, width = back.shape
    tokens, model = rows * length, n_blk * width
    full = lambda a: pl.BlockSpec(a.shape, lambda w: (0, 0))
    return pl.pallas_call(
        turn_back_kernel,
        grid=(3,),
        in_specs=[full(cos), full(sin), pl.BlockSpec((n_blk, rows, 1, length, width), lambda w: (0, 0, w, 0, 0))],
        out_specs=[
            pl.BlockSpec((1, tokens, model), lambda w: (w, 0, 0)),
            pl.BlockSpec((tokens, model), lambda w: (0, 0)),
        ],
        out_shape=[jax.ShapeDtypeStruct((3, tokens, model), BF16), jax.ShapeDtypeStruct((tokens, model), F32)],
        compiler_params=pltpu.CompilerParams(vmem_limit_bytes=VMEM_LIMIT),
        name="turn_back",
    )(cos, sin, back)


def input_grad_kernel(hidden_ref, dres_ref, gain_ref, low_ref, wq_ref, wk_ref, wv_ref, out_ref, dgain_ref):
    tokens = hidden_ref.shape[0]
    half = tokens // 2
    d_gain = jnp.zeros(dgain_ref.shape, F32)
    for r in range(2):
        at = pl.ds(r * half, half)
        d_normed = (
            dot_nt(low_ref[0, at, :], wq_ref[...])
            + dot_nt(low_ref[1, at, :], wk_ref[...])
            + dot_nt(low_ref[2, at, :], wv_ref[...])
        )
        normed, inverse = rms_parts(hidden_ref[at, :].astype(F32))
        d_gain = d_gain + jnp.sum(d_normed * normed, axis=0, keepdims=True)
        out_ref[at, :] = dres_ref[at, :] + norm_back(d_normed * gain_ref[...], normed, inverse)
    dgain_ref[...] = d_gain


def input_grad(hidden, d_resid, gain, low, w_query, w_key, w_value):
    tokens, model = hidden.shape
    return pl.pallas_call(
        input_grad_kernel,
        out_shape=[jax.ShapeDtypeStruct((tokens, model), F32), jax.ShapeDtypeStruct((1, model), F32)],
        compiler_params=pltpu.CompilerParams(vmem_limit_bytes=VMEM_LIMIT),
        cost_estimate=pl.CostEstimate(
            flops=6 * tokens * model * model, bytes_accessed=6 * model * model + 16 * tokens * model, transcendentals=0
        ),
        name="input_grad",
    )(hidden, d_resid, gain, low, w_query, w_key, w_value)


def rms_parts(values):
    inverse_rms = lax.rsqrt(jnp.mean(values * values, axis=-1, keepdims=True) + EPS)
    return values * inverse_rms, inverse_rms


def norm_back(d_normed, normed, inverse_rms):
    return inverse_rms * (d_normed - normed * jnp.mean(d_normed * normed, axis=-1, keepdims=True))


def rope_tables(doc_lengths, offset, length):
    half = HEAD_DIM // 2
    places = offset + jnp.arange(length, dtype=jnp.int32)
    ends = jnp.cumsum(doc_lengths, axis=1)
    start = jnp.max(jnp.where(ends[:, None, :] <= places[None, :, None], ends[:, None, :], 0), axis=2)
    position = (places[None, :] - start).astype(F32).reshape(-1, 1)
    lane = jnp.arange(128, dtype=jnp.int32)
    freq = jnp.power(10000.0, -(lane % half).astype(F32) * 2.0 / HEAD_DIM)
    angles = position * freq[None, :]
    sign = jnp.where(lane % HEAD_DIM < half, -1.0, 1.0)
    return jnp.cos(angles), jnp.sin(angles) * sign[None, :]


def body(
    hidden_in,
    first_values,
    doc_lengths,
    w_query,
    w_key,
    w_value,
    w_out,
    w_gate,
    w_up,
    w_down,
    attn_gain,
    ffn_gain,
    out_cotangent,
):
    length, rows, model = hidden_in.shape
    n_docs = doc_lengths.shape[1]
    n_blk, n_dp = lax.axis_size("blk"), lax.axis_size("dp")
    width = model // n_blk
    tokens = rows * length
    flat = lambda a: jnp.transpose(a, (1, 0, 2)).reshape(tokens, model)
    unflat = lambda a: jnp.transpose(a.reshape(rows, length, model), (1, 0, 2))
    lens = doc_lengths.reshape(-1)

    hidden, cot, first = flat(hidden_in), flat(out_cotangent), flat(first_values)
    row_gain = lambda gain: gain.reshape(1, model)

    cos, sin = rope_tables(doc_lengths, lax.axis_index("blk") * length, length)
    *qkv_own, normed_in, sums = project_qkv(
        hidden, first, cos, sin, row_gain(attn_gain), w_query, w_key, w_value, rows, n_blk
    )
    qkv, attended, lse, gathered = [], [], [], []
    for r in range(rows):
        qkv.append(exchange(qkv_own[r]))
    for r in range(rows):
        o_f, o_low, lse_r = attn_fwd(lens, qkv[r], r, n_docs)
        attended.append(o_f)
        lse.append(lse_r)
        gathered.append(exchange(o_low))
    shared, d_gains, d_attn = None, [], []
    for r in range(rows):
        *shared, d_gain, d_attn_r = feed_forward(
            r, shared, gathered[r], hidden, cot, row_gain(ffn_gain), w_out, w_gate, w_up, w_down
        )
        d_gains.append(d_gain)
        d_attn.append(d_attn_r)
    attn_low_t, normed_mid, inner_t, d_gate_t, d_up_t, block_out, d_resid_mid, d_branch = shared
    d_gain_two = sum(d_gains)

    inner = w_gate.shape[1]
    by_blocks = (model // n_dp) % 128 == 0 and width == 128 and (inner // n_blk) % 32 == 0
    early, late, middle = block_order(False), block_order(True), z_order()
    if by_blocks:
        orders = (early, late, middle)
        pieces = (0, 1, 2, 3)
        exchanged = lambda pairs, stages: [(keep, swap(sent, *stage)) for (keep, sent), stage in zip(pairs, stages)]
        folded, d_own = ffn_wgrad(
            (
                (early, pieces, [(False, d_gate_t, normed_mid)]),
                (late, pieces, [(False, d_up_t, normed_mid)]),
                (middle, pieces, [(True, inner_t, cot)]),
            ),
            d_attn,
            10**9,
            1,
        )
        ffn_pairs = exchanged(folded, [order[1] for order in orders])
        back_own = attn_bwd(lens, qkv, d_own, attended, lse, n_docs)
        back = exchange(back_own)
        kept = [keep for keep, got in ffn_pairs]
        token, kept = lax.optimization_barrier((back_own, kept))
        second = [order[2] for order in orders]
        folded = fold([(keep, got) for keep, (_, got) in zip(kept, ffn_pairs)], second, 10**9)
        ffn_pairs = exchanged(folded, second)
        folded, attn_low_t = lax.optimization_barrier((folded, attn_low_t))
        ffn_pairs = [(keep, got) for (keep, _), (_, got) in zip(folded, ffn_pairs)]
        project, _ = ffn_wgrad(((early, pieces, [(True, attn_low_t, d_branch)]),), [], 10**11, 2)
        project = exchanged(project, [early[1]])
        ffn_pairs += exchanged(fold(project, [early[2]], 10**9), [early[2]])
        orders += (early,)
    else:
        d_own = [exchange(d_attn[r]) for r in range(rows)]
        back = exchange(attn_bwd(lens, qkv, d_own, attended, lse, n_docs))

    squares = jnp.sum(sums, axis=(0, 2)).reshape(1, 2)
    small = jnp.concatenate([d_gain_two, squares, jnp.zeros((1, 126), F32)], axis=1)
    if by_blocks:
        *blocks, grad_first, grad_input, small = tail(
            ffn_pairs,
            ((model // n_dp, inner // n_blk),) * 2 + ((inner // n_dp, model // n_blk), (model // n_dp, model // n_blk)),
            tuple(order[2:] for order in orders),
            (early, late),
            back,
            normed_in.T,
            hidden,
            d_resid_mid,
            (w_query, w_key, w_value),
            cos,
            sin,
            row_gain(attn_gain),
            small,
            0,
        )
        small = small.reshape(-1)
        grad_gate, grad_up, grad_down, grad_project = blocks[:4]
        grad_query, grad_key, grad_value = blocks[4:]
    else:
        low, grad_first = turn_back(back, cos, sin)
        mid_cf, in_cf = core_first(normed_mid), core_first(normed_in)
        sent = lambda a, b, name, y: scatter(dot_tn(a, b).astype(BF16), name, y).astype(F32)
        grad_down = sent(inner_t.T, y_first(cot), "dp", False)
        grad_gate = sent(d_gate_t.T, mid_cf, "blk", False).T
        grad_up = sent(d_up_t.T, mid_cf, "blk", True).T
        grad_project = sent(d_branch, core_first(attn_low_t.T), "blk", True).T
        grad_query, grad_key, grad_value = [sent(low[k], in_cf, "blk", True).T for k in range(3)]
        grad_first = unflat(grad_first)
        grad_input, d_gain_one = input_grad(hidden, d_resid_mid, row_gain(attn_gain), low, w_query, w_key, w_value)
        grad_input = unflat(grad_input)
        small = total(jnp.concatenate([d_gain_one.reshape(model), small.reshape(-1)]))
    n_entries = n_blk * length * rows * n_dp * model
    return (
        unflat(block_out),
        grad_input,
        grad_first,
        grad_query,
        grad_key,
        grad_value,
        grad_project,
        grad_gate,
        grad_up,
        grad_down,
        small[:model],
        small[model : 2 * model],
        small[2 * model] / n_entries,
        small[2 * model + 1] / n_entries,
    )


def solution(mesh):
    tokens = P("blk", "dp", None)
    return jax.shard_map(
        body,
        mesh=mesh,
        in_specs=(tokens, tokens, P("dp", None)) + (P(),) * 9 + (tokens,),
        out_specs=(tokens,) * 3 + (P("dp", "blk"),) * 7 + (P(),) * 4,
        check_vma=False,
    )
```

```python
import functools

import jax
import jax.numpy as jnp
from jax import lax
from jax.experimental import pallas as pl
from jax.experimental.pallas import tpu as pltpu
from jax.sharding import PartitionSpec as P

HEADS = 16
HEAD_DIM = 64
NEG = -1e30
EPS = 1e-06
F32 = jnp.float32
BF16 = jnp.bfloat16
VMEM_LIMIT = 56 * 2**20
LAST_FLOPS = 6 * 10**10
MESH = pl.DeviceIdType.MESH


def dot(a, b):
    return jnp.dot(a, b, preferred_element_type=F32)


def dot_nt(a, b):
    return lax.dot_general(a, b, (((1,), (1,)), ((), ())), preferred_element_type=F32)


def dot_tn(a, b):
    return lax.dot_general(a, b, (((0,), (0,)), ((), ())), preferred_element_type=F32)


def swap_halves(v):
    half = HEAD_DIM // 2
    width = v.shape[-1]
    lane = lax.broadcasted_iota(jnp.int32, v.shape, v.ndim - 1)
    left = pltpu.roll(v, width - half, v.ndim - 1)
    right = pltpu.roll(v, half, v.ndim - 1)
    return jnp.where(lane % HEAD_DIM < half, left, right)


def qkv_kernel(rows, length, width, hidden_ref, first_ref, cos_ref, sin_ref, gain_ref, wq_ref, wk_ref, wv_ref, *outs):
    out_refs, (normed_ref, sums_ref) = outs[:rows], outs[rows:]
    chunk = wq_ref.shape[1]

    @pl.when(pl.program_id(0) == 0)
    def _():
        for r in range(rows):
            at = pl.ds(r * length, length)
            normed, _ = rms_parts(hidden_ref[at, :].astype(F32))
            normed_ref[at, :] = (normed * gain_ref[...]).astype(BF16)

    first_sum = jnp.zeros((1, chunk), F32)
    mixed_sum = jnp.zeros((1, chunk), F32)
    for r in range(rows):
        at = pl.ds(r * length, length)
        normed = normed_ref[at, :]
        cos, sin = cos_ref[at, :], sin_ref[at, :]
        for which, w_ref in ((0, wq_ref), (1, wk_ref)):
            raw = dot(normed, w_ref[...])
            for c in range(chunk // 128):
                part = raw[:, c * 128 : (c + 1) * 128]
                turned = (part * cos + swap_halves(part) * sin).astype(BF16)
                for s in range(128 // width):
                    out_refs[r][c * (128 // width) + s, which] = turned[:, s * width : (s + 1) * width]
        first = first_ref[at, :].astype(F32)
        mixed = 0.5 * dot(normed, wv_ref[...]) + 0.5 * first
        first_sum = first_sum + jnp.sum(first * first, axis=0, keepdims=True)
        mixed_sum = mixed_sum + jnp.sum(mixed * mixed, axis=0, keepdims=True)
        low = mixed.astype(BF16)
        for s in range(chunk // width):
            out_refs[r][s, 2] = low[:, s * width : (s + 1) * width]
    sums_ref[0, 0:1] = first_sum
    sums_ref[0, 1:2] = mixed_sum


def project_qkv(hidden, first, cos, sin, gain, w_query, w_key, w_value, rows, n_blk):
    tokens, model = hidden.shape
    length, width = tokens // rows, model // n_blk
    chunk = 256
    steps = model // chunk
    full = lambda rows, cols: pl.BlockSpec((rows, cols), lambda j: (0, 0))
    weight = pl.BlockSpec((model, chunk), lambda j: (0, j))
    return pl.pallas_call(
        functools.partial(qkv_kernel, rows, length, width),
        grid=(steps,),
        in_specs=[
            full(tokens, model),
            pl.BlockSpec((tokens, chunk), lambda j: (0, j)),
            full(tokens, 128),
            full(tokens, 128),
            full(1, model),
            weight,
            weight,
            weight,
        ],
        out_specs=[pl.BlockSpec((chunk // width, 3, length, width), lambda j: (j, 0, 0, 0))] * rows
        + [full(tokens, model), pl.BlockSpec((1, 2, chunk), lambda j: (j, 0, 0))],
        out_shape=[jax.ShapeDtypeStruct((n_blk, 3, length, width), BF16)] * rows
        + [jax.ShapeDtypeStruct((tokens, model), BF16), jax.ShapeDtypeStruct((steps, 2, chunk), F32)],
        compiler_params=pltpu.CompilerParams(vmem_limit_bytes=VMEM_LIMIT),
        cost_estimate=pl.CostEstimate(
            flops=6 * tokens * model * model, bytes_accessed=6 * model * model + 10 * tokens * model, transcendentals=0
        ),
        name="qkv",
    )(hidden, first, cos, sin, gain, w_query, w_key, w_value)


def doc_ends(lens_ref, row, n_docs):
    ends, total = [], jnp.int32(0)
    for d in range(n_docs):
        total = total + lens_ref[row * n_docs + d]
        ends.append(total)
    return ends


def start_rows(ends, tile, length, heads):
    place = tile * length + lax.broadcasted_iota(jnp.int32, (1, length), 1)
    start = jnp.zeros((1, length), jnp.int32)
    for end in ends:
        start = jnp.where(end <= place, end, start)
    return jnp.concatenate([start] * heads, axis=1), jnp.concatenate([place] * heads, axis=1)


def head_masks(heads, width):
    lane = lax.broadcasted_iota(jnp.int32, (1, width), 1) // HEAD_DIM
    return [jnp.where(lane == h, 1.0, 0.0).astype(BF16) for h in range(heads)]


def by_head(values, masks):
    return jnp.concatenate([values * mask for mask in masks], axis=0)


def attn_fwd_kernel(row, n_docs, heads, lens_ref, qkv_ref, o_ref, low_ref, lse_ref, acc_ref):
    length, width = qkv_ref.shape[2:]
    i = pl.program_id(0)
    ends = doc_ends(lens_ref, row, n_docs)
    start, place = start_rows(ends, i, length, heads)
    lowest = jnp.int32(0)
    for end in ends:
        lowest = jnp.where(end <= i * length, end, lowest)
    lowest = lax.div(lowest, jnp.int32(length))
    masks = head_masks(heads, width)
    queries = by_head(qkv_ref[i, 0] * jnp.asarray(HEAD_DIM**-0.5, BF16), masks)

    def tile(step, carry):
        run_max, run_sum = carry
        j = i - step
        scores = dot_nt(qkv_ref[j, 1], queries)
        key = j * length + lax.broadcasted_iota(jnp.int32, scores.shape, 0)
        scores = jnp.where((key <= place) & (key >= start), scores, NEG)
        new_max = jnp.maximum(run_max, jnp.max(scores, axis=0, keepdims=True))
        weights = jnp.exp(scores - new_max)
        factor = jnp.exp(run_max - new_max)
        run_sum = run_sum * factor + jnp.sum(weights, axis=0, keepdims=True)
        acc_ref[...] = acc_ref[...] * factor + dot_tn(qkv_ref[j, 2], weights.astype(BF16))
        return new_max, run_sum

    acc_ref[...] = jnp.zeros_like(acc_ref)
    run_max, run_sum = lax.fori_loop(
        0,
        i - lowest + 1,
        tile,
        (jnp.full((1, heads * length), NEG, F32), jnp.zeros((1, heads * length), F32)),
    )
    result = acc_ref[...] / run_sum
    joined = jnp.concatenate(
        [
            result[h * HEAD_DIM : (h + 1) * HEAD_DIM, h * length : (h + 1) * length]
            for h in range(heads)
        ],
        axis=0,
    )
    attended = joined.T
    o_ref[0] = attended
    low_ref[0] = attended.astype(BF16)
    total = run_max + jnp.log(run_sum)
    for h in range(heads):
        lse_ref[0, h : h + 1, :] = total[:, h * length : (h + 1) * length]


def attn_fwd(lens, qkv, row, n_docs):
    n_blk, _, length, width = qkv.shape
    heads = width // HEAD_DIM
    tile = pl.BlockSpec((1, length, width), lambda i, lens: (i, 0, 0))
    return pl.pallas_call(
        functools.partial(attn_fwd_kernel, row, n_docs, heads),
        grid_spec=pltpu.PrefetchScalarGridSpec(
            num_scalar_prefetch=1,
            grid=(n_blk,),
            in_specs=[pl.BlockSpec(qkv.shape, lambda i, lens: (0, 0, 0, 0))],
            out_specs=[tile, tile, pl.BlockSpec((1, heads, length), lambda i, lens: (i, 0, 0))],
            scratch_shapes=[pltpu.VMEM((width, heads * length), F32)],
        ),
        out_shape=[
            jax.ShapeDtypeStruct((n_blk, length, width), F32),
            jax.ShapeDtypeStruct((n_blk, length, width), BF16),
            jax.ShapeDtypeStruct((n_blk, heads, length), F32),
        ],
        compiler_params=pltpu.CompilerParams(vmem_limit_bytes=VMEM_LIMIT),
        cost_estimate=pl.CostEstimate(flops=10**10, bytes_accessed=3 * 10**6, transcendentals=10**7),
        name="attn_fwd",
    )(lens, qkv)


def attn_bwd_kernel(rows, first_row, n_docs, heads, lens_ref, *refs):
    scratch = refs[4 * rows :]
    for row in range(rows):

        @pl.when(pl.program_id(0) == row)
        def _():
            attn_bwd_row(first_row + row, n_docs, heads, lens_ref, *refs[4 * row : 4 * row + 4], *scratch)


def attn_bwd_row(row, n_docs, heads, lens_ref, qkv_ref, do_ref, o_ref, lse_ref, out_ref, dq_ref, delta_ref):
    n_blk, _, length, width = qkv_ref.shape
    j = pl.program_id(1)
    ends = doc_ends(lens_ref, row, n_docs)
    masks = head_masks(heads, width)
    scale = HEAD_DIM**-0.5

    @pl.when(j == 0)
    def _():
        def one(i, _):
            prod = (do_ref[i].astype(F32) * o_ref[i]).T
            for h in range(heads):
                delta_ref[i, h : h + 1, :] = jnp.sum(
                    prod[h * HEAD_DIM : (h + 1) * HEAD_DIM], axis=0, keepdims=True
                )
            dq_ref[i] = jnp.zeros((length, width), F32)
            return 0

        lax.fori_loop(0, n_blk, one, 0)

    last = jnp.int32(n_blk * length)
    final = (j + 1) * length - 1
    for end in reversed(ends):
        last = jnp.where(end > final, end, last)
    highest = lax.div(last - 1, jnp.int32(length))
    keys, values = qkv_ref[j, 1], qkv_ref[j, 2]
    key_heads = [keys * mask for mask in masks]

    def tile(i, carry):
        d_key, d_value = carry
        start, place = start_rows(ends, i, length, heads)
        queries = by_head(qkv_ref[i, 0] * jnp.asarray(scale, BF16), masks)
        d_out = by_head(do_ref[i], masks)
        lse = jnp.concatenate([lse_ref[i, h : h + 1, :] for h in range(heads)], axis=1)
        delta = jnp.concatenate([delta_ref[i, h : h + 1, :] for h in range(heads)], axis=1)
        scores = dot_nt(keys, queries)
        key = j * length + lax.broadcasted_iota(jnp.int32, scores.shape, 0)
        probs = jnp.exp(jnp.where((key <= place) & (key >= start), scores - lse, NEG))
        d_probs = dot_nt(values, d_out)
        d_scores = (probs * (d_probs - delta)).astype(BF16)
        d_value = d_value + dot(probs.astype(BF16), d_out)
        d_key = d_key + dot(d_scores, queries)
        d_query = dq_ref[i]
        for h in range(heads):
            d_query = d_query + dot_tn(d_scores[:, h * length : (h + 1) * length], key_heads[h])
        dq_ref[i] = d_query
        return d_key, d_value

    zero = jnp.zeros((length, width), F32)
    d_key, d_value = lax.fori_loop(j, highest + 1, tile, (zero, zero))
    out_ref[0, 0, 0] = (dq_ref[j] * scale).astype(BF16)
    out_ref[0, 0, 1] = d_key.astype(BF16)
    out_ref[0, 0, 2] = d_value.astype(BF16)


def attn_bwd(lens, qkv, d_out, attended, lse, first_row, n_docs):
    rows = len(qkv)
    n_blk, _, length, width = qkv[0].shape
    heads = width // HEAD_DIM
    whole = lambda a: pl.BlockSpec(a.shape, lambda r, j, lens: (0,) * a.ndim)
    arrays = [a for per_row in zip(qkv, d_out, attended, lse) for a in per_row]
    return pl.pallas_call(
        functools.partial(attn_bwd_kernel, rows, first_row, n_docs, heads),
        grid_spec=pltpu.PrefetchScalarGridSpec(
            num_scalar_prefetch=1,
            grid=(rows, n_blk),
            in_specs=[whole(a) for a in arrays],
            out_specs=pl.BlockSpec((1, 1, 3, length, width), lambda r, j, lens: (j, r, 0, 0, 0)),
            scratch_shapes=[
                pltpu.VMEM((n_blk, length, width), F32),
                pltpu.VMEM((n_blk, heads, length), F32),
            ],
        ),
        out_shape=jax.ShapeDtypeStruct((n_blk, rows, 3, length, width), BF16),
        compiler_params=pltpu.CompilerParams(vmem_limit_bytes=VMEM_LIMIT),
        cost_estimate=pl.CostEstimate(flops=4 * 10**9, bytes_accessed=12 * 10**6, transcendentals=10**7),
        name="attn_bwd",
    )(lens, *arrays)


def exchange(values):
    return lax.all_to_all(values, "blk", 0, 0, tiled=True)


def bits_of(axis):
    return lax.axis_size(axis).bit_length() - 1


def halve(current, axis, name, bit):
    size = lax.axis_size(name)
    mine = (lax.axis_index(name) >> bit) & 1
    half = current.shape[axis] // 2
    keep = lax.dynamic_slice_in_dim(current, mine * half, half, axis)
    send = lax.dynamic_slice_in_dim(current, (1 - mine) * half, half, axis)
    got = lax.ppermute(send, name, [(k, k ^ (1 << bit)) for k in range(size)])
    return (keep.astype(F32) + got.astype(F32)).astype(BF16)


def core_first(values):
    n_dp = lax.axis_size("dp")
    tokens, cols = values.shape
    return values.reshape(tokens, n_dp // 2, 2, cols // n_dp).transpose(0, 2, 1, 3).reshape(tokens, cols)


def y_first(values):
    n_blk = lax.axis_size("blk")
    tokens, cols = values.shape
    return values.reshape(tokens, n_blk // 2, 2, cols // n_blk).transpose(0, 2, 1, 3).reshape(tokens, cols)


def scatter_steps(y_early):
    dp_bits, blk_bits = bits_of("dp"), bits_of("blk")
    rest = [("dp", b) for b in reversed(range(1, dp_bits))]
    blk = [("blk", 0)] + [("blk", b) for b in reversed(range(1, blk_bits))]
    if y_early:
        return [("dp", 0)] + blk[:1] + rest + blk[1:]
    return [("dp", 0)] + rest + blk


def block_order(y_early):
    rest = [("dp", b) for b in range(1, bits_of("dp"))]
    blk = [("blk", b) for b in range(bits_of("blk"))]
    if y_early:
        return [("dp", 0)] + blk[:1] + rest + blk[1:]
    return [("dp", 0)] + rest + blk


def z_order():
    rest = [("dp", b) for b in range(1, bits_of("dp"))]
    blk = [("blk", b) for b in range(bits_of("blk"))]
    return [("dp", 0)] + blk[1:2] + rest + blk[:1] + blk[2:]


def scatter(grad, rows_name, y_early):
    n_rows = lax.axis_size(rows_name)
    rows, cols = grad.shape
    current = grad.reshape((n_rows // 2, 2, rows // n_rows, cols))
    for name, bit in scatter_steps(y_early):
        if name != rows_name:
            current = halve(current, 3, name, bit)
        elif bit == 0:
            current = halve(current, 1, name, bit)
        else:
            current = halve(current, 0, name, bit)
    return current.reshape(rows // n_rows, current.shape[3])


def total(values):
    for name in ("dp", "blk"):
        size = lax.axis_size(name)
        for bit in range(bits_of(name)):
            values = values + lax.ppermute(values, name, [(k, k ^ (1 << bit)) for k in range(size)])
    return values


def chunks_of(block_rows, block_cols):
    cols = block_cols // 128
    return 4 // cols, cols, block_rows // (4 // cols)


def place_of(order, dp, blk):
    place = 0
    for name, bit in order[1:]:
        place = 2 * place + (((dp if name == "dp" else blk) >> bit) & 1)
    return place


def blocks_dot(left_ref, right_ref, left_is_dp, side, col, order, n_dp, n_blk, row, out_ref, *at):
    size = left_ref.shape[2]
    tokens = left_ref.shape[3]
    if left_is_dp:
        left = jnp.concatenate([left_ref[2 * k + side, 0] for k in range(n_dp // 2)], axis=0)
        right = right_ref[...]
    else:
        cols = right_ref.shape[1] // n_dp
        left = left_ref[:, 0].reshape(n_blk * size, tokens)
        right = jnp.concatenate(
            [
                right_ref[:, pl.ds(pl.multiple_of((2 * k + side) * cols + col * 128, 128), 128)]
                for k in range(n_dp // 2)
            ],
            axis=1,
        )
    result = dot(left, right).astype(BF16)
    for d in range(n_dp // 2):
        for e in range(n_blk):
            k, m = (d, e) if left_is_dp else (e, d)
            out_ref[(*at, place_of(order, 2 * d, e), slice(row, row + size))] = result[
                k * size : (k + 1) * size, m * 128 : (m + 1) * 128
            ]


def ffn_wgrad_kernel(plans, n_dp, n_blk, rows, *refs):
    source = iter(refs)
    take = lambda n: [next(source) for _ in range(n)]
    n, n_terms = len(plans), sum(len(terms) for _, terms, _ in plans)
    lefts, rights, moved, outs, arrived = take(n_terms), take(n_terms), take(rows), take(2 * n), take(rows)
    sents, landed, keeps = take(n), take(n), take(n)
    send_sem, recv_sem = take(2)
    own_sem, out_sem, in_sem = take(3) if rows else (None, None, None)
    step = pl.program_id(0)
    core, device = partner("dp", 0)
    here = lax.axis_index("blk")

    def own(r):
        return pltpu.make_async_copy(moved[r].at[here], arrived[r].at[here], own_sem.at[r])

    def across(r, m):
        there = (here + m) % n_blk
        return pltpu.make_async_remote_copy(
            src_ref=moved[r].at[there],
            dst_ref=arrived[r].at[here],
            send_sem=out_sem.at[r, m],
            recv_sem=in_sem.at[r, m],
            device_id=(lax.axis_index("dp"), there),
            device_id_type=MESH,
        )

    @pl.when(step == 0)
    def _():
        barrier = pltpu.get_barrier_semaphore()
        pl.semaphore_signal(barrier, inc=1, device_id=device, device_id_type=MESH)
        for m in range(1, n_blk if rows else 1):
            there = (lax.axis_index("dp"), (here + m) % n_blk)
            pl.semaphore_signal(barrier, inc=1, device_id=there, device_id_type=MESH)
        pl.semaphore_wait(barrier, n_blk if rows else 1)
        for r in range(rows):
            own(r).start()
            for m in range(1, n_blk):
                across(r, m).start()

    def remote(n, c):
        return pltpu.make_async_remote_copy(
            src_ref=sents[n].at[c],
            dst_ref=landed[n].at[c],
            send_sem=send_sem.at[n, c],
            recv_sem=recv_sem.at[n, c],
            device_id=device,
            device_id_type=MESH,
        )

    first = 0
    for k, (order, terms, pieces) in enumerate(plans):
        c = step - first
        first += pieces

        @pl.when((c >= 0) & (c < pieces))
        def _():
            def make(side, *out):
                for at, left_is_dp, col_parts, row in terms:
                    blocks_dot(lefts[at], rights[at], left_is_dp, side, c % col_parts, order, n_dp, n_blk, row, *out)

            make(1 - core, sents[k], c)
            remote(k, c).start()
            make(core, keeps[k], c % 2)

        @pl.when((c >= 1) & (c < pieces + 1))
        def _():
            remote(k, c - 1).wait_recv()
            mine, _ = partner(*order[1])
            half = keeps[k].shape[1] // 2
            for out_ref, side in ((outs[2 * k], mine), (outs[2 * k + 1], 1 - mine)):

                def one(d, _):
                    at = side * half + d
                    out_ref[0, d] = keeps[k][(c - 1) % 2, at] + landed[k][c - 1, at]
                    return 0

                lax.fori_loop(0, half, one, 0)

    @pl.when(step == first)
    def _():
        for k in range(n):
            for c in range(plans[k][2]):
                remote(k, c).wait_send()
        for r in range(rows):
            own(r).wait()
            for m in range(1, n_blk):
                across(r, m).wait()


def ffn_wgrad(items, moved, flops, collective_id):
    n_dp, n_blk = lax.axis_size("dp"), lax.axis_size("blk")
    lefts, rights, plans, left_specs, right_specs, out_specs, outs, scratch = [], [], [], [], [], [], [], []
    held = n_dp * n_blk // 2
    steps = 0
    for order, wanted, terms in items:
        count, row, plan = len(wanted), 0, []
        for left_is_dp, left, right in terms:
            n_left, n_right = (n_dp, n_blk) if left_is_dp else (n_blk, n_dp)
            cols, tokens = left.shape
            row_parts, col_parts, size = chunks_of(cols // n_left, right.shape[1] // n_right)
            plan.append((len(lefts), left_is_dp, col_parts, row))
            row += size
            lefts.append(left.reshape(n_left, row_parts, size, tokens))
            rights.append(right)
            left_specs.append(
                pl.BlockSpec(
                    (n_left, 1, size, tokens),
                    lambda p, at=steps, low=wanted[0], count=count, col_parts=col_parts: (
                        0,
                        (low + jnp.clip(p - at, 0, count - 1)) // col_parts,
                        0,
                        0,
                    ),
                )
            )
            right_specs.append(pl.BlockSpec(right.shape, lambda p: (0, 0), pipeline_mode=pl.Buffered(1)))
        plans.append((order, plan, count))
        out_specs += [
            pl.BlockSpec(
                (1, held // 2, row, 128), lambda p, at=steps, count=count: (jnp.clip(p - 1 - at, 0, count - 1), 0, 0, 0)
            )
        ] * 2
        outs += [jax.ShapeDtypeStruct((count, held // 2, row, 128), BF16)] * 2
        scratch.append((count, held, row, 128))
        steps += count
    n = len(items)
    flat = pl.pallas_call(
        functools.partial(ffn_wgrad_kernel, plans, n_dp, n_blk, len(moved)),
        grid=(steps + 1,),
        in_specs=left_specs + right_specs + [pl.BlockSpec(memory_space=pl.ANY)] * len(moved),
        out_specs=out_specs + [pl.BlockSpec(memory_space=pl.ANY)] * len(moved),
        out_shape=outs + [jax.ShapeDtypeStruct(a.shape, a.dtype) for a in moved],
        scratch_shapes=[pltpu.VMEM(a, BF16) for a in scratch] * 2
        + [pltpu.VMEM((2,) + a[1:], BF16) for a in scratch]
        + [pltpu.SemaphoreType.DMA((n, 4))] * 2
        + ([pltpu.SemaphoreType.DMA((len(moved),))] + [pltpu.SemaphoreType.DMA((len(moved), n_blk))] * 2 if moved else []),
        compiler_params=pltpu.CompilerParams(
            collective_id=collective_id, has_side_effects=True, vmem_limit_bytes=VMEM_LIMIT
        ),
        cost_estimate=pl.CostEstimate(flops=flops, bytes_accessed=10**7, transcendentals=0),
        name="ffn_wgrad",
    )(*lefts, *rights, *moved)
    return [tuple(flat[2 * k : 2 * k + 2]) for k in range(n)], list(flat[2 * n :])


def fold_kernel(stages, *refs):
    n = len(stages)
    for k, (name, bit) in enumerate(stages):
        mine, _ = partner(name, bit)
        keep_ref, got_ref = refs[2 * k], refs[2 * k + 1]
        half = keep_ref.shape[1] // 2
        for out_ref, side in ((refs[2 * n + 2 * k], mine), (refs[2 * n + 2 * k + 1], 1 - mine)):

            def one(d, _):
                at = side * half + d
                out_ref[0, d] = keep_ref[0, at] + got_ref[0, at]
                return 0

            lax.fori_loop(0, half, one, 0)


def fold(pairs, stages, flops):
    n = len(pairs)
    arrays = [a for pair in pairs for a in pair]
    block = lambda a, parts: pl.BlockSpec((1, a.shape[1] // parts) + a.shape[2:], lambda c: (c, 0, 0, 0))
    half = lambda a: jax.ShapeDtypeStruct((a.shape[0], a.shape[1] // 2) + a.shape[2:], BF16)
    flat = pl.pallas_call(
        functools.partial(fold_kernel, stages),
        grid=(arrays[0].shape[0],),
        in_specs=[block(a, 1) for a in arrays],
        out_specs=[block(a, 2) for a in arrays],
        out_shape=[half(a) for a in arrays],
        compiler_params=pltpu.CompilerParams(vmem_limit_bytes=VMEM_LIMIT),
        cost_estimate=pl.CostEstimate(flops=flops, bytes_accessed=10**7, transcendentals=0),
        name="fold",
    )(*arrays)
    return [tuple(flat[2 * k : 2 * k + 2]) for k in range(n)]


def swap(values, name, bit):
    size = lax.axis_size(name)
    return lax.ppermute(values, name, [(k, k ^ (1 << bit)) for k in range(size)])


def partner(name, bit):
    here = {"dp": lax.axis_index("dp"), "blk": lax.axis_index("blk")}
    mine = (here[name] // (1 << bit)) % 2
    other = dict(here)
    other[name] = here[name] + (1 - 2 * mine) * (1 << bit)
    return mine, (other["dp"], other["blk"])


def ffn_kernel(gathered_ref, hidden_ref, cot_ref, gain_ref, wo_ref, wg_ref, wu_ref, wd_ref, *refs):
    out_refs, (low_ref, resid_ref, acc_ref, dmid_ref) = refs[-14:-4], refs[-4:]
    lowt_ref, mid_ref, inner_ref, dgate_ref, dup_ref, out_ref, dres_ref, dbranch_ref, dgain_ref, dattn_ref = out_refs
    n_blk, length, width = gathered_ref.shape
    step = pl.program_id(0)

    @pl.when(step == 0)
    def _():
        for s in range(n_blk):
            low_ref[:, s * width : (s + 1) * width] = gathered_ref[s]
        resid = hidden_ref[...].astype(F32) + dot(low_ref[...], wo_ref[...])
        resid_ref[...] = resid
        normed, _ = rms_parts(resid)
        mid_ref[...] = (normed * gain_ref[...]).astype(BF16)
        acc_ref[...] = jnp.zeros_like(acc_ref)
        dmid_ref[...] = jnp.zeros_like(dmid_ref)
        lowt_ref[...] = low_ref[...].T

    gate = dot(mid_ref[...], wg_ref[...])
    up = dot(mid_ref[...], wu_ref[...])
    d_inner = dot_nt(cot_ref[...], wd_ref[...])
    sigma = 1.0 / (1.0 + jnp.exp(-gate))
    act = gate * sigma
    inner = (act * up).astype(BF16)
    d_gate = (d_inner * up * (sigma * (1.0 + gate * (1.0 - sigma)))).astype(BF16)
    d_up = (d_inner * act).astype(BF16)
    inner_ref[...] = inner.T
    dgate_ref[...] = d_gate.T
    dup_ref[...] = d_up.T
    acc_ref[...] += dot(inner, wd_ref[...])
    dmid_ref[...] += dot_nt(d_gate, wg_ref[...]) + dot_nt(d_up, wu_ref[...])

    @pl.when(step == pl.num_programs(0) - 1)
    def _():
        resid = resid_ref[...]
        out_ref[...] = (resid + acc_ref[...]).astype(BF16)
        normed, inverse = rms_parts(resid)
        d_mid = dmid_ref[...]
        dgain_ref[...] = jnp.sum(d_mid * normed, axis=0, keepdims=True)
        d_resid = cot_ref[...].astype(F32) + norm_back(d_mid * gain_ref[...], normed, inverse)
        dres_ref[...] = d_resid
        d_branch = d_resid.astype(BF16)
        dbranch_ref[...] = d_branch
        back = dot_nt(d_branch, wo_ref[...]).astype(BF16)
        for s in range(n_blk):
            dattn_ref[s] = back[:, s * width : (s + 1) * width]


def feed_forward(row, before, gathered, hidden, cot, gain, w_out, w_gate, w_up, w_down):
    n_blk, length, width = gathered.shape
    tokens, model = hidden.shape
    inner = w_gate.shape[1]
    chunk = 256
    once = lambda a: pl.BlockSpec(a.shape, lambda j: (0,) * len(a.shape), pipeline_mode=pl.Buffered(1))
    whole = lambda a: pl.BlockSpec(a.shape, lambda j: (0,) * len(a.shape))
    cols = pl.BlockSpec((model, chunk), lambda j: (0, j))
    own = pl.BlockSpec((length, model), lambda j: (row, 0), pipeline_mode=pl.Buffered(1))
    mine = pl.BlockSpec((length, model), lambda j: (row, 0))
    turned = pl.BlockSpec((chunk, length), lambda j: (j, row))
    shape = jax.ShapeDtypeStruct
    shared = (
        [shape((model, tokens), BF16), shape((tokens, model), BF16)]
        + [shape((inner, tokens), BF16)] * 3
        + [shape((tokens, model), BF16), shape((tokens, model), F32), shape((tokens, model), BF16)]
    )
    outs = shared + [shape((1, model), F32), shape((n_blk, length, width), BF16)]
    before = list(before or [])
    return pl.pallas_call(
        ffn_kernel,
        grid=(inner // chunk,),
        in_specs=[once(gathered), own, own, once(gain), once(w_out)]
        + [cols, cols, pl.BlockSpec((chunk, model), lambda j: (j, 0))]
        + [pl.BlockSpec(memory_space=pl.ANY)] * len(before),
        out_specs=[pl.BlockSpec((model, length), lambda j: (0, row)), mine]
        + [turned] * 3
        + [mine] * 3
        + [whole(a) for a in outs[8:]],
        out_shape=outs,
        scratch_shapes=[pltpu.VMEM((length, model), BF16)] + [pltpu.VMEM((length, model), F32)] * 3,
        input_output_aliases={8 + k: k for k in range(len(before))},
        compiler_params=pltpu.CompilerParams(vmem_limit_bytes=VMEM_LIMIT),
        cost_estimate=pl.CostEstimate(
            flops=12 * length * model * inner + 4 * length * model * model,
            bytes_accessed=6 * model * inner + 6 * length * inner + 20 * length * model,
            transcendentals=length * inner,
        ),
        name="ffn",
    )(gathered, hidden, cot, gain, w_out, w_gate, w_up, w_down, *before)


class Halving:
    def __init__(self, order, work, sent, landed, send_sem, recv_sem):
        self.order, self.work, self.sent, self.landed = order, work, sent, landed
        self.send_sem, self.recv_sem = send_sem, recv_sem
        self.held = work.shape[1]

    def base(self, stage):
        base = 0
        for earlier in range(1, stage):
            base = base + partner(*self.order[earlier])[0] * (self.held >> earlier)
        return base

    def remote(self, stage, c):
        mine, device = partner(*self.order[stage])
        half = self.held >> stage
        if stage == 0:
            sent = self.sent.at[c]
        else:
            sent = self.work.at[c, pl.ds(self.base(stage) + (1 - mine) * half, half)]
        return pltpu.make_async_remote_copy(
            src_ref=sent,
            dst_ref=self.landed[stage].at[c],
            send_sem=self.send_sem.at[stage, c],
            recv_sem=self.recv_sem.at[stage, c],
            device_id=device,
            device_id_type=MESH,
        )

    def add(self, stage, c):
        base = self.base(stage + 1)

        def one(d, _):
            self.work[c, base + d] = self.work[c, base + d] + self.landed[stage][c, d]
            return 0

        lax.fori_loop(0, self.held >> stage, one, 0)

    def result(self, c):
        stage = len(self.order) - 1
        return self.work[c, self.base(stage + 1)].astype(F32) + self.landed[stage][c, 0].astype(F32)


def store_piece(out_ref, c, piece):
    size, cols = piece.shape[0], out_ref.shape[1] // 128
    row, col = c // cols, c % cols
    out_ref[row * size : (row + 1) * size, col * 128 : (col + 1) * 128] = piece


def tail_kernel(ffn_orders, own_order, qkv_orders, n_dp, n_blk, rows, *refs):
    source = iter(refs)
    take = lambda n: [next(source) for _ in range(n)]
    n_ffn, n_qkv = len(ffn_orders), 3
    ffn_stages, qkv_stages = len(ffn_orders[0]), len(qkv_orders[0])
    cos_ref, sin_ref, gain_ref, small_ref = take(4)
    loads = take(6 + rows)
    keeps, gots = take(n_ffn), take(n_ffn)
    own_keep, own_sent = take(2)
    ffn_outs, (own_out,), qkv_outs = take(n_ffn), take(1), take(n_qkv)
    first_ref, input_ref, total_ref = take(3)
    here = take(6 + rows)
    back_refs, (turned_ref, hidden_ref, dres_ref, *weights) = here[:rows], here[rows:]
    low_ref, acc_ref, vecs, vec_landed = take(4)
    load_sem, keep_sem, got_sem, vec_send, vec_recv = take(5)
    streams = []
    for k, order in enumerate(ffn_orders):
        work, *landed = take(1 + ffn_stages)
        streams.append(Halving(order, work, None, landed, *take(2)))
    work, *landed = take(1 + len(own_order))
    own = Halving(own_order, work, own_sent, landed, *take(2))
    (own_sem,) = take(1)
    own_copy = pltpu.make_async_copy(own_keep, own.work, own_sem)
    late = []
    for u in range(n_qkv):
        late.append([])
        for order in qkv_orders:
            work, sent, *landed = take(2 + qkv_stages)
            late[u].append(Halving(order, work, sent, landed, *take(2)))
    length, width = back_refs[0].shape[3:]
    core, _ = partner("dp", 0)
    counts = [a.shape[0] for a in keeps]

    load = [pltpu.make_async_copy(a, b, load_sem.at[k]) for k, (a, b) in enumerate(zip(loads, here))]
    keep_copy = lambda k, c: pltpu.make_async_copy(keeps[k].at[c], streams[k].work.at[c], keep_sem.at[k, c])
    got_copy = lambda k, c: pltpu.make_async_copy(gots[k].at[c], streams[k].landed[0].at[c], got_sem.at[k, c])
    for copy in load[: rows + 1]:
        copy.start()
    for c in range(max(counts)):
        for k in range(n_ffn):
            if c < counts[k]:
                keep_copy(k, c).start()
                got_copy(k, c).start()
    own_copy.start()
    for copy in load[rows + 1 :]:
        copy.start()

    everyone = qkv_orders[0]
    barrier = pltpu.get_barrier_semaphore()
    for name, bit in everyone:
        pl.semaphore_signal(barrier, inc=1, device_id=partner(name, bit)[1], device_id_type=MESH)
    pl.semaphore_wait(barrier, len(everyone))

    def ffn(c, stage):
        for k, stream in enumerate(streams):
            if c >= counts[k]:
                continue
            if stage == 1:
                keep_copy(k, c).wait()
                got_copy(k, c).wait()
            else:
                stream.remote(stage - 1, c).wait_recv()
            if stage < ffn_stages:
                stream.add(stage - 1, c)
                stream.remote(stage, c).start()
            else:
                store_piece(ffn_outs[k], c, stream.result(c))

    def projections(which):
        for r in range(rows):
            at = pl.ds(r * length, length)
            for s in range(n_blk):
                cols = slice(s * width, (s + 1) * width)
                values = back_refs[r][s, 0, which].astype(F32)
                if which < 2:
                    turned = values * cos_ref[at, :] - swap_halves(values) * sin_ref[at, :]
                else:
                    turned = 0.5 * values
                    first_ref[:, r, cols] = turned
                low_ref[which, at, cols] = turned.astype(BF16)
        for fresh in range(2):
            side = 1 - core if fresh == 0 else core
            left = jnp.concatenate([turned_ref[2 * k + side] for k in range(n_dp // 2)], axis=0)
            size, half = turned_ref.shape[1], turned_ref.shape[1] // 2
            result = dot(left, low_ref[which]).astype(BF16)
            for h, stream in enumerate(late[which]):
                out_ref = stream.sent if fresh == 0 else stream.work
                for d in range(n_dp // 2):
                    for e in range(n_blk):
                        out_ref[0, place_of(stream.order, 2 * d, e)] = result[
                            d * size + h * half : d * size + (h + 1) * half, e * width : (e + 1) * width
                        ]
                if fresh == 0:
                    stream.remote(0, 0).start()

    def own_step(stage):
        if stage == 1:
            own_copy.wait()
        for c in range(own.work.shape[0]):
            own.remote(stage - 1, c).wait_recv()
            if stage < len(own.order):
                own.add(stage - 1, c)
                own.remote(stage, c).start()
            else:
                store_piece(own_out, c, own.result(c))

    def late_step(which, stage):
        for h, stream in enumerate(late[which]):
            stream.remote(stage - 1, 0).wait_recv()
            if stage < qkv_stages:
                stream.add(stage - 1, 0)
                stream.remote(stage, 0).start()
            else:
                half = stream.work.shape[2]
                qkv_outs[which][h * half : (h + 1) * half, :] = stream.result(0)

    def vec_copy(e):
        return pltpu.make_async_remote_copy(
            src_ref=vecs.at[e],
            dst_ref=vec_landed.at[e],
            send_sem=vec_send.at[e],
            recv_sem=vec_recv.at[e],
            device_id=partner(*everyone[e])[1],
            device_id_type=MESH,
        )

    model = hidden_ref.shape[1]
    n_vec = len(everyone)

    def matmul():
        for copy in load[rows + 1 :]:
            copy.wait()
        for r in range(rows):
            at = pl.ds(r * length, length)
            acc_ref[at, :] = (
                dot_nt(low_ref[0, at, :], weights[0][...])
                + dot_nt(low_ref[1, at, :], weights[1][...])
                + dot_nt(low_ref[2, at, :], weights[2][...])
            )

    def norm():
        d_gain = jnp.zeros((1, model), F32)
        for r in range(rows):
            at = pl.ds(r * length, length)
            normed, inverse = rms_parts(hidden_ref[at, :].astype(F32))
            d_normed = acc_ref[at, :]
            d_gain = d_gain + jnp.sum(d_normed * normed, axis=0, keepdims=True)
            input_ref[:, r, :] = dres_ref[at, :] + norm_back(d_normed * gain_ref[...], normed, inverse)
        vecs[0, :, :model] = d_gain
        vecs[0, :, model:] = small_ref[...]
        vec_copy(0).start()

    def vec(e):
        vec_copy(e).wait_recv()
        summed = vecs[e] + vec_landed[e]
        if e == n_vec - 1:
            total_ref[...] = summed
        else:
            vecs[e + 1] = summed
            vec_copy(e + 1).start()

    chunks = range(max(counts))
    for c in range(own.work.shape[0]):
        own.remote(0, c).start()
    for c in chunks:
        ffn(c, 1)
    for copy in load[: rows + 1]:
        copy.wait()
    projections(2)
    projections(1)
    late_step(2, 1)
    own_step(1)
    projections(0)
    late_step(1, 1)
    ffn(0, 2)
    late_step(0, 1)
    matmul()
    own_step(2)
    late_step(2, 2)
    ffn(1, 2)
    norm()
    own_step(3)
    late_step(1, 2)
    ffn(2, 2)
    vecs_left = list(range(n_vec))
    vec(vecs_left.pop(0))
    own_step(4)
    late_step(2, 3)
    late_step(0, 2)
    ffn(3, 2)
    vec(vecs_left.pop(0))
    late_step(1, 3)
    late_step(0, 3)
    for stage in range(4, qkv_stages + 1):
        vec(vecs_left.pop(0))
        for which in (2, 1, 0):
            late_step(which, stage)
    for c in chunks:
        for stage in range(3, ffn_stages + 1):
            ffn(c, stage)
    for e in vecs_left:
        vec(e)

    for stream, count in zip(streams, counts):
        for c in range(count):
            for stage in range(1, ffn_stages):
                stream.remote(stage, c).wait_send()
    for c in range(own.work.shape[0]):
        for stage in range(len(own.order)):
            own.remote(stage, c).wait_send()
    for stream in late[0] + late[1] + late[2]:
        for stage in range(qkv_stages):
            stream.remote(stage, 0).wait_send()
    for e in range(n_vec):
        vec_copy(e).wait_send()


def tail(ffn_pairs, ffn_blocks, ffn_orders, own_pair, own_order, qkv_orders, backs, normed_t, hidden, d_resid, weights, cos, sin, gain, small, collective_id):
    n_dp, n_blk = lax.axis_size("dp"), lax.axis_size("blk")
    tokens, model = hidden.shape
    rows, length = len(backs), backs[0].shape[3]
    keeps, gots = [pair[0] for pair in ffn_pairs], [pair[1] for pair in ffn_pairs]
    loads = [*backs, normed_t.reshape(n_dp, model // n_dp, tokens), hidden, d_resid, *weights]
    ffn_stages, qkv_stages, n_qkv = len(ffn_orders[0]), len(qkv_orders[0]), 3
    n_chunks = max(a.shape[0] for a in keeps)
    block = (model // n_dp, model // n_blk)
    held = n_dp * n_blk // 2
    shape = jax.ShapeDtypeStruct
    vec = (1, model + small.shape[1])
    outs = (
        [shape(a, F32) for a in ffn_blocks]
        + [shape(block, F32)] * n_qkv
        + [shape((length, rows, model), F32)] * 2
        + [shape(vec, F32)]
    )
    scratch = [pltpu.VMEM(a.shape, a.dtype) for a in loads]
    scratch += [
        pltpu.VMEM((n_qkv, tokens, model), BF16),
        pltpu.VMEM((tokens, model), F32),
        pltpu.VMEM((qkv_stages,) + vec, F32),
        pltpu.VMEM((qkv_stages,) + vec, F32),
        pltpu.SemaphoreType.DMA((len(loads),)),
        pltpu.SemaphoreType.DMA((len(keeps), n_chunks)),
        pltpu.SemaphoreType.DMA((len(keeps), n_chunks)),
        pltpu.SemaphoreType.DMA((qkv_stages,)),
        pltpu.SemaphoreType.DMA((qkv_stages,)),
    ]
    for a in keeps:
        scratch.append(pltpu.VMEM(a.shape, BF16))
        scratch += [pltpu.VMEM((a.shape[0], a.shape[1] >> stage) + a.shape[2:], BF16) for stage in range(ffn_stages)]
        scratch += [pltpu.SemaphoreType.DMA((ffn_stages, a.shape[0]))] * 2
    part = (block[0] // len(qkv_orders), block[1])
    keep = own_pair[0]
    scratch.append(pltpu.VMEM(keep.shape, BF16))
    scratch += [pltpu.VMEM((keep.shape[0], keep.shape[1] >> stage) + keep.shape[2:], BF16) for stage in range(len(own_order))]
    scratch += [pltpu.SemaphoreType.DMA((len(own_order), keep.shape[0]))] * 2 + [pltpu.SemaphoreType.DMA]
    for _ in range(n_qkv * len(qkv_orders)):
        scratch += [pltpu.VMEM((1, held) + part, BF16)] * 2
        scratch += [pltpu.VMEM((1, held >> stage) + part, BF16) for stage in range(qkv_stages)]
        scratch += [pltpu.SemaphoreType.DMA((qkv_stages, 1))] * 2
    vmem, anywhere = pl.BlockSpec(memory_space=pltpu.VMEM), pl.BlockSpec(memory_space=pl.ANY)
    return pl.pallas_call(
        functools.partial(tail_kernel, ffn_orders, own_order, qkv_orders, n_dp, n_blk, rows),
        in_specs=[vmem] * 4 + [anywhere] * (len(loads) + 2 * len(keeps) + 2),
        out_specs=[vmem] * len(outs),
        out_shape=outs,
        scratch_shapes=scratch,
        compiler_params=pltpu.CompilerParams(
            collective_id=collective_id, has_side_effects=True, vmem_limit_bytes=60 * 2**20
        ),
        cost_estimate=pl.CostEstimate(flops=10**11, bytes_accessed=10**8, transcendentals=0),
        name="tail",
    )(cos, sin, gain, small, *loads, *keeps, *gots, *own_pair)


def turn_back_kernel(cos_ref, sin_ref, back_ref, low_ref, first_ref):
    n_blk, rows, _, length, width = back_ref.shape
    which = pl.program_id(0)
    for r in range(rows):
        at = pl.ds(r * length, length)
        for s in range(n_blk):
            cols = slice(s * width, (s + 1) * width)
            values = back_ref[s, r, 0].astype(F32)

            @pl.when(which < 2)
            def _():
                cos, sin = cos_ref[at, :width], sin_ref[at, :width]
                wide = values if width == 128 else jnp.concatenate([values, values], axis=1)
                swapped = swap_halves(wide)[:, :width]
                low_ref[0, at, cols] = (values * cos - swapped * sin).astype(BF16)

            @pl.when(which == 2)
            def _():
                first_ref[at, cols] = 0.5 * values
                low_ref[0, at, cols] = (0.5 * values).astype(BF16)


def turn_back(back, cos, sin):
    n_blk, rows, _, length, width = back.shape
    tokens, model = rows * length, n_blk * width
    full = lambda a: pl.BlockSpec(a.shape, lambda w: (0, 0))
    return pl.pallas_call(
        turn_back_kernel,
        grid=(3,),
        in_specs=[full(cos), full(sin), pl.BlockSpec((n_blk, rows, 1, length, width), lambda w: (0, 0, w, 0, 0))],
        out_specs=[
            pl.BlockSpec((1, tokens, model), lambda w: (w, 0, 0)),
            pl.BlockSpec((tokens, model), lambda w: (0, 0)),
        ],
        out_shape=[jax.ShapeDtypeStruct((3, tokens, model), BF16), jax.ShapeDtypeStruct((tokens, model), F32)],
        compiler_params=pltpu.CompilerParams(vmem_limit_bytes=VMEM_LIMIT),
        name="turn_back",
    )(cos, sin, back)


def input_grad_kernel(hidden_ref, dres_ref, gain_ref, low_ref, wq_ref, wk_ref, wv_ref, out_ref, dgain_ref):
    tokens = hidden_ref.shape[0]
    half = tokens // 2
    d_gain = jnp.zeros(dgain_ref.shape, F32)
    for r in range(2):
        at = pl.ds(r * half, half)
        d_normed = (
            dot_nt(low_ref[0, at, :], wq_ref[...])
            + dot_nt(low_ref[1, at, :], wk_ref[...])
            + dot_nt(low_ref[2, at, :], wv_ref[...])
        )
        normed, inverse = rms_parts(hidden_ref[at, :].astype(F32))
        d_gain = d_gain + jnp.sum(d_normed * normed, axis=0, keepdims=True)
        out_ref[at, :] = dres_ref[at, :] + norm_back(d_normed * gain_ref[...], normed, inverse)
    dgain_ref[...] = d_gain


def input_grad(hidden, d_resid, gain, low, w_query, w_key, w_value):
    tokens, model = hidden.shape
    return pl.pallas_call(
        input_grad_kernel,
        out_shape=[jax.ShapeDtypeStruct((tokens, model), F32), jax.ShapeDtypeStruct((1, model), F32)],
        compiler_params=pltpu.CompilerParams(vmem_limit_bytes=VMEM_LIMIT),
        cost_estimate=pl.CostEstimate(
            flops=6 * tokens * model * model, bytes_accessed=6 * model * model + 16 * tokens * model, transcendentals=0
        ),
        name="input_grad",
    )(hidden, d_resid, gain, low, w_query, w_key, w_value)


def rms_parts(values):
    inverse_rms = lax.rsqrt(jnp.mean(values * values, axis=-1, keepdims=True) + EPS)
    return values * inverse_rms, inverse_rms


def norm_back(d_normed, normed, inverse_rms):
    return inverse_rms * (d_normed - normed * jnp.mean(d_normed * normed, axis=-1, keepdims=True))


def rope_tables(doc_lengths, offset, length):
    half = HEAD_DIM // 2
    places = offset + jnp.arange(length, dtype=jnp.int32)
    ends = jnp.cumsum(doc_lengths, axis=1)
    start = jnp.max(jnp.where(ends[:, None, :] <= places[None, :, None], ends[:, None, :], 0), axis=2)
    position = (places[None, :] - start).astype(F32).reshape(-1, 1)
    lane = jnp.arange(128, dtype=jnp.int32)
    freq = jnp.power(10000.0, -(lane % half).astype(F32) * 2.0 / HEAD_DIM)
    angles = position * freq[None, :]
    sign = jnp.where(lane % HEAD_DIM < half, -1.0, 1.0)
    return jnp.cos(angles), jnp.sin(angles) * sign[None, :]


def body(
    hidden_in,
    first_values,
    doc_lengths,
    w_query,
    w_key,
    w_value,
    w_out,
    w_gate,
    w_up,
    w_down,
    attn_gain,
    ffn_gain,
    out_cotangent,
):
    length, rows, model = hidden_in.shape
    n_docs = doc_lengths.shape[1]
    n_blk, n_dp = lax.axis_size("blk"), lax.axis_size("dp")
    width = model // n_blk
    tokens = rows * length
    flat = lambda a: jnp.transpose(a, (1, 0, 2)).reshape(tokens, model)
    unflat = lambda a: jnp.transpose(a.reshape(rows, length, model), (1, 0, 2))
    lens = doc_lengths.reshape(-1)

    hidden, cot, first = flat(hidden_in), flat(out_cotangent), flat(first_values)
    row_gain = lambda gain: gain.reshape(1, model)

    cos, sin = rope_tables(doc_lengths, lax.axis_index("blk") * length, length)
    *qkv_own, normed_in, sums = project_qkv(
        hidden, first, cos, sin, row_gain(attn_gain), w_query, w_key, w_value, rows, n_blk
    )
    qkv, attended, lse, gathered = [], [], [], []
    for r in range(rows):
        qkv.append(exchange(qkv_own[r]))
    for r in range(rows):
        o_f, o_low, lse_r = attn_fwd(lens, qkv[r], r, n_docs)
        attended.append(o_f)
        lse.append(lse_r)
        gathered.append(exchange(o_low))
    shared, d_gains, d_attn = None, [], []
    for r in range(rows):
        *shared, d_gain, d_attn_r = feed_forward(
            r, shared, gathered[r], hidden, cot, row_gain(ffn_gain), w_out, w_gate, w_up, w_down
        )
        d_gains.append(d_gain)
        d_attn.append(d_attn_r)
    attn_low_t, normed_mid, inner_t, d_gate_t, d_up_t, block_out, d_resid_mid, d_branch = shared
    d_gain_two = sum(d_gains)

    inner = w_gate.shape[1]
    by_blocks = (model // n_dp) % 128 == 0 and width == 128 and (inner // n_blk) % 32 == 0
    early, late, middle = block_order(False), block_order(True), z_order()
    if by_blocks:
        orders = (early, late, middle)
        pieces = (0, 1, 2, 3)
        exchanged = lambda pairs, stages: [(keep, swap(sent, *stage)) for (keep, sent), stage in zip(pairs, stages)]
        folded, d_own = ffn_wgrad(
            (
                (early, pieces, [(False, d_gate_t, normed_mid)]),
                (late, pieces, [(False, d_up_t, normed_mid)]),
                (middle, pieces, [(True, inner_t, cot)]),
            ),
            d_attn,
            10**9,
            1,
        )
        ffn_pairs = exchanged(folded, [order[1] for order in orders])
        back_own = [
            attn_bwd(lens, qkv[r : r + 1], d_own[r : r + 1], attended[r : r + 1], lse[r : r + 1], r, n_docs)
            for r in range(rows)
        ]
        backs = [exchange(b) for b in back_own[:-1]]
        kept = [keep for keep, got in ffn_pairs]
        token, kept = lax.optimization_barrier((back_own, kept))
        second = [order[2] for order in orders]
        folded = fold([(keep, got) for keep, (_, got) in zip(kept, ffn_pairs)], second, 10**9)
        ffn_pairs = exchanged(folded, second)
        folded, attn_low_t = lax.optimization_barrier((folded, attn_low_t))
        ffn_pairs = [(keep, got) for (keep, _), (_, got) in zip(folded, ffn_pairs)]
        project, back_last = ffn_wgrad(
            ((early, pieces, [(True, attn_low_t, d_branch)]),), back_own[-1:], LAST_FLOPS, 2
        )
        backs += back_last
    else:
        d_own = [exchange(d_attn[r]) for r in range(rows)]
        back = exchange(attn_bwd(lens, qkv, d_own, attended, lse, 0, n_docs))

    squares = jnp.sum(sums, axis=(0, 2)).reshape(1, 2)
    small = jnp.concatenate([d_gain_two, squares, jnp.zeros((1, 126), F32)], axis=1)
    if by_blocks:
        *blocks, grad_first, grad_input, small = tail(
            ffn_pairs,
            ((inner // n_blk, model // n_dp),) * 2 + ((inner // n_dp, model // n_blk), (model // n_dp, model // n_blk)),
            tuple(order[2:] for order in orders),
            project[0],
            early[1:],
            (early, late),
            backs,
            normed_in.T,
            hidden,
            d_resid_mid,
            (w_query, w_key, w_value),
            cos,
            sin,
            row_gain(attn_gain),
            small,
            0,
        )
        small = small.reshape(-1)
        grad_gate, grad_up = blocks[0].T, blocks[1].T
        grad_down, grad_project = blocks[2:4]
        grad_query, grad_key, grad_value = blocks[4:]
    else:
        low, grad_first = turn_back(back, cos, sin)
        mid_cf, in_cf = core_first(normed_mid), core_first(normed_in)
        sent = lambda a, b, name, y: scatter(dot_tn(a, b).astype(BF16), name, y).astype(F32)
        grad_down = sent(inner_t.T, y_first(cot), "dp", False)
        grad_gate = sent(d_gate_t.T, mid_cf, "blk", False).T
        grad_up = sent(d_up_t.T, mid_cf, "blk", True).T
        grad_project = sent(d_branch, core_first(attn_low_t.T), "blk", True).T
        grad_query, grad_key, grad_value = [sent(low[k], in_cf, "blk", True).T for k in range(3)]
        grad_first = unflat(grad_first)
        grad_input, d_gain_one = input_grad(hidden, d_resid_mid, row_gain(attn_gain), low, w_query, w_key, w_value)
        grad_input = unflat(grad_input)
        small = total(jnp.concatenate([d_gain_one.reshape(model), small.reshape(-1)]))
    n_entries = n_blk * length * rows * n_dp * model
    return (
        unflat(block_out),
        grad_input,
        grad_first,
        grad_query,
        grad_key,
        grad_value,
        grad_project,
        grad_gate,
        grad_up,
        grad_down,
        small[:model],
        small[model : 2 * model],
        small[2 * model] / n_entries,
        small[2 * model + 1] / n_entries,
    )


def solution(mesh):
    tokens = P("blk", "dp", None)
    return jax.shard_map(
        body,
        mesh=mesh,
        in_specs=(tokens, tokens, P("dp", None)) + (P(),) * 9 + (tokens,),
        out_specs=(tokens,) * 3 + (P("dp", "blk"),) * 7 + (P(),) * 4,
        check_vma=False,
    )
```

```python
import functools

import jax
import jax.numpy as jnp
from jax import lax
from jax.experimental import pallas as pl
from jax.experimental.pallas import tpu as pltpu
from jax.sharding import PartitionSpec as P

HEADS = 16
HEAD_DIM = 64
NEG = -1e30
EPS = 1e-06
F32 = jnp.float32
BF16 = jnp.bfloat16
VMEM_LIMIT = 56 * 2**20
LAST_FLOPS = 6 * 10**10
MESH = pl.DeviceIdType.MESH


def dot(a, b):
    return jnp.dot(a, b, preferred_element_type=F32)


def dot_nt(a, b):
    return lax.dot_general(a, b, (((1,), (1,)), ((), ())), preferred_element_type=F32)


def dot_tn(a, b):
    return lax.dot_general(a, b, (((0,), (0,)), ((), ())), preferred_element_type=F32)


def swap_halves(v):
    half = HEAD_DIM // 2
    width = v.shape[-1]
    lane = lax.broadcasted_iota(jnp.int32, v.shape, v.ndim - 1)
    left = pltpu.roll(v, width - half, v.ndim - 1)
    right = pltpu.roll(v, half, v.ndim - 1)
    return jnp.where(lane % HEAD_DIM < half, left, right)


def qkv_kernel(rows, length, width, hidden_ref, first_ref, cos_ref, sin_ref, gain_ref, wq_ref, wk_ref, wv_ref, *outs):
    out_refs, (normed_ref, sums_ref) = outs[:rows], outs[rows:]
    chunk = wq_ref.shape[1]

    @pl.when(pl.program_id(0) == 0)
    def _():
        for r in range(rows):
            at = pl.ds(r * length, length)
            normed, _ = rms_parts(hidden_ref[at, :].astype(F32))
            normed_ref[at, :] = (normed * gain_ref[...]).astype(BF16)

    first_sum = jnp.zeros((1, chunk), F32)
    mixed_sum = jnp.zeros((1, chunk), F32)
    for r in range(rows):
        at = pl.ds(r * length, length)
        normed = normed_ref[at, :]
        cos, sin = cos_ref[at, :], sin_ref[at, :]
        for which, w_ref in ((0, wq_ref), (1, wk_ref)):
            raw = dot(normed, w_ref[...])
            for c in range(chunk // 128):
                part = raw[:, c * 128 : (c + 1) * 128]
                turned = (part * cos + swap_halves(part) * sin).astype(BF16)
                for s in range(128 // width):
                    out_refs[r][c * (128 // width) + s, which] = turned[:, s * width : (s + 1) * width]
        first = first_ref[at, :].astype(F32)
        mixed = 0.5 * dot(normed, wv_ref[...]) + 0.5 * first
        first_sum = first_sum + jnp.sum(first * first, axis=0, keepdims=True)
        mixed_sum = mixed_sum + jnp.sum(mixed * mixed, axis=0, keepdims=True)
        low = mixed.astype(BF16)
        for s in range(chunk // width):
            out_refs[r][s, 2] = low[:, s * width : (s + 1) * width]
    sums_ref[0, 0:1] = first_sum
    sums_ref[0, 1:2] = mixed_sum


def project_qkv(hidden, first, cos, sin, gain, w_query, w_key, w_value, rows, n_blk):
    tokens, model = hidden.shape
    length, width = tokens // rows, model // n_blk
    chunk = 256
    steps = model // chunk
    full = lambda rows, cols: pl.BlockSpec((rows, cols), lambda j: (0, 0))
    weight = pl.BlockSpec((model, chunk), lambda j: (0, j))
    return pl.pallas_call(
        functools.partial(qkv_kernel, rows, length, width),
        grid=(steps,),
        in_specs=[
            full(tokens, model),
            pl.BlockSpec((tokens, chunk), lambda j: (0, j)),
            full(tokens, 128),
            full(tokens, 128),
            full(1, model),
            weight,
            weight,
            weight,
        ],
        out_specs=[pl.BlockSpec((chunk // width, 3, length, width), lambda j: (j, 0, 0, 0))] * rows
        + [full(tokens, model), pl.BlockSpec((1, 2, chunk), lambda j: (j, 0, 0))],
        out_shape=[jax.ShapeDtypeStruct((n_blk, 3, length, width), BF16)] * rows
        + [jax.ShapeDtypeStruct((tokens, model), BF16), jax.ShapeDtypeStruct((steps, 2, chunk), F32)],
        compiler_params=pltpu.CompilerParams(vmem_limit_bytes=VMEM_LIMIT),
        cost_estimate=pl.CostEstimate(
            flops=6 * tokens * model * model, bytes_accessed=6 * model * model + 10 * tokens * model, transcendentals=0
        ),
        name="qkv",
    )(hidden, first, cos, sin, gain, w_query, w_key, w_value)


def doc_ends(lens_ref, row, n_docs):
    ends, total = [], jnp.int32(0)
    for d in range(n_docs):
        total = total + lens_ref[row * n_docs + d]
        ends.append(total)
    return ends


def start_rows(ends, tile, length, heads):
    place = tile * length + lax.broadcasted_iota(jnp.int32, (1, length), 1)
    start = jnp.zeros((1, length), jnp.int32)
    for end in ends:
        start = jnp.where(end <= place, end, start)
    return jnp.concatenate([start] * heads, axis=1), jnp.concatenate([place] * heads, axis=1)


def head_masks(heads, width):
    lane = lax.broadcasted_iota(jnp.int32, (1, width), 1) // HEAD_DIM
    return [jnp.where(lane == h, 1.0, 0.0).astype(BF16) for h in range(heads)]


def by_head(values, masks):
    return jnp.concatenate([values * mask for mask in masks], axis=0)


def attn_fwd_kernel(row, n_docs, heads, lens_ref, qkv_ref, o_ref, low_ref, lse_ref, acc_ref):
    length, width = qkv_ref.shape[2:]
    i = pl.program_id(0)
    ends = doc_ends(lens_ref, row, n_docs)
    start, place = start_rows(ends, i, length, heads)
    lowest = jnp.int32(0)
    for end in ends:
        lowest = jnp.where(end <= i * length, end, lowest)
    lowest = lax.div(lowest, jnp.int32(length))
    masks = head_masks(heads, width)
    queries = by_head(qkv_ref[i, 0] * jnp.asarray(HEAD_DIM**-0.5, BF16), masks)

    def pair(step, carry):
        run_max, run_sum = carry
        tiles = [i - 2 * step, i - 2 * step - 1]
        at = [tiles[0], jnp.maximum(tiles[1], 0)]
        scores = []
        for j, source in zip(tiles, at):
            raw = dot_nt(qkv_ref[source, 1], queries)
            key = j * length + lax.broadcasted_iota(jnp.int32, raw.shape, 0)
            scores.append(jnp.where((key <= place) & (key >= start), raw, NEG))
        highest = jnp.max(jnp.maximum(scores[0], scores[1]), axis=0, keepdims=True)
        new_max = jnp.maximum(run_max, highest)
        weights = [jnp.exp(one - new_max) for one in scores]
        factor = jnp.exp(run_max - new_max)
        run_sum = run_sum * factor + jnp.sum(weights[0] + weights[1], axis=0, keepdims=True)
        added = dot_tn(qkv_ref[at[0], 2], weights[0].astype(BF16)) + dot_tn(qkv_ref[at[1], 2], weights[1].astype(BF16))
        acc_ref[...] = acc_ref[...] * factor + added
        return new_max, run_sum

    acc_ref[...] = jnp.zeros_like(acc_ref)
    run_max, run_sum = lax.fori_loop(
        0,
        (i - lowest + 2) // 2,
        pair,
        (jnp.full((1, heads * length), NEG, F32), jnp.zeros((1, heads * length), F32)),
    )
    result = acc_ref[...] / run_sum
    joined = jnp.concatenate(
        [
            result[h * HEAD_DIM : (h + 1) * HEAD_DIM, h * length : (h + 1) * length]
            for h in range(heads)
        ],
        axis=0,
    )
    attended = joined.T
    o_ref[0] = attended
    low_ref[0] = attended.astype(BF16)
    total = run_max + jnp.log(run_sum)
    for h in range(heads):
        lse_ref[0, h : h + 1, :] = total[:, h * length : (h + 1) * length]


def attn_fwd(lens, qkv, row, n_docs):
    n_blk, _, length, width = qkv.shape
    heads = width // HEAD_DIM
    tile = pl.BlockSpec((1, length, width), lambda i, lens: (i, 0, 0))
    return pl.pallas_call(
        functools.partial(attn_fwd_kernel, row, n_docs, heads),
        grid_spec=pltpu.PrefetchScalarGridSpec(
            num_scalar_prefetch=1,
            grid=(n_blk,),
            in_specs=[pl.BlockSpec(qkv.shape, lambda i, lens: (0, 0, 0, 0))],
            out_specs=[tile, tile, pl.BlockSpec((1, heads, length), lambda i, lens: (i, 0, 0))],
            scratch_shapes=[pltpu.VMEM((width, heads * length), F32)],
        ),
        out_shape=[
            jax.ShapeDtypeStruct((n_blk, length, width), F32),
            jax.ShapeDtypeStruct((n_blk, length, width), BF16),
            jax.ShapeDtypeStruct((n_blk, heads, length), F32),
        ],
        compiler_params=pltpu.CompilerParams(vmem_limit_bytes=VMEM_LIMIT),
        cost_estimate=pl.CostEstimate(flops=10**10, bytes_accessed=3 * 10**6, transcendentals=10**7),
        name="attn_fwd",
    )(lens, qkv)


def attn_bwd_kernel(rows, first_row, n_docs, heads, lens_ref, *refs):
    scratch = refs[4 * rows :]
    for row in range(rows):

        @pl.when(pl.program_id(0) == row)
        def _():
            attn_bwd_row(first_row + row, n_docs, heads, lens_ref, *refs[4 * row : 4 * row + 4], *scratch)


def attn_bwd_row(row, n_docs, heads, lens_ref, qkv_ref, do_ref, o_ref, lse_ref, out_ref, dq_ref, delta_ref):
    n_blk, _, length, width = qkv_ref.shape
    j = pl.program_id(1)
    ends = doc_ends(lens_ref, row, n_docs)
    masks = head_masks(heads, width)
    scale = HEAD_DIM**-0.5

    @pl.when(j == 0)
    def _():
        def one(i, _):
            prod = (do_ref[i].astype(F32) * o_ref[i]).T
            for h in range(heads):
                delta_ref[i, h : h + 1, :] = jnp.sum(
                    prod[h * HEAD_DIM : (h + 1) * HEAD_DIM], axis=0, keepdims=True
                )
            dq_ref[i] = jnp.zeros((length, width), F32)
            return 0

        lax.fori_loop(0, n_blk, one, 0)

    last = jnp.int32(n_blk * length)
    final = (j + 1) * length - 1
    for end in reversed(ends):
        last = jnp.where(end > final, end, last)
    highest = lax.div(last - 1, jnp.int32(length))
    keys, values = qkv_ref[j, 1], qkv_ref[j, 2]
    key_heads = [keys * mask for mask in masks]

    def tile(step, carry):
        first = j + 2 * step
        carry = one_tile(first, first, carry)
        return one_tile(first + 1, jnp.minimum(first + 1, n_blk - 1), carry)

    def one_tile(index, i, carry):
        d_key, d_value = carry
        start, place = start_rows(ends, index, length, heads)
        queries = by_head(qkv_ref[i, 0] * jnp.asarray(scale, BF16), masks)
        d_out = by_head(do_ref[i], masks)
        lse = jnp.concatenate([lse_ref[i, h : h + 1, :] for h in range(heads)], axis=1)
        delta = jnp.concatenate([delta_ref[i, h : h + 1, :] for h in range(heads)], axis=1)
        scores = dot_nt(keys, queries)
        key = j * length + lax.broadcasted_iota(jnp.int32, scores.shape, 0)
        probs = jnp.exp(jnp.where((key <= place) & (key >= start), scores - lse, NEG))
        d_probs = dot_nt(values, d_out)
        d_scores = (probs * (d_probs - delta)).astype(BF16)
        d_value = d_value + dot(probs.astype(BF16), d_out)
        d_key = d_key + dot(d_scores, queries)
        d_query = dq_ref[i]
        for h in range(heads):
            d_query = d_query + dot_tn(d_scores[:, h * length : (h + 1) * length], key_heads[h])
        dq_ref[i] = d_query
        return d_key, d_value

    zero = jnp.zeros((length, width), F32)
    d_key, d_value = lax.fori_loop(0, (highest - j + 2) // 2, tile, (zero, zero))
    out_ref[0, 0, 0] = (dq_ref[j] * scale).astype(BF16)
    out_ref[0, 0, 1] = d_key.astype(BF16)
    out_ref[0, 0, 2] = d_value.astype(BF16)


def attn_bwd(lens, qkv, d_out, attended, lse, first_row, n_docs):
    rows = len(qkv)
    n_blk, _, length, width = qkv[0].shape
    heads = width // HEAD_DIM
    whole = lambda a: pl.BlockSpec(a.shape, lambda r, j, lens: (0,) * a.ndim)
    arrays = [a for per_row in zip(qkv, d_out, attended, lse) for a in per_row]
    return pl.pallas_call(
        functools.partial(attn_bwd_kernel, rows, first_row, n_docs, heads),
        grid_spec=pltpu.PrefetchScalarGridSpec(
            num_scalar_prefetch=1,
            grid=(rows, n_blk),
            in_specs=[whole(a) for a in arrays],
            out_specs=pl.BlockSpec((1, 1, 3, length, width), lambda r, j, lens: (j, r, 0, 0, 0)),
            scratch_shapes=[
                pltpu.VMEM((n_blk, length, width), F32),
                pltpu.VMEM((n_blk, heads, length), F32),
            ],
        ),
        out_shape=jax.ShapeDtypeStruct((n_blk, rows, 3, length, width), BF16),
        compiler_params=pltpu.CompilerParams(vmem_limit_bytes=VMEM_LIMIT),
        cost_estimate=pl.CostEstimate(flops=4 * 10**9, bytes_accessed=12 * 10**6, transcendentals=10**7),
        name="attn_bwd",
    )(lens, *arrays)


def exchange(values):
    return lax.all_to_all(values, "blk", 0, 0, tiled=True)


def bits_of(axis):
    return lax.axis_size(axis).bit_length() - 1


def halve(current, axis, name, bit):
    size = lax.axis_size(name)
    mine = (lax.axis_index(name) >> bit) & 1
    half = current.shape[axis] // 2
    keep = lax.dynamic_slice_in_dim(current, mine * half, half, axis)
    send = lax.dynamic_slice_in_dim(current, (1 - mine) * half, half, axis)
    got = lax.ppermute(send, name, [(k, k ^ (1 << bit)) for k in range(size)])
    return (keep.astype(F32) + got.astype(F32)).astype(BF16)


def core_first(values):
    n_dp = lax.axis_size("dp")
    tokens, cols = values.shape
    return values.reshape(tokens, n_dp // 2, 2, cols // n_dp).transpose(0, 2, 1, 3).reshape(tokens, cols)


def y_first(values):
    n_blk = lax.axis_size("blk")
    tokens, cols = values.shape
    return values.reshape(tokens, n_blk // 2, 2, cols // n_blk).transpose(0, 2, 1, 3).reshape(tokens, cols)


def scatter_steps(y_early):
    dp_bits, blk_bits = bits_of("dp"), bits_of("blk")
    rest = [("dp", b) for b in reversed(range(1, dp_bits))]
    blk = [("blk", 0)] + [("blk", b) for b in reversed(range(1, blk_bits))]
    if y_early:
        return [("dp", 0)] + blk[:1] + rest + blk[1:]
    return [("dp", 0)] + rest + blk


def block_order(y_early):
    rest = [("dp", b) for b in range(1, bits_of("dp"))]
    blk = [("blk", b) for b in range(bits_of("blk"))]
    if y_early:
        return [("dp", 0)] + blk[:1] + rest + blk[1:]
    return [("dp", 0)] + rest + blk


def z_order():
    rest = [("dp", b) for b in range(1, bits_of("dp"))]
    blk = [("blk", b) for b in range(bits_of("blk"))]
    return [("dp", 0)] + blk[1:2] + rest + blk[:1] + blk[2:]


def scatter(grad, rows_name, y_early):
    n_rows = lax.axis_size(rows_name)
    rows, cols = grad.shape
    current = grad.reshape((n_rows // 2, 2, rows // n_rows, cols))
    for name, bit in scatter_steps(y_early):
        if name != rows_name:
            current = halve(current, 3, name, bit)
        elif bit == 0:
            current = halve(current, 1, name, bit)
        else:
            current = halve(current, 0, name, bit)
    return current.reshape(rows // n_rows, current.shape[3])


def total(values):
    for name in ("dp", "blk"):
        size = lax.axis_size(name)
        for bit in range(bits_of(name)):
            values = values + lax.ppermute(values, name, [(k, k ^ (1 << bit)) for k in range(size)])
    return values


def chunks_of(block_rows, block_cols):
    cols = block_cols // 128
    return 4 // cols, cols, block_rows // (4 // cols)


def place_of(order, dp, blk):
    place = 0
    for name, bit in order[1:]:
        place = 2 * place + (((dp if name == "dp" else blk) >> bit) & 1)
    return place


def blocks_dot(left_ref, right_ref, left_is_dp, side, col, order, n_dp, n_blk, row, out_ref, *at):
    size = left_ref.shape[2]
    tokens = left_ref.shape[3]
    if left_is_dp:
        left = jnp.concatenate([left_ref[2 * k + side, 0] for k in range(n_dp // 2)], axis=0)
        right = right_ref[...]
    else:
        cols = right_ref.shape[1] // n_dp
        left = left_ref[:, 0].reshape(n_blk * size, tokens)
        right = jnp.concatenate(
            [
                right_ref[:, pl.ds(pl.multiple_of((2 * k + side) * cols + col * 128, 128), 128)]
                for k in range(n_dp // 2)
            ],
            axis=1,
        )
    result = dot(left, right).astype(BF16)
    for d in range(n_dp // 2):
        for e in range(n_blk):
            k, m = (d, e) if left_is_dp else (e, d)
            out_ref[(*at, place_of(order, 2 * d, e), slice(row, row + size))] = result[
                k * size : (k + 1) * size, m * 128 : (m + 1) * 128
            ]


def ffn_wgrad_kernel(plans, n_dp, n_blk, rows, *refs):
    source = iter(refs)
    take = lambda n: [next(source) for _ in range(n)]
    n, n_terms = len(plans), sum(len(terms) for _, terms, _ in plans)
    lefts, rights, moved, outs, arrived = take(n_terms), take(n_terms), take(rows), take(2 * n), take(rows)
    sents, landed, keeps = take(n), take(n), take(n)
    send_sem, recv_sem = take(2)
    own_sem, out_sem, in_sem = take(3) if rows else (None, None, None)
    step = pl.program_id(0)
    core, device = partner("dp", 0)
    here = lax.axis_index("blk")

    def own(r):
        return pltpu.make_async_copy(moved[r].at[here], arrived[r].at[here], own_sem.at[r])

    def across(r, m):
        there = (here + m) % n_blk
        return pltpu.make_async_remote_copy(
            src_ref=moved[r].at[there],
            dst_ref=arrived[r].at[here],
            send_sem=out_sem.at[r, m],
            recv_sem=in_sem.at[r, m],
            device_id=(lax.axis_index("dp"), there),
            device_id_type=MESH,
        )

    @pl.when(step == 0)
    def _():
        barrier = pltpu.get_barrier_semaphore()
        pl.semaphore_signal(barrier, inc=1, device_id=device, device_id_type=MESH)
        for m in range(1, n_blk if rows else 1):
            there = (lax.axis_index("dp"), (here + m) % n_blk)
            pl.semaphore_signal(barrier, inc=1, device_id=there, device_id_type=MESH)
        pl.semaphore_wait(barrier, n_blk if rows else 1)
        for r in range(rows):
            own(r).start()
            for m in range(1, n_blk):
                across(r, m).start()

    def remote(n, c):
        return pltpu.make_async_remote_copy(
            src_ref=sents[n].at[c],
            dst_ref=landed[n].at[c],
            send_sem=send_sem.at[n, c],
            recv_sem=recv_sem.at[n, c],
            device_id=device,
            device_id_type=MESH,
        )

    first = 0
    for k, (order, terms, pieces) in enumerate(plans):
        c = step - first
        first += pieces

        @pl.when((c >= 0) & (c < pieces))
        def _():
            def make(side, *out):
                for at, left_is_dp, col_parts, row in terms:
                    blocks_dot(lefts[at], rights[at], left_is_dp, side, c % col_parts, order, n_dp, n_blk, row, *out)

            make(1 - core, sents[k], c)
            remote(k, c).start()
            make(core, keeps[k], c % 2)

        @pl.when((c >= 1) & (c < pieces + 1))
        def _():
            remote(k, c - 1).wait_recv()
            mine, _ = partner(*order[1])
            half = keeps[k].shape[1] // 2
            for out_ref, side in ((outs[2 * k], mine), (outs[2 * k + 1], 1 - mine)):

                def one(d, _):
                    at = side * half + d
                    out_ref[0, d] = keeps[k][(c - 1) % 2, at] + landed[k][c - 1, at]
                    return 0

                lax.fori_loop(0, half, one, 0)

    @pl.when(step == first)
    def _():
        for k in range(n):
            for c in range(plans[k][2]):
                remote(k, c).wait_send()
        for r in range(rows):
            own(r).wait()
            for m in range(1, n_blk):
                across(r, m).wait()


def ffn_wgrad(items, moved, flops, collective_id):
    n_dp, n_blk = lax.axis_size("dp"), lax.axis_size("blk")
    lefts, rights, plans, left_specs, right_specs, out_specs, outs, scratch = [], [], [], [], [], [], [], []
    held = n_dp * n_blk // 2
    steps = 0
    for order, wanted, terms in items:
        count, row, plan = len(wanted), 0, []
        for left_is_dp, left, right in terms:
            n_left, n_right = (n_dp, n_blk) if left_is_dp else (n_blk, n_dp)
            cols, tokens = left.shape
            row_parts, col_parts, size = chunks_of(cols // n_left, right.shape[1] // n_right)
            plan.append((len(lefts), left_is_dp, col_parts, row))
            row += size
            lefts.append(left.reshape(n_left, row_parts, size, tokens))
            rights.append(right)
            left_specs.append(
                pl.BlockSpec(
                    (n_left, 1, size, tokens),
                    lambda p, at=steps, low=wanted[0], count=count, col_parts=col_parts: (
                        0,
                        (low + jnp.clip(p - at, 0, count - 1)) // col_parts,
                        0,
                        0,
                    ),
                )
            )
            right_specs.append(pl.BlockSpec(right.shape, lambda p: (0, 0), pipeline_mode=pl.Buffered(1)))
        plans.append((order, plan, count))
        out_specs += [
            pl.BlockSpec(
                (1, held // 2, row, 128), lambda p, at=steps, count=count: (jnp.clip(p - 1 - at, 0, count - 1), 0, 0, 0)
            )
        ] * 2
        outs += [jax.ShapeDtypeStruct((count, held // 2, row, 128), BF16)] * 2
        scratch.append((count, held, row, 128))
        steps += count
    n = len(items)
    flat = pl.pallas_call(
        functools.partial(ffn_wgrad_kernel, plans, n_dp, n_blk, len(moved)),
        grid=(steps + 1,),
        in_specs=left_specs + right_specs + [pl.BlockSpec(memory_space=pl.ANY)] * len(moved),
        out_specs=out_specs + [pl.BlockSpec(memory_space=pl.ANY)] * len(moved),
        out_shape=outs + [jax.ShapeDtypeStruct(a.shape, a.dtype) for a in moved],
        scratch_shapes=[pltpu.VMEM(a, BF16) for a in scratch] * 2
        + [pltpu.VMEM((2,) + a[1:], BF16) for a in scratch]
        + [pltpu.SemaphoreType.DMA((n, 4))] * 2
        + ([pltpu.SemaphoreType.DMA((len(moved),))] + [pltpu.SemaphoreType.DMA((len(moved), n_blk))] * 2 if moved else []),
        compiler_params=pltpu.CompilerParams(
            collective_id=collective_id, has_side_effects=True, vmem_limit_bytes=VMEM_LIMIT
        ),
        cost_estimate=pl.CostEstimate(flops=flops, bytes_accessed=10**7, transcendentals=0),
        name="ffn_wgrad",
    )(*lefts, *rights, *moved)
    return [tuple(flat[2 * k : 2 * k + 2]) for k in range(n)], list(flat[2 * n :])


def fold_kernel(stages, *refs):
    n = len(stages)
    for k, (name, bit) in enumerate(stages):
        mine, _ = partner(name, bit)
        keep_ref, got_ref = refs[2 * k], refs[2 * k + 1]
        half = keep_ref.shape[1] // 2
        for out_ref, side in ((refs[2 * n + 2 * k], mine), (refs[2 * n + 2 * k + 1], 1 - mine)):

            def one(d, _):
                at = side * half + d
                out_ref[0, d] = keep_ref[0, at] + got_ref[0, at]
                return 0

            lax.fori_loop(0, half, one, 0)


def fold(pairs, stages, flops):
    n = len(pairs)
    arrays = [a for pair in pairs for a in pair]
    block = lambda a, parts: pl.BlockSpec((1, a.shape[1] // parts) + a.shape[2:], lambda c: (c, 0, 0, 0))
    half = lambda a: jax.ShapeDtypeStruct((a.shape[0], a.shape[1] // 2) + a.shape[2:], BF16)
    flat = pl.pallas_call(
        functools.partial(fold_kernel, stages),
        grid=(arrays[0].shape[0],),
        in_specs=[block(a, 1) for a in arrays],
        out_specs=[block(a, 2) for a in arrays],
        out_shape=[half(a) for a in arrays],
        compiler_params=pltpu.CompilerParams(vmem_limit_bytes=VMEM_LIMIT),
        cost_estimate=pl.CostEstimate(flops=flops, bytes_accessed=10**7, transcendentals=0),
        name="fold",
    )(*arrays)
    return [tuple(flat[2 * k : 2 * k + 2]) for k in range(n)]


def swap(values, name, bit):
    size = lax.axis_size(name)
    return lax.ppermute(values, name, [(k, k ^ (1 << bit)) for k in range(size)])


def partner(name, bit):
    here = {"dp": lax.axis_index("dp"), "blk": lax.axis_index("blk")}
    mine = (here[name] // (1 << bit)) % 2
    other = dict(here)
    other[name] = here[name] + (1 - 2 * mine) * (1 << bit)
    return mine, (other["dp"], other["blk"])


def ffn_kernel(gathered_ref, hidden_ref, cot_ref, gain_ref, wo_ref, wg_ref, wu_ref, wd_ref, *refs):
    out_refs, (low_ref, resid_ref, acc_ref, dmid_ref) = refs[-14:-4], refs[-4:]
    lowt_ref, mid_ref, inner_ref, dgate_ref, dup_ref, out_ref, dres_ref, dbranch_ref, dgain_ref, dattn_ref = out_refs
    n_blk, length, width = gathered_ref.shape
    step = pl.program_id(0)

    @pl.when(step == 0)
    def _():
        for s in range(n_blk):
            low_ref[:, s * width : (s + 1) * width] = gathered_ref[s]
        resid = hidden_ref[...].astype(F32) + dot(low_ref[...], wo_ref[...])
        resid_ref[...] = resid
        normed, _ = rms_parts(resid)
        mid_ref[...] = (normed * gain_ref[...]).astype(BF16)
        acc_ref[...] = jnp.zeros_like(acc_ref)
        dmid_ref[...] = jnp.zeros_like(dmid_ref)
        lowt_ref[...] = low_ref[...].T

    gate = dot(mid_ref[...], wg_ref[...])
    up = dot(mid_ref[...], wu_ref[...])
    d_inner = dot_nt(cot_ref[...], wd_ref[...])
    sigma = 1.0 / (1.0 + jnp.exp(-gate))
    act = gate * sigma
    inner = (act * up).astype(BF16)
    d_gate = (d_inner * up * (sigma * (1.0 + gate * (1.0 - sigma)))).astype(BF16)
    d_up = (d_inner * act).astype(BF16)
    inner_ref[...] = inner.T
    dgate_ref[...] = d_gate.T
    dup_ref[...] = d_up.T
    acc_ref[...] += dot(inner, wd_ref[...])
    dmid_ref[...] += dot_nt(d_gate, wg_ref[...]) + dot_nt(d_up, wu_ref[...])

    @pl.when(step == pl.num_programs(0) - 1)
    def _():
        resid = resid_ref[...]
        out_ref[...] = (resid + acc_ref[...]).astype(BF16)
        normed, inverse = rms_parts(resid)
        d_mid = dmid_ref[...]
        dgain_ref[...] = jnp.sum(d_mid * normed, axis=0, keepdims=True)
        d_resid = cot_ref[...].astype(F32) + norm_back(d_mid * gain_ref[...], normed, inverse)
        dres_ref[...] = d_resid
        d_branch = d_resid.astype(BF16)
        dbranch_ref[...] = d_branch
        back = dot_nt(d_branch, wo_ref[...]).astype(BF16)
        for s in range(n_blk):
            dattn_ref[s] = back[:, s * width : (s + 1) * width]


def feed_forward(row, before, gathered, hidden, cot, gain, w_out, w_gate, w_up, w_down):
    n_blk, length, width = gathered.shape
    tokens, model = hidden.shape
    inner = w_gate.shape[1]
    chunk = 256
    once = lambda a: pl.BlockSpec(a.shape, lambda j: (0,) * len(a.shape), pipeline_mode=pl.Buffered(1))
    whole = lambda a: pl.BlockSpec(a.shape, lambda j: (0,) * len(a.shape))
    cols = pl.BlockSpec((model, chunk), lambda j: (0, j))
    own = pl.BlockSpec((length, model), lambda j: (row, 0), pipeline_mode=pl.Buffered(1))
    mine = pl.BlockSpec((length, model), lambda j: (row, 0))
    turned = pl.BlockSpec((chunk, length), lambda j: (j, row))
    shape = jax.ShapeDtypeStruct
    shared = (
        [shape((model, tokens), BF16), shape((tokens, model), BF16)]
        + [shape((inner, tokens), BF16)] * 3
        + [shape((tokens, model), BF16), shape((tokens, model), F32), shape((tokens, model), BF16)]
    )
    outs = shared + [shape((1, model), F32), shape((n_blk, length, width), BF16)]
    before = list(before or [])
    return pl.pallas_call(
        ffn_kernel,
        grid=(inner // chunk,),
        in_specs=[once(gathered), own, own, once(gain), once(w_out)]
        + [cols, cols, pl.BlockSpec((chunk, model), lambda j: (j, 0))]
        + [pl.BlockSpec(memory_space=pl.ANY)] * len(before),
        out_specs=[pl.BlockSpec((model, length), lambda j: (0, row)), mine]
        + [turned] * 3
        + [mine] * 3
        + [whole(a) for a in outs[8:]],
        out_shape=outs,
        scratch_shapes=[pltpu.VMEM((length, model), BF16)] + [pltpu.VMEM((length, model), F32)] * 3,
        input_output_aliases={8 + k: k for k in range(len(before))},
        compiler_params=pltpu.CompilerParams(vmem_limit_bytes=VMEM_LIMIT),
        cost_estimate=pl.CostEstimate(
            flops=12 * length * model * inner + 4 * length * model * model,
            bytes_accessed=6 * model * inner + 6 * length * inner + 20 * length * model,
            transcendentals=length * inner,
        ),
        name="ffn",
    )(gathered, hidden, cot, gain, w_out, w_gate, w_up, w_down, *before)


class Halving:
    def __init__(self, order, work, sent, landed, send_sem, recv_sem):
        self.order, self.work, self.sent, self.landed = order, work, sent, landed
        self.send_sem, self.recv_sem = send_sem, recv_sem
        self.held = work.shape[1]

    def base(self, stage):
        base = 0
        for earlier in range(1, stage):
            base = base + partner(*self.order[earlier])[0] * (self.held >> earlier)
        return base

    def remote(self, stage, c):
        mine, device = partner(*self.order[stage])
        half = self.held >> stage
        if stage == 0:
            sent = self.sent.at[c]
        else:
            sent = self.work.at[c, pl.ds(self.base(stage) + (1 - mine) * half, half)]
        return pltpu.make_async_remote_copy(
            src_ref=sent,
            dst_ref=self.landed[stage].at[c],
            send_sem=self.send_sem.at[stage, c],
            recv_sem=self.recv_sem.at[stage, c],
            device_id=device,
            device_id_type=MESH,
        )

    def add(self, stage, c):
        base = self.base(stage + 1)

        def one(d, _):
            self.work[c, base + d] = self.work[c, base + d] + self.landed[stage][c, d]
            return 0

        lax.fori_loop(0, self.held >> stage, one, 0)

    def result(self, c):
        stage = len(self.order) - 1
        return self.work[c, self.base(stage + 1)].astype(F32) + self.landed[stage][c, 0].astype(F32)


def store_piece(out_ref, c, piece):
    size, cols = piece.shape[0], out_ref.shape[1] // 128
    row, col = c // cols, c % cols
    out_ref[row * size : (row + 1) * size, col * 128 : (col + 1) * 128] = piece


def tail_kernel(ffn_orders, own_order, qkv_orders, n_dp, n_blk, rows, *refs):
    source = iter(refs)
    take = lambda n: [next(source) for _ in range(n)]
    n_ffn, n_qkv = len(ffn_orders), 3
    ffn_stages, qkv_stages = len(ffn_orders[0]), len(qkv_orders[0])
    cos_ref, sin_ref, gain_ref, small_ref = take(4)
    loads = take(6 + rows)
    keeps, gots = take(n_ffn), take(n_ffn)
    own_keep, own_sent = take(2)
    ffn_outs, (own_out,), qkv_outs = take(n_ffn), take(1), take(n_qkv)
    first_ref, input_ref, total_ref = take(3)
    here = take(6 + rows)
    back_refs, (turned_ref, hidden_ref, dres_ref, *weights) = here[:rows], here[rows:]
    low_ref, acc_ref, vecs, vec_landed = take(4)
    load_sem, keep_sem, got_sem, vec_send, vec_recv = take(5)
    streams = []
    for k, order in enumerate(ffn_orders):
        work, *landed = take(1 + ffn_stages)
        streams.append(Halving(order, work, None, landed, *take(2)))
    work, *landed = take(1 + len(own_order))
    own = Halving(own_order, work, own_sent, landed, *take(2))
    (own_sem,) = take(1)
    own_copy = pltpu.make_async_copy(own_keep, own.work, own_sem)
    late = []
    for u in range(n_qkv):
        late.append([])
        for order in qkv_orders:
            work, sent, *landed = take(2 + qkv_stages)
            late[u].append(Halving(order, work, sent, landed, *take(2)))
    length, width = back_refs[0].shape[3:]
    core, _ = partner("dp", 0)
    counts = [a.shape[0] for a in keeps]

    load = [pltpu.make_async_copy(a, b, load_sem.at[k]) for k, (a, b) in enumerate(zip(loads, here))]
    keep_copy = lambda k, c: pltpu.make_async_copy(keeps[k].at[c], streams[k].work.at[c], keep_sem.at[k, c])
    got_copy = lambda k, c: pltpu.make_async_copy(gots[k].at[c], streams[k].landed[0].at[c], got_sem.at[k, c])
    for copy in load[: rows + 1]:
        copy.start()
    for c in range(max(counts)):
        for k in range(n_ffn):
            if c < counts[k]:
                keep_copy(k, c).start()
                got_copy(k, c).start()
    own_copy.start()
    for copy in load[rows + 1 :]:
        copy.start()

    everyone = qkv_orders[0]
    barrier = pltpu.get_barrier_semaphore()
    for name, bit in everyone:
        pl.semaphore_signal(barrier, inc=1, device_id=partner(name, bit)[1], device_id_type=MESH)
    pl.semaphore_wait(barrier, len(everyone))

    def ffn(c, stage):
        for k, stream in enumerate(streams):
            if c >= counts[k]:
                continue
            if stage == 1:
                keep_copy(k, c).wait()
                got_copy(k, c).wait()
            else:
                stream.remote(stage - 1, c).wait_recv()
            if stage < ffn_stages:
                stream.add(stage - 1, c)
                stream.remote(stage, c).start()
            else:
                store_piece(ffn_outs[k], c, stream.result(c))

    def projections(which):
        for r in range(rows):
            at = pl.ds(r * length, length)
            for s in range(n_blk):
                cols = slice(s * width, (s + 1) * width)
                values = back_refs[r][s, 0, which].astype(F32)
                if which < 2:
                    turned = values * cos_ref[at, :] - swap_halves(values) * sin_ref[at, :]
                else:
                    turned = 0.5 * values
                    first_ref[:, r, cols] = turned
                low_ref[which, at, cols] = turned.astype(BF16)
        for fresh in range(2):
            side = 1 - core if fresh == 0 else core
            left = jnp.concatenate([turned_ref[2 * k + side] for k in range(n_dp // 2)], axis=0)
            size, half = turned_ref.shape[1], turned_ref.shape[1] // 2
            result = dot(left, low_ref[which]).astype(BF16)
            for h, stream in enumerate(late[which]):
                out_ref = stream.sent if fresh == 0 else stream.work
                for d in range(n_dp // 2):
                    for e in range(n_blk):
                        out_ref[0, place_of(stream.order, 2 * d, e)] = result[
                            d * size + h * half : d * size + (h + 1) * half, e * width : (e + 1) * width
                        ]
                if fresh == 0:
                    stream.remote(0, 0).start()

    def own_step(stage):
        if stage == 1:
            own_copy.wait()
        for c in range(own.work.shape[0]):
            own.remote(stage - 1, c).wait_recv()
            if stage < len(own.order):
                own.add(stage - 1, c)
                own.remote(stage, c).start()
            else:
                store_piece(own_out, c, own.result(c))

    def late_step(which, stage):
        for h, stream in enumerate(late[which]):
            stream.remote(stage - 1, 0).wait_recv()
            if stage < qkv_stages:
                stream.add(stage - 1, 0)
                stream.remote(stage, 0).start()
            else:
                half = stream.work.shape[2]
                qkv_outs[which][h * half : (h + 1) * half, :] = stream.result(0)

    def vec_copy(e):
        return pltpu.make_async_remote_copy(
            src_ref=vecs.at[e],
            dst_ref=vec_landed.at[e],
            send_sem=vec_send.at[e],
            recv_sem=vec_recv.at[e],
            device_id=partner(*everyone[e])[1],
            device_id_type=MESH,
        )

    model = hidden_ref.shape[1]
    n_vec = len(everyone)

    def matmul():
        for copy in load[rows + 1 :]:
            copy.wait()
        for r in range(rows):
            at = pl.ds(r * length, length)
            acc_ref[at, :] = (
                dot_nt(low_ref[0, at, :], weights[0][...])
                + dot_nt(low_ref[1, at, :], weights[1][...])
                + dot_nt(low_ref[2, at, :], weights[2][...])
            )

    def norm():
        d_gain = jnp.zeros((1, model), F32)
        for r in range(rows):
            at = pl.ds(r * length, length)
            normed, inverse = rms_parts(hidden_ref[at, :].astype(F32))
            d_normed = acc_ref[at, :]
            d_gain = d_gain + jnp.sum(d_normed * normed, axis=0, keepdims=True)
            input_ref[:, r, :] = dres_ref[at, :] + norm_back(d_normed * gain_ref[...], normed, inverse)
        vecs[0, :, :model] = d_gain
        vecs[0, :, model:] = small_ref[...]
        vec_copy(0).start()

    def vec(e):
        vec_copy(e).wait_recv()
        summed = vecs[e] + vec_landed[e]
        if e == n_vec - 1:
            total_ref[...] = summed
        else:
            vecs[e + 1] = summed
            vec_copy(e + 1).start()

    chunks = range(max(counts))
    for c in range(own.work.shape[0]):
        own.remote(0, c).start()
    for c in chunks:
        ffn(c, 1)
    for copy in load[: rows + 1]:
        copy.wait()
    projections(2)
    projections(1)
    late_step(2, 1)
    own_step(1)
    projections(0)
    late_step(1, 1)
    ffn(0, 2)
    late_step(0, 1)
    matmul()
    own_step(2)
    late_step(2, 2)
    ffn(1, 2)
    norm()
    own_step(3)
    late_step(1, 2)
    ffn(2, 2)
    vecs_left = list(range(n_vec))
    vec(vecs_left.pop(0))
    own_step(4)
    late_step(2, 3)
    late_step(0, 2)
    ffn(3, 2)
    vec(vecs_left.pop(0))
    late_step(1, 3)
    late_step(0, 3)
    for stage in range(4, qkv_stages + 1):
        vec(vecs_left.pop(0))
        for which in (2, 1, 0):
            late_step(which, stage)
    for c in chunks:
        for stage in range(3, ffn_stages + 1):
            ffn(c, stage)
    for e in vecs_left:
        vec(e)

    for stream, count in zip(streams, counts):
        for c in range(count):
            for stage in range(1, ffn_stages):
                stream.remote(stage, c).wait_send()
    for c in range(own.work.shape[0]):
        for stage in range(len(own.order)):
            own.remote(stage, c).wait_send()
    for stream in late[0] + late[1] + late[2]:
        for stage in range(qkv_stages):
            stream.remote(stage, 0).wait_send()
    for e in range(n_vec):
        vec_copy(e).wait_send()


def tail(ffn_pairs, ffn_blocks, ffn_orders, own_pair, own_order, qkv_orders, backs, normed_t, hidden, d_resid, weights, cos, sin, gain, small, collective_id):
    n_dp, n_blk = lax.axis_size("dp"), lax.axis_size("blk")
    tokens, model = hidden.shape
    rows, length = len(backs), backs[0].shape[3]
    keeps, gots = [pair[0] for pair in ffn_pairs], [pair[1] for pair in ffn_pairs]
    loads = [*backs, normed_t.reshape(n_dp, model // n_dp, tokens), hidden, d_resid, *weights]
    ffn_stages, qkv_stages, n_qkv = len(ffn_orders[0]), len(qkv_orders[0]), 3
    n_chunks = max(a.shape[0] for a in keeps)
    block = (model // n_dp, model // n_blk)
    held = n_dp * n_blk // 2
    shape = jax.ShapeDtypeStruct
    vec = (1, model + small.shape[1])
    outs = (
        [shape(a, F32) for a in ffn_blocks]
        + [shape(block, F32)] * n_qkv
        + [shape((length, rows, model), F32)] * 2
        + [shape(vec, F32)]
    )
    scratch = [pltpu.VMEM(a.shape, a.dtype) for a in loads]
    scratch += [
        pltpu.VMEM((n_qkv, tokens, model), BF16),
        pltpu.VMEM((tokens, model), F32),
        pltpu.VMEM((qkv_stages,) + vec, F32),
        pltpu.VMEM((qkv_stages,) + vec, F32),
        pltpu.SemaphoreType.DMA((len(loads),)),
        pltpu.SemaphoreType.DMA((len(keeps), n_chunks)),
        pltpu.SemaphoreType.DMA((len(keeps), n_chunks)),
        pltpu.SemaphoreType.DMA((qkv_stages,)),
        pltpu.SemaphoreType.DMA((qkv_stages,)),
    ]
    for a in keeps:
        scratch.append(pltpu.VMEM(a.shape, BF16))
        scratch += [pltpu.VMEM((a.shape[0], a.shape[1] >> stage) + a.shape[2:], BF16) for stage in range(ffn_stages)]
        scratch += [pltpu.SemaphoreType.DMA((ffn_stages, a.shape[0]))] * 2
    part = (block[0] // len(qkv_orders), block[1])
    keep = own_pair[0]
    scratch.append(pltpu.VMEM(keep.shape, BF16))
    scratch += [pltpu.VMEM((keep.shape[0], keep.shape[1] >> stage) + keep.shape[2:], BF16) for stage in range(len(own_order))]
    scratch += [pltpu.SemaphoreType.DMA((len(own_order), keep.shape[0]))] * 2 + [pltpu.SemaphoreType.DMA]
    for _ in range(n_qkv * len(qkv_orders)):
        scratch += [pltpu.VMEM((1, held) + part, BF16)] * 2
        scratch += [pltpu.VMEM((1, held >> stage) + part, BF16) for stage in range(qkv_stages)]
        scratch += [pltpu.SemaphoreType.DMA((qkv_stages, 1))] * 2
    vmem, anywhere = pl.BlockSpec(memory_space=pltpu.VMEM), pl.BlockSpec(memory_space=pl.ANY)
    return pl.pallas_call(
        functools.partial(tail_kernel, ffn_orders, own_order, qkv_orders, n_dp, n_blk, rows),
        in_specs=[vmem] * 4 + [anywhere] * (len(loads) + 2 * len(keeps) + 2),
        out_specs=[vmem] * len(outs),
        out_shape=outs,
        scratch_shapes=scratch,
        compiler_params=pltpu.CompilerParams(
            collective_id=collective_id, has_side_effects=True, vmem_limit_bytes=60 * 2**20
        ),
        cost_estimate=pl.CostEstimate(flops=10**11, bytes_accessed=10**8, transcendentals=0),
        name="tail",
    )(cos, sin, gain, small, *loads, *keeps, *gots, *own_pair)


def turn_back_kernel(cos_ref, sin_ref, back_ref, low_ref, first_ref):
    n_blk, rows, _, length, width = back_ref.shape
    which = pl.program_id(0)
    for r in range(rows):
        at = pl.ds(r * length, length)
        for s in range(n_blk):
            cols = slice(s * width, (s + 1) * width)
            values = back_ref[s, r, 0].astype(F32)

            @pl.when(which < 2)
            def _():
                cos, sin = cos_ref[at, :width], sin_ref[at, :width]
                wide = values if width == 128 else jnp.concatenate([values, values], axis=1)
                swapped = swap_halves(wide)[:, :width]
                low_ref[0, at, cols] = (values * cos - swapped * sin).astype(BF16)

            @pl.when(which == 2)
            def _():
                first_ref[at, cols] = 0.5 * values
                low_ref[0, at, cols] = (0.5 * values).astype(BF16)


def turn_back(back, cos, sin):
    n_blk, rows, _, length, width = back.shape
    tokens, model = rows * length, n_blk * width
    full = lambda a: pl.BlockSpec(a.shape, lambda w: (0, 0))
    return pl.pallas_call(
        turn_back_kernel,
        grid=(3,),
        in_specs=[full(cos), full(sin), pl.BlockSpec((n_blk, rows, 1, length, width), lambda w: (0, 0, w, 0, 0))],
        out_specs=[
            pl.BlockSpec((1, tokens, model), lambda w: (w, 0, 0)),
            pl.BlockSpec((tokens, model), lambda w: (0, 0)),
        ],
        out_shape=[jax.ShapeDtypeStruct((3, tokens, model), BF16), jax.ShapeDtypeStruct((tokens, model), F32)],
        compiler_params=pltpu.CompilerParams(vmem_limit_bytes=VMEM_LIMIT),
        name="turn_back",
    )(cos, sin, back)


def input_grad_kernel(hidden_ref, dres_ref, gain_ref, low_ref, wq_ref, wk_ref, wv_ref, out_ref, dgain_ref):
    tokens = hidden_ref.shape[0]
    half = tokens // 2
    d_gain = jnp.zeros(dgain_ref.shape, F32)
    for r in range(2):
        at = pl.ds(r * half, half)
        d_normed = (
            dot_nt(low_ref[0, at, :], wq_ref[...])
            + dot_nt(low_ref[1, at, :], wk_ref[...])
            + dot_nt(low_ref[2, at, :], wv_ref[...])
        )
        normed, inverse = rms_parts(hidden_ref[at, :].astype(F32))
        d_gain = d_gain + jnp.sum(d_normed * normed, axis=0, keepdims=True)
        out_ref[at, :] = dres_ref[at, :] + norm_back(d_normed * gain_ref[...], normed, inverse)
    dgain_ref[...] = d_gain


def input_grad(hidden, d_resid, gain, low, w_query, w_key, w_value):
    tokens, model = hidden.shape
    return pl.pallas_call(
        input_grad_kernel,
        out_shape=[jax.ShapeDtypeStruct((tokens, model), F32), jax.ShapeDtypeStruct((1, model), F32)],
        compiler_params=pltpu.CompilerParams(vmem_limit_bytes=VMEM_LIMIT),
        cost_estimate=pl.CostEstimate(
            flops=6 * tokens * model * model, bytes_accessed=6 * model * model + 16 * tokens * model, transcendentals=0
        ),
        name="input_grad",
    )(hidden, d_resid, gain, low, w_query, w_key, w_value)


def rms_parts(values):
    inverse_rms = lax.rsqrt(jnp.mean(values * values, axis=-1, keepdims=True) + EPS)
    return values * inverse_rms, inverse_rms


def norm_back(d_normed, normed, inverse_rms):
    return inverse_rms * (d_normed - normed * jnp.mean(d_normed * normed, axis=-1, keepdims=True))


def rope_tables(doc_lengths, offset, length):
    half = HEAD_DIM // 2
    places = offset + jnp.arange(length, dtype=jnp.int32)
    ends = jnp.cumsum(doc_lengths, axis=1)
    start = jnp.max(jnp.where(ends[:, None, :] <= places[None, :, None], ends[:, None, :], 0), axis=2)
    position = (places[None, :] - start).astype(F32).reshape(-1, 1)
    lane = jnp.arange(128, dtype=jnp.int32)
    freq = jnp.power(10000.0, -(lane % half).astype(F32) * 2.0 / HEAD_DIM)
    angles = position * freq[None, :]
    sign = jnp.where(lane % HEAD_DIM < half, -1.0, 1.0)
    return jnp.cos(angles), jnp.sin(angles) * sign[None, :]


def body(
    hidden_in,
    first_values,
    doc_lengths,
    w_query,
    w_key,
    w_value,
    w_out,
    w_gate,
    w_up,
    w_down,
    attn_gain,
    ffn_gain,
    out_cotangent,
):
    length, rows, model = hidden_in.shape
    n_docs = doc_lengths.shape[1]
    n_blk, n_dp = lax.axis_size("blk"), lax.axis_size("dp")
    width = model // n_blk
    tokens = rows * length
    flat = lambda a: jnp.transpose(a, (1, 0, 2)).reshape(tokens, model)
    unflat = lambda a: jnp.transpose(a.reshape(rows, length, model), (1, 0, 2))
    lens = doc_lengths.reshape(-1)

    hidden, cot, first = flat(hidden_in), flat(out_cotangent), flat(first_values)
    row_gain = lambda gain: gain.reshape(1, model)

    cos, sin = rope_tables(doc_lengths, lax.axis_index("blk") * length, length)
    *qkv_own, normed_in, sums = project_qkv(
        hidden, first, cos, sin, row_gain(attn_gain), w_query, w_key, w_value, rows, n_blk
    )
    qkv, attended, lse, gathered = [], [], [], []
    for r in range(rows):
        qkv.append(exchange(qkv_own[r]))
    for r in range(rows):
        o_f, o_low, lse_r = attn_fwd(lens, qkv[r], r, n_docs)
        attended.append(o_f)
        lse.append(lse_r)
        gathered.append(exchange(o_low))
    shared, d_gains, d_attn = None, [], []
    for r in range(rows):
        *shared, d_gain, d_attn_r = feed_forward(
            r, shared, gathered[r], hidden, cot, row_gain(ffn_gain), w_out, w_gate, w_up, w_down
        )
        d_gains.append(d_gain)
        d_attn.append(d_attn_r)
    attn_low_t, normed_mid, inner_t, d_gate_t, d_up_t, block_out, d_resid_mid, d_branch = shared
    d_gain_two = sum(d_gains)

    inner = w_gate.shape[1]
    by_blocks = (model // n_dp) % 128 == 0 and width == 128 and (inner // n_blk) % 32 == 0
    early, late, middle = block_order(False), block_order(True), z_order()
    if by_blocks:
        orders = (early, late, middle)
        pieces = (0, 1, 2, 3)
        exchanged = lambda pairs, stages: [(keep, swap(sent, *stage)) for (keep, sent), stage in zip(pairs, stages)]
        folded, d_own = ffn_wgrad(
            (
                (early, pieces, [(False, d_gate_t, normed_mid)]),
                (late, pieces, [(False, d_up_t, normed_mid)]),
                (middle, pieces, [(True, inner_t, cot)]),
            ),
            d_attn,
            10**9,
            1,
        )
        ffn_pairs = exchanged(folded, [order[1] for order in orders])
        back_own = [
            attn_bwd(lens, qkv[r : r + 1], d_own[r : r + 1], attended[r : r + 1], lse[r : r + 1], r, n_docs)
            for r in range(rows)
        ]
        backs = [exchange(b) for b in back_own[:-1]]
        kept = [keep for keep, got in ffn_pairs]
        token, kept = lax.optimization_barrier((back_own, kept))
        second = [order[2] for order in orders]
        folded = fold([(keep, got) for keep, (_, got) in zip(kept, ffn_pairs)], second, 10**9)
        ffn_pairs = exchanged(folded, second)
        folded, attn_low_t = lax.optimization_barrier((folded, attn_low_t))
        ffn_pairs = [(keep, got) for (keep, _), (_, got) in zip(folded, ffn_pairs)]
        project, back_last = ffn_wgrad(
            ((early, pieces, [(True, attn_low_t, d_branch)]),), back_own[-1:], LAST_FLOPS, 2
        )
        backs += back_last
    else:
        d_own = [exchange(d_attn[r]) for r in range(rows)]
        back = exchange(attn_bwd(lens, qkv, d_own, attended, lse, 0, n_docs))

    squares = jnp.sum(sums, axis=(0, 2)).reshape(1, 2)
    small = jnp.concatenate([d_gain_two, squares, jnp.zeros((1, 126), F32)], axis=1)
    if by_blocks:
        *blocks, grad_first, grad_input, small = tail(
            ffn_pairs,
            ((inner // n_blk, model // n_dp),) * 2 + ((inner // n_dp, model // n_blk), (model // n_dp, model // n_blk)),
            tuple(order[2:] for order in orders),
            project[0],
            early[1:],
            (early, late),
            backs,
            normed_in.T,
            hidden,
            d_resid_mid,
            (w_query, w_key, w_value),
            cos,
            sin,
            row_gain(attn_gain),
            small,
            0,
        )
        small = small.reshape(-1)
        grad_gate, grad_up = blocks[0].T, blocks[1].T
        grad_down, grad_project = blocks[2:4]
        grad_query, grad_key, grad_value = blocks[4:]
    else:
        low, grad_first = turn_back(back, cos, sin)
        mid_cf, in_cf = core_first(normed_mid), core_first(normed_in)
        sent = lambda a, b, name, y: scatter(dot_tn(a, b).astype(BF16), name, y).astype(F32)
        grad_down = sent(inner_t.T, y_first(cot), "dp", False)
        grad_gate = sent(d_gate_t.T, mid_cf, "blk", False).T
        grad_up = sent(d_up_t.T, mid_cf, "blk", True).T
        grad_project = sent(d_branch, core_first(attn_low_t.T), "blk", True).T
        grad_query, grad_key, grad_value = [sent(low[k], in_cf, "blk", True).T for k in range(3)]
        grad_first = unflat(grad_first)
        grad_input, d_gain_one = input_grad(hidden, d_resid_mid, row_gain(attn_gain), low, w_query, w_key, w_value)
        grad_input = unflat(grad_input)
        small = total(jnp.concatenate([d_gain_one.reshape(model), small.reshape(-1)]))
    n_entries = n_blk * length * rows * n_dp * model
    return (
        unflat(block_out),
        grad_input,
        grad_first,
        grad_query,
        grad_key,
        grad_value,
        grad_project,
        grad_gate,
        grad_up,
        grad_down,
        small[:model],
        small[model : 2 * model],
        small[2 * model] / n_entries,
        small[2 * model + 1] / n_entries,
    )


def solution(mesh):
    tokens = P("blk", "dp", None)
    return jax.shard_map(
        body,
        mesh=mesh,
        in_specs=(tokens, tokens, P("dp", None)) + (P(),) * 9 + (tokens,),
        out_specs=(tokens,) * 3 + (P("dp", "blk"),) * 7 + (P(),) * 4,
        check_vma=False,
    )
```

```python
import functools

import jax
import jax.numpy as jnp
from jax import lax
from jax.experimental import pallas as pl
from jax.experimental.pallas import tpu as pltpu
from jax.sharding import PartitionSpec as P

HEADS = 16
HEAD_DIM = 64
NEG = -1e30
EPS = 1e-06
F32 = jnp.float32
BF16 = jnp.bfloat16
VMEM_LIMIT = 56 * 2**20
LAST_FLOPS = 6 * 10**10
MESH = pl.DeviceIdType.MESH


def dot(a, b):
    return jnp.dot(a, b, preferred_element_type=F32)


def dot_nt(a, b):
    return lax.dot_general(a, b, (((1,), (1,)), ((), ())), preferred_element_type=F32)


def dot_tn(a, b):
    return lax.dot_general(a, b, (((0,), (0,)), ((), ())), preferred_element_type=F32)


def swap_halves(v):
    half = HEAD_DIM // 2
    width = v.shape[-1]
    lane = lax.broadcasted_iota(jnp.int32, v.shape, v.ndim - 1)
    left = pltpu.roll(v, width - half, v.ndim - 1)
    right = pltpu.roll(v, half, v.ndim - 1)
    return jnp.where(lane % HEAD_DIM < half, left, right)


def qkv_kernel(rows, length, width, hidden_ref, first_ref, cos_ref, sin_ref, gain_ref, wq_ref, wk_ref, wv_ref, *outs):
    out_refs, (normed_ref, sums_ref) = outs[:rows], outs[rows:]
    chunk = wq_ref.shape[1]

    @pl.when(pl.program_id(0) == 0)
    def _():
        for r in range(rows):
            at = pl.ds(r * length, length)
            normed, _ = rms_parts(hidden_ref[at, :].astype(F32))
            normed_ref[at, :] = (normed * gain_ref[...]).astype(BF16)

    first_sum = jnp.zeros((1, chunk), F32)
    mixed_sum = jnp.zeros((1, chunk), F32)
    raws = [dot(normed_ref[...], w_ref[...]) for w_ref in (wq_ref, wk_ref, wv_ref)]
    for r in range(rows):
        at = pl.ds(r * length, length)
        own = slice(r * length, (r + 1) * length)
        cos, sin = cos_ref[at, :], sin_ref[at, :]
        for which in range(2):
            raw = raws[which][own]
            for c in range(chunk // 128):
                part = raw[:, c * 128 : (c + 1) * 128]
                turned = (part * cos + swap_halves(part) * sin).astype(BF16)
                for s in range(128 // width):
                    out_refs[r][c * (128 // width) + s, which] = turned[:, s * width : (s + 1) * width]
        first = first_ref[at, :].astype(F32)
        mixed = 0.5 * raws[2][own] + 0.5 * first
        first_sum = first_sum + jnp.sum(first * first, axis=0, keepdims=True)
        mixed_sum = mixed_sum + jnp.sum(mixed * mixed, axis=0, keepdims=True)
        low = mixed.astype(BF16)
        for s in range(chunk // width):
            out_refs[r][s, 2] = low[:, s * width : (s + 1) * width]
    sums_ref[0, 0:1] = first_sum
    sums_ref[0, 1:2] = mixed_sum


def project_qkv(hidden, first, cos, sin, gain, w_query, w_key, w_value, rows, n_blk):
    tokens, model = hidden.shape
    length, width = tokens // rows, model // n_blk
    chunk = 256
    steps = model // chunk
    full = lambda rows, cols: pl.BlockSpec((rows, cols), lambda j: (0, 0))
    weight = pl.BlockSpec((model, chunk), lambda j: (0, j))
    return pl.pallas_call(
        functools.partial(qkv_kernel, rows, length, width),
        grid=(steps,),
        in_specs=[
            full(tokens, model),
            pl.BlockSpec((tokens, chunk), lambda j: (0, j)),
            full(tokens, 128),
            full(tokens, 128),
            full(1, model),
            weight,
            weight,
            weight,
        ],
        out_specs=[pl.BlockSpec((chunk // width, 3, length, width), lambda j: (j, 0, 0, 0))] * rows
        + [full(tokens, model), pl.BlockSpec((1, 2, chunk), lambda j: (j, 0, 0))],
        out_shape=[jax.ShapeDtypeStruct((n_blk, 3, length, width), BF16)] * rows
        + [jax.ShapeDtypeStruct((tokens, model), BF16), jax.ShapeDtypeStruct((steps, 2, chunk), F32)],
        compiler_params=pltpu.CompilerParams(vmem_limit_bytes=VMEM_LIMIT),
        cost_estimate=pl.CostEstimate(
            flops=6 * tokens * model * model, bytes_accessed=6 * model * model + 10 * tokens * model, transcendentals=0
        ),
        name="qkv",
    )(hidden, first, cos, sin, gain, w_query, w_key, w_value)


def doc_ends(lens_ref, row, n_docs):
    ends, total = [], jnp.int32(0)
    for d in range(n_docs):
        total = total + lens_ref[row * n_docs + d]
        ends.append(total)
    return ends


def start_rows(ends, tile, length, heads):
    place = tile * length + lax.broadcasted_iota(jnp.int32, (1, length), 1)
    start = jnp.zeros((1, length), jnp.int32)
    for end in ends:
        start = jnp.where(end <= place, end, start)
    return jnp.concatenate([start] * heads, axis=1), jnp.concatenate([place] * heads, axis=1)


def head_masks(heads, width):
    lane = lax.broadcasted_iota(jnp.int32, (1, width), 1) // HEAD_DIM
    return [jnp.where(lane == h, 1.0, 0.0).astype(BF16) for h in range(heads)]


def by_head(values, masks):
    return jnp.concatenate([values * mask for mask in masks], axis=0)


def attn_fwd_kernel(row, n_docs, heads, lens_ref, qkv_ref, o_ref, low_ref, lse_ref, acc_ref):
    length, width = qkv_ref.shape[2:]
    i = pl.program_id(0)
    ends = doc_ends(lens_ref, row, n_docs)
    start, place = start_rows(ends, i, length, heads)
    lowest = jnp.int32(0)
    for end in ends:
        lowest = jnp.where(end <= i * length, end, lowest)
    lowest = lax.div(lowest, jnp.int32(length))
    masks = head_masks(heads, width)
    queries = by_head(qkv_ref[i, 0] * jnp.asarray(HEAD_DIM**-0.5, BF16), masks)

    def pair(step, carry):
        run_max, run_sum = carry
        tiles = [i - 2 * step, i - 2 * step - 1]
        at = [tiles[0], jnp.maximum(tiles[1], 0)]
        scores = []
        for j, source in zip(tiles, at):
            raw = dot_nt(qkv_ref[source, 1], queries)
            key = j * length + lax.broadcasted_iota(jnp.int32, raw.shape, 0)
            scores.append(jnp.where((key <= place) & (key >= start), raw, NEG))
        highest = jnp.max(jnp.maximum(scores[0], scores[1]), axis=0, keepdims=True)
        new_max = jnp.maximum(run_max, highest)
        weights = [jnp.exp(one - new_max) for one in scores]
        factor = jnp.exp(run_max - new_max)
        run_sum = run_sum * factor + jnp.sum(weights[0] + weights[1], axis=0, keepdims=True)
        added = dot_tn(qkv_ref[at[0], 2], weights[0].astype(BF16)) + dot_tn(qkv_ref[at[1], 2], weights[1].astype(BF16))
        acc_ref[...] = acc_ref[...] * factor + added
        return new_max, run_sum

    acc_ref[...] = jnp.zeros_like(acc_ref)
    run_max, run_sum = lax.fori_loop(
        0,
        (i - lowest + 2) // 2,
        pair,
        (jnp.full((1, heads * length), NEG, F32), jnp.zeros((1, heads * length), F32)),
    )
    result = acc_ref[...] / run_sum
    joined = jnp.concatenate(
        [
            result[h * HEAD_DIM : (h + 1) * HEAD_DIM, h * length : (h + 1) * length]
            for h in range(heads)
        ],
        axis=0,
    )
    attended = joined.T
    o_ref[0] = attended
    low_ref[0] = attended.astype(BF16)
    total = run_max + jnp.log(run_sum)
    for h in range(heads):
        lse_ref[0, h : h + 1, :] = total[:, h * length : (h + 1) * length]


def attn_fwd(lens, qkv, row, n_docs):
    n_blk, _, length, width = qkv.shape
    heads = width // HEAD_DIM
    tile = pl.BlockSpec((1, length, width), lambda i, lens: (i, 0, 0))
    return pl.pallas_call(
        functools.partial(attn_fwd_kernel, row, n_docs, heads),
        grid_spec=pltpu.PrefetchScalarGridSpec(
            num_scalar_prefetch=1,
            grid=(n_blk,),
            in_specs=[pl.BlockSpec(qkv.shape, lambda i, lens: (0, 0, 0, 0))],
            out_specs=[tile, tile, pl.BlockSpec((1, heads, length), lambda i, lens: (i, 0, 0))],
            scratch_shapes=[pltpu.VMEM((width, heads * length), F32)],
        ),
        out_shape=[
            jax.ShapeDtypeStruct((n_blk, length, width), F32),
            jax.ShapeDtypeStruct((n_blk, length, width), BF16),
            jax.ShapeDtypeStruct((n_blk, heads, length), F32),
        ],
        compiler_params=pltpu.CompilerParams(vmem_limit_bytes=VMEM_LIMIT),
        cost_estimate=pl.CostEstimate(flops=10**10, bytes_accessed=3 * 10**6, transcendentals=10**7),
        name="attn_fwd",
    )(lens, qkv)


def attn_bwd_kernel(rows, first_row, n_docs, heads, lens_ref, *refs):
    scratch = refs[4 * rows :]
    for row in range(rows):

        @pl.when(pl.program_id(0) == row)
        def _():
            attn_bwd_row(first_row + row, n_docs, heads, lens_ref, *refs[4 * row : 4 * row + 4], *scratch)


def attn_bwd_row(row, n_docs, heads, lens_ref, qkv_ref, do_ref, o_ref, lse_ref, out_ref, dq_ref, delta_ref):
    n_blk, _, length, width = qkv_ref.shape
    j = pl.program_id(1)
    ends = doc_ends(lens_ref, row, n_docs)
    masks = head_masks(heads, width)
    scale = HEAD_DIM**-0.5

    @pl.when(j == 0)
    def _():
        def one(i, _):
            prod = (do_ref[i].astype(F32) * o_ref[i]).T
            for h in range(heads):
                delta_ref[i, h : h + 1, :] = jnp.sum(
                    prod[h * HEAD_DIM : (h + 1) * HEAD_DIM], axis=0, keepdims=True
                )
            dq_ref[i] = jnp.zeros((length, width), F32)
            return 0

        lax.fori_loop(0, n_blk, one, 0)

    last = jnp.int32(n_blk * length)
    final = (j + 1) * length - 1
    for end in reversed(ends):
        last = jnp.where(end > final, end, last)
    highest = lax.div(last - 1, jnp.int32(length))
    keys, values = qkv_ref[j, 1], qkv_ref[j, 2]
    key_heads = [keys * mask for mask in masks]

    def tile(step, carry):
        first = j + 2 * step
        carry = one_tile(first, first, carry)
        return one_tile(first + 1, jnp.minimum(first + 1, n_blk - 1), carry)

    def one_tile(index, i, carry):
        d_key, d_value = carry
        start, place = start_rows(ends, index, length, heads)
        queries = by_head(qkv_ref[i, 0] * jnp.asarray(scale, BF16), masks)
        d_out = by_head(do_ref[i], masks)
        lse = jnp.concatenate([lse_ref[i, h : h + 1, :] for h in range(heads)], axis=1)
        delta = jnp.concatenate([delta_ref[i, h : h + 1, :] for h in range(heads)], axis=1)
        scores = dot_nt(keys, queries)
        key = j * length + lax.broadcasted_iota(jnp.int32, scores.shape, 0)
        probs = jnp.exp(jnp.where((key <= place) & (key >= start), scores - lse, NEG))
        d_probs = dot_nt(values, d_out)
        d_scores = (probs * (d_probs - delta)).astype(BF16)
        d_value = d_value + dot(probs.astype(BF16), d_out)
        d_key = d_key + dot(d_scores, queries)
        d_query = dq_ref[i]
        for h in range(heads):
            d_query = d_query + dot_tn(d_scores[:, h * length : (h + 1) * length], key_heads[h])
        dq_ref[i] = d_query
        return d_key, d_value

    zero = jnp.zeros((length, width), F32)
    d_key, d_value = lax.fori_loop(0, (highest - j + 2) // 2, tile, (zero, zero))
    out_ref[0, 0, 0] = (dq_ref[j] * scale).astype(BF16)
    out_ref[0, 0, 1] = d_key.astype(BF16)
    out_ref[0, 0, 2] = d_value.astype(BF16)


def attn_bwd(lens, qkv, d_out, attended, lse, first_row, n_docs):
    rows = len(qkv)
    n_blk, _, length, width = qkv[0].shape
    heads = width // HEAD_DIM
    whole = lambda a: pl.BlockSpec(a.shape, lambda r, j, lens: (0,) * a.ndim)
    arrays = [a for per_row in zip(qkv, d_out, attended, lse) for a in per_row]
    return pl.pallas_call(
        functools.partial(attn_bwd_kernel, rows, first_row, n_docs, heads),
        grid_spec=pltpu.PrefetchScalarGridSpec(
            num_scalar_prefetch=1,
            grid=(rows, n_blk),
            in_specs=[whole(a) for a in arrays],
            out_specs=pl.BlockSpec((1, 1, 3, length, width), lambda r, j, lens: (j, r, 0, 0, 0)),
            scratch_shapes=[
                pltpu.VMEM((n_blk, length, width), F32),
                pltpu.VMEM((n_blk, heads, length), F32),
            ],
        ),
        out_shape=jax.ShapeDtypeStruct((n_blk, rows, 3, length, width), BF16),
        compiler_params=pltpu.CompilerParams(vmem_limit_bytes=VMEM_LIMIT),
        cost_estimate=pl.CostEstimate(flops=4 * 10**9, bytes_accessed=12 * 10**6, transcendentals=10**7),
        name="attn_bwd",
    )(lens, *arrays)


def exchange(values):
    return lax.all_to_all(values, "blk", 0, 0, tiled=True)


def bits_of(axis):
    return lax.axis_size(axis).bit_length() - 1


def halve(current, axis, name, bit):
    size = lax.axis_size(name)
    mine = (lax.axis_index(name) >> bit) & 1
    half = current.shape[axis] // 2
    keep = lax.dynamic_slice_in_dim(current, mine * half, half, axis)
    send = lax.dynamic_slice_in_dim(current, (1 - mine) * half, half, axis)
    got = lax.ppermute(send, name, [(k, k ^ (1 << bit)) for k in range(size)])
    return (keep.astype(F32) + got.astype(F32)).astype(BF16)


def core_first(values):
    n_dp = lax.axis_size("dp")
    tokens, cols = values.shape
    return values.reshape(tokens, n_dp // 2, 2, cols // n_dp).transpose(0, 2, 1, 3).reshape(tokens, cols)


def y_first(values):
    n_blk = lax.axis_size("blk")
    tokens, cols = values.shape
    return values.reshape(tokens, n_blk // 2, 2, cols // n_blk).transpose(0, 2, 1, 3).reshape(tokens, cols)


def scatter_steps(y_early):
    dp_bits, blk_bits = bits_of("dp"), bits_of("blk")
    rest = [("dp", b) for b in reversed(range(1, dp_bits))]
    blk = [("blk", 0)] + [("blk", b) for b in reversed(range(1, blk_bits))]
    if y_early:
        return [("dp", 0)] + blk[:1] + rest + blk[1:]
    return [("dp", 0)] + rest + blk


def block_order(y_early):
    rest = [("dp", b) for b in range(1, bits_of("dp"))]
    blk = [("blk", b) for b in range(bits_of("blk"))]
    if y_early:
        return [("dp", 0)] + blk[:1] + rest + blk[1:]
    return [("dp", 0)] + rest + blk


def z_order():
    rest = [("dp", b) for b in range(1, bits_of("dp"))]
    blk = [("blk", b) for b in range(bits_of("blk"))]
    return [("dp", 0)] + blk[1:2] + rest + blk[:1] + blk[2:]


def scatter(grad, rows_name, y_early):
    n_rows = lax.axis_size(rows_name)
    rows, cols = grad.shape
    current = grad.reshape((n_rows // 2, 2, rows // n_rows, cols))
    for name, bit in scatter_steps(y_early):
        if name != rows_name:
            current = halve(current, 3, name, bit)
        elif bit == 0:
            current = halve(current, 1, name, bit)
        else:
            current = halve(current, 0, name, bit)
    return current.reshape(rows // n_rows, current.shape[3])


def total(values):
    for name in ("dp", "blk"):
        size = lax.axis_size(name)
        for bit in range(bits_of(name)):
            values = values + lax.ppermute(values, name, [(k, k ^ (1 << bit)) for k in range(size)])
    return values


def chunks_of(block_rows, block_cols):
    cols = block_cols // 128
    return 4 // cols, cols, block_rows // (4 // cols)


def place_of(order, dp, blk):
    place = 0
    for name, bit in order[1:]:
        place = 2 * place + (((dp if name == "dp" else blk) >> bit) & 1)
    return place


def blocks_dot(left_ref, right_ref, left_is_dp, side, col, order, n_dp, n_blk, row, out_ref, *at):
    size = left_ref.shape[2]
    tokens = left_ref.shape[3]
    if left_is_dp:
        left = jnp.concatenate([left_ref[2 * k + side, 0] for k in range(n_dp // 2)], axis=0)
        right = right_ref[...]
    else:
        cols = right_ref.shape[1] // n_dp
        left = left_ref[:, 0].reshape(n_blk * size, tokens)
        right = jnp.concatenate(
            [
                right_ref[:, pl.ds(pl.multiple_of((2 * k + side) * cols + col * 128, 128), 128)]
                for k in range(n_dp // 2)
            ],
            axis=1,
        )
    result = dot(left, right).astype(BF16)
    for d in range(n_dp // 2):
        for e in range(n_blk):
            k, m = (d, e) if left_is_dp else (e, d)
            out_ref[(*at, place_of(order, 2 * d, e), slice(row, row + size))] = result[
                k * size : (k + 1) * size, m * 128 : (m + 1) * 128
            ]


def ffn_wgrad_kernel(plans, n_dp, n_blk, rows, *refs):
    source = iter(refs)
    take = lambda n: [next(source) for _ in range(n)]
    n, n_terms = len(plans), sum(len(terms) for _, terms, _ in plans)
    lefts, rights, moved, outs, arrived = take(n_terms), take(n_terms), take(rows), take(2 * n), take(rows)
    sents, landed, keeps = take(n), take(n), take(n)
    send_sem, recv_sem = take(2)
    own_sem, out_sem, in_sem = take(3) if rows else (None, None, None)
    step = pl.program_id(0)
    core, device = partner("dp", 0)
    here = lax.axis_index("blk")

    def own(r):
        return pltpu.make_async_copy(moved[r].at[here], arrived[r].at[here], own_sem.at[r])

    def across(r, m):
        there = (here + m) % n_blk
        return pltpu.make_async_remote_copy(
            src_ref=moved[r].at[there],
            dst_ref=arrived[r].at[here],
            send_sem=out_sem.at[r, m],
            recv_sem=in_sem.at[r, m],
            device_id=(lax.axis_index("dp"), there),
            device_id_type=MESH,
        )

    @pl.when(step == 0)
    def _():
        barrier = pltpu.get_barrier_semaphore()
        pl.semaphore_signal(barrier, inc=1, device_id=device, device_id_type=MESH)
        for m in range(1, n_blk if rows else 1):
            there = (lax.axis_index("dp"), (here + m) % n_blk)
            pl.semaphore_signal(barrier, inc=1, device_id=there, device_id_type=MESH)
        pl.semaphore_wait(barrier, n_blk if rows else 1)
        for r in range(rows):
            own(r).start()
            for m in range(1, n_blk):
                across(r, m).start()

    def remote(n, c):
        return pltpu.make_async_remote_copy(
            src_ref=sents[n].at[c],
            dst_ref=landed[n].at[c],
            send_sem=send_sem.at[n, c],
            recv_sem=recv_sem.at[n, c],
            device_id=device,
            device_id_type=MESH,
        )

    first = 0
    for k, (order, terms, pieces) in enumerate(plans):
        c = step - first
        first += pieces

        @pl.when((c >= 0) & (c < pieces))
        def _():
            def make(side, *out):
                for at, left_is_dp, col_parts, row in terms:
                    blocks_dot(lefts[at], rights[at], left_is_dp, side, c % col_parts, order, n_dp, n_blk, row, *out)

            make(1 - core, sents[k], c)
            remote(k, c).start()
            make(core, keeps[k], c % 2)

        @pl.when((c >= 1) & (c < pieces + 1))
        def _():
            remote(k, c - 1).wait_recv()
            mine, _ = partner(*order[1])
            half = keeps[k].shape[1] // 2
            for out_ref, side in ((outs[2 * k], mine), (outs[2 * k + 1], 1 - mine)):

                def one(d, _):
                    at = side * half + d
                    out_ref[0, d] = keeps[k][(c - 1) % 2, at] + landed[k][c - 1, at]
                    return 0

                lax.fori_loop(0, half, one, 0)

    @pl.when(step == first)
    def _():
        for k in range(n):
            for c in range(plans[k][2]):
                remote(k, c).wait_send()
        for r in range(rows):
            own(r).wait()
            for m in range(1, n_blk):
                across(r, m).wait()


def ffn_wgrad(items, moved, flops, collective_id):
    n_dp, n_blk = lax.axis_size("dp"), lax.axis_size("blk")
    lefts, rights, plans, left_specs, right_specs, out_specs, outs, scratch = [], [], [], [], [], [], [], []
    held = n_dp * n_blk // 2
    steps = 0
    for order, wanted, terms in items:
        count, row, plan = len(wanted), 0, []
        for left_is_dp, left, right in terms:
            n_left, n_right = (n_dp, n_blk) if left_is_dp else (n_blk, n_dp)
            cols, tokens = left.shape
            row_parts, col_parts, size = chunks_of(cols // n_left, right.shape[1] // n_right)
            plan.append((len(lefts), left_is_dp, col_parts, row))
            row += size
            lefts.append(left.reshape(n_left, row_parts, size, tokens))
            rights.append(right)
            left_specs.append(
                pl.BlockSpec(
                    (n_left, 1, size, tokens),
                    lambda p, at=steps, low=wanted[0], count=count, col_parts=col_parts: (
                        0,
                        (low + jnp.clip(p - at, 0, count - 1)) // col_parts,
                        0,
                        0,
                    ),
                )
            )
            right_specs.append(pl.BlockSpec(right.shape, lambda p: (0, 0), pipeline_mode=pl.Buffered(1)))
        plans.append((order, plan, count))
        out_specs += [
            pl.BlockSpec(
                (1, held // 2, row, 128), lambda p, at=steps, count=count: (jnp.clip(p - 1 - at, 0, count - 1), 0, 0, 0)
            )
        ] * 2
        outs += [jax.ShapeDtypeStruct((count, held // 2, row, 128), BF16)] * 2
        scratch.append((count, held, row, 128))
        steps += count
    n = len(items)
    flat = pl.pallas_call(
        functools.partial(ffn_wgrad_kernel, plans, n_dp, n_blk, len(moved)),
        grid=(steps + 1,),
        in_specs=left_specs + right_specs + [pl.BlockSpec(memory_space=pl.ANY)] * len(moved),
        out_specs=out_specs + [pl.BlockSpec(memory_space=pl.ANY)] * len(moved),
        out_shape=outs + [jax.ShapeDtypeStruct(a.shape, a.dtype) for a in moved],
        scratch_shapes=[pltpu.VMEM(a, BF16) for a in scratch] * 2
        + [pltpu.VMEM((2,) + a[1:], BF16) for a in scratch]
        + [pltpu.SemaphoreType.DMA((n, 4))] * 2
        + ([pltpu.SemaphoreType.DMA((len(moved),))] + [pltpu.SemaphoreType.DMA((len(moved), n_blk))] * 2 if moved else []),
        compiler_params=pltpu.CompilerParams(
            collective_id=collective_id, has_side_effects=True, vmem_limit_bytes=VMEM_LIMIT
        ),
        cost_estimate=pl.CostEstimate(flops=flops, bytes_accessed=10**7, transcendentals=0),
        name="ffn_wgrad",
    )(*lefts, *rights, *moved)
    return [tuple(flat[2 * k : 2 * k + 2]) for k in range(n)], list(flat[2 * n :])


def fold_kernel(stages, *refs):
    n = len(stages)
    for k, (name, bit) in enumerate(stages):
        mine, _ = partner(name, bit)
        keep_ref, got_ref = refs[2 * k], refs[2 * k + 1]
        half = keep_ref.shape[1] // 2
        for out_ref, side in ((refs[2 * n + 2 * k], mine), (refs[2 * n + 2 * k + 1], 1 - mine)):

            def one(d, _):
                at = side * half + d
                out_ref[0, d] = keep_ref[0, at] + got_ref[0, at]
                return 0

            lax.fori_loop(0, half, one, 0)


def fold(pairs, stages, flops):
    n = len(pairs)
    arrays = [a for pair in pairs for a in pair]
    block = lambda a, parts: pl.BlockSpec((1, a.shape[1] // parts) + a.shape[2:], lambda c: (c, 0, 0, 0))
    half = lambda a: jax.ShapeDtypeStruct((a.shape[0], a.shape[1] // 2) + a.shape[2:], BF16)
    flat = pl.pallas_call(
        functools.partial(fold_kernel, stages),
        grid=(arrays[0].shape[0],),
        in_specs=[block(a, 1) for a in arrays],
        out_specs=[block(a, 2) for a in arrays],
        out_shape=[half(a) for a in arrays],
        compiler_params=pltpu.CompilerParams(vmem_limit_bytes=VMEM_LIMIT),
        cost_estimate=pl.CostEstimate(flops=flops, bytes_accessed=10**7, transcendentals=0),
        name="fold",
    )(*arrays)
    return [tuple(flat[2 * k : 2 * k + 2]) for k in range(n)]


def swap(values, name, bit):
    size = lax.axis_size(name)
    return lax.ppermute(values, name, [(k, k ^ (1 << bit)) for k in range(size)])


def partner(name, bit):
    here = {"dp": lax.axis_index("dp"), "blk": lax.axis_index("blk")}
    mine = (here[name] // (1 << bit)) % 2
    other = dict(here)
    other[name] = here[name] + (1 - 2 * mine) * (1 << bit)
    return mine, (other["dp"], other["blk"])


def ffn_kernel(gathered_ref, hidden_ref, cot_ref, gain_ref, wo_ref, wg_ref, wu_ref, wd_ref, *refs):
    out_refs, (low_ref, resid_ref, acc_ref, dmid_ref) = refs[-14:-4], refs[-4:]
    lowt_ref, mid_ref, inner_ref, dgate_ref, dup_ref, out_ref, dres_ref, dbranch_ref, dgain_ref, dattn_ref = out_refs
    n_blk, length, width = gathered_ref.shape
    step = pl.program_id(0)

    @pl.when(step == 0)
    def _():
        for s in range(n_blk):
            low_ref[:, s * width : (s + 1) * width] = gathered_ref[s]
        resid = hidden_ref[...].astype(F32) + dot(low_ref[...], wo_ref[...])
        resid_ref[...] = resid
        normed, _ = rms_parts(resid)
        mid_ref[...] = (normed * gain_ref[...]).astype(BF16)
        acc_ref[...] = jnp.zeros_like(acc_ref)
        dmid_ref[...] = jnp.zeros_like(dmid_ref)
        lowt_ref[...] = low_ref[...].T

    gate = dot(mid_ref[...], wg_ref[...])
    up = dot(mid_ref[...], wu_ref[...])
    d_inner = dot_nt(cot_ref[...], wd_ref[...])
    sigma = 1.0 / (1.0 + jnp.exp(-gate))
    act = gate * sigma
    inner = (act * up).astype(BF16)
    d_gate = (d_inner * up * (sigma * (1.0 + gate * (1.0 - sigma)))).astype(BF16)
    d_up = (d_inner * act).astype(BF16)
    inner_ref[...] = inner.T
    dgate_ref[...] = d_gate.T
    dup_ref[...] = d_up.T
    acc_ref[...] += dot(inner, wd_ref[...])
    dmid_ref[...] += dot_nt(d_gate, wg_ref[...]) + dot_nt(d_up, wu_ref[...])

    @pl.when(step == pl.num_programs(0) - 1)
    def _():
        resid = resid_ref[...]
        out_ref[...] = (resid + acc_ref[...]).astype(BF16)
        normed, inverse = rms_parts(resid)
        d_mid = dmid_ref[...]
        dgain_ref[...] = jnp.sum(d_mid * normed, axis=0, keepdims=True)
        d_resid = cot_ref[...].astype(F32) + norm_back(d_mid * gain_ref[...], normed, inverse)
        dres_ref[...] = d_resid
        d_branch = d_resid.astype(BF16)
        dbranch_ref[...] = d_branch
        back = dot_nt(d_branch, wo_ref[...]).astype(BF16)
        for s in range(n_blk):
            dattn_ref[s] = back[:, s * width : (s + 1) * width]


def feed_forward(row, before, gathered, hidden, cot, gain, w_out, w_gate, w_up, w_down):
    n_blk, length, width = gathered.shape
    tokens, model = hidden.shape
    inner = w_gate.shape[1]
    chunk = 256
    once = lambda a: pl.BlockSpec(a.shape, lambda j: (0,) * len(a.shape), pipeline_mode=pl.Buffered(1))
    whole = lambda a: pl.BlockSpec(a.shape, lambda j: (0,) * len(a.shape))
    cols = pl.BlockSpec((model, chunk), lambda j: (0, j))
    own = pl.BlockSpec((length, model), lambda j: (row, 0), pipeline_mode=pl.Buffered(1))
    mine = pl.BlockSpec((length, model), lambda j: (row, 0))
    turned = pl.BlockSpec((chunk, length), lambda j: (j, row))
    shape = jax.ShapeDtypeStruct
    shared = (
        [shape((model, tokens), BF16), shape((tokens, model), BF16)]
        + [shape((inner, tokens), BF16)] * 3
        + [shape((tokens, model), BF16), shape((tokens, model), F32), shape((tokens, model), BF16)]
    )
    outs = shared + [shape((1, model), F32), shape((n_blk, length, width), BF16)]
    before = list(before or [])
    return pl.pallas_call(
        ffn_kernel,
        grid=(inner // chunk,),
        in_specs=[once(gathered), own, own, once(gain), once(w_out)]
        + [cols, cols, pl.BlockSpec((chunk, model), lambda j: (j, 0))]
        + [pl.BlockSpec(memory_space=pl.ANY)] * len(before),
        out_specs=[pl.BlockSpec((model, length), lambda j: (0, row)), mine]
        + [turned] * 3
        + [mine] * 3
        + [whole(a) for a in outs[8:]],
        out_shape=outs,
        scratch_shapes=[pltpu.VMEM((length, model), BF16)] + [pltpu.VMEM((length, model), F32)] * 3,
        input_output_aliases={8 + k: k for k in range(len(before))},
        compiler_params=pltpu.CompilerParams(vmem_limit_bytes=VMEM_LIMIT),
        cost_estimate=pl.CostEstimate(
            flops=12 * length * model * inner + 4 * length * model * model,
            bytes_accessed=6 * model * inner + 6 * length * inner + 20 * length * model,
            transcendentals=length * inner,
        ),
        name="ffn",
    )(gathered, hidden, cot, gain, w_out, w_gate, w_up, w_down, *before)


class Halving:
    def __init__(self, order, work, sent, landed, send_sem, recv_sem):
        self.order, self.work, self.sent, self.landed = order, work, sent, landed
        self.send_sem, self.recv_sem = send_sem, recv_sem
        self.held = work.shape[1]

    def base(self, stage):
        base = 0
        for earlier in range(1, stage):
            base = base + partner(*self.order[earlier])[0] * (self.held >> earlier)
        return base

    def remote(self, stage, c):
        mine, device = partner(*self.order[stage])
        half = self.held >> stage
        if stage == 0:
            sent = self.sent.at[c]
        else:
            sent = self.work.at[c, pl.ds(self.base(stage) + (1 - mine) * half, half)]
        return pltpu.make_async_remote_copy(
            src_ref=sent,
            dst_ref=self.landed[stage].at[c],
            send_sem=self.send_sem.at[stage, c],
            recv_sem=self.recv_sem.at[stage, c],
            device_id=device,
            device_id_type=MESH,
        )

    def add(self, stage, c):
        base = self.base(stage + 1)

        def one(d, _):
            self.work[c, base + d] = self.work[c, base + d] + self.landed[stage][c, d]
            return 0

        lax.fori_loop(0, self.held >> stage, one, 0)

    def result(self, c):
        stage = len(self.order) - 1
        return self.work[c, self.base(stage + 1)].astype(F32) + self.landed[stage][c, 0].astype(F32)


def store_piece(out_ref, c, piece):
    size, cols = piece.shape[0], out_ref.shape[1] // 128
    row, col = c // cols, c % cols
    out_ref[row * size : (row + 1) * size, col * 128 : (col + 1) * 128] = piece


def tail_kernel(ffn_orders, own_order, qkv_orders, n_dp, n_blk, rows, *refs):
    source = iter(refs)
    take = lambda n: [next(source) for _ in range(n)]
    n_ffn, n_qkv = len(ffn_orders), 3
    ffn_stages, qkv_stages = len(ffn_orders[0]), len(qkv_orders[0])
    cos_ref, sin_ref, gain_ref, small_ref = take(4)
    loads = take(6 + rows)
    keeps, gots = take(n_ffn), take(n_ffn)
    own_keep, own_sent = take(2)
    ffn_outs, (own_out,), qkv_outs = take(n_ffn), take(1), take(n_qkv)
    first_ref, input_ref, total_ref = take(3)
    here = take(6 + rows)
    back_refs, (turned_ref, hidden_ref, dres_ref, *weights) = here[:rows], here[rows:]
    low_ref, acc_ref, vecs, vec_landed = take(4)
    load_sem, keep_sem, got_sem, vec_send, vec_recv = take(5)
    streams = []
    for k, order in enumerate(ffn_orders):
        work, *landed = take(1 + ffn_stages)
        streams.append(Halving(order, work, None, landed, *take(2)))
    work, *landed = take(1 + len(own_order))
    own = Halving(own_order, work, own_sent, landed, *take(2))
    (own_sem,) = take(1)
    own_copy = pltpu.make_async_copy(own_keep, own.work, own_sem)
    late = []
    for u in range(n_qkv):
        late.append([])
        for order in qkv_orders:
            work, sent, *landed = take(2 + qkv_stages)
            late[u].append(Halving(order, work, sent, landed, *take(2)))
    length, width = back_refs[0].shape[3:]
    core, _ = partner("dp", 0)
    counts = [a.shape[0] for a in keeps]

    load = [pltpu.make_async_copy(a, b, load_sem.at[k]) for k, (a, b) in enumerate(zip(loads, here))]
    keep_copy = lambda k, c: pltpu.make_async_copy(keeps[k].at[c], streams[k].work.at[c], keep_sem.at[k, c])
    got_copy = lambda k, c: pltpu.make_async_copy(gots[k].at[c], streams[k].landed[0].at[c], got_sem.at[k, c])
    for copy in load[: rows + 1]:
        copy.start()
    for c in range(max(counts)):
        for k in range(n_ffn):
            if c < counts[k]:
                keep_copy(k, c).start()
                got_copy(k, c).start()
    own_copy.start()
    for copy in load[rows + 1 :]:
        copy.start()

    everyone = qkv_orders[0]
    barrier = pltpu.get_barrier_semaphore()
    for name, bit in everyone:
        pl.semaphore_signal(barrier, inc=1, device_id=partner(name, bit)[1], device_id_type=MESH)
    pl.semaphore_wait(barrier, len(everyone))

    def ffn(c, stage):
        for k, stream in enumerate(streams):
            if c >= counts[k]:
                continue
            if stage == 1:
                keep_copy(k, c).wait()
                got_copy(k, c).wait()
            else:
                stream.remote(stage - 1, c).wait_recv()
            if stage < ffn_stages:
                stream.add(stage - 1, c)
                stream.remote(stage, c).start()
            else:
                store_piece(ffn_outs[k], c, stream.result(c))

    def projections(which):
        for r in range(rows):
            at = pl.ds(r * length, length)
            for s in range(n_blk):
                cols = slice(s * width, (s + 1) * width)
                values = back_refs[r][s, 0, which].astype(F32)
                if which < 2:
                    turned = values * cos_ref[at, :] - swap_halves(values) * sin_ref[at, :]
                else:
                    turned = 0.5 * values
                    first_ref[:, r, cols] = turned
                low_ref[which, at, cols] = turned.astype(BF16)
        for fresh in range(2):
            side = 1 - core if fresh == 0 else core
            left = jnp.concatenate([turned_ref[2 * k + side] for k in range(n_dp // 2)], axis=0)
            size, half = turned_ref.shape[1], turned_ref.shape[1] // 2
            result = dot(left, low_ref[which]).astype(BF16)
            for h, stream in enumerate(late[which]):
                out_ref = stream.sent if fresh == 0 else stream.work
                for d in range(n_dp // 2):
                    for e in range(n_blk):
                        out_ref[0, place_of(stream.order, 2 * d, e)] = result[
                            d * size + h * half : d * size + (h + 1) * half, e * width : (e + 1) * width
                        ]
                if fresh == 0:
                    stream.remote(0, 0).start()

    def own_step(stage):
        if stage == 1:
            own_copy.wait()
        for c in range(own.work.shape[0]):
            own.remote(stage - 1, c).wait_recv()
            if stage < len(own.order):
                own.add(stage - 1, c)
                own.remote(stage, c).start()
            else:
                store_piece(own_out, c, own.result(c))

    def late_step(which, stage):
        for h, stream in enumerate(late[which]):
            stream.remote(stage - 1, 0).wait_recv()
            if stage < qkv_stages:
                stream.add(stage - 1, 0)
                stream.remote(stage, 0).start()
            else:
                half = stream.work.shape[2]
                qkv_outs[which][h * half : (h + 1) * half, :] = stream.result(0)

    def vec_copy(e):
        return pltpu.make_async_remote_copy(
            src_ref=vecs.at[e],
            dst_ref=vec_landed.at[e],
            send_sem=vec_send.at[e],
            recv_sem=vec_recv.at[e],
            device_id=partner(*everyone[e])[1],
            device_id_type=MESH,
        )

    model = hidden_ref.shape[1]
    n_vec = len(everyone)

    def matmul():
        for copy in load[rows + 1 :]:
            copy.wait()
        for r in range(rows):
            at = pl.ds(r * length, length)
            acc_ref[at, :] = (
                dot_nt(low_ref[0, at, :], weights[0][...])
                + dot_nt(low_ref[1, at, :], weights[1][...])
                + dot_nt(low_ref[2, at, :], weights[2][...])
            )

    def norm():
        d_gain = jnp.zeros((1, model), F32)
        for r in range(rows):
            at = pl.ds(r * length, length)
            normed, inverse = rms_parts(hidden_ref[at, :].astype(F32))
            d_normed = acc_ref[at, :]
            d_gain = d_gain + jnp.sum(d_normed * normed, axis=0, keepdims=True)
            input_ref[:, r, :] = dres_ref[at, :] + norm_back(d_normed * gain_ref[...], normed, inverse)
        vecs[0, :, :model] = d_gain
        vecs[0, :, model:] = small_ref[...]
        vec_copy(0).start()

    def vec(e):
        vec_copy(e).wait_recv()
        summed = vecs[e] + vec_landed[e]
        if e == n_vec - 1:
            total_ref[...] = summed
        else:
            vecs[e + 1] = summed
            vec_copy(e + 1).start()

    chunks = range(max(counts))
    for c in range(own.work.shape[0]):
        own.remote(0, c).start()
    for c in chunks:
        ffn(c, 1)
    for copy in load[: rows + 1]:
        copy.wait()
    projections(2)
    projections(1)
    late_step(2, 1)
    own_step(1)
    projections(0)
    late_step(1, 1)
    ffn(0, 2)
    late_step(0, 1)
    matmul()
    own_step(2)
    late_step(2, 2)
    ffn(1, 2)
    norm()
    own_step(3)
    late_step(1, 2)
    ffn(2, 2)
    vecs_left = list(range(n_vec))
    vec(vecs_left.pop(0))
    own_step(4)
    late_step(2, 3)
    late_step(0, 2)
    ffn(3, 2)
    vec(vecs_left.pop(0))
    late_step(1, 3)
    late_step(0, 3)
    for stage in range(4, qkv_stages + 1):
        vec(vecs_left.pop(0))
        for which in (2, 1, 0):
            late_step(which, stage)
    for c in chunks:
        for stage in range(3, ffn_stages + 1):
            ffn(c, stage)
    for e in vecs_left:
        vec(e)

    for stream, count in zip(streams, counts):
        for c in range(count):
            for stage in range(1, ffn_stages):
                stream.remote(stage, c).wait_send()
    for c in range(own.work.shape[0]):
        for stage in range(len(own.order)):
            own.remote(stage, c).wait_send()
    for stream in late[0] + late[1] + late[2]:
        for stage in range(qkv_stages):
            stream.remote(stage, 0).wait_send()
    for e in range(n_vec):
        vec_copy(e).wait_send()


def tail(ffn_pairs, ffn_blocks, ffn_orders, own_pair, own_order, qkv_orders, backs, normed_t, hidden, d_resid, weights, cos, sin, gain, small, collective_id):
    n_dp, n_blk = lax.axis_size("dp"), lax.axis_size("blk")
    tokens, model = hidden.shape
    rows, length = len(backs), backs[0].shape[3]
    keeps, gots = [pair[0] for pair in ffn_pairs], [pair[1] for pair in ffn_pairs]
    loads = [*backs, normed_t.reshape(n_dp, model // n_dp, tokens), hidden, d_resid, *weights]
    ffn_stages, qkv_stages, n_qkv = len(ffn_orders[0]), len(qkv_orders[0]), 3
    n_chunks = max(a.shape[0] for a in keeps)
    block = (model // n_dp, model // n_blk)
    held = n_dp * n_blk // 2
    shape = jax.ShapeDtypeStruct
    vec = (1, model + small.shape[1])
    outs = (
        [shape(a, F32) for a in ffn_blocks]
        + [shape(block, F32)] * n_qkv
        + [shape((length, rows, model), F32)] * 2
        + [shape(vec, F32)]
    )
    scratch = [pltpu.VMEM(a.shape, a.dtype) for a in loads]
    scratch += [
        pltpu.VMEM((n_qkv, tokens, model), BF16),
        pltpu.VMEM((tokens, model), F32),
        pltpu.VMEM((qkv_stages,) + vec, F32),
        pltpu.VMEM((qkv_stages,) + vec, F32),
        pltpu.SemaphoreType.DMA((len(loads),)),
        pltpu.SemaphoreType.DMA((len(keeps), n_chunks)),
        pltpu.SemaphoreType.DMA((len(keeps), n_chunks)),
        pltpu.SemaphoreType.DMA((qkv_stages,)),
        pltpu.SemaphoreType.DMA((qkv_stages,)),
    ]
    for a in keeps:
        scratch.append(pltpu.VMEM(a.shape, BF16))
        scratch += [pltpu.VMEM((a.shape[0], a.shape[1] >> stage) + a.shape[2:], BF16) for stage in range(ffn_stages)]
        scratch += [pltpu.SemaphoreType.DMA((ffn_stages, a.shape[0]))] * 2
    part = (block[0] // len(qkv_orders), block[1])
    keep = own_pair[0]
    scratch.append(pltpu.VMEM(keep.shape, BF16))
    scratch += [pltpu.VMEM((keep.shape[0], keep.shape[1] >> stage) + keep.shape[2:], BF16) for stage in range(len(own_order))]
    scratch += [pltpu.SemaphoreType.DMA((len(own_order), keep.shape[0]))] * 2 + [pltpu.SemaphoreType.DMA]
    for _ in range(n_qkv * len(qkv_orders)):
        scratch += [pltpu.VMEM((1, held) + part, BF16)] * 2
        scratch += [pltpu.VMEM((1, held >> stage) + part, BF16) for stage in range(qkv_stages)]
        scratch += [pltpu.SemaphoreType.DMA((qkv_stages, 1))] * 2
    vmem, anywhere = pl.BlockSpec(memory_space=pltpu.VMEM), pl.BlockSpec(memory_space=pl.ANY)
    return pl.pallas_call(
        functools.partial(tail_kernel, ffn_orders, own_order, qkv_orders, n_dp, n_blk, rows),
        in_specs=[vmem] * 4 + [anywhere] * (len(loads) + 2 * len(keeps) + 2),
        out_specs=[vmem] * len(outs),
        out_shape=outs,
        scratch_shapes=scratch,
        compiler_params=pltpu.CompilerParams(
            collective_id=collective_id, has_side_effects=True, vmem_limit_bytes=60 * 2**20
        ),
        cost_estimate=pl.CostEstimate(flops=10**11, bytes_accessed=10**8, transcendentals=0),
        name="tail",
    )(cos, sin, gain, small, *loads, *keeps, *gots, *own_pair)


def turn_back_kernel(cos_ref, sin_ref, back_ref, low_ref, first_ref):
    n_blk, rows, _, length, width = back_ref.shape
    which = pl.program_id(0)
    for r in range(rows):
        at = pl.ds(r * length, length)
        for s in range(n_blk):
            cols = slice(s * width, (s + 1) * width)
            values = back_ref[s, r, 0].astype(F32)

            @pl.when(which < 2)
            def _():
                cos, sin = cos_ref[at, :width], sin_ref[at, :width]
                wide = values if width == 128 else jnp.concatenate([values, values], axis=1)
                swapped = swap_halves(wide)[:, :width]
                low_ref[0, at, cols] = (values * cos - swapped * sin).astype(BF16)

            @pl.when(which == 2)
            def _():
                first_ref[at, cols] = 0.5 * values
                low_ref[0, at, cols] = (0.5 * values).astype(BF16)


def turn_back(back, cos, sin):
    n_blk, rows, _, length, width = back.shape
    tokens, model = rows * length, n_blk * width
    full = lambda a: pl.BlockSpec(a.shape, lambda w: (0, 0))
    return pl.pallas_call(
        turn_back_kernel,
        grid=(3,),
        in_specs=[full(cos), full(sin), pl.BlockSpec((n_blk, rows, 1, length, width), lambda w: (0, 0, w, 0, 0))],
        out_specs=[
            pl.BlockSpec((1, tokens, model), lambda w: (w, 0, 0)),
            pl.BlockSpec((tokens, model), lambda w: (0, 0)),
        ],
        out_shape=[jax.ShapeDtypeStruct((3, tokens, model), BF16), jax.ShapeDtypeStruct((tokens, model), F32)],
        compiler_params=pltpu.CompilerParams(vmem_limit_bytes=VMEM_LIMIT),
        name="turn_back",
    )(cos, sin, back)


def input_grad_kernel(hidden_ref, dres_ref, gain_ref, low_ref, wq_ref, wk_ref, wv_ref, out_ref, dgain_ref):
    tokens = hidden_ref.shape[0]
    half = tokens // 2
    d_gain = jnp.zeros(dgain_ref.shape, F32)
    for r in range(2):
        at = pl.ds(r * half, half)
        d_normed = (
            dot_nt(low_ref[0, at, :], wq_ref[...])
            + dot_nt(low_ref[1, at, :], wk_ref[...])
            + dot_nt(low_ref[2, at, :], wv_ref[...])
        )
        normed, inverse = rms_parts(hidden_ref[at, :].astype(F32))
        d_gain = d_gain + jnp.sum(d_normed * normed, axis=0, keepdims=True)
        out_ref[at, :] = dres_ref[at, :] + norm_back(d_normed * gain_ref[...], normed, inverse)
    dgain_ref[...] = d_gain


def input_grad(hidden, d_resid, gain, low, w_query, w_key, w_value):
    tokens, model = hidden.shape
    return pl.pallas_call(
        input_grad_kernel,
        out_shape=[jax.ShapeDtypeStruct((tokens, model), F32), jax.ShapeDtypeStruct((1, model), F32)],
        compiler_params=pltpu.CompilerParams(vmem_limit_bytes=VMEM_LIMIT),
        cost_estimate=pl.CostEstimate(
            flops=6 * tokens * model * model, bytes_accessed=6 * model * model + 16 * tokens * model, transcendentals=0
        ),
        name="input_grad",
    )(hidden, d_resid, gain, low, w_query, w_key, w_value)


def rms_parts(values):
    inverse_rms = lax.rsqrt(jnp.mean(values * values, axis=-1, keepdims=True) + EPS)
    return values * inverse_rms, inverse_rms


def norm_back(d_normed, normed, inverse_rms):
    return inverse_rms * (d_normed - normed * jnp.mean(d_normed * normed, axis=-1, keepdims=True))


def rope_tables(doc_lengths, offset, length):
    half = HEAD_DIM // 2
    places = offset + jnp.arange(length, dtype=jnp.int32)
    ends = jnp.cumsum(doc_lengths, axis=1)
    start = jnp.max(jnp.where(ends[:, None, :] <= places[None, :, None], ends[:, None, :], 0), axis=2)
    position = (places[None, :] - start).astype(F32).reshape(-1, 1)
    lane = jnp.arange(128, dtype=jnp.int32)
    freq = jnp.power(10000.0, -(lane % half).astype(F32) * 2.0 / HEAD_DIM)
    angles = position * freq[None, :]
    sign = jnp.where(lane % HEAD_DIM < half, -1.0, 1.0)
    return jnp.cos(angles), jnp.sin(angles) * sign[None, :]


def body(
    hidden_in,
    first_values,
    doc_lengths,
    w_query,
    w_key,
    w_value,
    w_out,
    w_gate,
    w_up,
    w_down,
    attn_gain,
    ffn_gain,
    out_cotangent,
):
    length, rows, model = hidden_in.shape
    n_docs = doc_lengths.shape[1]
    n_blk, n_dp = lax.axis_size("blk"), lax.axis_size("dp")
    width = model // n_blk
    tokens = rows * length
    flat = lambda a: jnp.transpose(a, (1, 0, 2)).reshape(tokens, model)
    unflat = lambda a: jnp.transpose(a.reshape(rows, length, model), (1, 0, 2))
    lens = doc_lengths.reshape(-1)

    hidden, cot, first = flat(hidden_in), flat(out_cotangent), flat(first_values)
    row_gain = lambda gain: gain.reshape(1, model)

    cos, sin = rope_tables(doc_lengths, lax.axis_index("blk") * length, length)
    *qkv_own, normed_in, sums = project_qkv(
        hidden, first, cos, sin, row_gain(attn_gain), w_query, w_key, w_value, rows, n_blk
    )
    qkv, attended, lse, gathered = [], [], [], []
    for r in range(rows):
        qkv.append(exchange(qkv_own[r]))
    for r in range(rows):
        o_f, o_low, lse_r = attn_fwd(lens, qkv[r], r, n_docs)
        attended.append(o_f)
        lse.append(lse_r)
        gathered.append(exchange(o_low))
    shared, d_gains, d_attn = None, [], []
    for r in range(rows):
        *shared, d_gain, d_attn_r = feed_forward(
            r, shared, gathered[r], hidden, cot, row_gain(ffn_gain), w_out, w_gate, w_up, w_down
        )
        d_gains.append(d_gain)
        d_attn.append(d_attn_r)
    attn_low_t, normed_mid, inner_t, d_gate_t, d_up_t, block_out, d_resid_mid, d_branch = shared
    d_gain_two = sum(d_gains)

    inner = w_gate.shape[1]
    by_blocks = (model // n_dp) % 128 == 0 and width == 128 and (inner // n_blk) % 32 == 0
    early, late, middle = block_order(False), block_order(True), z_order()
    if by_blocks:
        orders = (early, late, middle)
        pieces = (0, 1, 2, 3)
        exchanged = lambda pairs, stages: [(keep, swap(sent, *stage)) for (keep, sent), stage in zip(pairs, stages)]
        folded, d_own = ffn_wgrad(
            (
                (early, pieces, [(False, d_gate_t, normed_mid)]),
                (late, pieces, [(False, d_up_t, normed_mid)]),
                (middle, pieces, [(True, inner_t, cot)]),
            ),
            d_attn,
            10**9,
            1,
        )
        ffn_pairs = exchanged(folded, [order[1] for order in orders])
        back_own = [
            attn_bwd(lens, qkv[r : r + 1], d_own[r : r + 1], attended[r : r + 1], lse[r : r + 1], r, n_docs)
            for r in range(rows)
        ]
        backs = [exchange(b) for b in back_own[:-1]]
        kept = [keep for keep, got in ffn_pairs]
        token, kept = lax.optimization_barrier((back_own, kept))
        second = [order[2] for order in orders]
        folded = fold([(keep, got) for keep, (_, got) in zip(kept, ffn_pairs)], second, 10**9)
        ffn_pairs = exchanged(folded, second)
        folded, attn_low_t = lax.optimization_barrier((folded, attn_low_t))
        ffn_pairs = [(keep, got) for (keep, _), (_, got) in zip(folded, ffn_pairs)]
        project, back_last = ffn_wgrad(
            ((early, pieces, [(True, attn_low_t, d_branch)]),), back_own[-1:], LAST_FLOPS, 2
        )
        backs += back_last
    else:
        d_own = [exchange(d_attn[r]) for r in range(rows)]
        back = exchange(attn_bwd(lens, qkv, d_own, attended, lse, 0, n_docs))

    squares = jnp.sum(sums, axis=(0, 2)).reshape(1, 2)
    small = jnp.concatenate([d_gain_two, squares, jnp.zeros((1, 126), F32)], axis=1)
    if by_blocks:
        *blocks, grad_first, grad_input, small = tail(
            ffn_pairs,
            ((inner // n_blk, model // n_dp),) * 2 + ((inner // n_dp, model // n_blk), (model // n_dp, model // n_blk)),
            tuple(order[2:] for order in orders),
            project[0],
            early[1:],
            (early, late),
            backs,
            normed_in.T,
            hidden,
            d_resid_mid,
            (w_query, w_key, w_value),
            cos,
            sin,
            row_gain(attn_gain),
            small,
            0,
        )
        small = small.reshape(-1)
        grad_gate, grad_up = blocks[0].T, blocks[1].T
        grad_down, grad_project = blocks[2:4]
        grad_query, grad_key, grad_value = blocks[4:]
    else:
        low, grad_first = turn_back(back, cos, sin)
        mid_cf, in_cf = core_first(normed_mid), core_first(normed_in)
        sent = lambda a, b, name, y: scatter(dot_tn(a, b).astype(BF16), name, y).astype(F32)
        grad_down = sent(inner_t.T, y_first(cot), "dp", False)
        grad_gate = sent(d_gate_t.T, mid_cf, "blk", False).T
        grad_up = sent(d_up_t.T, mid_cf, "blk", True).T
        grad_project = sent(d_branch, core_first(attn_low_t.T), "blk", True).T
        grad_query, grad_key, grad_value = [sent(low[k], in_cf, "blk", True).T for k in range(3)]
        grad_first = unflat(grad_first)
        grad_input, d_gain_one = input_grad(hidden, d_resid_mid, row_gain(attn_gain), low, w_query, w_key, w_value)
        grad_input = unflat(grad_input)
        small = total(jnp.concatenate([d_gain_one.reshape(model), small.reshape(-1)]))
    n_entries = n_blk * length * rows * n_dp * model
    return (
        unflat(block_out),
        grad_input,
        grad_first,
        grad_query,
        grad_key,
        grad_value,
        grad_project,
        grad_gate,
        grad_up,
        grad_down,
        small[:model],
        small[model : 2 * model],
        small[2 * model] / n_entries,
        small[2 * model + 1] / n_entries,
    )


def solution(mesh):
    tokens = P("blk", "dp", None)
    return jax.shard_map(
        body,
        mesh=mesh,
        in_specs=(tokens, tokens, P("dp", None)) + (P(),) * 9 + (tokens,),
        out_specs=(tokens,) * 3 + (P("dp", "blk"),) * 7 + (P(),) * 4,
        check_vma=False,
    )
```
